32 devices in a mesh: dp: 8 (over z, x), mp: 4 (over y, core).
Axes of the slice: x: 2, y: 2, z: 4, core: 2. Of those that a mesh axis runs over, the one named last changes fastest.
Arguments:
- tokens: bfloat16 [8192, 2048], P('dp'), may hold values from -24 to 24
- doc_ids: int32 [8192], P('dp'), may hold values from 0 to 1, as said below
- q_weight: bfloat16 [2048, 2048], P('dp', 'mp'), may hold values from -0.125 to 0.125
- k_weight: bfloat16 [2048, 2048], P('dp', 'mp'), may hold values from -0.125 to 0.125
- v_weight: bfloat16 [2048, 2048], P('dp', 'mp'), may hold values from -0.125 to 0.125
- o_weight: bfloat16 [2048, 2048], P('mp', 'dp'), may hold values from -0.125 to 0.125
- q_gain: bfloat16 [16, 128], P('mp', 'dp'), may hold values from 0.25 to 1.75
- k_gain: bfloat16 [16, 128], P('mp', 'dp'), may hold values from 0.25 to 1.75
- attn_gain: bfloat16 [2048], P('dp'), may hold values from 0.25 to 1.75
- gate_weight: bfloat16 [2048, 8192], P('dp', 'mp'), may hold values from -0.125 to 0.125
- up_weight: bfloat16 [2048, 8192], P('dp', 'mp'), may hold values from -0.125 to 0.125
- down_weight: bfloat16 [8192, 2048], P('mp', 'dp'), may hold values from -0.0625 to 0.0625
- mlp_gain: bfloat16 [2048], P('dp'), may hold values from 0.25 to 1.75
- cotangent: bfloat16 [8192, 2048], P('dp'), may hold values from -6 to 6
Outputs:
- block_out: bfloat16 [8192, 2048], P('dp')
- grad_tokens: bfloat16 [8192, 2048], P('dp')
- grad_q_weight: float32 [2048, 2048], P('dp', 'mp')
- grad_k_weight: float32 [2048, 2048], P('dp', 'mp')
- grad_v_weight: float32 [2048, 2048], P('dp', 'mp')
- grad_o_weight: float32 [2048, 2048], P('mp', 'dp')
- grad_q_gain: float32 [16, 128], P('mp', 'dp')
- grad_k_gain: float32 [16, 128], P('mp', 'dp')
- grad_attn_gain: float32 [2048], P('dp')
- grad_gate_weight: float32 [2048, 8192], P('dp', 'mp')
- grad_up_weight: float32 [2048, 8192], P('dp', 'mp')
- grad_down_weight: float32 [8192, 2048], P('mp', 'dp')
- grad_mlp_gain: float32 [2048], P('dp')
The draws below stay inside these ranges and needn't reach their ends.
Inputs may be any that keep to these rules, and one draw needn't show every extreme that they name: `doc_ids`: each aligned run of 1024 tokens holds two documents, ids 0 then 1; the first is 256 to 768 tokens long.
All inputs are finite; a program needn't handle non-finite values.
Results may differ from the reference program's by a relative error of at most 0.02.
Values may be sent and summed in bfloat16 or wider, within the bound.
A program may use at most 256 MiB of HBM per device.

```python
import math
import jax
import jax.numpy as jnp
from jax import lax

D = 2048
HEADS = 16
HEAD_CHANNELS = 128
FF = 8192
SEQ_LEN = 1024
TOKENS = 8192


def draw_tokens(key, part):
    base_key = jax.random.fold_in(key, 101)
    first_key, second_key, third_key = jax.random.split(base_key, 3)
    entries = jnp.clip(jax.random.normal(first_key, (TOKENS, D), jnp.float32), -4.0, 4.0)
    row_scale = jnp.exp(jax.random.uniform(second_key, (TOKENS, 1), jnp.float32, math.log(0.3), math.log(3.0)))
    column_scale = jnp.exp(jax.random.uniform(third_key, (1, D), jnp.float32, math.log(0.5), math.log(2.0)))
    return (entries * row_scale * column_scale).astype(jnp.bfloat16)


def draw_doc_ids(key, part):
    cut_key = jax.random.fold_in(key, 7)
    sequences = TOKENS // SEQ_LEN
    cuts = jax.random.randint(cut_key, (sequences, 1), SEQ_LEN // 4, 3 * SEQ_LEN // 4 + 1, dtype=jnp.int32)
    places = jnp.arange(SEQ_LEN, dtype=jnp.int32)[None, :]
    return (places >= cuts).astype(jnp.int32).reshape(-1)


def spiked(result, own_key, source, target, blocks, factor):
    owner, partner = [(jnp.arange(result.shape[position]) // (result.shape[position] // blocks)).reshape([-1 if axis == position else 1 for axis in range(result.ndim)]) for position in (source, target)]
    chosen = jax.random.permutation(own_key, blocks)[partner]
    strong = (owner == chosen) | (owner == (partner + blocks // 2) % blocks)
    return jnp.where(strong, factor * result, result)


def shard_levels(rng, extent, cuts, least, largest):
    gain = 1.0
    for position, blocks in cuts:
        heights = jax.random.uniform(jax.random.fold_in(jax.random.fold_in(rng, 6), position), (blocks,), jnp.float32, least / len(cuts), largest / len(cuts))
        gain = gain * jnp.repeat(jnp.exp(heights), extent[position] // blocks).reshape((-1,) + (1,) * (len(extent) - 1 - position))
    return gain


def normal_values(rng, dims, spread, reach, cuts=(), held_as=jnp.bfloat16):
    values = spread * jax.random.normal(rng, dims, jnp.float32)
    if cuts:
        values = values * shard_levels(rng, dims, cuts, -0.22, 0.18)
    return jnp.clip(values, -reach, reach).astype(held_as)


def heavy_noise(key, extent, scale, bound, shards, heavy, held_as=jnp.bfloat16):
    result = scale * jax.random.normal(key, extent, jnp.float32)
    if shards:
        result = result * shard_levels(key, extent, shards, -0.22, 0.18)
    return jnp.clip(spiked(result, jax.random.fold_in(key, 3), *heavy), -bound, bound).astype(held_as)


def setup_inputs(seed: int = 0) -> dict:
    splits = jax.random.split(jax.random.key(seed), 15)
    return {
        "tokens": draw_tokens(jax.random.fold_in(splits[14], 71), 0),
        "doc_ids": draw_doc_ids(jax.random.fold_in(splits[14], 71), 0),
        "q_weight": normal_values(splits[2], (D, D), D ** -0.5, 0.125, ((0, 8), (1, 4))),
        "k_weight": normal_values(splits[3], (D, D), D ** -0.5, 0.125, ((0, 8), (1, 4))),
        "v_weight": normal_values(splits[4], (D, D), D ** -0.5, 0.125, ((0, 8), (1, 4))),
        "o_weight": normal_values(splits[5], (D, D), D ** -0.5, 0.125, ((0, 4), (1, 8))),
        "q_gain": jnp.clip(1.0 + 0.15 * jax.random.normal(splits[6], (HEADS, HEAD_CHANNELS), jnp.float32), 0.25, 1.75).astype(jnp.bfloat16),
        "k_gain": jnp.clip(1.0 + 0.15 * jax.random.normal(splits[7], (HEADS, HEAD_CHANNELS), jnp.float32), 0.25, 1.75).astype(jnp.bfloat16),
        "attn_gain": jnp.clip(1.0 + 0.15 * jax.random.normal(splits[8], (D,), jnp.float32), 0.25, 1.75).astype(jnp.bfloat16),
        "gate_weight": normal_values(splits[9], (D, FF), D ** -0.5, 0.125, ((0, 8), (1, 4))),
        "up_weight": normal_values(splits[10], (D, FF), D ** -0.5, 0.125, ((0, 8), (1, 4))),
        "down_weight": normal_values(splits[11], (FF, D), FF ** -0.5, 0.0625, ((0, 4), (1, 8))),
        "mlp_gain": jnp.clip(1.0 + 0.15 * jax.random.normal(splits[12], (D,), jnp.float32), 0.25, 1.75).astype(jnp.bfloat16),
        "cotangent": heavy_noise(splits[13], (TOKENS, D), 1.0, 6.0, ((0, 8),), (0, 1, 8, 2.0)),
    }


EPSILON = 1e-06
ROPE_BASE = 500000.0
MASKED = -1e+30
PRECISE = lax.Precision.HIGHEST

@jax.custom_vjp
def low(v):
    return lax.optimization_barrier(v.astype(jnp.bfloat16)).astype(jnp.float32)

@jax.custom_vjp
def low_back(v):
    return v

def low_keep(v):
    return (low(v), None)

def low_pass(kept, grad):
    return (grad,)

def back_keep(v):
    return (v, None)

def back_low(kept, grad):
    return (low(grad),)
low.defvjp(low_keep, low_pass)
low_back.defvjp(back_keep, back_low)

def matmul(left_side, right_side):
    return jnp.dot(left_side, right_side, precision=PRECISE)

def rms_scale(vectors):
    return lax.rsqrt(lax.optimization_barrier(jnp.mean(vectors * vectors, axis=-1, keepdims=True)) + EPSILON)

def angles_of(doc_rows, seq_len, head_dim):
    shaped = doc_rows.reshape(-1, seq_len)
    leading = lax.optimization_barrier(jnp.sum(1 - shaped, axis=1, keepdims=True, dtype=jnp.int32))
    places = jnp.arange(seq_len, dtype=jnp.int32)[None, :] - shaped * leading
    frequency = jnp.exp(jnp.arange(head_dim // 2, dtype=jnp.float32) * (-2.0 * math.log(ROPE_BASE) / head_dim))
    return places.reshape(-1).astype(jnp.float32)[:, None] * frequency[None, :]

def rotate(vectors, angles):
    halfway = vectors.shape[-1] // 2
    cosine = jnp.cos(angles)[:, None, :]
    sine_wave = jnp.sin(angles)[:, None, :]
    former = vectors[..., :halfway]
    latter = vectors[..., halfway:]
    return jnp.concatenate([former * cosine - latter * sine_wave, latter * cosine + former * sine_wave], axis=-1)

def attend_one(inputs):
    query_seq, key_seq, value_seq, doc_seq = inputs
    factor = 1.0 / math.sqrt(query_seq.shape[-1])
    scores = jnp.einsum('qhd,khd->hqk', query_seq, key_seq, precision=PRECISE) * factor
    places = jnp.arange(query_seq.shape[0], dtype=jnp.int32)
    allowed = (places[None, :] <= places[:, None]) & (doc_seq[None, :] == doc_seq[:, None])
    scores = jnp.where(allowed[None], scores, MASKED)
    scores = low_back(scores)
    weights = low(jax.nn.softmax(scores, axis=-1))
    return jnp.einsum('hqk,khd->qhd', weights, value_seq, precision=PRECISE)

def forward(tokens, q_weight, k_weight, v_weight, o_weight, q_gain, k_gain, attn_gain, gate_weight, up_weight, down_weight, mlp_gain, angles, doc_ids):
    heads_all = q_gain.shape[0]
    head_width = q_gain.shape[1]
    sequences = tokens.shape[0] // SEQ_LEN
    q_raw = low_back(matmul(tokens, q_weight))
    k_raw = low_back(matmul(tokens, k_weight))
    values = low(low_back(matmul(tokens, v_weight)))
    q_norm = q_raw * rms_scale(q_raw) * q_gain.reshape(-1)
    k_norm = k_raw * rms_scale(k_raw) * k_gain.reshape(-1)
    q_rot = low(rotate(q_norm.reshape(-1, heads_all, head_width), angles))
    k_rot = low(rotate(k_norm.reshape(-1, heads_all, head_width), angles))
    value_heads = values.reshape(-1, heads_all, head_width)
    attended = lax.map(jax.checkpoint(attend_one), (q_rot.reshape(sequences, SEQ_LEN, heads_all, head_width), k_rot.reshape(sequences, SEQ_LEN, heads_all, head_width), value_heads.reshape(sequences, SEQ_LEN, heads_all, head_width), doc_ids.reshape(sequences, SEQ_LEN)))
    attended = low(low_back(attended.reshape(tokens.shape[0], -1)))
    branch = low_back(matmul(attended, o_weight))
    hidden_state = tokens + branch * rms_scale(branch) * attn_gain
    hidden_low = low(hidden_state)
    gate_act = low_back(matmul(hidden_low, gate_weight))
    up_part = low_back(matmul(hidden_low, up_weight))
    product = low(jax.nn.silu(gate_act) * up_part)
    mlp_branch = low_back(matmul(product, down_weight))
    return hidden_state + mlp_branch * rms_scale(mlp_branch) * mlp_gain

def reference(tokens, doc_ids, q_weight, k_weight, v_weight, o_weight, q_gain, k_gain, attn_gain, gate_weight, up_weight, down_weight, mlp_gain, cotangent):
    angles = angles_of(doc_ids, SEQ_LEN, HEAD_CHANNELS)

    def run_layer(tok_in, wq_in, wk_in, wv_in, wo_in, qg_in, kg_in, ag_in, wg_in, wu_in, wd_in, mg_in):
        return forward(tok_in, wq_in, wk_in, wv_in, wo_in, qg_in, kg_in, ag_in, wg_in, wu_in, wd_in, mg_in, angles, doc_ids)
    layer_result, pullback = jax.vjp(run_layer, tokens.astype(jnp.float32), q_weight.astype(jnp.float32), k_weight.astype(jnp.float32), v_weight.astype(jnp.float32), o_weight.astype(jnp.float32), q_gain.astype(jnp.float32), k_gain.astype(jnp.float32), attn_gain.astype(jnp.float32), gate_weight.astype(jnp.float32), up_weight.astype(jnp.float32), down_weight.astype(jnp.float32), mlp_gain.astype(jnp.float32))
    grads = pullback(cotangent.astype(jnp.float32))
    return (layer_result.astype(jnp.bfloat16), grads[0].astype(jnp.bfloat16), grads[1], grads[2], grads[3], grads[4], grads[5], grads[6], grads[7], grads[8], grads[9], grads[10], grads[11])
```

```python
import math

import jax
import jax.numpy as jnp
from jax import lax
from jax.sharding import PartitionSpec as P

D = 2048
HEAD_CHANNELS = 128
SEQ_LEN = 1024
RING_MAX = 8


EPSILON = 1e-06
ROPE_BASE = 500000.0
MASKED = -1e30
ROW_LIMIT = 512

CORE_SWAP = ((0, 1), (1, 0), (2, 3), (3, 2))
FAR_SWAP = ((0, 2), (2, 0), (1, 3), (3, 1))


def matmul(left_side, right_side):
    return jnp.dot(left_side, right_side, preferred_element_type=jnp.float32)


def transposed_left(left_side, right_side):
    return lax.dot_general(
        left_side, right_side, (((0,), (0,)), ((), ())), preferred_element_type=jnp.float32
    )


def transposed_right(left_side, right_side):
    return lax.dot_general(
        left_side, right_side, (((1,), (1,)), ((), ())), preferred_element_type=jnp.float32
    )


def angles_of(doc_rows, seq_len, head_dim):
    shaped = doc_rows.reshape(-1, seq_len)
    leading = jnp.sum(1 - shaped, axis=1, keepdims=True, dtype=jnp.int32)
    places = jnp.arange(seq_len, dtype=jnp.int32)[None, :] - shaped * leading
    frequency = jnp.exp(
        jnp.arange(head_dim // 2, dtype=jnp.float32) * (-2.0 * math.log(ROPE_BASE) / head_dim)
    )
    return places.reshape(-1).astype(jnp.float32)[:, None] * frequency[None, :]


def rotate(vectors, angles):
    halfway = vectors.shape[-1] // 2
    cosine = jnp.cos(angles)[:, None, :]
    sine_wave = jnp.sin(angles)[:, None, :]
    former = vectors[..., :halfway]
    latter = vectors[..., halfway:]
    return jnp.concatenate(
        [former * cosine - latter * sine_wave, latter * cosine + former * sine_wave], axis=-1
    )


def rotate_back(vectors, angles):
    halfway = vectors.shape[-1] // 2
    cosine = jnp.cos(angles)[:, None, :]
    sine_wave = jnp.sin(angles)[:, None, :]
    former = vectors[..., :halfway]
    latter = vectors[..., halfway:]
    return jnp.concatenate(
        [former * cosine + latter * sine_wave, latter * cosine - former * sine_wave], axis=-1
    )


def block_scores(query_block, key_seq, doc_seq, offset):
    factor = 1.0 / math.sqrt(query_block.shape[-1])
    scores = (
        jnp.einsum("qhd,khd->hqk", query_block, key_seq, preferred_element_type=jnp.float32)
        * factor
    )
    row_places = offset + jnp.arange(query_block.shape[0], dtype=jnp.int32)
    key_places = jnp.arange(key_seq.shape[0], dtype=jnp.int32)
    row_docs = doc_seq[offset : offset + query_block.shape[0]]
    allowed = (key_places[None, :] <= row_places[:, None]) & (doc_seq[None, :] == row_docs[:, None])
    return jnp.where(allowed[None], scores, MASKED)


def attend_sequence(inputs):
    query_seq, key_seq, value_seq, doc_seq = inputs
    row_block = math.gcd(query_seq.shape[0], ROW_LIMIT)
    outputs = []
    totals = []
    for offset in range(0, query_seq.shape[0], row_block):
        scores = block_scores(query_seq[offset : offset + row_block], key_seq, doc_seq, offset)
        maximum = jnp.max(scores, axis=-1, keepdims=True)
        weights = jnp.exp(scores - maximum)
        denominator = jnp.sum(weights, axis=-1, keepdims=True)
        rounded = (weights / denominator).astype(jnp.bfloat16)
        outputs.append(
            jnp.einsum(
                "hqk,khd->qhd", rounded, value_seq, preferred_element_type=jnp.float32
            ).astype(jnp.bfloat16)
        )
        totals.append((maximum + jnp.log(denominator))[..., 0])
    return (jnp.concatenate(outputs, axis=0), jnp.concatenate(totals, axis=1))


def attend_backward(inputs):
    query_seq, key_seq, value_seq, doc_seq, grad_seq, lse_seq = inputs
    row_block = math.gcd(query_seq.shape[0], ROW_LIMIT)
    factor = 1.0 / math.sqrt(query_seq.shape[-1])
    grad_keys = jnp.zeros(key_seq.shape, jnp.float32)
    grad_values = jnp.zeros(value_seq.shape, jnp.float32)
    grad_rows = []
    for offset in range(0, query_seq.shape[0], row_block):
        query_block = query_seq[offset : offset + row_block]
        grad_block = grad_seq[offset : offset + row_block]
        scores = block_scores(query_block, key_seq, doc_seq, offset)
        weights = jnp.exp(scores - lse_seq[:, offset : offset + row_block, None])
        d_weights = jnp.einsum(
            "qhd,khd->hqk", grad_block, value_seq, preferred_element_type=jnp.float32
        )
        correction = jnp.sum(d_weights * weights, axis=-1, keepdims=True)
        d_scores = (weights * (d_weights - correction)).astype(jnp.bfloat16)
        grad_rows.append(
            jnp.einsum("hqk,khd->qhd", d_scores, key_seq, preferred_element_type=jnp.float32)
            * factor
        )
        grad_keys = (
            grad_keys
            + jnp.einsum("hqk,qhd->khd", d_scores, query_block, preferred_element_type=jnp.float32)
            * factor
        )
        grad_values = grad_values + jnp.einsum(
            "hqk,qhd->khd",
            weights.astype(jnp.bfloat16),
            grad_block,
            preferred_element_type=jnp.float32,
        )
    return (jnp.concatenate(grad_rows, axis=0), grad_keys, grad_values)


def after(value, earlier):
    if earlier is None:
        return value
    return lax.optimization_barrier((value, earlier))[0]


class Ring:
    def __init__(self, n):
        self.n = n
        self.order = [*range(0, n, 2), *range(n - 1 - n % 2, 0, -2)]
        index = lax.axis_index("dp")
        self.index = index
        self.place = jnp.where(index % 2 == 0, index // 2, n - 1 - index // 2)
        pairs = [(self.order[i], self.order[(i + 1) % n]) for i in range(n)]
        self.ways = (pairs, [(b, a) for a, b in pairs])

    def holder(self, steps):
        place = (self.place + steps + 2 * self.n) % self.n
        return jnp.where(place < self.n // 2, 2 * place, 2 * (self.n - 1 - place) + 1)

    def gathers(self, shards, gates):
        n = self.n
        held, full, marks = [], [], []
        for shard, gate in zip(shards, gates):
            rows, width = shard.shape
            halves = after(shard, gate).reshape(2, rows // 2, width)
            held.append([halves[0], halves[1]])
            start = jnp.zeros((n, 2, rows // 2, width), shard.dtype)
            full.append(lax.dynamic_update_slice(start, halves[None], (self.index, 0, 0, 0)))
            marks.append(None)
        for step in range(1, n):
            for unit in range(len(shards)):
                for way in range(2):
                    got = lax.ppermute(held[unit][way], "dp", self.ways[way])
                    held[unit][way] = got
                    source = self.holder(-step if way == 0 else step)
                    full[unit] = lax.dynamic_update_slice(
                        full[unit], got[None, None], (source, way, 0, 0)
                    )
                if step == n - 2:
                    marks[unit] = tuple(held[unit])
        return [f.reshape(-1, f.shape[-1]) for f in full], marks

    def scatters(self, grads, gates):
        n = self.n
        local, held, marks, outs = [], [], [], []
        for grad, gate in zip(grads, gates):
            rows, width = grad.shape[0] // n, grad.shape[1]
            parts = grad.reshape(n, 2, rows // 2, width)
            local.append(parts)
            held.append(
                [after(self.part(parts, way, -1 if way == 0 else 1), gate) for way in range(2)]
            )
            marks.append(None)
            outs.append([None, None])
        for step in range(1, n):
            for unit in range(len(grads)):
                for way in range(2):
                    got = lax.ppermute(held[unit][way], "dp", self.ways[way])
                    own = self.part(local[unit], way, -1 - step if way == 0 else 1 + step)
                    total = got.astype(jnp.float32) + own.astype(jnp.float32)
                    if step == n - 1:
                        outs[unit][way] = total
                    held[unit][way] = total.astype(jnp.bfloat16)
                if step == n - 2:
                    marks[unit] = tuple(held[unit])
        return [jnp.concatenate(o, axis=0) for o in outs], marks

    def part(self, parts, way, steps):
        spot = self.holder(steps)
        return lax.dynamic_slice(parts, (spot, way, 0, 0), (1, 1, *parts.shape[2:]))[0, 0]


class Plain:
    def __init__(self, n):
        self.n = n

    def gathers(self, shards, gates):
        full = [lax.all_gather(shard, "dp", axis=0, tiled=True) for shard in shards]
        return full, [None] * len(shards)

    def scatters(self, grads, gates):
        outs = [
            lax.psum_scatter(grad, "dp", scatter_dimension=0, tiled=True).astype(jnp.float32)
            for grad in grads
        ]
        return outs, [None] * len(grads)


def small_gather(packed, n):
    index = lax.axis_index("dp")
    parts = [packed]
    for shift in range(1, n):
        parts.append(lax.ppermute(packed, "dp", [(i, (i + shift) % n) for i in range(n)]))
    ascending = jnp.stack(parts[::-1])
    doubled = jnp.concatenate([ascending, ascending], axis=0)
    return lax.dynamic_slice(doubled, (n - 1 - index, 0), (n, packed.shape[0]))


def small_scatter(table, n):
    index = lax.axis_index("dp")
    total = lax.dynamic_index_in_dim(table, index, 0, keepdims=False)
    for shift in range(1, n):
        row = lax.dynamic_index_in_dim(table, (index + shift) % n, 0, keepdims=False)
        total = total + lax.ppermute(row, "dp", [(i, (i + shift) % n) for i in range(n)])
    return total


def small_sum(values):
    values = values + lax.ppermute(values, "mp", CORE_SWAP)
    return values + lax.ppermute(values, "mp", FAR_SWAP)


def half_of(full, core):
    rows = full.shape[0] // 2
    return lax.dynamic_index_in_dim(full.reshape(2, rows, -1), core, 0, keepdims=False)


def half_sum(partial, core):
    low = partial.astype(jnp.bfloat16)
    got = lax.ppermute(half_of(low, 1 - core), "mp", CORE_SWAP)
    pair = half_of(low, core).astype(jnp.float32) + got.astype(jnp.float32)
    pair = lax.reduce_precision(pair, 8, 7)
    far = lax.ppermute(pair.astype(jnp.bfloat16), "mp", FAR_SWAP)
    return pair + far.astype(jnp.float32)


def join_halves(half, core):
    got = lax.ppermute(half, "mp", CORE_SWAP)
    first = jnp.where(core == 0, half, got)
    second = jnp.where(core == 0, got, half)
    return jnp.concatenate([first, second], axis=0)


def on_device(
    n,
    tokens,
    doc_ids,
    q_weight,
    k_weight,
    v_weight,
    o_weight,
    q_gain,
    k_gain,
    attn_gain,
    gate_weight,
    up_weight,
    down_weight,
    mlp_gain,
    cotangent,
):
    core = lax.axis_index("mp") % 2
    net = Ring(n) if n <= RING_MAX else Plain(n)
    row_count = tokens.shape[0]
    heads = q_gain.shape[0]
    width = heads * HEAD_CHANNELS
    sequences = row_count // SEQ_LEN
    seq_shape = (sequences, SEQ_LEN, heads, HEAD_CHANNELS)

    shard_a = jnp.concatenate([q_weight, k_weight], axis=1)
    shard_b = jnp.concatenate([v_weight, o_weight.T], axis=1)
    down_shard = down_weight.T
    ff_half = down_shard.shape[1] // 2
    (qk_full, vo_full), marks = net.gathers([shard_a, shard_b], [None, None])
    (gate_full, up_full), marks = net.gathers([gate_weight, up_weight], marks)
    (down_left, down_right), marks = net.gathers(
        [down_shard[:, :ff_half], down_shard[:, ff_half:]], marks
    )

    packed = jnp.concatenate(
        [q_gain.reshape(-1), k_gain.reshape(-1), attn_gain, mlp_gain], axis=0
    )
    gains = small_gather(packed, n)
    head_part = q_gain.size
    col_part = attn_gain.size
    query_scale = gains[:, :head_part].reshape(n, heads, -1).transpose(1, 0, 2).reshape(-1)
    key_scale = (
        gains[:, head_part : 2 * head_part].reshape(n, heads, -1).transpose(1, 0, 2).reshape(-1)
    )
    attn_gains = gains[:, 2 * head_part : 2 * head_part + col_part].reshape(-1)
    mlp_gains = gains[:, 2 * head_part + col_part :].reshape(-1)

    angles = angles_of(doc_ids, SEQ_LEN, HEAD_CHANNELS)
    doc_seqs = doc_ids.reshape(sequences, SEQ_LEN)
    token_half = half_of(tokens, core).astype(jnp.float32)
    upstream = half_of(cotangent, core).astype(jnp.float32)

    query_key = matmul(tokens, qk_full)
    query_raw = query_key[:, :width]
    key_raw = query_key[:, width:]
    value_full = vo_full[:, :width]
    output_full = vo_full[:, width:]
    values = matmul(tokens, value_full).astype(jnp.bfloat16)
    squares = small_sum(
        jnp.stack([jnp.sum(query_raw * query_raw, axis=1), jnp.sum(key_raw * key_raw, axis=1)])
    )
    query_inv = lax.rsqrt(squares[0] / D + EPSILON)[:, None]
    key_inv = lax.rsqrt(squares[1] / D + EPSILON)[:, None]
    query_rot = rotate(
        (query_raw * query_inv * query_scale).reshape(row_count, heads, HEAD_CHANNELS), angles
    ).astype(jnp.bfloat16)
    key_rot = rotate(
        (key_raw * key_inv * key_scale).reshape(row_count, heads, HEAD_CHANNELS), angles
    ).astype(jnp.bfloat16)
    query_seqs = query_rot.reshape(seq_shape)
    key_seqs = key_rot.reshape(seq_shape)
    value_seqs = values.reshape(seq_shape)
    attended, lse_all = lax.map(attend_sequence, (query_seqs, key_seqs, value_seqs, doc_seqs))
    attended = attended.reshape(row_count, width)

    branch = half_sum(transposed_right(attended, output_full), core)
    branch_inv = lax.rsqrt(jnp.mean(branch * branch, axis=1, keepdims=True) + EPSILON)
    hidden_state = token_half + branch * branch_inv * attn_gains
    hidden_low = join_halves(hidden_state.astype(jnp.bfloat16), core)
    gate_act = matmul(hidden_low, gate_full)
    up_part = matmul(hidden_low, up_full)
    product = (jax.nn.silu(gate_act) * up_part).astype(jnp.bfloat16)
    mlp_branch = half_sum(
        transposed_right(product[:, :ff_half], down_left)
        + transposed_right(product[:, ff_half:], down_right),
        core,
    )
    mlp_inv = lax.rsqrt(jnp.mean(mlp_branch * mlp_branch, axis=1, keepdims=True) + EPSILON)
    block_out = join_halves(
        (hidden_state + mlp_branch * mlp_inv * mlp_gains).astype(jnp.bfloat16), core
    )

    grad_mlp_scale = jnp.sum(upstream * mlp_branch * mlp_inv, axis=0)
    mlp_scaled = mlp_gains * upstream
    mlp_cube = mlp_inv * mlp_inv * mlp_inv
    d_mlp_half = (
        mlp_inv * mlp_scaled
        - mlp_branch * mlp_cube * jnp.mean(mlp_scaled * mlp_branch, axis=1, keepdims=True)
    ).astype(jnp.bfloat16)
    d_mlp = join_halves(d_mlp_half, core)
    grad_down_left = transposed_left(d_mlp, product[:, :ff_half]).astype(jnp.bfloat16)
    grad_down_right = transposed_left(d_mlp, product[:, ff_half:]).astype(jnp.bfloat16)
    (out_down_left, out_down_right), marks = net.scatters(
        [grad_down_left, grad_down_right], [None, None]
    )
    d_product = jnp.concatenate(
        [matmul(d_mlp, down_left), matmul(d_mlp, down_right)], axis=1
    )
    sigmoid = jax.nn.sigmoid(gate_act)
    d_gate = (d_product * up_part * sigmoid * (1.0 + gate_act * (1.0 - sigmoid))).astype(
        jnp.bfloat16
    )
    d_up = (d_product * gate_act * sigmoid).astype(jnp.bfloat16)
    mlp_input = transposed_right(d_gate, gate_full) + transposed_right(d_up, up_full)
    grad_gate = transposed_left(hidden_low, d_gate).astype(jnp.bfloat16)
    grad_up = transposed_left(hidden_low, d_up).astype(jnp.bfloat16)
    (out_gate, out_up), marks = net.scatters([grad_gate, grad_up], marks)
    d_hidden = upstream + half_sum(mlp_input, core)

    grad_attn_scale = jnp.sum(d_hidden * branch * branch_inv, axis=0)
    attn_scaled = attn_gains * d_hidden
    branch_cube = branch_inv * branch_inv * branch_inv
    d_branch_half = (
        branch_inv * attn_scaled
        - branch * branch_cube * jnp.mean(attn_scaled * branch, axis=1, keepdims=True)
    ).astype(jnp.bfloat16)
    d_branch = join_halves(d_branch_half, core)
    grad_output = transposed_left(d_branch, attended).astype(jnp.bfloat16)
    d_attended = matmul(d_branch, output_full).astype(jnp.bfloat16)
    grad_qrot, grad_krot, grad_vals = lax.map(
        attend_backward,
        (query_seqs, key_seqs, value_seqs, doc_seqs, d_attended.reshape(seq_shape), lse_all),
    )
    d_values = grad_vals.reshape(row_count, width).astype(jnp.bfloat16)
    d_qnorm = rotate_back(
        grad_qrot.reshape(row_count, heads, HEAD_CHANNELS), angles
    ).reshape(row_count, width)
    d_knorm = rotate_back(
        grad_krot.reshape(row_count, heads, HEAD_CHANNELS), angles
    ).reshape(row_count, width)
    grad_qscale = jnp.sum(d_qnorm * query_raw * query_inv, axis=0)
    grad_kscale = jnp.sum(d_knorm * key_raw * key_inv, axis=0)
    query_scaled = query_scale * d_qnorm
    key_scaled = key_scale * d_knorm
    inner = small_sum(
        jnp.stack(
            [jnp.sum(query_scaled * query_raw, axis=1), jnp.sum(key_scaled * key_raw, axis=1)]
        )
    )
    query_cube = query_inv * query_inv * query_inv
    key_cube = key_inv * key_inv * key_inv
    d_query = (
        query_inv * query_scaled - query_raw * query_cube * (inner[0] / D)[:, None]
    ).astype(jnp.bfloat16)
    d_key = (key_inv * key_scaled - key_raw * key_cube * (inner[1] / D)[:, None]).astype(
        jnp.bfloat16
    )
    grad_value = transposed_left(tokens, d_values).astype(jnp.bfloat16)
    d_query_key = jnp.concatenate([d_query, d_key], axis=1)
    grad_qk = transposed_left(tokens, d_query_key).astype(jnp.bfloat16)
    grad_vo = jnp.concatenate([grad_value, grad_output], axis=1)
    (out_vo, out_qk), marks = net.scatters([grad_vo, grad_qk], marks)
    token_back = transposed_right(d_query_key, qk_full) + transposed_right(d_values, value_full)
    grad_tokens = join_halves((d_hidden + half_sum(token_back, core)).astype(jnp.bfloat16), core)

    def by_owner(flat):
        return flat.reshape(heads, n, -1).transpose(1, 0, 2).reshape(n, -1)

    head_rows = jnp.concatenate([by_owner(grad_qscale), by_owner(grad_kscale)], axis=1)
    col_rows = jnp.concatenate(
        [grad_attn_scale.reshape(n, -1), grad_mlp_scale.reshape(n, -1)], axis=1
    )
    summed = small_scatter(jnp.concatenate([head_rows, col_rows], axis=1), n)
    out_qgain = summed[:head_part].reshape(q_gain.shape)
    out_kgain = summed[head_part : 2 * head_part].reshape(k_gain.shape)
    cols = summed[2 * head_part :]
    cols = cols + lax.ppermute(cols, "mp", CORE_SWAP)
    return (
        block_out,
        grad_tokens,
        out_qk[:, :width],
        out_qk[:, width:],
        out_vo[:, :width],
        out_vo[:, width:].T,
        out_qgain,
        out_kgain,
        cols[:col_part],
        out_gate,
        out_up,
        jnp.concatenate([out_down_left, out_down_right], axis=1).T,
        cols[col_part:],
    )


def solution(mesh):
    in_specs = (
        P("dp", None),
        P("dp"),
        P("dp", "mp"),
        P("dp", "mp"),
        P("dp", "mp"),
        P("mp", "dp"),
        P("mp", "dp"),
        P("mp", "dp"),
        P("dp"),
        P("dp", "mp"),
        P("dp", "mp"),
        P("mp", "dp"),
        P("dp"),
        P("dp", None),
    )
    out_specs = (
        P("dp", None),
        P("dp", None),
        P("dp", "mp"),
        P("dp", "mp"),
        P("dp", "mp"),
        P("mp", "dp"),
        P("mp", "dp"),
        P("mp", "dp"),
        P("dp"),
        P("dp", "mp"),
        P("dp", "mp"),
        P("mp", "dp"),
        P("dp"),
    )
    n = mesh.shape["dp"]

    def program(*arrays):
        return on_device(n, *arrays)

    return jax.shard_map(
        program, mesh=mesh, in_specs=in_specs, out_specs=out_specs, check_vma=False
    )
```

```python
import functools
import math

import jax
import jax.numpy as jnp
from jax import lax
from jax.experimental import pallas as pl
from jax.experimental.pallas import tpu as pltpu
from jax.sharding import PartitionSpec as P

D = 2048
HEAD_CHANNELS = 128
SEQ_LEN = 1024
RING_MAX = 8


EPSILON = 1e-06
ROPE_BASE = 500000.0
MASKED = -1e30
ROW_LIMIT = 512

CORE_SWAP = ((0, 1), (1, 0), (2, 3), (3, 2))
FAR_SWAP = ((0, 2), (2, 0), (1, 3), (3, 1))


def matmul(left_side, right_side):
    return jnp.dot(left_side, right_side, preferred_element_type=jnp.float32)


def transposed_left(left_side, right_side):
    return lax.dot_general(
        left_side, right_side, (((0,), (0,)), ((), ())), preferred_element_type=jnp.float32
    )


def transposed_right(left_side, right_side):
    return lax.dot_general(
        left_side, right_side, (((1,), (1,)), ((), ())), preferred_element_type=jnp.float32
    )


def angles_of(doc_rows, seq_len, head_dim):
    shaped = doc_rows.reshape(-1, seq_len)
    leading = jnp.sum(1 - shaped, axis=1, keepdims=True, dtype=jnp.int32)
    places = jnp.arange(seq_len, dtype=jnp.int32)[None, :] - shaped * leading
    frequency = jnp.exp(
        jnp.arange(head_dim // 2, dtype=jnp.float32) * (-2.0 * math.log(ROPE_BASE) / head_dim)
    )
    return places.reshape(-1).astype(jnp.float32)[:, None] * frequency[None, :]


def rotate(vectors, angles):
    halfway = vectors.shape[-1] // 2
    cosine = jnp.cos(angles)[:, None, :]
    sine_wave = jnp.sin(angles)[:, None, :]
    former = vectors[..., :halfway]
    latter = vectors[..., halfway:]
    return jnp.concatenate(
        [former * cosine - latter * sine_wave, latter * cosine + former * sine_wave], axis=-1
    )


def rotate_back(vectors, angles):
    halfway = vectors.shape[-1] // 2
    cosine = jnp.cos(angles)[:, None, :]
    sine_wave = jnp.sin(angles)[:, None, :]
    former = vectors[..., :halfway]
    latter = vectors[..., halfway:]
    return jnp.concatenate(
        [former * cosine + latter * sine_wave, latter * cosine - former * sine_wave], axis=-1
    )


def block_scores(query_block, key_seq, doc_seq, offset):
    factor = 1.0 / math.sqrt(query_block.shape[-1])
    scores = (
        jnp.einsum("qhd,khd->hqk", query_block, key_seq, preferred_element_type=jnp.float32)
        * factor
    )
    row_places = offset + jnp.arange(query_block.shape[0], dtype=jnp.int32)
    key_places = jnp.arange(key_seq.shape[0], dtype=jnp.int32)
    row_docs = doc_seq[offset : offset + query_block.shape[0]]
    allowed = (key_places[None, :] <= row_places[:, None]) & (doc_seq[None, :] == row_docs[:, None])
    return jnp.where(allowed[None], scores, MASKED)


def attend_sequence(inputs):
    query_seq, key_seq, value_seq, doc_seq = inputs
    row_block = math.gcd(query_seq.shape[0], ROW_LIMIT)
    outputs = []
    totals = []
    for offset in range(0, query_seq.shape[0], row_block):
        scores = block_scores(query_seq[offset : offset + row_block], key_seq, doc_seq, offset)
        maximum = jnp.max(scores, axis=-1, keepdims=True)
        weights = jnp.exp(scores - maximum)
        denominator = jnp.sum(weights, axis=-1, keepdims=True)
        rounded = (weights / denominator).astype(jnp.bfloat16)
        outputs.append(
            jnp.einsum(
                "hqk,khd->qhd", rounded, value_seq, preferred_element_type=jnp.float32
            ).astype(jnp.bfloat16)
        )
        totals.append((maximum + jnp.log(denominator))[..., 0])
    return (jnp.concatenate(outputs, axis=0), jnp.concatenate(totals, axis=1))


def attend_backward(inputs):
    query_seq, key_seq, value_seq, doc_seq, grad_seq, lse_seq = inputs
    row_block = math.gcd(query_seq.shape[0], ROW_LIMIT)
    factor = 1.0 / math.sqrt(query_seq.shape[-1])
    grad_keys = jnp.zeros(key_seq.shape, jnp.float32)
    grad_values = jnp.zeros(value_seq.shape, jnp.float32)
    grad_rows = []
    for offset in range(0, query_seq.shape[0], row_block):
        query_block = query_seq[offset : offset + row_block]
        grad_block = grad_seq[offset : offset + row_block]
        scores = block_scores(query_block, key_seq, doc_seq, offset)
        weights = jnp.exp(scores - lse_seq[:, offset : offset + row_block, None])
        d_weights = jnp.einsum(
            "qhd,khd->hqk", grad_block, value_seq, preferred_element_type=jnp.float32
        )
        correction = jnp.sum(d_weights * weights, axis=-1, keepdims=True)
        d_scores = (weights * (d_weights - correction)).astype(jnp.bfloat16)
        grad_rows.append(
            jnp.einsum("hqk,khd->qhd", d_scores, key_seq, preferred_element_type=jnp.float32)
            * factor
        )
        grad_keys = (
            grad_keys
            + jnp.einsum("hqk,qhd->khd", d_scores, query_block, preferred_element_type=jnp.float32)
            * factor
        )
        grad_values = grad_values + jnp.einsum(
            "hqk,qhd->khd",
            weights.astype(jnp.bfloat16),
            grad_block,
            preferred_element_type=jnp.float32,
        )
    return (jnp.concatenate(grad_rows, axis=0), grad_keys, grad_values)


def after(value, earlier):
    if earlier is None:
        return value
    return lax.optimization_barrier((value, earlier))[0]


class Ring:
    def __init__(self, n):
        self.n = n
        self.order = [*range(0, n, 2), *range(n - 1 - n % 2, 0, -2)]
        index = lax.axis_index("dp")
        self.index = index
        self.place = jnp.where(index % 2 == 0, index // 2, n - 1 - index // 2)
        pairs = [(self.order[i], self.order[(i + 1) % n]) for i in range(n)]
        self.ways = (pairs, [(b, a) for a, b in pairs])

    def holder(self, steps):
        place = (self.place + steps + 2 * self.n) % self.n
        return jnp.where(place < self.n // 2, 2 * place, 2 * (self.n - 1 - place) + 1)

    def gathers(self, shards, gates):
        n = self.n
        held, full, marks = [], [], []
        for shard, gate in zip(shards, gates):
            rows, width = shard.shape
            halves = after(shard, gate).reshape(2, rows // 2, width)
            held.append([halves[0], halves[1]])
            start = jnp.zeros((n, 2, rows // 2, width), shard.dtype)
            full.append(lax.dynamic_update_slice(start, halves[None], (self.index, 0, 0, 0)))
            marks.append(None)
        for step in range(1, n):
            for unit in range(len(shards)):
                for way in range(2):
                    got = lax.ppermute(held[unit][way], "dp", self.ways[way])
                    held[unit][way] = got
                    source = self.holder(-step if way == 0 else step)
                    full[unit] = lax.dynamic_update_slice(
                        full[unit], got[None, None], (source, way, 0, 0)
                    )
                if step == n - 2:
                    marks[unit] = tuple(held[unit])
        return [f.reshape(-1, f.shape[-1]) for f in full], marks

    def scatters(self, grads, gates):
        n = self.n
        local, held, marks, outs = [], [], [], []
        for grad, gate in zip(grads, gates):
            rows, width = grad.shape[0] // n, grad.shape[1]
            parts = grad.reshape(n, 2, rows // 2, width)
            local.append(parts)
            held.append(
                [after(self.part(parts, way, -1 if way == 0 else 1), gate) for way in range(2)]
            )
            marks.append(None)
            outs.append([None, None])
        for step in range(1, n):
            for unit in range(len(grads)):
                for way in range(2):
                    got = lax.ppermute(held[unit][way], "dp", self.ways[way])
                    own = self.part(local[unit], way, -1 - step if way == 0 else 1 + step)
                    total = got.astype(jnp.float32) + own.astype(jnp.float32)
                    if step == n - 1:
                        outs[unit][way] = total
                    held[unit][way] = total.astype(jnp.bfloat16)
                if step == n - 2:
                    marks[unit] = tuple(held[unit])
        return [jnp.concatenate(o, axis=0) for o in outs], marks

    def part(self, parts, way, steps):
        spot = self.holder(steps)
        return lax.dynamic_slice(parts, (spot, way, 0, 0), (1, 1, *parts.shape[2:]))[0, 0]


class Plain:
    def __init__(self, n):
        self.n = n

    def gathers(self, shards, gates):
        full = [lax.all_gather(shard, "dp", axis=0, tiled=True) for shard in shards]
        return full, [None] * len(shards)

    def scatters(self, grads, gates):
        outs = [
            lax.psum_scatter(grad, "dp", scatter_dimension=0, tiled=True).astype(jnp.float32)
            for grad in grads
        ]
        return outs, [None] * len(grads)


def small_sum(values):
    values = values + lax.ppermute(values, "mp", CORE_SWAP)
    return values + lax.ppermute(values, "mp", FAR_SWAP)


def half_of(full, core):
    rows = full.shape[0] // 2
    return lax.dynamic_index_in_dim(full.reshape(2, rows, -1), core, 0, keepdims=False)


def half_sum(partial, core):
    low = partial.astype(jnp.bfloat16)
    got = lax.ppermute(half_of(low, 1 - core), "mp", CORE_SWAP)
    pair = half_of(low, core).astype(jnp.float32) + got.astype(jnp.float32)
    pair = lax.reduce_precision(pair, 8, 7)
    far = lax.ppermute(pair.astype(jnp.bfloat16), "mp", FAR_SWAP)
    return pair + far.astype(jnp.float32)


def join_halves(half, core):
    got = lax.ppermute(half, "mp", CORE_SWAP)
    first = jnp.where(core == 0, half, got)
    second = jnp.where(core == 0, got, half)
    return jnp.concatenate([first, second], axis=0)


MESH = pl.DeviceIdType.MESH
SUBS = 2


def place_of(index, n):
    odd = lax.rem(index, 2)
    half = lax.div(index, 2)
    return (1 - odd) * half + odd * (n - 1 - half)


def device_at(place, n):
    late = lax.div(place, n // 2)
    return (1 - late) * (2 * place) + late * (2 * (n - 1 - place) + 1)


def holder_of(index, steps, n):
    return device_at(lax.rem(place_of(index, n) + (steps + 2 * n), n), n)


def greet(targets):
    barrier = pltpu.get_barrier_semaphore()
    for target in targets:
        pl.semaphore_signal(barrier, inc=1, device_id=target, device_id_type=MESH)
    pl.semaphore_wait(barrier, len(targets))


def gather_kernel(n, shard, small, full, small_full, send, recv, small_send, small_recv, local):
    index = lax.axis_index("dp")
    right = {"dp": holder_of(index, 1, n)}
    left = {"dp": holder_of(index, -1, n)}
    greet((right, left))
    rows = shard.shape[1] // SUBS

    def hop(way, sub, step):
        owner = holder_of(index, (step - 1) * (2 * way - 1), n)
        span = pl.ds(sub * rows, rows)
        target = full.at[owner, way, span]
        return pltpu.make_async_remote_copy(
            src_ref=shard.at[way, span] if step == 1 else target,
            dst_ref=target,
            send_sem=send.at[way, sub, step - 1],
            recv_sem=recv.at[way, sub, step - 1],
            device_id=left if way else right,
            device_id_type=MESH,
        )

    def arrival(way, sub, step):
        owner = holder_of(index, step * (2 * way - 1), n)
        span = pl.ds(sub * rows, rows)
        target = full.at[owner, way, span]
        return pltpu.make_async_remote_copy(
            src_ref=target,
            dst_ref=target,
            send_sem=send.at[way, sub, step - 1],
            recv_sem=recv.at[way, sub, step - 1],
            device_id=left if way else right,
            device_id_type=MESH,
        )

    def small_hop(step, back):
        owner = holder_of(index, back - step, n)
        target = small_full.at[owner]
        return pltpu.make_async_remote_copy(
            src_ref=small if step == 1 and back else target,
            dst_ref=target,
            send_sem=small_send.at[step - 1],
            recv_sem=small_recv.at[step - 1],
            device_id=right,
            device_id_type=MESH,
        )

    for sub in range(SUBS):
        for way in range(2):
            hop(way, sub, 1).start()
    small_hop(1, 1).start()
    own = pltpu.make_async_copy(shard, full.at[index], local.at[0])
    own_small = pltpu.make_async_copy(small, small_full.at[index], local.at[1])
    own.start()
    own_small.start()
    for step in range(1, n):
        for sub in range(SUBS):
            for way in range(2):
                arrival(way, sub, step).wait_recv()
                if step < n - 1:
                    hop(way, sub, step + 1).start()
        small_hop(step, 0).wait_recv()
        if step < n - 1:
            small_hop(step + 1, 1).start()
    own.wait()
    own_small.wait()
    for step in range(1, n):
        for sub in range(SUBS):
            for way in range(2):
                hop(way, sub, step).wait_send()
        small_hop(step, 1).wait_send()


def kernel_gather(shard, small, n):
    rows, width = shard.shape
    full, small_full = pl.pallas_call(
        functools.partial(gather_kernel, n),
        out_shape=(
            jax.ShapeDtypeStruct((n, 2, rows // 2, width), shard.dtype),
            jax.ShapeDtypeStruct((n, *small.shape), small.dtype),
        ),
        in_specs=[pl.BlockSpec(memory_space=pl.ANY)] * 2,
        out_specs=(pl.BlockSpec(memory_space=pl.ANY),) * 2,
        scratch_shapes=[
            pltpu.SemaphoreType.DMA((2, SUBS, n - 1)),
            pltpu.SemaphoreType.DMA((2, SUBS, n - 1)),
            pltpu.SemaphoreType.DMA((n - 1,)),
            pltpu.SemaphoreType.DMA((n - 1,)),
            pltpu.SemaphoreType.DMA((2,)),
        ],
        compiler_params=pltpu.CompilerParams(collective_id=0, has_side_effects=True),
    )(shard.reshape(2, rows // 2, width), small)
    return full.reshape(n * rows, width), small_full


def scatter_kernel(
    n,
    parts,
    small,
    out,
    small_out,
    inbox,
    outbox,
    small_inbox,
    small_outbox,
    send,
    recv,
    small_send,
    small_recv,
):
    index = lax.axis_index("dp")
    rank = lax.axis_index("mp")
    right = {"dp": holder_of(index, 1, n)}
    left = {"dp": holder_of(index, -1, n)}
    twin = {"mp": rank + 1 - 2 * lax.rem(rank, 2)}
    greet((right, left, twin))
    rows = parts.shape[2] // SUBS

    def hop(way, sub, step):
        span = pl.ds(sub * rows, rows)
        first = parts.at[holder_of(index, 2 * way - 1, n), way, span]
        return pltpu.make_async_remote_copy(
            src_ref=first if step == 1 else outbox.at[step - 2, way, sub],
            dst_ref=inbox.at[step - 1, way, sub],
            send_sem=send.at[way, sub, step - 1],
            recv_sem=recv.at[way, sub, step - 1],
            device_id=left if way else right,
            device_id_type=MESH,
        )

    def small_hop(step):
        first = small.at[holder_of(index, -1, n)]
        return pltpu.make_async_remote_copy(
            src_ref=first if step == 1 else small_outbox.at[step - 2],
            dst_ref=small_inbox.at[step - 1],
            send_sem=small_send.at[step - 1],
            recv_sem=small_recv.at[step - 1],
            device_id=twin if step == n else right,
            device_id_type=MESH,
        )

    for sub in range(SUBS):
        for way in range(2):
            hop(way, sub, 1).start()
    small_hop(1).start()
    for step in range(1, n):
        for sub in range(SUBS):
            for way in range(2):
                hop(way, sub, step).wait_recv()
                owner = holder_of(index, (1 + step) * (2 * way - 1), n)

                @pl.loop(0, rows // 16)
                def _(tile, way=way, sub=sub, step=step, owner=owner):
                    near = pl.ds(pl.multiple_of(tile * 16, 16), 16)
                    far = pl.ds(pl.multiple_of(sub * rows + tile * 16, 16), 16)
                    total = inbox[step - 1, way, sub, near, :].astype(jnp.float32) + parts[
                        owner, way, far, :
                    ].astype(jnp.float32)
                    if step < n - 1:
                        outbox[step - 1, way, sub, near, :] = total.astype(outbox.dtype)
                    else:
                        out[way, far, :] = total

                if step < n - 1:
                    hop(way, sub, step + 1).start()
        small_hop(step).wait_recv()
        small_outbox[step - 1] = small_inbox[step - 1] + small[holder_of(index, -1 - step, n)]
        small_hop(step + 1).start()
    small_hop(n).wait_recv()
    line = lax.broadcasted_iota(jnp.int32, small_out.shape, 0)
    small_out[...] = small_outbox[n - 2] + jnp.where(line > 0, small_inbox[n - 1], 0.0)
    for step in range(1, n):
        for sub in range(SUBS):
            for way in range(2):
                hop(way, sub, step).wait_send()
        small_hop(step).wait_send()
    small_hop(n).wait_send()


def kernel_scatter(grad, small, n):
    rows, width = grad.shape[0] // n, grad.shape[1]
    out, small_out = pl.pallas_call(
        functools.partial(scatter_kernel, n),
        out_shape=(
            jax.ShapeDtypeStruct((2, rows // 2, width), jnp.float32),
            jax.ShapeDtypeStruct(small.shape[1:], jnp.float32),
        ),
        in_specs=[pl.BlockSpec(memory_space=pltpu.VMEM)] * 2,
        out_specs=(pl.BlockSpec(memory_space=pltpu.VMEM),) * 2,
        scratch_shapes=[
            pltpu.VMEM((n - 1, 2, SUBS, rows // 2 // SUBS, width), grad.dtype),
            pltpu.VMEM((n - 2, 2, SUBS, rows // 2 // SUBS, width), grad.dtype),
            pltpu.VMEM((n, *small.shape[1:]), jnp.float32),
            pltpu.VMEM((n - 1, *small.shape[1:]), jnp.float32),
            pltpu.SemaphoreType.DMA((2, SUBS, n - 1)),
            pltpu.SemaphoreType.DMA((2, SUBS, n - 1)),
            pltpu.SemaphoreType.DMA((n,)),
            pltpu.SemaphoreType.DMA((n,)),
        ],
        compiler_params=pltpu.CompilerParams(
            collective_id=1, has_side_effects=True, vmem_limit_bytes=48 * 2**20
        ),
    )(grad.reshape(n, 2, rows // 2, width), small)
    return out.reshape(rows, width), small_out


TILE = 256


def feed_kernel(
    n,
    hidden_low,
    gate_full,
    up_full,
    down_shard,
    hidden,
    upstream,
    gains,
    product_out,
    gate_slope,
    silu_out,
    down_full,
    d_mlp,
    block_half,
    gain_grad,
    lhs,
    product,
    held,
    gate_tile,
    up_tile,
    slope_tile,
    silu_tile,
    twin_out,
    twin_in,
    pair,
    far_in,
    branch,
    hidden_buf,
    upstream_buf,
    d_buf,
    block_buf,
    ring_send,
    ring_recv,
    twin_send,
    twin_recv,
    far_send,
    far_recv,
    join_send,
    join_recv,
    load_sem,
    tile_sem,
    stage_sem,
    store_sem,
):
    index = lax.axis_index("dp")
    rank = lax.axis_index("mp")
    core = lax.rem(rank, 2)
    right = {"dp": holder_of(index, 1, n)}
    left = {"dp": holder_of(index, -1, n)}
    twin = {"mp": rank + 1 - 2 * core}
    far = {"mp": lax.rem(rank + 2, 4)}
    half = hidden.shape[0]
    chunk = held.shape[2]
    rows = chunk // SUBS
    tiles = product.shape[1] // TILE
    width = branch.shape[1]

    loads = [
        pltpu.make_async_copy(hidden_low, lhs, load_sem.at[0]),
        pltpu.make_async_copy(down_shard, held.at[index], load_sem.at[1]),
        pltpu.make_async_copy(hidden, hidden_buf, load_sem.at[2]),
        pltpu.make_async_copy(upstream, upstream_buf, load_sem.at[3]),
    ]

    def weight_copies(tile, slot):
        cols = pl.ds(pl.multiple_of(tile * TILE, TILE), TILE)
        return (
            pltpu.make_async_copy(gate_full.at[:, cols], gate_tile.at[slot], tile_sem.at[slot, 0]),
            pltpu.make_async_copy(up_full.at[:, cols], up_tile.at[slot], tile_sem.at[slot, 1]),
        )

    def stage_copies(tile, slot):
        cols = pl.ds(pl.multiple_of(tile * TILE, TILE), TILE)
        return (
            pltpu.make_async_copy(slope_tile.at[slot], gate_slope.at[:, cols], stage_sem.at[slot, 0]),
            pltpu.make_async_copy(silu_tile.at[slot], silu_out.at[:, cols], stage_sem.at[slot, 1]),
        )

    def ring(way, sub, step, incoming):
        owner = holder_of(index, (step - 1 + incoming) * (2 * way - 1), n)
        span = pl.ds(sub * rows, rows)
        target = held.at[owner, way, span]
        return pltpu.make_async_remote_copy(
            src_ref=down_shard.at[way, span] if step == 1 and not incoming else target,
            dst_ref=target,
            send_sem=ring_send.at[way, sub, step - 1],
            recv_sem=ring_recv.at[way, sub, step - 1],
            device_id=left if way else right,
            device_id_type=MESH,
        )

    def serve(step, sub):
        for way in range(2):
            ring(way, sub, step, 1).wait_recv()
            if step < n - 1:
                ring(way, sub, step + 1, 0).start()

    def twin_copy(step):
        return pltpu.make_async_remote_copy(
            src_ref=twin_out.at[step],
            dst_ref=twin_in.at[step],
            send_sem=twin_send.at[step],
            recv_sem=twin_recv.at[step],
            device_id=twin,
            device_id_type=MESH,
        )

    def far_copy(step):
        return pltpu.make_async_remote_copy(
            src_ref=pair.at[step],
            dst_ref=far_in.at[step],
            send_sem=far_send.at[step],
            recv_sem=far_recv.at[step],
            device_id=far,
            device_id_type=MESH,
        )

    greet((right, left, twin, far))
    for sub in range(SUBS):
        for way in range(2):
            ring(way, sub, 1, 0).start()
    for copy in loads:
        copy.start()
    for copy in weight_copies(0, 0):
        copy.start()
    loads[0].wait()

    def feed_tile(tile):
        slot = lax.rem(tile, 2)
        for copy in weight_copies(tile, slot):
            copy.wait()

        @pl.when(tile + 1 < tiles)
        def _():
            for copy in weight_copies(tile + 1, 1 - slot):
                copy.start()

        @pl.when(tile >= 2)
        def _():
            for copy in stage_copies(tile - 2, slot):
                copy.wait()

        cols = pl.ds(pl.multiple_of(tile * TILE, TILE), TILE)

        @pl.loop(0, 2)
        def _(part):
            span = pl.ds(pl.multiple_of(part * half, half), half)
            gate = jnp.dot(lhs[span, :], gate_tile[slot], preferred_element_type=jnp.float32)
            up = jnp.dot(lhs[span, :], up_tile[slot], preferred_element_type=jnp.float32)
            sigmoid = jax.nn.sigmoid(gate)
            silu = gate * sigmoid
            product[span, cols] = (silu * up).astype(jnp.bfloat16)
            slope_tile[slot, span, :] = (up * sigmoid * (1.0 + gate * (1.0 - sigmoid))).astype(
                jnp.bfloat16
            )
            silu_tile[slot, span, :] = silu.astype(jnp.bfloat16)

        for copy in stage_copies(tile, slot):
            copy.start()

    events = [(step, sub) for step in range(1, n) for sub in range(SUBS)]
    groups = 4
    for group in range(groups):
        pl.loop(group * tiles // groups, (group + 1) * tiles // groups)(feed_tile)
        serve(*events.pop(0))
    stores = [pltpu.make_async_copy(product, product_out, store_sem.at[0])]
    stores[0].start()
    loads[1].wait()

    def multiply(step):
        first = held[holder_of(index, -step, n), 0]
        second = held[holder_of(index, step, n), 1]
        rhs = jnp.concatenate([first, second], axis=0)
        contract = (((1,), (1,)), ((), ()))
        span = pl.ds(pl.multiple_of((1 - core) * half, half), half)
        twin_out[step] = lax.dot_general(
            product[span, :], rhs, contract, preferred_element_type=jnp.float32
        ).astype(jnp.bfloat16)
        twin_copy(step).start()
        span = pl.ds(pl.multiple_of(core * half, half), half)
        pair[step] = lax.dot_general(
            product[span, :], rhs, contract, preferred_element_type=jnp.float32
        ).astype(jnp.bfloat16)

    def add_twin(step):
        twin_copy(step).wait_recv()

        @pl.loop(0, half // 32)
        def _(tile):
            span = pl.ds(pl.multiple_of(tile * 32, 32), 32)
            total = pair[step, span, :].astype(jnp.float32) + twin_in[step, span, :].astype(
                jnp.float32
            )
            pair[step, span, :] = total.astype(jnp.bfloat16)

        far_copy(step).start()

    def add_far(step):
        far_copy(step).wait_recv()
        first = holder_of(index, -step, n) * 2 * chunk
        second = holder_of(index, step, n) * 2 * chunk + chunk

        @pl.loop(0, half // 32)
        def _(tile):
            span = pl.ds(pl.multiple_of(tile * 32, 32), 32)
            total = pair[step, span, :].astype(jnp.float32) + far_in[step, span, :].astype(
                jnp.float32
            )
            branch[span, pl.ds(pl.multiple_of(first, chunk), chunk)] = total[:, :chunk]
            branch[span, pl.ds(pl.multiple_of(second, chunk), chunk)] = total[:, chunk:]

    for step in range(n):
        while events and events[0][0] <= step:
            serve(*events.pop(0))
        multiply(step)
        if step >= 1:
            add_twin(step - 1)
        if step >= 2:
            add_far(step - 2)
        if step < 2 and events:
            serve(*events.pop(0))
    add_twin(n - 1)
    stores.append(pltpu.make_async_copy(held, down_full, store_sem.at[1]))
    stores[1].start()
    add_far(n - 2)
    loads[2].wait()
    loads[3].wait()
    gain_grad[...] = jnp.zeros_like(gain_grad)
    add_far(n - 1)

    def finish(tile):
        span = pl.ds(pl.multiple_of(tile * 16, 16), 16)
        mixed = branch[span, :]
        scale = gains[...]
        inverse = lax.rsqrt(jnp.sum(mixed * mixed, axis=1, keepdims=True) / width + EPSILON)
        grad = upstream_buf[span, :].astype(jnp.float32)
        scaled = scale * grad
        mean = jnp.sum(scaled * mixed, axis=1, keepdims=True) / width
        normed = mixed * inverse
        d_buf[span, :] = (
            inverse * scaled - mixed * (inverse * inverse * inverse * mean)
        ).astype(jnp.bfloat16)
        block_buf[span, :] = (hidden_buf[span, :] + normed * scale).astype(jnp.bfloat16)
        terms = grad * normed
        gain_grad[...] += terms[:8] + terms[8:]

    def join(part, own):
        span = pl.ds(part * (half // 4), half // 4)
        if own:
            return pltpu.make_async_copy(d_buf.at[span], d_mlp.at[core, span], store_sem.at[3 + part])
        return pltpu.make_async_remote_copy(
            src_ref=d_buf.at[span],
            dst_ref=d_mlp.at[core, span],
            send_sem=join_send.at[part],
            recv_sem=join_recv.at[part],
            device_id=twin,
            device_id_type=MESH,
        )

    def joined(part):
        span = pl.ds(part * (half // 4), half // 4)
        target = d_mlp.at[1 - core, span]
        return pltpu.make_async_remote_copy(
            src_ref=target,
            dst_ref=target,
            send_sem=join_send.at[part],
            recv_sem=join_recv.at[part],
            device_id=twin,
            device_id_type=MESH,
        )

    for part in range(4):
        pl.loop(part * (half // 64), (part + 1) * (half // 64))(finish)
        join(part, False).start()
        join(part, True).start()
    stores.append(pltpu.make_async_copy(block_buf, block_half, store_sem.at[2]))
    stores[2].start()
    for part in range(4):
        joined(part).wait_recv()
        join(part, False).wait_send()
        join(part, True).wait()
    for copy in stores:
        copy.wait()
    for tile in (tiles - 2, tiles - 1):
        for copy in stage_copies(tile, tile % 2):
            copy.wait()
    for step in range(n):
        twin_copy(step).wait_send()
        far_copy(step).wait_send()
    for step in range(1, n):
        for sub in range(SUBS):
            for way in range(2):
                ring(way, sub, step, 0).wait_send()


def kernel_feed(hidden_low, gate_full, up_full, down_shard, hidden, upstream, gains, n):
    count, width = hidden_low.shape
    units = gate_full.shape[1]
    half = count // 2
    chunk = width // n // 2
    rows = chunk // SUBS
    low = jnp.bfloat16
    hbm = pl.BlockSpec(memory_space=pl.ANY)
    vmem = pl.BlockSpec(memory_space=pltpu.VMEM)
    dma = pltpu.SemaphoreType.DMA
    product, slope, silu, down_full, d_mlp, block, gain_grad = pl.pallas_call(
        functools.partial(feed_kernel, n),
        out_shape=(
            jax.ShapeDtypeStruct((count, units), low),
            jax.ShapeDtypeStruct((count, units), low),
            jax.ShapeDtypeStruct((count, units), low),
            jax.ShapeDtypeStruct((n, 2, chunk, units), low),
            jax.ShapeDtypeStruct((2, half, width), low),
            jax.ShapeDtypeStruct((half, width), low),
            jax.ShapeDtypeStruct((8, width), jnp.float32),
        ),
        in_specs=[hbm] * 6 + [vmem],
        out_specs=(hbm,) * 6 + (vmem,),
        scratch_shapes=[
            pltpu.VMEM((count, width), low),
            pltpu.VMEM((count, units), low),
            pltpu.VMEM((n, 2, chunk, units), low),
            pltpu.VMEM((2, width, TILE), low),
            pltpu.VMEM((2, width, TILE), low),
            pltpu.VMEM((2, count, TILE), low),
            pltpu.VMEM((2, count, TILE), low),
            pltpu.VMEM((n, half, 2 * chunk), low),
            pltpu.VMEM((n, half, 2 * chunk), low),
            pltpu.VMEM((n, half, 2 * chunk), low),
            pltpu.VMEM((n, half, 2 * chunk), low),
            pltpu.VMEM((half, width), jnp.float32),
            pltpu.VMEM((half, width), jnp.float32),
            pltpu.VMEM((half, width), low),
            pltpu.VMEM((half, width), low),
            pltpu.VMEM((half, width), low),
            dma((2, SUBS, n - 1)),
            dma((2, SUBS, n - 1)),
            dma((n,)),
            dma((n,)),
            dma((n,)),
            dma((n,)),
            dma((4,)),
            dma((4,)),
            dma((4,)),
            dma((2, 2)),
            dma((2, 2)),
            dma((7,)),
        ],
        compiler_params=pltpu.CompilerParams(
            collective_id=2, has_side_effects=True, vmem_limit_bytes=58 * 2**20
        ),
    )(
        hidden_low,
        gate_full,
        up_full,
        down_shard.reshape(2, chunk, units),
        hidden,
        upstream,
        gains.astype(jnp.float32).reshape(1, width),
    )
    return (
        product,
        slope,
        silu,
        down_full.reshape(width, units),
        d_mlp.reshape(count, width),
        block,
        jnp.sum(gain_grad, axis=0),
    )


def back_kernel(
    n,
    d_mlp,
    product,
    down_full,
    gate_slope,
    silu_in,
    gate_full,
    up_full,
    hidden_low,
    upstream,
    branch,
    gains,
    out_down,
    d_hidden_out,
    d_branch,
    grad_gate,
    grad_up,
    gain_grad,
    d_out,
    prod,
    d_gate,
    d_up,
    down_tile,
    slope_tile,
    silu_tile,
    gate_tile,
    up_tile,
    hidden_tile,
    first,
    own,
    inbox,
    mixed,
    twin_in,
    pair,
    far_in,
    d_hidden,
    branch_tile,
    upstream_tile,
    d_buf,
    stage,
    ring_send,
    ring_recv,
    twin_send,
    twin_recv,
    far_send,
    far_recv,
    join_send,
    join_recv,
    load_sem,
    down_sem,
    weight_sem,
    hidden_sem,
    row_sem,
    stage_sem,
    store_sem,
):
    index = lax.axis_index("dp")
    rank = lax.axis_index("mp")
    core = lax.rem(rank, 2)
    right = {"dp": holder_of(index, 1, n)}
    left = {"dp": holder_of(index, -1, n)}
    twin = {"mp": rank + 1 - 2 * core}
    far = {"mp": lax.rem(rank + 2, 4)}
    count, width = d_out.shape
    half = count // 2
    chunk = inbox.shape[3] * SUBS
    rows = chunk // SUBS
    tiles = prod.shape[1] // TILE
    quarter = half // 4
    left_side = (((0,), (0,)), ((), ()))
    right_side = (((1,), (1,)), ((), ()))

    def tile_span(tile):
        return pl.ds(pl.multiple_of(tile * TILE, TILE), TILE)

    def down_copies(tile, slot):
        cols = tile_span(tile)
        return (
            pltpu.make_async_copy(down_full.at[:, cols], down_tile.at[slot], down_sem.at[slot, 0]),
            pltpu.make_async_copy(gate_slope.at[:, cols], slope_tile.at[slot], down_sem.at[slot, 1]),
            pltpu.make_async_copy(silu_in.at[:, cols], silu_tile.at[slot], down_sem.at[slot, 2]),
        )

    def weight_copies(tile, slot):
        span = tile_span(tile)
        return (
            pltpu.make_async_copy(gate_full.at[span], gate_tile.at[slot], weight_sem.at[slot, 0]),
            pltpu.make_async_copy(up_full.at[span], up_tile.at[slot], weight_sem.at[slot, 1]),
        )

    def hidden_copy(tile, slot):
        return pltpu.make_async_copy(
            hidden_low.at[:, tile_span(tile)], hidden_tile.at[slot], hidden_sem.at[slot]
        )

    def row_copies(part, slot):
        span = pl.ds(part * quarter, quarter)
        return (
            pltpu.make_async_copy(branch.at[span], branch_tile.at[slot], row_sem.at[slot, 0]),
            pltpu.make_async_copy(upstream.at[span], upstream_tile.at[slot], row_sem.at[slot, 1]),
        )

    def stage_copy(tile, which):
        target = (grad_gate, grad_up)[which]
        return pltpu.make_async_copy(stage.at[which], target.at[tile_span(tile)], stage_sem.at[which])

    def ring(way, sub, step):
        return pltpu.make_async_remote_copy(
            src_ref=first.at[way, pl.ds(sub * rows, rows)]
            if step == 1
            else inbox.at[step - 2, way, sub],
            dst_ref=inbox.at[step - 1, way, sub],
            send_sem=ring_send.at[way, sub, step - 1],
            recv_sem=ring_recv.at[way, sub, step - 1],
            device_id=left if way else right,
            device_id_type=MESH,
        )

    def grad_block(step):
        cols = []
        for way in range(2):
            owner = holder_of(index, (1 + step) * (2 * way - 1), n)
            start = pl.multiple_of(owner * 2 * chunk + way * chunk, chunk)
            cols.append(d_out[:, pl.ds(start, chunk)])
        block = lax.dot_general(
            jnp.concatenate(cols, axis=1),
            prod[...],
            left_side,
            preferred_element_type=jnp.float32,
        ).astype(jnp.bfloat16)
        target = first if step == 0 else own.at[step % 2]
        target[0] = block[:chunk]
        target[1] = block[chunk:]

    def serve(step, sub):
        for way in range(2):
            ring(way, sub, step).wait_recv()

            @pl.loop(0, rows // 16)
            def _(tile, way=way):
                near = pl.ds(pl.multiple_of(tile * 16, 16), 16)
                mine = pl.ds(pl.multiple_of(sub * rows + tile * 16, 16), 16)
                total = inbox[step - 1, way, sub, near, :].astype(jnp.float32) + own[
                    step % 2, way, mine, :
                ].astype(jnp.float32)
                if step < n - 1:
                    inbox[step - 1, way, sub, near, :] = total.astype(jnp.bfloat16)
                else:
                    out_down[way, mine, :] = total

            if step < n - 1:
                ring(way, sub, step + 1).start()

    def twin_copy(tile):
        span = pl.ds(pl.multiple_of((1 - core) * half, half), half)
        return pltpu.make_async_remote_copy(
            src_ref=mixed.at[tile % 4, span],
            dst_ref=twin_in.at[tile % 4],
            send_sem=twin_send.at[tile],
            recv_sem=twin_recv.at[tile],
            device_id=twin,
            device_id_type=MESH,
        )

    def far_copy(tile):
        return pltpu.make_async_remote_copy(
            src_ref=pair.at[tile],
            dst_ref=far_in.at[tile],
            send_sem=far_send.at[tile],
            recv_sem=far_recv.at[tile],
            device_id=far,
            device_id_type=MESH,
        )

    greet((right, left, twin, far))
    loads = [
        pltpu.make_async_copy(d_mlp, d_out, load_sem.at[0]),
        pltpu.make_async_copy(product, prod, load_sem.at[1]),
    ]
    for copy in loads:
        copy.start()
    for copy in down_copies(0, 0):
        copy.start()
    for copy in weight_copies(0, 0):
        copy.start()
    for copy in loads:
        copy.wait()
    grad_block(0)
    for sub in range(SUBS):
        for way in range(2):
            ring(way, sub, 1).start()
    grad_block(1)

    def product_tile(tile):
        slot = lax.rem(tile, 2)
        for copy in down_copies(tile, slot):
            copy.wait()

        @pl.when(tile + 1 < tiles)
        def _():
            for copy in down_copies(tile + 1, 1 - slot):
                copy.start()

        cols = tile_span(tile)
        grad = jnp.dot(d_out[...], down_tile[slot], preferred_element_type=jnp.float32)
        d_gate[:, cols] = (grad * slope_tile[slot].astype(jnp.float32)).astype(jnp.bfloat16)
        d_up[:, cols] = (grad * silu_tile[slot].astype(jnp.float32)).astype(jnp.bfloat16)

    def input_tile(tile):
        slot = tile % 2
        for copy in weight_copies(tile, slot):
            copy.wait()
        if tile + 1 < width // TILE:
            for copy in weight_copies(tile + 1, 1 - slot):
                copy.start()
        total = lax.dot_general(
            d_gate[...], gate_tile[slot], right_side, preferred_element_type=jnp.float32
        ) + lax.dot_general(
            d_up[...], up_tile[slot], right_side, preferred_element_type=jnp.float32
        )
        mixed[tile % 4] = total.astype(jnp.bfloat16)
        twin_copy(tile).start()

    def add_twin(tile):
        twin_copy(tile).wait_recv()

        @pl.loop(0, half // 32)
        def _(row):
            span = pl.ds(pl.multiple_of(row * 32, 32), 32)
            mine = pl.ds(pl.multiple_of(core * half + row * 32, 32), 32)
            total = mixed[tile % 4, mine, :].astype(jnp.float32) + twin_in[
                tile % 4, span, :
            ].astype(jnp.float32)
            pair[tile, span, :] = total.astype(jnp.bfloat16)

        far_copy(tile).start()
        twin_copy(tile).wait_send()

    def add_far(tile):
        far_copy(tile).wait_recv()

        @pl.loop(0, half // 32)
        def _(row):
            span = pl.ds(pl.multiple_of(row * 32, 32), 32)
            d_hidden[span, tile * TILE : (tile + 1) * TILE] = pair[tile, span, :].astype(
                jnp.float32
            ) + far_in[tile, span, :].astype(jnp.float32)

    def weight_tile(tile):
        slot = tile % 2
        hidden_copy(tile, slot).wait()
        if tile + 1 < width // TILE:
            hidden_copy(tile + 1, 1 - slot).start()
        for which, source in enumerate((d_gate, d_up)):
            if tile >= 1:
                stage_copy(tile - 1, which).wait()
            stage[which] = lax.dot_general(
                hidden_tile[slot], source[...], left_side, preferred_element_type=jnp.float32
            ).astype(jnp.bfloat16)
            stage_copy(tile, which).start()

    events = [(step, sub) for step in range(1, n) for sub in range(SUBS)]

    def next_event():
        step, sub = events.pop(0)
        serve(step, sub)
        if sub == SUBS - 1 and step < n - 1:
            grad_block(step + 1)

    pl.loop(0, tiles // 4)(product_tile)
    next_event()
    pl.loop(tiles // 4, tiles // 2)(product_tile)
    next_event()
    pl.loop(tiles // 2, 3 * tiles // 4)(product_tile)
    next_event()
    pl.loop(3 * tiles // 4, tiles)(product_tile)
    next_event()
    blocks = width // TILE
    hidden_copy(0, 0).start()
    for tile in range(blocks):
        input_tile(tile)
        if tile >= 1:
            add_twin(tile - 1)
        if tile >= 3:
            add_far(tile - 3)
        if tile % 2 == 1:
            next_event()
    add_twin(blocks - 1)
    for copy in row_copies(0, 0):
        copy.start()
    for tile in range(blocks):
        weight_tile(tile)
        if tile % 2 == 1:
            if tile // 2 < 3:
                add_far(blocks - 3 + tile // 2)
            if events:
                next_event()
    gain_grad[...] = jnp.zeros_like(gain_grad)

    def finish(part, slot, tile):
        near = pl.ds(pl.multiple_of(tile * 16, 16), 16)
        span = pl.ds(pl.multiple_of(part * quarter + tile * 16, 16), 16)
        total = d_hidden[span, :] + upstream_tile[slot, near, :].astype(jnp.float32)
        d_hidden[span, :] = total
        mix = branch_tile[slot, near, :]
        inverse = lax.rsqrt(jnp.sum(mix * mix, axis=1, keepdims=True) / width + EPSILON)
        scaled = gains[...] * total
        mean = jnp.sum(scaled * mix, axis=1, keepdims=True) / width
        d_buf[span, :] = (inverse * scaled - mix * (inverse * inverse * inverse * mean)).astype(
            jnp.bfloat16
        )
        terms = total * mix * inverse
        gain_grad[...] += terms[:8] + terms[8:]

    def join(part, kind):
        span = pl.ds(part * quarter, quarter)
        if kind == 2:
            return pltpu.make_async_copy(
                d_buf.at[span], d_branch.at[core, span], store_sem.at[part]
            )
        target = d_branch.at[1 - core if kind else core, span]
        return pltpu.make_async_remote_copy(
            src_ref=target if kind else d_buf.at[span],
            dst_ref=target,
            send_sem=join_send.at[part],
            recv_sem=join_recv.at[part],
            device_id=twin,
            device_id_type=MESH,
        )

    for part in range(4):
        slot = part % 2
        for copy in row_copies(part, slot):
            copy.wait()
        if part < 3:
            for copy in row_copies(part + 1, 1 - slot):
                copy.start()
        pl.loop(0, quarter // 16)(functools.partial(finish, part, slot))
        join(part, 0).start()
        join(part, 2).start()
    stores = pltpu.make_async_copy(d_hidden, d_hidden_out, store_sem.at[4])
    stores.start()
    while events:
        next_event()
    for part in range(4):
        join(part, 1).wait_recv()
        join(part, 0).wait_send()
        join(part, 2).wait()
    stores.wait()
    for which in range(2):
        stage_copy(blocks - 1, which).wait()
    for tile in range(blocks):
        far_copy(tile).wait_send()
    for step in range(1, n):
        for sub in range(SUBS):
            for way in range(2):
                ring(way, sub, step).wait_send()


def kernel_back(
    d_mlp,
    product,
    down_full,
    gate_slope,
    silu,
    gate_full,
    up_full,
    hidden_low,
    upstream,
    branch,
    gains,
    n,
):
    count, width = d_mlp.shape
    units = product.shape[1]
    half = count // 2
    chunk = width // n // 2
    rows = chunk // SUBS
    blocks = width // TILE
    low = jnp.bfloat16
    hbm = pl.BlockSpec(memory_space=pl.ANY)
    vmem = pl.BlockSpec(memory_space=pltpu.VMEM)
    dma = pltpu.SemaphoreType.DMA
    out_down, d_hidden, d_branch, grad_gate, grad_up, gain_grad = pl.pallas_call(
        functools.partial(back_kernel, n),
        out_shape=(
            jax.ShapeDtypeStruct((2, chunk, units), jnp.float32),
            jax.ShapeDtypeStruct((half, width), jnp.float32),
            jax.ShapeDtypeStruct((2, half, width), low),
            jax.ShapeDtypeStruct((width, units), low),
            jax.ShapeDtypeStruct((width, units), low),
            jax.ShapeDtypeStruct((8, width), jnp.float32),
        ),
        in_specs=[hbm] * 10 + [vmem],
        out_specs=(vmem,) + (hbm,) * 4 + (vmem,),
        scratch_shapes=[
            pltpu.VMEM((count, width), low),
            pltpu.VMEM((count, units), low),
            pltpu.VMEM((count, units), low),
            pltpu.VMEM((count, units), low),
            pltpu.VMEM((2, width, TILE), low),
            pltpu.VMEM((2, count, TILE), low),
            pltpu.VMEM((2, count, TILE), low),
            pltpu.VMEM((2, TILE, units), low),
            pltpu.VMEM((2, TILE, units), low),
            pltpu.VMEM((2, count, TILE), low),
            pltpu.VMEM((2, chunk, units), low),
            pltpu.VMEM((2, 2, chunk, units), low),
            pltpu.VMEM((n - 1, 2, SUBS, rows, units), low),
            pltpu.VMEM((4, count, TILE), low),
            pltpu.VMEM((4, half, TILE), low),
            pltpu.VMEM((blocks, half, TILE), low),
            pltpu.VMEM((blocks, half, TILE), low),
            pltpu.VMEM((half, width), jnp.float32),
            pltpu.VMEM((2, half // 4, width), jnp.float32),
            pltpu.VMEM((2, half // 4, width), low),
            pltpu.VMEM((half, width), low),
            pltpu.VMEM((2, TILE, units), low),
            dma((2, SUBS, n - 1)),
            dma((2, SUBS, n - 1)),
            dma((blocks,)),
            dma((blocks,)),
            dma((blocks,)),
            dma((blocks,)),
            dma((4,)),
            dma((4,)),
            dma((2,)),
            dma((2, 3)),
            dma((2, 2)),
            dma((2,)),
            dma((2, 2)),
            dma((2,)),
            dma((5,)),
        ],
        compiler_params=pltpu.CompilerParams(
            collective_id=3, has_side_effects=True, vmem_limit_bytes=60 * 2**20
        ),
    )(
        d_mlp,
        product,
        down_full,
        gate_slope,
        silu,
        gate_full,
        up_full,
        hidden_low,
        upstream,
        branch,
        gains.astype(jnp.float32).reshape(1, width),
    )
    return (
        out_down.reshape(2 * chunk, units),
        d_hidden,
        d_branch.reshape(count, width),
        grad_gate,
        grad_up,
        jnp.sum(gain_grad, axis=0),
    )


def plain_feed(
    hidden_low, gate_full, up_full, down_shard, hidden_state, upstream, mlp_gains, core, net
):
    (down_full,), marks = net.gathers([down_shard], [None])
    gate_act = matmul(hidden_low, gate_full)
    up_part = matmul(hidden_low, up_full)
    sigmoid = jax.nn.sigmoid(gate_act)
    silu = gate_act * sigmoid
    product = (silu * up_part).astype(jnp.bfloat16)
    slope = (up_part * sigmoid * (1.0 + gate_act * (1.0 - sigmoid))).astype(jnp.bfloat16)
    mlp_branch = half_sum(transposed_right(product, down_full), core)
    mlp_inv = lax.rsqrt(jnp.mean(mlp_branch * mlp_branch, axis=1, keepdims=True) + EPSILON)
    block_half = (hidden_state + mlp_branch * mlp_inv * mlp_gains).astype(jnp.bfloat16)
    mlp_gain_rows = jnp.sum(upstream * mlp_branch * mlp_inv, axis=0)
    mlp_scaled = mlp_gains * upstream
    mlp_cube = mlp_inv * mlp_inv * mlp_inv
    d_mlp_half = (
        mlp_inv * mlp_scaled
        - mlp_branch * mlp_cube * jnp.mean(mlp_scaled * mlp_branch, axis=1, keepdims=True)
    ).astype(jnp.bfloat16)
    d_mlp = join_halves(d_mlp_half, core)
    return product, slope, silu.astype(jnp.bfloat16), down_full, d_mlp, block_half, mlp_gain_rows


def plain_back(
    d_mlp,
    product,
    down_full,
    gate_slope,
    silu,
    gate_full,
    up_full,
    hidden_low,
    upstream,
    branch,
    attn_gains,
    core,
    net,
):
    grad_down = transposed_left(d_mlp, product).astype(jnp.bfloat16)
    (out_down,), marks = net.scatters([grad_down], [None])
    d_product = matmul(d_mlp, down_full)
    d_gate = (d_product * gate_slope).astype(jnp.bfloat16)
    d_up = (d_product * silu).astype(jnp.bfloat16)
    mlp_input = transposed_right(d_gate, gate_full) + transposed_right(d_up, up_full)
    grad_gate = transposed_left(hidden_low, d_gate).astype(jnp.bfloat16)
    grad_up = transposed_left(hidden_low, d_up).astype(jnp.bfloat16)
    d_hidden = upstream + half_sum(mlp_input, core)
    branch_inv = lax.rsqrt(jnp.mean(branch * branch, axis=1, keepdims=True) + EPSILON)
    attn_gain_rows = jnp.sum(d_hidden * branch * branch_inv, axis=0)
    attn_scaled = attn_gains * d_hidden
    branch_cube = branch_inv * branch_inv * branch_inv
    d_branch_half = (
        branch_inv * attn_scaled
        - branch * branch_cube * jnp.mean(attn_scaled * branch, axis=1, keepdims=True)
    ).astype(jnp.bfloat16)
    d_branch = join_halves(d_branch_half, core)
    return out_down, d_hidden, d_branch, grad_gate, grad_up, attn_gain_rows, marks * 2


def on_device(
    n,
    tokens,
    doc_ids,
    q_weight,
    k_weight,
    v_weight,
    o_weight,
    q_gain,
    k_gain,
    attn_gain,
    gate_weight,
    up_weight,
    down_weight,
    mlp_gain,
    cotangent,
):
    core = lax.axis_index("mp") % 2
    fused = n == RING_MAX
    net = Ring(n) if fused else Plain(n)
    row_count = tokens.shape[0]
    heads = q_gain.shape[0]
    width = heads * HEAD_CHANNELS
    sequences = row_count // SEQ_LEN
    seq_shape = (sequences, SEQ_LEN, heads, HEAD_CHANNELS)
    head_part = q_gain.size
    col_part = attn_gain.size

    packed = jnp.concatenate(
        [q_gain.reshape(-1), k_gain.reshape(-1), attn_gain, mlp_gain], axis=0
    )
    shard = jnp.concatenate([q_weight, k_weight, v_weight, o_weight.T], axis=1)
    down_shard = down_weight.T
    if fused:
        size = packed.shape[0]
        small = jnp.pad(packed, (0, 2048 - size)).reshape(16, 128)
        attn_full, gains = kernel_gather(shard, small, n)
        gains = gains.reshape(n, -1)[:, :size]
        (gate_full, up_full), marks = net.gathers([gate_weight, up_weight], [attn_full, attn_full])
    else:
        gains = lax.all_gather(packed, "dp")
        (attn_full, gate_full, up_full), marks = net.gathers(
            [shard, gate_weight, up_weight], [None] * 3
        )
    query_scale = gains[:, :head_part].reshape(n, heads, -1).transpose(1, 0, 2).reshape(-1)
    key_scale = (
        gains[:, head_part : 2 * head_part].reshape(n, heads, -1).transpose(1, 0, 2).reshape(-1)
    )
    attn_gains = gains[:, 2 * head_part : 2 * head_part + col_part].reshape(-1)
    mlp_gains = gains[:, 2 * head_part + col_part :].reshape(-1)

    angles = angles_of(doc_ids, SEQ_LEN, HEAD_CHANNELS)
    doc_seqs = doc_ids.reshape(sequences, SEQ_LEN)
    token_half = half_of(tokens, core).astype(jnp.float32)
    upstream = half_of(cotangent, core).astype(jnp.float32)

    projected = matmul(tokens, attn_full[:, : 3 * width])
    query_raw = projected[:, :width]
    key_raw = projected[:, width : 2 * width]
    values = projected[:, 2 * width :].astype(jnp.bfloat16)
    output_full = attn_full[:, 3 * width :]
    squares = small_sum(
        jnp.stack([jnp.sum(query_raw * query_raw, axis=1), jnp.sum(key_raw * key_raw, axis=1)])
    )
    query_inv = lax.rsqrt(squares[0] / D + EPSILON)[:, None]
    key_inv = lax.rsqrt(squares[1] / D + EPSILON)[:, None]
    query_rot = rotate(
        (query_raw * query_inv * query_scale).reshape(row_count, heads, HEAD_CHANNELS), angles
    ).astype(jnp.bfloat16)
    key_rot = rotate(
        (key_raw * key_inv * key_scale).reshape(row_count, heads, HEAD_CHANNELS), angles
    ).astype(jnp.bfloat16)
    query_seqs = query_rot.reshape(seq_shape)
    key_seqs = key_rot.reshape(seq_shape)
    value_seqs = values.reshape(seq_shape)
    attended, lse_all = lax.map(attend_sequence, (query_seqs, key_seqs, value_seqs, doc_seqs))
    attended = attended.reshape(row_count, width)

    branch = half_sum(transposed_right(attended, output_full), core)
    branch_inv = lax.rsqrt(jnp.mean(branch * branch, axis=1, keepdims=True) + EPSILON)
    hidden_state = token_half + branch * branch_inv * attn_gains
    hidden_low = join_halves(hidden_state.astype(jnp.bfloat16), core)
    if fused:
        product, gate_slope, silu, down_full, d_mlp, block_half, mlp_gain_rows = kernel_feed(
            hidden_low,
            gate_full,
            up_full,
            down_shard,
            hidden_state,
            half_of(cotangent, core),
            mlp_gains,
            n,
        )
    else:
        product, gate_slope, silu, down_full, d_mlp, block_half, mlp_gain_rows = plain_feed(
            hidden_low, gate_full, up_full, down_shard, hidden_state, upstream, mlp_gains, core, net
        )
    block_out = join_halves(block_half, core)

    if fused:
        out_down, d_hidden, d_branch, grad_gate, grad_up, attn_gain_rows = kernel_back(
            d_mlp,
            product,
            down_full,
            gate_slope,
            silu,
            gate_full,
            up_full,
            hidden_low,
            half_of(cotangent, core),
            branch,
            attn_gains,
            n,
        )
        marks = [out_down] * 2
    else:
        out_down, d_hidden, d_branch, grad_gate, grad_up, attn_gain_rows, marks = plain_back(
            d_mlp,
            product,
            down_full,
            gate_slope,
            silu,
            gate_full,
            up_full,
            hidden_low,
            upstream,
            branch,
            attn_gains,
            core,
            net,
        )
    (out_gate, out_up), marks = net.scatters([grad_gate, grad_up], marks)
    grad_output = transposed_left(d_branch, attended).astype(jnp.bfloat16)
    d_attended = matmul(d_branch, output_full).astype(jnp.bfloat16)
    grad_qrot, grad_krot, grad_vals = lax.map(
        attend_backward,
        (query_seqs, key_seqs, value_seqs, doc_seqs, d_attended.reshape(seq_shape), lse_all),
    )
    d_values = grad_vals.reshape(row_count, width).astype(jnp.bfloat16)
    d_qnorm = rotate_back(
        grad_qrot.reshape(row_count, heads, HEAD_CHANNELS), angles
    ).reshape(row_count, width)
    d_knorm = rotate_back(
        grad_krot.reshape(row_count, heads, HEAD_CHANNELS), angles
    ).reshape(row_count, width)
    grad_qscale = jnp.sum(d_qnorm * query_raw * query_inv, axis=0)
    grad_kscale = jnp.sum(d_knorm * key_raw * key_inv, axis=0)
    query_scaled = query_scale * d_qnorm
    key_scaled = key_scale * d_knorm
    inner = small_sum(
        jnp.stack(
            [jnp.sum(query_scaled * query_raw, axis=1), jnp.sum(key_scaled * key_raw, axis=1)]
        )
    )
    query_cube = query_inv * query_inv * query_inv
    key_cube = key_inv * key_inv * key_inv
    d_query = (
        query_inv * query_scaled - query_raw * query_cube * (inner[0] / D)[:, None]
    ).astype(jnp.bfloat16)
    d_key = (key_inv * key_scaled - key_raw * key_cube * (inner[1] / D)[:, None]).astype(
        jnp.bfloat16
    )
    d_projected = jnp.concatenate([d_query, d_key, d_values], axis=1)
    grad_projected = transposed_left(tokens, d_projected).astype(jnp.bfloat16)
    grad_attn = jnp.concatenate([grad_projected, grad_output], axis=1)
    token_back = transposed_right(d_projected, attn_full[:, : 3 * width])
    grad_tokens = join_halves((d_hidden + half_sum(token_back, core)).astype(jnp.bfloat16), core)

    def by_owner(flat):
        return flat.reshape(heads, n, -1).transpose(1, 0, 2).reshape(n, -1)

    head_rows = jnp.concatenate([by_owner(grad_qscale), by_owner(grad_kscale)], axis=1)
    col_rows = jnp.concatenate(
        [attn_gain_rows.reshape(n, -1), mlp_gain_rows.reshape(n, -1)], axis=1
    )
    if fused:
        head_rows = jnp.pad(head_rows, ((0, 0), (0, 128 - head_rows.shape[1])))
        col_rows = jnp.pad(col_rows, ((0, 0), (0, 896 - col_rows.shape[1])))
        rows = jnp.concatenate([head_rows, col_rows], axis=1).reshape(n, 8, 128)
        grad_attn = after(grad_attn, (out_down, out_gate, out_up))
        out_attn, summed = kernel_scatter(grad_attn, rows, n)
        summed = summed.reshape(-1)
        cols = summed[128:]
    else:
        (out_attn,), marks = net.scatters([grad_attn], [None])
        summed = lax.psum_scatter(head_rows, "dp", scatter_dimension=0, tiled=True)[0]
        cols = lax.psum_scatter(col_rows, "dp", scatter_dimension=0, tiled=True)[0]
        cols = cols + lax.ppermute(cols, "mp", CORE_SWAP)
    return (
        block_out,
        grad_tokens,
        out_attn[:, :width],
        out_attn[:, width : 2 * width],
        out_attn[:, 2 * width : 3 * width],
        out_attn[:, 3 * width :].T,
        summed[:head_part].reshape(q_gain.shape),
        summed[head_part : 2 * head_part].reshape(k_gain.shape),
        cols[:col_part],
        out_gate,
        out_up,
        out_down.T,
        cols[col_part : 2 * col_part],
    )


def solution(mesh):
    in_specs = (
        P("dp", None),
        P("dp"),
        P("dp", "mp"),
        P("dp", "mp"),
        P("dp", "mp"),
        P("mp", "dp"),
        P("mp", "dp"),
        P("mp", "dp"),
        P("dp"),
        P("dp", "mp"),
        P("dp", "mp"),
        P("mp", "dp"),
        P("dp"),
        P("dp", None),
    )
    out_specs = (
        P("dp", None),
        P("dp", None),
        P("dp", "mp"),
        P("dp", "mp"),
        P("dp", "mp"),
        P("mp", "dp"),
        P("mp", "dp"),
        P("mp", "dp"),
        P("dp"),
        P("dp", "mp"),
        P("dp", "mp"),
        P("mp", "dp"),
        P("dp"),
    )
    n = mesh.shape["dp"]

    def program(*arrays):
        return on_device(n, *arrays)

    return jax.shard_map(
        program, mesh=mesh, in_specs=in_specs, out_specs=out_specs, check_vma=False
    )
```

```python
import functools
import math

import jax
import jax.numpy as jnp
from jax import lax
from jax.experimental import pallas as pl
from jax.experimental.pallas import tpu as pltpu
from jax.sharding import PartitionSpec as P

D = 2048
HEAD_CHANNELS = 128
SEQ_LEN = 1024
RING = 8


EPSILON = 1e-06
ROPE_BASE = 500000.0
MASKED = -1e30
ROW_LIMIT = 512


def matmul(left_side, right_side):
    return jnp.dot(left_side, right_side, preferred_element_type=jnp.float32)


def transposed_left(left_side, right_side):
    return lax.dot_general(
        left_side, right_side, (((0,), (0,)), ((), ())), preferred_element_type=jnp.float32
    )


def transposed_right(left_side, right_side):
    return lax.dot_general(
        left_side, right_side, (((1,), (1,)), ((), ())), preferred_element_type=jnp.float32
    )


def angles_of(doc_rows, seq_len, head_dim):
    shaped = doc_rows.reshape(-1, seq_len)
    leading = jnp.sum(1 - shaped, axis=1, keepdims=True, dtype=jnp.int32)
    places = jnp.arange(seq_len, dtype=jnp.int32)[None, :] - shaped * leading
    frequency = jnp.exp(
        jnp.arange(head_dim // 2, dtype=jnp.float32) * (-2.0 * math.log(ROPE_BASE) / head_dim)
    )
    return places.reshape(-1).astype(jnp.float32)[:, None] * frequency[None, :]


def rotate(vectors, angles):
    halfway = vectors.shape[-1] // 2
    cosine = jnp.cos(angles)[:, None, :]
    sine_wave = jnp.sin(angles)[:, None, :]
    former = vectors[..., :halfway]
    latter = vectors[..., halfway:]
    return jnp.concatenate(
        [former * cosine - latter * sine_wave, latter * cosine + former * sine_wave], axis=-1
    )


def rotate_back(vectors, angles):
    halfway = vectors.shape[-1] // 2
    cosine = jnp.cos(angles)[:, None, :]
    sine_wave = jnp.sin(angles)[:, None, :]
    former = vectors[..., :halfway]
    latter = vectors[..., halfway:]
    return jnp.concatenate(
        [former * cosine + latter * sine_wave, latter * cosine - former * sine_wave], axis=-1
    )


def block_scores(query_block, key_seq, doc_seq, offset):
    factor = 1.0 / math.sqrt(query_block.shape[-1])
    scores = (
        jnp.einsum("qhd,khd->hqk", query_block, key_seq, preferred_element_type=jnp.float32)
        * factor
    )
    row_places = offset + jnp.arange(query_block.shape[0], dtype=jnp.int32)
    key_places = jnp.arange(key_seq.shape[0], dtype=jnp.int32)
    row_docs = doc_seq[offset : offset + query_block.shape[0]]
    allowed = (key_places[None, :] <= row_places[:, None]) & (doc_seq[None, :] == row_docs[:, None])
    return jnp.where(allowed[None], scores, MASKED)


def attend_sequence(inputs):
    query_seq, key_seq, value_seq, doc_seq = inputs
    row_block = math.gcd(query_seq.shape[0], ROW_LIMIT)
    outputs = []
    totals = []
    for offset in range(0, query_seq.shape[0], row_block):
        scores = block_scores(query_seq[offset : offset + row_block], key_seq, doc_seq, offset)
        maximum = jnp.max(scores, axis=-1, keepdims=True)
        weights = jnp.exp(scores - maximum)
        denominator = jnp.sum(weights, axis=-1, keepdims=True)
        rounded = (weights / denominator).astype(jnp.bfloat16)
        outputs.append(
            jnp.einsum(
                "hqk,khd->qhd", rounded, value_seq, preferred_element_type=jnp.float32
            ).astype(jnp.bfloat16)
        )
        totals.append((maximum + jnp.log(denominator))[..., 0])
    return (jnp.concatenate(outputs, axis=0), jnp.concatenate(totals, axis=1))


def attend_backward(inputs):
    query_seq, key_seq, value_seq, doc_seq, grad_seq, lse_seq = inputs
    row_block = math.gcd(query_seq.shape[0], ROW_LIMIT)
    factor = 1.0 / math.sqrt(query_seq.shape[-1])
    grad_keys = jnp.zeros(key_seq.shape, jnp.float32)
    grad_values = jnp.zeros(value_seq.shape, jnp.float32)
    grad_rows = []
    for offset in range(0, query_seq.shape[0], row_block):
        query_block = query_seq[offset : offset + row_block]
        grad_block = grad_seq[offset : offset + row_block]
        scores = block_scores(query_block, key_seq, doc_seq, offset)
        weights = jnp.exp(scores - lse_seq[:, offset : offset + row_block, None])
        d_weights = jnp.einsum(
            "qhd,khd->hqk", grad_block, value_seq, preferred_element_type=jnp.float32
        )
        correction = jnp.sum(d_weights * weights, axis=-1, keepdims=True)
        d_scores = (weights * (d_weights - correction)).astype(jnp.bfloat16)
        grad_rows.append(
            jnp.einsum("hqk,khd->qhd", d_scores, key_seq, preferred_element_type=jnp.float32)
            * factor
        )
        grad_keys = (
            grad_keys
            + jnp.einsum("hqk,qhd->khd", d_scores, query_block, preferred_element_type=jnp.float32)
            * factor
        )
        grad_values = grad_values + jnp.einsum(
            "hqk,qhd->khd",
            weights.astype(jnp.bfloat16),
            grad_block,
            preferred_element_type=jnp.float32,
        )
    return (jnp.concatenate(grad_rows, axis=0), grad_keys, grad_values)


def plain_layer(
    tokens,
    doc_ids,
    q_weight,
    k_weight,
    v_weight,
    o_weight,
    q_gain,
    k_gain,
    attn_gain,
    gate_weight,
    up_weight,
    down_weight,
    mlp_gain,
    cotangent,
):
    query_full, key_complete, value_full, output_full, query_gains, key_gains, attn_gains = (
        lax.all_gather(q_weight, "dp", axis=0, tiled=True),
        lax.all_gather(k_weight, "dp", axis=0, tiled=True),
        lax.all_gather(v_weight, "dp", axis=0, tiled=True),
        lax.all_gather(o_weight, "dp", axis=1, tiled=True),
        lax.all_gather(q_gain, "dp", axis=1, tiled=True),
        lax.all_gather(k_gain, "dp", axis=1, tiled=True),
        lax.all_gather(attn_gain, "dp", axis=0, tiled=True),
    )
    gate_full, up_full, down_full, mlp_gains = (
        lax.all_gather(gate_weight, "dp", axis=0, tiled=True),
        lax.all_gather(up_weight, "dp", axis=0, tiled=True),
        lax.all_gather(down_weight, "dp", axis=1, tiled=True),
        lax.all_gather(mlp_gain, "dp", axis=0, tiled=True),
    )
    row_count = tokens.shape[0]
    heads_on_device = q_gain.shape[0]
    local_width = heads_on_device * HEAD_CHANNELS
    sequences = row_count // SEQ_LEN
    seq_shape = (sequences, SEQ_LEN, heads_on_device, HEAD_CHANNELS)
    angles = angles_of(doc_ids, SEQ_LEN, HEAD_CHANNELS)
    doc_seqs = doc_ids.reshape(sequences, SEQ_LEN)
    query_raw = matmul(tokens, query_full)
    key_unnormed = matmul(tokens, key_complete)
    values = matmul(tokens, value_full).astype(jnp.bfloat16)
    query_sq, key_sq = lax.psum(
        (jnp.sum(query_raw * query_raw, axis=1), jnp.sum(key_unnormed * key_unnormed, axis=1)), "mp"
    )
    query_inv = lax.rsqrt(query_sq / D + EPSILON)[:, None]
    key_inverse_norm = lax.rsqrt(key_sq / D + EPSILON)[:, None]
    query_scale = query_gains.reshape(-1)
    key_scale = key_gains.reshape(-1)
    query_rot = rotate(
        (query_raw * query_inv * query_scale).reshape(row_count, heads_on_device, HEAD_CHANNELS),
        angles,
    ).astype(jnp.bfloat16)
    key_rot = rotate(
        (key_unnormed * key_inverse_norm * key_scale).reshape(
            row_count, heads_on_device, HEAD_CHANNELS
        ),
        angles,
    ).astype(jnp.bfloat16)
    query_seqs = query_rot.reshape(seq_shape)
    key_seqs = key_rot.reshape(seq_shape)
    value_seqs = values.reshape(seq_shape)
    attended, lse_all = lax.map(attend_sequence, (query_seqs, key_seqs, value_seqs, doc_seqs))
    attended = attended.reshape(row_count, local_width)
    branch = lax.psum(matmul(attended, output_full), "mp")
    branch_inv = lax.rsqrt(jnp.mean(branch * branch, axis=1, keepdims=True) + EPSILON)
    hidden_state = tokens.astype(jnp.float32) + branch * branch_inv * attn_gains
    hidden_low = hidden_state.astype(jnp.bfloat16)
    gate_act = matmul(hidden_low, gate_full)
    up_part = matmul(hidden_low, up_full)
    product = (jax.nn.silu(gate_act) * up_part).astype(jnp.bfloat16)
    mlp_branch = lax.psum(matmul(product, down_full).astype(jnp.bfloat16), "mp").astype(jnp.float32)
    mlp_inv = lax.rsqrt(jnp.mean(mlp_branch * mlp_branch, axis=1, keepdims=True) + EPSILON)
    block_out = (hidden_state + mlp_branch * mlp_inv * mlp_gains).astype(jnp.bfloat16)
    gate_full, up_full, down_full, mlp_gains = (
        lax.all_gather(gate_weight, "dp", axis=0, tiled=True),
        lax.all_gather(up_weight, "dp", axis=0, tiled=True),
        lax.all_gather(down_weight, "dp", axis=1, tiled=True),
        lax.all_gather(mlp_gain, "dp", axis=0, tiled=True),
    )
    upstream = cotangent.astype(jnp.float32)
    grad_mlp_scale = jnp.sum(upstream * mlp_branch * mlp_inv, axis=0)
    mlp_scaled = mlp_gains * upstream
    mlp_cube = mlp_inv * mlp_inv * mlp_inv
    d_mlp = (
        mlp_inv * mlp_scaled
        - mlp_branch * mlp_cube * jnp.mean(mlp_scaled * mlp_branch, axis=1, keepdims=True)
    ).astype(jnp.bfloat16)
    grad_down = transposed_left(product, d_mlp)
    d_product = transposed_right(d_mlp, down_full)
    sigmoid = jax.nn.sigmoid(gate_act)
    d_gate = (d_product * up_part * sigmoid * (1.0 + gate_act * (1.0 - sigmoid))).astype(
        jnp.bfloat16
    )
    d_up = (d_product * gate_act * sigmoid).astype(jnp.bfloat16)
    grad_gate = transposed_left(hidden_low, d_gate)
    grad_up = transposed_left(hidden_low, d_up)
    mlp_input = transposed_right(d_gate, gate_full) + transposed_right(d_up, up_full)
    d_hidden = upstream + lax.psum(mlp_input.astype(jnp.bfloat16), "mp").astype(jnp.float32)
    mlp_grads = (
        lax.psum_scatter(
            grad_gate.astype(jnp.bfloat16), "dp", scatter_dimension=0, tiled=True
        ).astype(jnp.float32),
        lax.psum_scatter(
            grad_up.astype(jnp.bfloat16), "dp", scatter_dimension=0, tiled=True
        ).astype(jnp.float32),
        lax.psum_scatter(
            grad_down.astype(jnp.bfloat16), "dp", scatter_dimension=1, tiled=True
        ).astype(jnp.float32),
        lax.psum_scatter(
            grad_mlp_scale.astype(jnp.bfloat16), "dp", scatter_dimension=0, tiled=True
        ).astype(jnp.float32),
    )
    query_full, key_complete, value_full, output_full, query_gains, key_gains, attn_gains = (
        lax.all_gather(q_weight, "dp", axis=0, tiled=True),
        lax.all_gather(k_weight, "dp", axis=0, tiled=True),
        lax.all_gather(v_weight, "dp", axis=0, tiled=True),
        lax.all_gather(o_weight, "dp", axis=1, tiled=True),
        lax.all_gather(q_gain, "dp", axis=1, tiled=True),
        lax.all_gather(k_gain, "dp", axis=1, tiled=True),
        lax.all_gather(attn_gain, "dp", axis=0, tiled=True),
    )
    query_scale = query_gains.reshape(-1)
    key_scale = key_gains.reshape(-1)
    grad_attn_scale = jnp.sum(d_hidden * branch * branch_inv, axis=0)
    attn_scaled = attn_gains * d_hidden
    branch_cube = branch_inv * branch_inv * branch_inv
    d_branch = (
        branch_inv * attn_scaled
        - branch * branch_cube * jnp.mean(attn_scaled * branch, axis=1, keepdims=True)
    ).astype(jnp.bfloat16)
    grad_output = transposed_left(attended, d_branch)
    d_attended = transposed_right(d_branch, output_full).astype(jnp.bfloat16)
    grad_qrot, grad_krot, grad_vals = lax.map(
        attend_backward,
        (query_seqs, key_seqs, value_seqs, doc_seqs, d_attended.reshape(seq_shape), lse_all),
    )
    d_values = grad_vals.reshape(row_count, local_width).astype(jnp.bfloat16)
    d_qnorm = rotate_back(
        grad_qrot.reshape(row_count, heads_on_device, HEAD_CHANNELS), angles
    ).reshape(row_count, local_width)
    grad_key_normed = rotate_back(
        grad_krot.reshape(row_count, heads_on_device, HEAD_CHANNELS), angles
    ).reshape(row_count, local_width)
    grad_qscale = jnp.sum(d_qnorm * query_raw * query_inv, axis=0).reshape(
        heads_on_device, HEAD_CHANNELS
    )
    grad_key_rms_factor = jnp.sum(
        grad_key_normed * key_unnormed * key_inverse_norm, axis=0
    ).reshape(heads_on_device, HEAD_CHANNELS)
    query_scaled = query_scale * d_qnorm
    key_scaled = key_scale * grad_key_normed
    query_inner, key_inner = lax.psum(
        (jnp.sum(query_scaled * query_raw, axis=1), jnp.sum(key_scaled * key_unnormed, axis=1)),
        "mp",
    )
    query_cube = query_inv * query_inv * query_inv
    key_cube = key_inverse_norm * key_inverse_norm * key_inverse_norm
    d_query = (
        query_inv * query_scaled - query_raw * query_cube * (query_inner / D)[:, None]
    ).astype(jnp.bfloat16)
    d_key = (
        key_inverse_norm * key_scaled - key_unnormed * key_cube * (key_inner / D)[:, None]
    ).astype(jnp.bfloat16)
    grad_query = transposed_left(tokens, d_query)
    grad_key = transposed_left(tokens, d_key)
    grad_value = transposed_left(tokens, d_values)
    token_back = (
        transposed_right(d_query, query_full)
        + transposed_right(d_key, key_complete)
        + transposed_right(d_values, value_full)
    )
    grad_tokens = (
        d_hidden + lax.psum(token_back.astype(jnp.bfloat16), "mp").astype(jnp.float32)
    ).astype(jnp.bfloat16)
    attn_grads = (
        lax.psum_scatter(
            grad_query.astype(jnp.bfloat16), "dp", scatter_dimension=0, tiled=True
        ).astype(jnp.float32),
        lax.psum_scatter(
            grad_key.astype(jnp.bfloat16), "dp", scatter_dimension=0, tiled=True
        ).astype(jnp.float32),
        lax.psum_scatter(
            grad_value.astype(jnp.bfloat16), "dp", scatter_dimension=0, tiled=True
        ).astype(jnp.float32),
        lax.psum_scatter(
            grad_output.astype(jnp.bfloat16), "dp", scatter_dimension=1, tiled=True
        ).astype(jnp.float32),
        lax.psum_scatter(
            grad_qscale.astype(jnp.bfloat16), "dp", scatter_dimension=1, tiled=True
        ).astype(jnp.float32),
        lax.psum_scatter(
            grad_key_rms_factor.astype(jnp.bfloat16), "dp", scatter_dimension=1, tiled=True
        ).astype(jnp.float32),
        lax.psum_scatter(
            grad_attn_scale.astype(jnp.bfloat16), "dp", scatter_dimension=0, tiled=True
        ).astype(jnp.float32),
    )
    return (
        block_out,
        grad_tokens,
        attn_grads[0],
        attn_grads[1],
        attn_grads[2],
        attn_grads[3],
        attn_grads[4],
        attn_grads[5],
        attn_grads[6],
        mlp_grads[0],
        mlp_grads[1],
        mlp_grads[2],
        mlp_grads[3],
    )


MESH = pl.DeviceIdType.MESH
SUBS = 2


def place_of(index, n):
    odd = lax.rem(index, 2)
    half = lax.div(index, 2)
    return (1 - odd) * half + odd * (n - 1 - half)


def device_at(place, n):
    late = lax.div(place, n // 2)
    return (1 - late) * (2 * place) + late * (2 * (n - 1 - place) + 1)


def holder_of(index, steps, n):
    return device_at(lax.rem(place_of(index, n) + (steps + 2 * n), n), n)


def greet(targets):
    barrier = pltpu.get_barrier_semaphore()
    for target in targets:
        pl.semaphore_signal(barrier, inc=1, device_id=target, device_id_type=MESH)
    pl.semaphore_wait(barrier, len(targets))


def gather_kernel(n, shard, small, full, small_full, send, recv, small_send, small_recv, local):
    index = lax.axis_index("dp")
    right = {"dp": holder_of(index, 1, n)}
    left = {"dp": holder_of(index, -1, n)}
    greet((right, left))
    rows = shard.shape[1] // SUBS

    def hop(way, sub, step):
        owner = holder_of(index, (step - 1) * (2 * way - 1), n)
        span = pl.ds(sub * rows, rows)
        target = full.at[owner, way, span]
        return pltpu.make_async_remote_copy(
            src_ref=shard.at[way, span] if step == 1 else target,
            dst_ref=target,
            send_sem=send.at[way, sub, step - 1],
            recv_sem=recv.at[way, sub, step - 1],
            device_id=left if way else right,
            device_id_type=MESH,
        )

    def arrival(way, sub, step):
        owner = holder_of(index, step * (2 * way - 1), n)
        span = pl.ds(sub * rows, rows)
        target = full.at[owner, way, span]
        return pltpu.make_async_remote_copy(
            src_ref=target,
            dst_ref=target,
            send_sem=send.at[way, sub, step - 1],
            recv_sem=recv.at[way, sub, step - 1],
            device_id=left if way else right,
            device_id_type=MESH,
        )

    def small_hop(step, back):
        owner = holder_of(index, back - step, n)
        target = small_full.at[owner]
        return pltpu.make_async_remote_copy(
            src_ref=small if step == 1 and back else target,
            dst_ref=target,
            send_sem=small_send.at[step - 1],
            recv_sem=small_recv.at[step - 1],
            device_id=right,
            device_id_type=MESH,
        )

    for sub in range(SUBS):
        for way in range(2):
            hop(way, sub, 1).start()
    small_hop(1, 1).start()
    own = pltpu.make_async_copy(shard, full.at[index], local.at[0])
    own_small = pltpu.make_async_copy(small, small_full.at[index], local.at[1])
    own.start()
    own_small.start()
    for step in range(1, n):
        for sub in range(SUBS):
            for way in range(2):
                arrival(way, sub, step).wait_recv()
                if step < n - 1:
                    hop(way, sub, step + 1).start()
        small_hop(step, 0).wait_recv()
        if step < n - 1:
            small_hop(step + 1, 1).start()
    own.wait()
    own_small.wait()
    for step in range(1, n):
        for sub in range(SUBS):
            for way in range(2):
                hop(way, sub, step).wait_send()
        small_hop(step, 1).wait_send()


def kernel_gather(shard, small, n):
    rows, width = shard.shape
    full, small_full = pl.pallas_call(
        functools.partial(gather_kernel, n),
        out_shape=(
            jax.ShapeDtypeStruct((n, 2, rows // 2, width), shard.dtype),
            jax.ShapeDtypeStruct((n, *small.shape), small.dtype),
        ),
        in_specs=[pl.BlockSpec(memory_space=pl.ANY)] * 2,
        out_specs=(pl.BlockSpec(memory_space=pl.ANY),) * 2,
        scratch_shapes=[
            pltpu.SemaphoreType.DMA((2, SUBS, n - 1)),
            pltpu.SemaphoreType.DMA((2, SUBS, n - 1)),
            pltpu.SemaphoreType.DMA((n - 1,)),
            pltpu.SemaphoreType.DMA((n - 1,)),
            pltpu.SemaphoreType.DMA((2,)),
        ],
        compiler_params=pltpu.CompilerParams(collective_id=0, has_side_effects=True),
    )(shard.reshape(2, rows // 2, width), small)
    return full.reshape(n * rows, width), small_full


def scatter_kernel(
    n,
    parts,
    small,
    out,
    small_out,
    inbox,
    outbox,
    small_inbox,
    small_outbox,
    send,
    recv,
    small_send,
    small_recv,
):
    index = lax.axis_index("dp")
    rank = lax.axis_index("mp")
    right = {"dp": holder_of(index, 1, n)}
    left = {"dp": holder_of(index, -1, n)}
    twin = {"mp": rank + 1 - 2 * lax.rem(rank, 2)}
    greet((right, left, twin))
    rows = parts.shape[2] // SUBS

    def hop(way, sub, step):
        span = pl.ds(sub * rows, rows)
        first = parts.at[holder_of(index, 2 * way - 1, n), way, span]
        return pltpu.make_async_remote_copy(
            src_ref=first if step == 1 else outbox.at[step - 2, way, sub],
            dst_ref=inbox.at[step - 1, way, sub],
            send_sem=send.at[way, sub, step - 1],
            recv_sem=recv.at[way, sub, step - 1],
            device_id=left if way else right,
            device_id_type=MESH,
        )

    def small_hop(step):
        first = small.at[holder_of(index, -1, n)]
        return pltpu.make_async_remote_copy(
            src_ref=first if step == 1 else small_outbox.at[step - 2],
            dst_ref=small_inbox.at[step - 1],
            send_sem=small_send.at[step - 1],
            recv_sem=small_recv.at[step - 1],
            device_id=twin if step == n else right,
            device_id_type=MESH,
        )

    for sub in range(SUBS):
        for way in range(2):
            hop(way, sub, 1).start()
    small_hop(1).start()
    for step in range(1, n):
        for sub in range(SUBS):
            for way in range(2):
                hop(way, sub, step).wait_recv()
                owner = holder_of(index, (1 + step) * (2 * way - 1), n)

                @pl.loop(0, rows // 16)
                def _(tile, way=way, sub=sub, step=step, owner=owner):
                    near = pl.ds(pl.multiple_of(tile * 16, 16), 16)
                    far = pl.ds(pl.multiple_of(sub * rows + tile * 16, 16), 16)
                    total = inbox[step - 1, way, sub, near, :].astype(jnp.float32) + parts[
                        owner, way, far, :
                    ].astype(jnp.float32)
                    if step < n - 1:
                        outbox[step - 1, way, sub, near, :] = total.astype(outbox.dtype)
                    else:
                        out[way, far, :] = total

                if step < n - 1:
                    hop(way, sub, step + 1).start()
        small_hop(step).wait_recv()
        small_outbox[step - 1] = small_inbox[step - 1] + small[holder_of(index, -1 - step, n)]
        small_hop(step + 1).start()
    small_hop(n).wait_recv()
    line = lax.broadcasted_iota(jnp.int32, small_out.shape, 0)
    small_out[...] = small_outbox[n - 2] + jnp.where(line > 0, small_inbox[n - 1], 0.0)
    for step in range(1, n):
        for sub in range(SUBS):
            for way in range(2):
                hop(way, sub, step).wait_send()
        small_hop(step).wait_send()
    small_hop(n).wait_send()


def kernel_scatter(grad, small, n):
    rows, width = grad.shape[0] // n, grad.shape[1]
    out, small_out = pl.pallas_call(
        functools.partial(scatter_kernel, n),
        out_shape=(
            jax.ShapeDtypeStruct((2, rows // 2, width), jnp.float32),
            jax.ShapeDtypeStruct(small.shape[1:], jnp.float32),
        ),
        in_specs=[pl.BlockSpec(memory_space=pltpu.VMEM)] * 2,
        out_specs=(pl.BlockSpec(memory_space=pltpu.VMEM),) * 2,
        scratch_shapes=[
            pltpu.VMEM((n - 1, 2, SUBS, rows // 2 // SUBS, width), grad.dtype),
            pltpu.VMEM((n - 2, 2, SUBS, rows // 2 // SUBS, width), grad.dtype),
            pltpu.VMEM((n, *small.shape[1:]), jnp.float32),
            pltpu.VMEM((n - 1, *small.shape[1:]), jnp.float32),
            pltpu.SemaphoreType.DMA((2, SUBS, n - 1)),
            pltpu.SemaphoreType.DMA((2, SUBS, n - 1)),
            pltpu.SemaphoreType.DMA((n,)),
            pltpu.SemaphoreType.DMA((n,)),
        ],
        compiler_params=pltpu.CompilerParams(
            collective_id=1, has_side_effects=True, vmem_limit_bytes=48 * 2**20
        ),
    )(grad.reshape(n, 2, rows // 2, width), small)
    return out.reshape(rows, width), small_out


BLOCK = 256


def neighbours(n):
    index = lax.axis_index("dp")
    rank = lax.axis_index("mp")
    core = lax.rem(rank, 2)
    right = {"dp": holder_of(index, 1, n)}
    left = {"dp": holder_of(index, -1, n)}
    twin = {"mp": rank + 1 - 2 * core}
    far = {"mp": lax.rem(rank + 2, 4)}
    return index, core, right, left, twin, far


def exchange(source, target, send, recv, slot, device):
    return pltpu.make_async_remote_copy(
        src_ref=source,
        dst_ref=target,
        send_sem=send.at[slot],
        recv_sem=recv.at[slot],
        device_id=device,
        device_id_type=MESH,
    )


def columns_to_rows(pieces, count):
    lane = lax.broadcasted_iota(jnp.int32, (count, 128), 1)
    spread = jnp.zeros((count, 128), jnp.float32)
    for place, piece in enumerate(pieces):
        spread = jnp.where(lane == place, piece, spread)
    return spread.T[:8]


def rows_to_columns(rows):
    padded = jnp.concatenate([rows] + [jnp.zeros_like(rows)] * 15, axis=0)
    return padded.T


def turned(vectors, cosine, sine):
    return vectors * cosine + pltpu.roll(vectors, HEAD_CHANNELS // 2, 1) * sine


def masked_scores(query, key, doc_col, doc_row, block):
    length = key.shape[0]
    scores = lax.dot_general(
        query, key, (((1,), (1,)), ((), ())), preferred_element_type=jnp.float32
    ) * (1.0 / math.sqrt(HEAD_CHANNELS))
    row = lax.broadcasted_iota(jnp.int32, scores.shape, 0) + block * BLOCK
    col = lax.broadcasted_iota(jnp.int32, scores.shape, 1)
    same = doc_col[block * BLOCK : (block + 1) * BLOCK, :] == doc_row[:, :length]
    return jnp.where((col <= row) & same, scores, MASKED)


def attend_kernel(
    n,
    tokens,
    attn_full,
    gate_shard,
    up_shard,
    token_half,
    cosine,
    sine,
    doc_col,
    doc_row,
    query_gain,
    key_gain,
    attn_gain,
    gate_full,
    up_full,
    query_raw_out,
    key_raw_out,
    query_rot_out,
    key_rot_out,
    value_out,
    attended_out,
    totals,
    inverses,
    branch_out,
    hidden_out,
    hidden_low,
    lhs,
    weights,
    query_raw,
    key_raw,
    query_rot,
    key_rot,
    value,
    attended,
    mixed,
    twin_in,
    pair,
    far_in,
    branch,
    half_buf,
    low_buf,
    stat,
    ring_send,
    ring_recv,
    stat_send,
    stat_recv,
    twin_send,
    twin_recv,
    far_send,
    far_recv,
    join_send,
    join_recv,
    load_sem,
    store_sem,
):
    index, core, right, left, twin, far = neighbours(n)
    count, width = lhs.shape
    half = count // 2
    local = query_raw.shape[1]
    heads = local // HEAD_CHANNELS
    blocks = width // TILE
    shards = (gate_shard, up_shard)
    fulls = (gate_full, up_full)
    right_side = (((1,), (1,)), ((), ()))

    def ring(way, unit, step, incoming):
        owner = holder_of(index, (step - 1 + incoming) * (2 * way - 1), n)
        target = fulls[unit].at[owner, way]
        return pltpu.make_async_remote_copy(
            src_ref=shards[unit].at[way] if step == 1 and not incoming else target,
            dst_ref=target,
            send_sem=ring_send.at[way, unit, step - 1],
            recv_sem=ring_recv.at[way, unit, step - 1],
            device_id=left if way else right,
            device_id_type=MESH,
        )

    events = [(step, unit) for step in range(1, n) for unit in range(2)]

    def serve():
        step, unit = events.pop(0)
        for way in range(2):
            ring(way, unit, step, 1).wait_recv()
            if step < n - 1:
                ring(way, unit, step + 1, 0).start()

    greet((right, left, twin, far))
    for unit in range(2):
        for way in range(2):
            ring(way, unit, 1, 0).start()
    loads = [
        pltpu.make_async_copy(tokens, lhs, load_sem.at[0]),
        pltpu.make_async_copy(attn_full, weights, load_sem.at[1]),
        pltpu.make_async_copy(token_half, half_buf, load_sem.at[2]),
        pltpu.make_async_copy(gate_shard, gate_full.at[index], load_sem.at[3]),
        pltpu.make_async_copy(up_shard, up_full.at[index], load_sem.at[4]),
    ]
    for copy in loads:
        copy.start()
    loads[0].wait()
    loads[1].wait()

    def project(target, start):
        for tile in range(local // TILE):
            cols = slice(start + tile * TILE, start + (tile + 1) * TILE)
            target[:, tile * TILE : (tile + 1) * TILE] = jnp.dot(
                lhs[...], weights[:, cols], preferred_element_type=jnp.float32
            ).astype(target.dtype)

    project(query_raw, 0)
    project(key_raw, local)
    squares = [
        jnp.sum(raw[...] * raw[...], axis=1, keepdims=True) for raw in (query_raw, key_raw)
    ]
    stat[0] = columns_to_rows(squares, count)
    first = exchange(stat.at[0], stat.at[1], stat_send, stat_recv, 0, twin)
    first.start()
    project(value, 2 * local)
    first.wait()
    stat[2] = stat[0] + stat[1]
    second = exchange(stat.at[2], stat.at[3], stat_send, stat_recv, 1, far)
    second.start()
    serve()
    second.wait()
    inverses[...] = lax.rsqrt(rows_to_columns(stat[2] + stat[3]) / width + EPSILON)

    @pl.loop(0, heads)
    def _(head):
        cols = pl.ds(pl.multiple_of(head * HEAD_CHANNELS, HEAD_CHANNELS), HEAD_CHANNELS)
        for place, (raw, gain, out) in enumerate(
            ((query_raw, query_gain, query_rot), (key_raw, key_gain, key_rot))
        ):
            normed = raw[:, cols] * inverses[:, place : place + 1] * gain[:, cols]
            out[:, cols] = turned(normed, cosine[...], sine[...]).astype(jnp.bfloat16)

    stores = [
        pltpu.make_async_copy(source, target, store_sem.at[place])
        for place, (source, target) in enumerate(
            (
                (query_raw, query_raw_out),
                (key_raw, key_raw_out),
                (query_rot, query_rot_out),
                (key_rot, key_rot_out),
                (value, value_out),
            )
        )
    ]
    for copy in stores:
        copy.start()
    serve()
    totals[...] = jnp.zeros_like(totals)

    @pl.loop(0, heads)
    def _(head):
        cols = pl.ds(pl.multiple_of(head * HEAD_CHANNELS, HEAD_CHANNELS), HEAD_CHANNELS)
        lane = lax.broadcasted_iota(jnp.int32, (BLOCK, 128), 1)
        for block in range(count // BLOCK):
            span = slice(block * BLOCK, (block + 1) * BLOCK)
            length = (block + 1) * BLOCK
            scores = masked_scores(
                query_rot[span, cols], key_rot[:length, cols], doc_col, doc_row, block
            )
            maximum = jnp.max(scores, axis=1, keepdims=True)
            powers = jnp.exp(scores - maximum)
            denominator = jnp.sum(powers, axis=1, keepdims=True)
            rounded = (powers * (1.0 / denominator)).astype(jnp.bfloat16)
            attended[span, cols] = jnp.dot(
                rounded, value[:length, cols], preferred_element_type=jnp.float32
            ).astype(jnp.bfloat16)
            totals[span, :] = jnp.where(
                lane == head, maximum + jnp.log(denominator), totals[span, :]
            )

    stores.append(pltpu.make_async_copy(attended, attended_out, store_sem.at[5]))
    stores[5].start()
    serve()

    def twin_copy(tile):
        span = pl.ds(pl.multiple_of((1 - core) * half, half), half)
        return exchange(
            mixed.at[tile % 4, span], twin_in.at[tile % 4], twin_send, twin_recv, tile, twin
        )

    def far_copy(tile):
        return exchange(pair.at[tile], far_in.at[tile], far_send, far_recv, tile, far)

    def output_tile(tile):
        span = slice(tile * TILE, (tile + 1) * TILE)
        mixed[tile % 4] = lax.dot_general(
            attended[...],
            weights[span, 3 * local :],
            right_side,
            preferred_element_type=jnp.float32,
        ).astype(jnp.bfloat16)
        twin_copy(tile).start()

    def add_twin(tile):
        twin_copy(tile).wait_recv()

        @pl.loop(0, half // 32)
        def _(row):
            span = pl.ds(pl.multiple_of(row * 32, 32), 32)
            mine = pl.ds(pl.multiple_of(core * half + row * 32, 32), 32)
            total = mixed[tile % 4, mine, :].astype(jnp.float32) + twin_in[
                tile % 4, span, :
            ].astype(jnp.float32)
            pair[tile, span, :] = total.astype(jnp.bfloat16)

        far_copy(tile).start()
        twin_copy(tile).wait_send()

    def add_far(tile):
        far_copy(tile).wait_recv()

        @pl.loop(0, half // 32)
        def _(row):
            span = pl.ds(pl.multiple_of(row * 32, 32), 32)
            branch[span, tile * TILE : (tile + 1) * TILE] = pair[tile, span, :].astype(
                jnp.float32
            ) + far_in[tile, span, :].astype(jnp.float32)

    for tile in range(blocks):
        output_tile(tile)
        if tile >= 1:
            add_twin(tile - 1)
    add_twin(blocks - 1)
    serve()
    for tile in range(blocks):
        add_far(tile)
        if tile % 2 == 1:
            serve()
    loads[2].wait()

    def finish(tile):
        span = pl.ds(pl.multiple_of(tile * 16, 16), 16)
        mix = branch[span, :]
        inverse = lax.rsqrt(jnp.sum(mix * mix, axis=1, keepdims=True) / width + EPSILON)
        state = half_buf[span, :].astype(jnp.float32) + mix * inverse * attn_gain[...]
        low_buf[span, :] = state.astype(jnp.bfloat16)
        hidden_out[span, :] = state

    def join(part, kind):
        span = pl.ds(part * (half // 4), half // 4)
        if kind == 2:
            return pltpu.make_async_copy(
                low_buf.at[span], hidden_low.at[core, span], store_sem.at[6 + part]
            )
        target = hidden_low.at[1 - core if kind else core, span]
        return exchange(
            target if kind else low_buf.at[span], target, join_send, join_recv, part, twin
        )

    for part in range(4):
        pl.loop(part * (half // 64), (part + 1) * (half // 64))(finish)
        join(part, 0).start()
        join(part, 2).start()
    stores.append(pltpu.make_async_copy(branch, branch_out, store_sem.at[10]))
    stores[6].start()
    while events:
        serve()
    for part in range(4):
        join(part, 1).wait_recv()
        join(part, 0).wait_send()
        join(part, 2).wait()
    for copy in stores + loads[3:]:
        copy.wait()
    for tile in range(blocks):
        far_copy(tile).wait_send()
    for step in range(1, n):
        for unit in range(2):
            for way in range(2):
                ring(way, unit, step, 0).wait_send()


def kernel_attend(
    tokens,
    attn_full,
    gate_shard,
    up_shard,
    token_half,
    cosine,
    sine,
    doc_ids,
    query_gain,
    key_gain,
    attn_gain,
    n,
):
    count, width = tokens.shape
    local = query_gain.shape[0]
    units = gate_shard.shape[1]
    half = count // 2
    chunk = width // n // 2
    blocks = width // TILE
    low = jnp.bfloat16
    full = jnp.float32
    hbm = pl.BlockSpec(memory_space=pl.ANY)
    vmem = pl.BlockSpec(memory_space=pltpu.VMEM)
    dma = pltpu.SemaphoreType.DMA
    shape = jax.ShapeDtypeStruct
    outs = pl.pallas_call(
        functools.partial(attend_kernel, n),
        out_shape=(
            shape((n, 2, chunk, units), low),
            shape((n, 2, chunk, units), low),
            shape((count, local), full),
            shape((count, local), full),
            shape((count, local), low),
            shape((count, local), low),
            shape((count, local), low),
            shape((count, local), low),
            shape((count, 128), full),
            shape((count, 128), full),
            shape((half, width), full),
            shape((half, width), full),
            shape((2, half, width), low),
        ),
        in_specs=[hbm] * 5 + [vmem] * 7,
        out_specs=(hbm,) * 8 + (vmem,) * 2 + (hbm, vmem, hbm),
        scratch_shapes=[
            pltpu.VMEM((count, width), low),
            pltpu.VMEM((width, 4 * local), low),
            pltpu.VMEM((count, local), full),
            pltpu.VMEM((count, local), full),
            pltpu.VMEM((count, local), low),
            pltpu.VMEM((count, local), low),
            pltpu.VMEM((count, local), low),
            pltpu.VMEM((count, local), low),
            pltpu.VMEM((4, count, TILE), low),
            pltpu.VMEM((4, half, TILE), low),
            pltpu.VMEM((blocks, half, TILE), low),
            pltpu.VMEM((blocks, half, TILE), low),
            pltpu.VMEM((half, width), full),
            pltpu.VMEM((half, width), low),
            pltpu.VMEM((half, width), low),
            pltpu.VMEM((4, 8, count), full),
            dma((2, 2, n - 1)),
            dma((2, 2, n - 1)),
            dma((2,)),
            dma((2,)),
            dma((blocks,)),
            dma((blocks,)),
            dma((blocks,)),
            dma((blocks,)),
            dma((4,)),
            dma((4,)),
            dma((5,)),
            dma((11,)),
        ],
        compiler_params=pltpu.CompilerParams(
            collective_id=4, has_side_effects=True, vmem_limit_bytes=58 * 2**20
        ),
    )(
        tokens,
        attn_full,
        gate_shard.reshape(2, chunk, units),
        up_shard.reshape(2, chunk, units),
        token_half,
        cosine,
        sine,
        doc_ids.reshape(count, 1),
        doc_ids.reshape(1, count),
        query_gain.astype(full).reshape(1, local),
        key_gain.astype(full).reshape(1, local),
        attn_gain.astype(full).reshape(1, width),
    )
    return (
        outs[0].reshape(width, units),
        outs[1].reshape(width, units),
        *outs[2:12],
        outs[12].reshape(count, width),
    )


TILE = 256


def feed_kernel(
    n,
    hidden_low,
    gate_full,
    up_full,
    down_shard,
    hidden,
    upstream,
    gains,
    product_out,
    gate_slope,
    silu_out,
    down_full,
    d_mlp,
    block_half,
    gain_grad,
    lhs,
    product,
    held,
    gate_tile,
    up_tile,
    slope_tile,
    silu_tile,
    twin_out,
    twin_in,
    pair,
    far_in,
    branch,
    hidden_buf,
    upstream_buf,
    d_buf,
    block_buf,
    ring_send,
    ring_recv,
    twin_send,
    twin_recv,
    far_send,
    far_recv,
    join_send,
    join_recv,
    load_sem,
    tile_sem,
    stage_sem,
    store_sem,
):
    index = lax.axis_index("dp")
    rank = lax.axis_index("mp")
    core = lax.rem(rank, 2)
    right = {"dp": holder_of(index, 1, n)}
    left = {"dp": holder_of(index, -1, n)}
    twin = {"mp": rank + 1 - 2 * core}
    far = {"mp": lax.rem(rank + 2, 4)}
    half = hidden.shape[0]
    chunk = held.shape[2]
    rows = chunk // SUBS
    tiles = product.shape[1] // TILE
    width = branch.shape[1]

    loads = [
        pltpu.make_async_copy(hidden_low, lhs, load_sem.at[0]),
        pltpu.make_async_copy(down_shard, held.at[index], load_sem.at[1]),
        pltpu.make_async_copy(hidden, hidden_buf, load_sem.at[2]),
        pltpu.make_async_copy(upstream, upstream_buf, load_sem.at[3]),
    ]

    def weight_copies(tile, slot):
        cols = pl.ds(pl.multiple_of(tile * TILE, TILE), TILE)
        return (
            pltpu.make_async_copy(gate_full.at[:, cols], gate_tile.at[slot], tile_sem.at[slot, 0]),
            pltpu.make_async_copy(up_full.at[:, cols], up_tile.at[slot], tile_sem.at[slot, 1]),
        )

    def stage_copies(tile, slot):
        cols = pl.ds(pl.multiple_of(tile * TILE, TILE), TILE)
        return (
            pltpu.make_async_copy(slope_tile.at[slot], gate_slope.at[:, cols], stage_sem.at[slot, 0]),
            pltpu.make_async_copy(silu_tile.at[slot], silu_out.at[:, cols], stage_sem.at[slot, 1]),
        )

    def ring(way, sub, step, incoming):
        owner = holder_of(index, (step - 1 + incoming) * (2 * way - 1), n)
        span = pl.ds(sub * rows, rows)
        target = held.at[owner, way, span]
        return pltpu.make_async_remote_copy(
            src_ref=down_shard.at[way, span] if step == 1 and not incoming else target,
            dst_ref=target,
            send_sem=ring_send.at[way, sub, step - 1],
            recv_sem=ring_recv.at[way, sub, step - 1],
            device_id=left if way else right,
            device_id_type=MESH,
        )

    def serve(step, sub):
        for way in range(2):
            ring(way, sub, step, 1).wait_recv()
            if step < n - 1:
                ring(way, sub, step + 1, 0).start()

    def twin_copy(step):
        return pltpu.make_async_remote_copy(
            src_ref=twin_out.at[step],
            dst_ref=twin_in.at[step],
            send_sem=twin_send.at[step],
            recv_sem=twin_recv.at[step],
            device_id=twin,
            device_id_type=MESH,
        )

    def far_copy(step):
        return pltpu.make_async_remote_copy(
            src_ref=pair.at[step],
            dst_ref=far_in.at[step],
            send_sem=far_send.at[step],
            recv_sem=far_recv.at[step],
            device_id=far,
            device_id_type=MESH,
        )

    greet((right, left, twin, far))
    for sub in range(SUBS):
        for way in range(2):
            ring(way, sub, 1, 0).start()
    for copy in loads:
        copy.start()
    for copy in weight_copies(0, 0):
        copy.start()
    loads[0].wait()

    def feed_tile(tile):
        slot = lax.rem(tile, 2)
        for copy in weight_copies(tile, slot):
            copy.wait()

        @pl.when(tile + 1 < tiles)
        def _():
            for copy in weight_copies(tile + 1, 1 - slot):
                copy.start()

        @pl.when(tile >= 2)
        def _():
            for copy in stage_copies(tile - 2, slot):
                copy.wait()

        cols = pl.ds(pl.multiple_of(tile * TILE, TILE), TILE)

        @pl.loop(0, 2)
        def _(part):
            span = pl.ds(pl.multiple_of(part * half, half), half)
            gate = jnp.dot(lhs[span, :], gate_tile[slot], preferred_element_type=jnp.float32)
            up = jnp.dot(lhs[span, :], up_tile[slot], preferred_element_type=jnp.float32)
            sigmoid = jax.nn.sigmoid(gate)
            silu = gate * sigmoid
            product[span, cols] = (silu * up).astype(jnp.bfloat16)
            slope_tile[slot, span, :] = (up * sigmoid * (1.0 + gate * (1.0 - sigmoid))).astype(
                jnp.bfloat16
            )
            silu_tile[slot, span, :] = silu.astype(jnp.bfloat16)

        for copy in stage_copies(tile, slot):
            copy.start()

    events = [(step, sub) for step in range(1, n) for sub in range(SUBS)]
    groups = 4
    for group in range(groups):
        pl.loop(group * tiles // groups, (group + 1) * tiles // groups)(feed_tile)
        serve(*events.pop(0))
    stores = [pltpu.make_async_copy(product, product_out, store_sem.at[0])]
    stores[0].start()
    loads[1].wait()

    def multiply(step):
        first = held[holder_of(index, -step, n), 0]
        second = held[holder_of(index, step, n), 1]
        rhs = jnp.concatenate([first, second], axis=0)
        contract = (((1,), (1,)), ((), ()))
        span = pl.ds(pl.multiple_of((1 - core) * half, half), half)
        twin_out[step] = lax.dot_general(
            product[span, :], rhs, contract, preferred_element_type=jnp.float32
        ).astype(jnp.bfloat16)
        twin_copy(step).start()
        span = pl.ds(pl.multiple_of(core * half, half), half)
        pair[step] = lax.dot_general(
            product[span, :], rhs, contract, preferred_element_type=jnp.float32
        ).astype(jnp.bfloat16)

    def add_twin(step):
        twin_copy(step).wait_recv()

        @pl.loop(0, half // 32)
        def _(tile):
            span = pl.ds(pl.multiple_of(tile * 32, 32), 32)
            total = pair[step, span, :].astype(jnp.float32) + twin_in[step, span, :].astype(
                jnp.float32
            )
            pair[step, span, :] = total.astype(jnp.bfloat16)

        far_copy(step).start()

    def add_far(step):
        far_copy(step).wait_recv()
        first = holder_of(index, -step, n) * 2 * chunk
        second = holder_of(index, step, n) * 2 * chunk + chunk

        @pl.loop(0, half // 32)
        def _(tile):
            span = pl.ds(pl.multiple_of(tile * 32, 32), 32)
            total = pair[step, span, :].astype(jnp.float32) + far_in[step, span, :].astype(
                jnp.float32
            )
            branch[span, pl.ds(pl.multiple_of(first, chunk), chunk)] = total[:, :chunk]
            branch[span, pl.ds(pl.multiple_of(second, chunk), chunk)] = total[:, chunk:]

    for step in range(n):
        while events and events[0][0] <= step:
            serve(*events.pop(0))
        multiply(step)
        if step >= 1:
            add_twin(step - 1)
        if step >= 2:
            add_far(step - 2)
        if step < 2 and events:
            serve(*events.pop(0))
    add_twin(n - 1)
    stores.append(pltpu.make_async_copy(held, down_full, store_sem.at[1]))
    stores[1].start()
    add_far(n - 2)
    loads[2].wait()
    loads[3].wait()
    gain_grad[...] = jnp.zeros_like(gain_grad)
    add_far(n - 1)

    def finish(tile):
        span = pl.ds(pl.multiple_of(tile * 16, 16), 16)
        mixed = branch[span, :]
        scale = gains[...]
        inverse = lax.rsqrt(jnp.sum(mixed * mixed, axis=1, keepdims=True) / width + EPSILON)
        grad = upstream_buf[span, :].astype(jnp.float32)
        scaled = scale * grad
        mean = jnp.sum(scaled * mixed, axis=1, keepdims=True) / width
        normed = mixed * inverse
        d_buf[span, :] = (
            inverse * scaled - mixed * (inverse * inverse * inverse * mean)
        ).astype(jnp.bfloat16)
        block_buf[span, :] = (hidden_buf[span, :] + normed * scale).astype(jnp.bfloat16)
        terms = grad * normed
        gain_grad[...] += terms[:8] + terms[8:]

    def join(part, own):
        span = pl.ds(part * (half // 4), half // 4)
        if own:
            return pltpu.make_async_copy(d_buf.at[span], d_mlp.at[core, span], store_sem.at[3 + part])
        return pltpu.make_async_remote_copy(
            src_ref=d_buf.at[span],
            dst_ref=d_mlp.at[core, span],
            send_sem=join_send.at[part],
            recv_sem=join_recv.at[part],
            device_id=twin,
            device_id_type=MESH,
        )

    def joined(part):
        span = pl.ds(part * (half // 4), half // 4)
        target = d_mlp.at[1 - core, span]
        return pltpu.make_async_remote_copy(
            src_ref=target,
            dst_ref=target,
            send_sem=join_send.at[part],
            recv_sem=join_recv.at[part],
            device_id=twin,
            device_id_type=MESH,
        )

    for part in range(4):
        pl.loop(part * (half // 64), (part + 1) * (half // 64))(finish)
        join(part, False).start()
        join(part, True).start()
    stores.append(pltpu.make_async_copy(block_buf, block_half, store_sem.at[2]))
    stores[2].start()
    for part in range(4):
        joined(part).wait_recv()
        join(part, False).wait_send()
        join(part, True).wait()
    for copy in stores:
        copy.wait()
    for tile in (tiles - 2, tiles - 1):
        for copy in stage_copies(tile, tile % 2):
            copy.wait()
    for step in range(n):
        twin_copy(step).wait_send()
        far_copy(step).wait_send()
    for step in range(1, n):
        for sub in range(SUBS):
            for way in range(2):
                ring(way, sub, step, 0).wait_send()


def kernel_feed(hidden_low, gate_full, up_full, down_shard, hidden, upstream, gains, n):
    count, width = hidden_low.shape
    units = gate_full.shape[1]
    half = count // 2
    chunk = width // n // 2
    rows = chunk // SUBS
    low = jnp.bfloat16
    hbm = pl.BlockSpec(memory_space=pl.ANY)
    vmem = pl.BlockSpec(memory_space=pltpu.VMEM)
    dma = pltpu.SemaphoreType.DMA
    product, slope, silu, down_full, d_mlp, block, gain_grad = pl.pallas_call(
        functools.partial(feed_kernel, n),
        out_shape=(
            jax.ShapeDtypeStruct((count, units), low),
            jax.ShapeDtypeStruct((count, units), low),
            jax.ShapeDtypeStruct((count, units), low),
            jax.ShapeDtypeStruct((n, 2, chunk, units), low),
            jax.ShapeDtypeStruct((2, half, width), low),
            jax.ShapeDtypeStruct((half, width), low),
            jax.ShapeDtypeStruct((8, width), jnp.float32),
        ),
        in_specs=[hbm] * 6 + [vmem],
        out_specs=(hbm,) * 6 + (vmem,),
        scratch_shapes=[
            pltpu.VMEM((count, width), low),
            pltpu.VMEM((count, units), low),
            pltpu.VMEM((n, 2, chunk, units), low),
            pltpu.VMEM((2, width, TILE), low),
            pltpu.VMEM((2, width, TILE), low),
            pltpu.VMEM((2, count, TILE), low),
            pltpu.VMEM((2, count, TILE), low),
            pltpu.VMEM((n, half, 2 * chunk), low),
            pltpu.VMEM((n, half, 2 * chunk), low),
            pltpu.VMEM((n, half, 2 * chunk), low),
            pltpu.VMEM((n, half, 2 * chunk), low),
            pltpu.VMEM((half, width), jnp.float32),
            pltpu.VMEM((half, width), jnp.float32),
            pltpu.VMEM((half, width), low),
            pltpu.VMEM((half, width), low),
            pltpu.VMEM((half, width), low),
            dma((2, SUBS, n - 1)),
            dma((2, SUBS, n - 1)),
            dma((n,)),
            dma((n,)),
            dma((n,)),
            dma((n,)),
            dma((4,)),
            dma((4,)),
            dma((4,)),
            dma((2, 2)),
            dma((2, 2)),
            dma((7,)),
        ],
        compiler_params=pltpu.CompilerParams(
            collective_id=2, has_side_effects=True, vmem_limit_bytes=58 * 2**20
        ),
    )(
        hidden_low,
        gate_full,
        up_full,
        down_shard.reshape(2, chunk, units),
        hidden,
        upstream,
        gains.astype(jnp.float32).reshape(1, width),
    )
    return (
        product,
        slope,
        silu,
        down_full.reshape(width, units),
        d_mlp.reshape(count, width),
        block,
        jnp.sum(gain_grad, axis=0),
    )


def back_kernel(
    n,
    d_mlp,
    product,
    down_full,
    gate_slope,
    silu_in,
    gate_full,
    up_full,
    hidden_low,
    upstream,
    branch,
    gains,
    out_down,
    d_hidden_out,
    d_branch,
    grad_gate,
    grad_up,
    gain_grad,
    d_out,
    prod,
    d_gate,
    d_up,
    down_tile,
    slope_tile,
    silu_tile,
    gate_tile,
    up_tile,
    hidden_tile,
    first,
    own,
    inbox,
    mixed,
    twin_in,
    pair,
    far_in,
    d_hidden,
    branch_tile,
    upstream_tile,
    d_buf,
    stage,
    ring_send,
    ring_recv,
    twin_send,
    twin_recv,
    far_send,
    far_recv,
    join_send,
    join_recv,
    load_sem,
    down_sem,
    weight_sem,
    hidden_sem,
    row_sem,
    stage_sem,
    store_sem,
):
    index = lax.axis_index("dp")
    rank = lax.axis_index("mp")
    core = lax.rem(rank, 2)
    right = {"dp": holder_of(index, 1, n)}
    left = {"dp": holder_of(index, -1, n)}
    twin = {"mp": rank + 1 - 2 * core}
    far = {"mp": lax.rem(rank + 2, 4)}
    count, width = d_out.shape
    half = count // 2
    chunk = inbox.shape[3] * SUBS
    rows = chunk // SUBS
    tiles = prod.shape[1] // TILE
    quarter = half // 4
    left_side = (((0,), (0,)), ((), ()))
    right_side = (((1,), (1,)), ((), ()))

    def tile_span(tile):
        return pl.ds(pl.multiple_of(tile * TILE, TILE), TILE)

    def down_copies(tile, slot):
        cols = tile_span(tile)
        return (
            pltpu.make_async_copy(down_full.at[:, cols], down_tile.at[slot], down_sem.at[slot, 0]),
            pltpu.make_async_copy(gate_slope.at[:, cols], slope_tile.at[slot], down_sem.at[slot, 1]),
            pltpu.make_async_copy(silu_in.at[:, cols], silu_tile.at[slot], down_sem.at[slot, 2]),
        )

    def weight_copies(tile, slot):
        span = tile_span(tile)
        return (
            pltpu.make_async_copy(gate_full.at[span], gate_tile.at[slot], weight_sem.at[slot, 0]),
            pltpu.make_async_copy(up_full.at[span], up_tile.at[slot], weight_sem.at[slot, 1]),
        )

    def hidden_copy(tile, slot):
        return pltpu.make_async_copy(
            hidden_low.at[:, tile_span(tile)], hidden_tile.at[slot], hidden_sem.at[slot]
        )

    def row_copies(part, slot):
        span = pl.ds(part * quarter, quarter)
        return (
            pltpu.make_async_copy(branch.at[span], branch_tile.at[slot], row_sem.at[slot, 0]),
            pltpu.make_async_copy(upstream.at[span], upstream_tile.at[slot], row_sem.at[slot, 1]),
        )

    def stage_copy(tile, which):
        target = (grad_gate, grad_up)[which]
        return pltpu.make_async_copy(stage.at[which], target.at[tile_span(tile)], stage_sem.at[which])

    def ring(way, sub, step):
        return pltpu.make_async_remote_copy(
            src_ref=first.at[way, pl.ds(sub * rows, rows)]
            if step == 1
            else inbox.at[step - 2, way, sub],
            dst_ref=inbox.at[step - 1, way, sub],
            send_sem=ring_send.at[way, sub, step - 1],
            recv_sem=ring_recv.at[way, sub, step - 1],
            device_id=left if way else right,
            device_id_type=MESH,
        )

    def grad_block(step):
        cols = []
        for way in range(2):
            owner = holder_of(index, (1 + step) * (2 * way - 1), n)
            start = pl.multiple_of(owner * 2 * chunk + way * chunk, chunk)
            cols.append(d_out[:, pl.ds(start, chunk)])
        block = lax.dot_general(
            jnp.concatenate(cols, axis=1),
            prod[...],
            left_side,
            preferred_element_type=jnp.float32,
        ).astype(jnp.bfloat16)
        target = first if step == 0 else own.at[step % 2]
        target[0] = block[:chunk]
        target[1] = block[chunk:]

    def serve(step, sub):
        for way in range(2):
            ring(way, sub, step).wait_recv()

            @pl.loop(0, rows // 16)
            def _(tile, way=way):
                near = pl.ds(pl.multiple_of(tile * 16, 16), 16)
                mine = pl.ds(pl.multiple_of(sub * rows + tile * 16, 16), 16)
                total = inbox[step - 1, way, sub, near, :].astype(jnp.float32) + own[
                    step % 2, way, mine, :
                ].astype(jnp.float32)
                if step < n - 1:
                    inbox[step - 1, way, sub, near, :] = total.astype(jnp.bfloat16)
                else:
                    out_down[way, mine, :] = total

            if step < n - 1:
                ring(way, sub, step + 1).start()

    def twin_copy(tile):
        span = pl.ds(pl.multiple_of((1 - core) * half, half), half)
        return pltpu.make_async_remote_copy(
            src_ref=mixed.at[tile % 4, span],
            dst_ref=twin_in.at[tile % 4],
            send_sem=twin_send.at[tile],
            recv_sem=twin_recv.at[tile],
            device_id=twin,
            device_id_type=MESH,
        )

    def far_copy(tile):
        return pltpu.make_async_remote_copy(
            src_ref=pair.at[tile],
            dst_ref=far_in.at[tile],
            send_sem=far_send.at[tile],
            recv_sem=far_recv.at[tile],
            device_id=far,
            device_id_type=MESH,
        )

    greet((right, left, twin, far))
    loads = [
        pltpu.make_async_copy(d_mlp, d_out, load_sem.at[0]),
        pltpu.make_async_copy(product, prod, load_sem.at[1]),
    ]
    for copy in loads:
        copy.start()
    for copy in down_copies(0, 0):
        copy.start()
    for copy in weight_copies(0, 0):
        copy.start()
    for copy in loads:
        copy.wait()
    grad_block(0)
    for sub in range(SUBS):
        for way in range(2):
            ring(way, sub, 1).start()
    grad_block(1)

    def product_tile(tile):
        slot = lax.rem(tile, 2)
        for copy in down_copies(tile, slot):
            copy.wait()

        @pl.when(tile + 1 < tiles)
        def _():
            for copy in down_copies(tile + 1, 1 - slot):
                copy.start()

        cols = tile_span(tile)
        grad = jnp.dot(d_out[...], down_tile[slot], preferred_element_type=jnp.float32)
        d_gate[:, cols] = (grad * slope_tile[slot].astype(jnp.float32)).astype(jnp.bfloat16)
        d_up[:, cols] = (grad * silu_tile[slot].astype(jnp.float32)).astype(jnp.bfloat16)

    def input_tile(tile):
        slot = tile % 2
        for copy in weight_copies(tile, slot):
            copy.wait()
        if tile + 1 < width // TILE:
            for copy in weight_copies(tile + 1, 1 - slot):
                copy.start()
        total = lax.dot_general(
            d_gate[...], gate_tile[slot], right_side, preferred_element_type=jnp.float32
        ) + lax.dot_general(
            d_up[...], up_tile[slot], right_side, preferred_element_type=jnp.float32
        )
        mixed[tile % 4] = total.astype(jnp.bfloat16)
        twin_copy(tile).start()

    def add_twin(tile):
        twin_copy(tile).wait_recv()

        @pl.loop(0, half // 32)
        def _(row):
            span = pl.ds(pl.multiple_of(row * 32, 32), 32)
            mine = pl.ds(pl.multiple_of(core * half + row * 32, 32), 32)
            total = mixed[tile % 4, mine, :].astype(jnp.float32) + twin_in[
                tile % 4, span, :
            ].astype(jnp.float32)
            pair[tile, span, :] = total.astype(jnp.bfloat16)

        far_copy(tile).start()
        twin_copy(tile).wait_send()

    def add_far(tile):
        far_copy(tile).wait_recv()

        @pl.loop(0, half // 32)
        def _(row):
            span = pl.ds(pl.multiple_of(row * 32, 32), 32)
            d_hidden[span, tile * TILE : (tile + 1) * TILE] = pair[tile, span, :].astype(
                jnp.float32
            ) + far_in[tile, span, :].astype(jnp.float32)

    def weight_tile(tile):
        slot = tile % 2
        hidden_copy(tile, slot).wait()
        if tile + 1 < width // TILE:
            hidden_copy(tile + 1, 1 - slot).start()
        for which, source in enumerate((d_gate, d_up)):
            if tile >= 1:
                stage_copy(tile - 1, which).wait()
            stage[which] = lax.dot_general(
                hidden_tile[slot], source[...], left_side, preferred_element_type=jnp.float32
            ).astype(jnp.bfloat16)
            stage_copy(tile, which).start()

    events = [(step, sub) for step in range(1, n) for sub in range(SUBS)]

    def next_event():
        step, sub = events.pop(0)
        serve(step, sub)
        if sub == SUBS - 1 and step < n - 1:
            grad_block(step + 1)

    pl.loop(0, tiles // 4)(product_tile)
    next_event()
    pl.loop(tiles // 4, tiles // 2)(product_tile)
    next_event()
    pl.loop(tiles // 2, 3 * tiles // 4)(product_tile)
    next_event()
    pl.loop(3 * tiles // 4, tiles)(product_tile)
    next_event()
    blocks = width // TILE
    hidden_copy(0, 0).start()
    for tile in range(blocks):
        input_tile(tile)
        if tile >= 1:
            add_twin(tile - 1)
        if tile >= 3:
            add_far(tile - 3)
        if tile % 2 == 1:
            next_event()
    add_twin(blocks - 1)
    for copy in row_copies(0, 0):
        copy.start()
    for tile in range(blocks):
        weight_tile(tile)
        if tile % 2 == 1:
            if tile // 2 < 3:
                add_far(blocks - 3 + tile // 2)
            if events:
                next_event()
    gain_grad[...] = jnp.zeros_like(gain_grad)

    def finish(part, slot, tile):
        near = pl.ds(pl.multiple_of(tile * 16, 16), 16)
        span = pl.ds(pl.multiple_of(part * quarter + tile * 16, 16), 16)
        total = d_hidden[span, :] + upstream_tile[slot, near, :].astype(jnp.float32)
        d_hidden[span, :] = total
        mix = branch_tile[slot, near, :]
        inverse = lax.rsqrt(jnp.sum(mix * mix, axis=1, keepdims=True) / width + EPSILON)
        scaled = gains[...] * total
        mean = jnp.sum(scaled * mix, axis=1, keepdims=True) / width
        d_buf[span, :] = (inverse * scaled - mix * (inverse * inverse * inverse * mean)).astype(
            jnp.bfloat16
        )
        terms = total * mix * inverse
        gain_grad[...] += terms[:8] + terms[8:]

    def join(part, kind):
        span = pl.ds(part * quarter, quarter)
        if kind == 2:
            return pltpu.make_async_copy(
                d_buf.at[span], d_branch.at[core, span], store_sem.at[part]
            )
        target = d_branch.at[1 - core if kind else core, span]
        return pltpu.make_async_remote_copy(
            src_ref=target if kind else d_buf.at[span],
            dst_ref=target,
            send_sem=join_send.at[part],
            recv_sem=join_recv.at[part],
            device_id=twin,
            device_id_type=MESH,
        )

    for part in range(4):
        slot = part % 2
        for copy in row_copies(part, slot):
            copy.wait()
        if part < 3:
            for copy in row_copies(part + 1, 1 - slot):
                copy.start()
        pl.loop(0, quarter // 16)(functools.partial(finish, part, slot))
        join(part, 0).start()
        join(part, 2).start()
    stores = pltpu.make_async_copy(d_hidden, d_hidden_out, store_sem.at[4])
    stores.start()
    while events:
        next_event()
    for part in range(4):
        join(part, 1).wait_recv()
        join(part, 0).wait_send()
        join(part, 2).wait()
    stores.wait()
    for which in range(2):
        stage_copy(blocks - 1, which).wait()
    for tile in range(blocks):
        far_copy(tile).wait_send()
    for step in range(1, n):
        for sub in range(SUBS):
            for way in range(2):
                ring(way, sub, step).wait_send()


def kernel_back(
    d_mlp,
    product,
    down_full,
    gate_slope,
    silu,
    gate_full,
    up_full,
    hidden_low,
    upstream,
    branch,
    gains,
    n,
):
    count, width = d_mlp.shape
    units = product.shape[1]
    half = count // 2
    chunk = width // n // 2
    rows = chunk // SUBS
    blocks = width // TILE
    low = jnp.bfloat16
    hbm = pl.BlockSpec(memory_space=pl.ANY)
    vmem = pl.BlockSpec(memory_space=pltpu.VMEM)
    dma = pltpu.SemaphoreType.DMA
    out_down, d_hidden, d_branch, grad_gate, grad_up, gain_grad = pl.pallas_call(
        functools.partial(back_kernel, n),
        out_shape=(
            jax.ShapeDtypeStruct((2, chunk, units), jnp.float32),
            jax.ShapeDtypeStruct((half, width), jnp.float32),
            jax.ShapeDtypeStruct((2, half, width), low),
            jax.ShapeDtypeStruct((width, units), low),
            jax.ShapeDtypeStruct((width, units), low),
            jax.ShapeDtypeStruct((8, width), jnp.float32),
        ),
        in_specs=[hbm] * 10 + [vmem],
        out_specs=(vmem,) + (hbm,) * 4 + (vmem,),
        scratch_shapes=[
            pltpu.VMEM((count, width), low),
            pltpu.VMEM((count, units), low),
            pltpu.VMEM((count, units), low),
            pltpu.VMEM((count, units), low),
            pltpu.VMEM((2, width, TILE), low),
            pltpu.VMEM((2, count, TILE), low),
            pltpu.VMEM((2, count, TILE), low),
            pltpu.VMEM((2, TILE, units), low),
            pltpu.VMEM((2, TILE, units), low),
            pltpu.VMEM((2, count, TILE), low),
            pltpu.VMEM((2, chunk, units), low),
            pltpu.VMEM((2, 2, chunk, units), low),
            pltpu.VMEM((n - 1, 2, SUBS, rows, units), low),
            pltpu.VMEM((4, count, TILE), low),
            pltpu.VMEM((4, half, TILE), low),
            pltpu.VMEM((blocks, half, TILE), low),
            pltpu.VMEM((blocks, half, TILE), low),
            pltpu.VMEM((half, width), jnp.float32),
            pltpu.VMEM((2, half // 4, width), jnp.float32),
            pltpu.VMEM((2, half // 4, width), low),
            pltpu.VMEM((half, width), low),
            pltpu.VMEM((2, TILE, units), low),
            dma((2, SUBS, n - 1)),
            dma((2, SUBS, n - 1)),
            dma((blocks,)),
            dma((blocks,)),
            dma((blocks,)),
            dma((blocks,)),
            dma((4,)),
            dma((4,)),
            dma((2,)),
            dma((2, 3)),
            dma((2, 2)),
            dma((2,)),
            dma((2, 2)),
            dma((2,)),
            dma((5,)),
        ],
        compiler_params=pltpu.CompilerParams(
            collective_id=3, has_side_effects=True, vmem_limit_bytes=60 * 2**20
        ),
    )(
        d_mlp,
        product,
        down_full,
        gate_slope,
        silu,
        gate_full,
        up_full,
        hidden_low,
        upstream,
        branch,
        gains.astype(jnp.float32).reshape(1, width),
    )
    return (
        out_down.reshape(2 * chunk, units),
        d_hidden,
        d_branch.reshape(count, width),
        grad_gate,
        grad_up,
        jnp.sum(gain_grad, axis=0),
    )


def detach_kernel(
    n,
    d_branch,
    attn_full,
    attended_in,
    query_rot_in,
    key_rot_in,
    value_in,
    query_raw_in,
    key_raw_in,
    tokens,
    d_hidden,
    grad_gate,
    grad_up,
    totals,
    inverses,
    cosine,
    sine,
    doc_col,
    doc_row,
    query_gain,
    key_gain,
    out_gate,
    out_up,
    grad_attn,
    grad_tokens,
    query_gain_grad,
    key_gain_grad,
    wide,
    output_weight,
    weight_tile,
    attended,
    query_rot,
    key_rot,
    value,
    query_raw,
    key_raw,
    d_attended,
    d_query_norm,
    d_key_norm,
    d_key_sum,
    d_value_sum,
    d_projected,
    own,
    inbox,
    total_buf,
    mixed,
    twin_in,
    pair,
    far_in,
    hidden_tile,
    stage_output,
    stage,
    stat,
    inner,
    ring_send,
    ring_recv,
    stat_send,
    stat_recv,
    twin_send,
    twin_recv,
    far_send,
    far_recv,
    join_send,
    join_recv,
    own_sem,
    load_sem,
    weight_sem,
    hidden_sem,
    stage_sem,
    store_sem,
    out_sem,
):
    index, core, right, left, twin, far = neighbours(n)
    count, width = wide.shape
    half = count // 2
    local = query_raw.shape[1]
    heads = local // HEAD_CHANNELS
    blocks = width // TILE
    chunk = inbox.shape[3]
    grads = (grad_gate, grad_up)
    outs = (out_gate, out_up)
    left_side = (((0,), (0,)), ((), ()))
    right_side = (((1,), (1,)), ((), ()))
    factor = 1.0 / math.sqrt(HEAD_CHANNELS)

    def ring(way, unit, step):
        first = grads[unit].at[holder_of(index, 2 * way - 1, n), way]
        return pltpu.make_async_remote_copy(
            src_ref=first if step == 1 else inbox.at[step - 2, way, unit],
            dst_ref=inbox.at[step - 1, way, unit],
            send_sem=ring_send.at[way, unit, step - 1],
            recv_sem=ring_recv.at[way, unit, step - 1],
            device_id=left if way else right,
            device_id_type=MESH,
        )

    events = [(step, unit) for step in range(1, n) for unit in range(2)]

    def own_copy(step, unit, way):
        owner = holder_of(index, (1 + step) * (2 * way - 1), n)
        return pltpu.make_async_copy(
            grads[unit].at[owner, way], own.at[unit, way], own_sem.at[unit, way]
        )

    def out_copy(unit):
        return pltpu.make_async_copy(total_buf, outs[unit], out_sem.at[unit])

    def serve():
        step, unit = events.pop(0)
        if step == n - 1 and unit == 1:
            out_copy(0).wait()
        for way in range(2):
            own_copy(step, unit, way).wait()
            ring(way, unit, step).wait_recv()

            @pl.loop(0, chunk // 16)
            def _(tile, way=way):
                span = pl.ds(pl.multiple_of(tile * 16, 16), 16)
                total = inbox[step - 1, way, unit, span, :].astype(jnp.float32) + own[
                    unit, way, span, :
                ].astype(jnp.float32)
                if step < n - 1:
                    inbox[step - 1, way, unit, span, :] = total.astype(jnp.bfloat16)
                else:
                    total_buf[way, span, :] = total

            if step < n - 1:
                ring(way, unit, step + 1).start()
                own_copy(step + 1, unit, way).start()
        if step == n - 1:
            out_copy(unit).start()

    greet((right, left, twin, far))
    for unit in range(2):
        for way in range(2):
            ring(way, unit, 1).start()
            own_copy(1, unit, way).start()

    def weight_copy(tile, slot):
        return pltpu.make_async_copy(
            attn_full.at[pl.ds(tile * TILE, TILE), pl.ds(0, 3 * local)],
            weight_tile.at[slot],
            weight_sem.at[slot],
        )

    def hidden_copy(tile, slot):
        return pltpu.make_async_copy(
            d_hidden.at[:, pl.ds(tile * TILE, TILE)], hidden_tile.at[slot], hidden_sem.at[slot]
        )

    loads = [
        pltpu.make_async_copy(source, target, load_sem.at[place])
        for place, (source, target) in enumerate(
            (
                (d_branch, wide),
                (attn_full.at[:, pl.ds(3 * local, local)], output_weight),
                (attended_in, attended),
                (query_rot_in, query_rot),
                (key_rot_in, key_rot),
                (value_in, value),
                (query_raw_in, query_raw),
                (key_raw_in, key_raw),
            )
        )
    ]
    for copy in loads:
        copy.start()
    loads[0].wait()
    loads[1].wait()
    for tile in range(local // TILE):
        cols = slice(tile * TILE, (tile + 1) * TILE)
        d_attended[:, cols] = jnp.dot(
            wide[...], output_weight[:, cols], preferred_element_type=jnp.float32
        ).astype(jnp.bfloat16)

    def output_copy(tile):
        return pltpu.make_async_copy(
            stage_output.at[tile % 2],
            grad_attn.at[pl.ds(tile * TILE, TILE), pl.ds(3 * local, local)],
            stage_sem.at[0, tile % 2],
        )

    loads[2].wait()
    for tile in range(blocks):
        if tile >= 2:
            output_copy(tile - 2).wait()
        stage_output[tile % 2] = lax.dot_general(
            wide[:, tile * TILE : (tile + 1) * TILE],
            attended[...],
            left_side,
            preferred_element_type=jnp.float32,
        ).astype(jnp.bfloat16)
        output_copy(tile).start()
    token_load = pltpu.make_async_copy(tokens, wide, load_sem.at[0])
    token_load.start()
    weight_copy(0, 0).start()
    for copy in loads[3:]:
        copy.wait()
    serve()

    def unturned(vectors, span):
        return vectors * cosine[span, :] - pltpu.roll(vectors, HEAD_CHANNELS // 2, 1) * sine[span, :]

    def head_backward(head):
        cols = pl.ds(pl.multiple_of(head * HEAD_CHANNELS, HEAD_CHANNELS), HEAD_CHANNELS)
        lane = lax.broadcasted_iota(jnp.int32, (BLOCK, 128), 1)
        for block in reversed(range(count // BLOCK)):
            span = slice(block * BLOCK, (block + 1) * BLOCK)
            length = (block + 1) * BLOCK
            query = query_rot[span, cols]
            key = key_rot[:length, cols]
            grad = d_attended[span, cols]
            scores = masked_scores(query, key, doc_col, doc_row, block)
            total = jnp.sum(jnp.where(lane == head, totals[span, :], 0.0), axis=1, keepdims=True)
            powers = jnp.exp(scores - total)
            d_powers = lax.dot_general(
                grad, value[:length, cols], right_side, preferred_element_type=jnp.float32
            )
            correction = jnp.sum(d_powers * powers, axis=1, keepdims=True)
            d_scores = (powers * (d_powers - correction)).astype(jnp.bfloat16)
            rounded = powers.astype(jnp.bfloat16)
            d_query = jnp.dot(d_scores, key, preferred_element_type=jnp.float32) * factor
            d_query_norm[span, cols] = unturned(d_query, span)
            d_key = lax.dot_general(
                d_scores, query, left_side, preferred_element_type=jnp.float32
            )
            d_value = lax.dot_general(
                rounded, grad, left_side, preferred_element_type=jnp.float32
            )
            if length == count:
                d_key_sum[...] = d_key
                d_value_sum[...] = d_value
            else:
                d_key_sum[:length, :] += d_key
                d_value_sum[:length, :] += d_value
        d_key_norm[:, cols] = unturned(d_key_sum[...] * factor, slice(None))
        start = pl.multiple_of(2 * local + head * HEAD_CHANNELS, HEAD_CHANNELS)
        d_projected[:, pl.ds(start, HEAD_CHANNELS)] = d_value_sum[...].astype(jnp.bfloat16)

    pl.loop(0, heads // 2)(head_backward)
    serve()
    pl.loop(heads // 2, heads)(head_backward)
    serve()
    parts = []
    for place, (norm, raw, gain, gain_grad) in enumerate(
        (
            (d_query_norm, query_raw, query_gain, query_gain_grad),
            (d_key_norm, key_raw, key_gain, key_gain_grad),
        )
    ):
        dots = jnp.zeros((count, HEAD_CHANNELS), jnp.float32)
        for head in range(heads):
            cols = slice(head * HEAD_CHANNELS, (head + 1) * HEAD_CHANNELS)
            both = norm[:, cols] * raw[:, cols]
            gain_grad[:, cols] = jnp.sum(
                both * inverses[:, place : place + 1], axis=0, keepdims=True
            )
            dots = dots + both * gain[:, cols]
        parts.append(jnp.sum(dots, axis=1, keepdims=True))
    stat[0] = columns_to_rows(parts, count)
    first = exchange(stat.at[0], stat.at[1], stat_send, stat_recv, 0, twin)
    first.start()
    first.wait()
    stat[2] = stat[0] + stat[1]
    second = exchange(stat.at[2], stat.at[3], stat_send, stat_recv, 1, far)
    second.start()
    serve()
    second.wait()
    inner[...] = rows_to_columns(stat[2] + stat[3]) / width

    @pl.loop(0, heads)
    def _(head):
        cols = pl.ds(pl.multiple_of(head * HEAD_CHANNELS, HEAD_CHANNELS), HEAD_CHANNELS)
        for place, (norm, raw, gain) in enumerate(
            ((d_query_norm, query_raw, query_gain), (d_key_norm, key_raw, key_gain))
        ):
            inverse = inverses[:, place : place + 1]
            cube = inverse * inverse * inverse * inner[:, place : place + 1]
            start = pl.multiple_of(place * local + head * HEAD_CHANNELS, HEAD_CHANNELS)
            d_projected[:, pl.ds(start, HEAD_CHANNELS)] = (
                norm[:, cols] * inverse * gain[:, cols] - raw[:, cols] * cube
            ).astype(jnp.bfloat16)

    def twin_copy(tile):
        span = pl.ds(pl.multiple_of((1 - core) * half, half), half)
        return exchange(
            mixed.at[tile % 4, span], twin_in.at[tile % 4], twin_send, twin_recv, tile, twin
        )

    def far_copy(tile):
        return exchange(pair.at[tile], far_in.at[tile], far_send, far_recv, tile, far)

    def token_tile(tile):
        slot = tile % 2
        weight_copy(tile, slot).wait()
        if tile + 1 < blocks:
            weight_copy(tile + 1, 1 - slot).start()
        mixed[tile % 4] = lax.dot_general(
            d_projected[...], weight_tile[slot], right_side, preferred_element_type=jnp.float32
        ).astype(jnp.bfloat16)
        twin_copy(tile).start()

    def add_twin(tile):
        twin_copy(tile).wait_recv()

        @pl.loop(0, half // 32)
        def _(row):
            span = pl.ds(pl.multiple_of(row * 32, 32), 32)
            mine = pl.ds(pl.multiple_of(core * half + row * 32, 32), 32)
            total = mixed[tile % 4, mine, :].astype(jnp.float32) + twin_in[
                tile % 4, span, :
            ].astype(jnp.float32)
            pair[tile, span, :] = total.astype(jnp.bfloat16)

        far_copy(tile).start()
        twin_copy(tile).wait_send()

    def join(tile, kind):
        cols = pl.ds(tile * TILE, TILE)
        if kind == 2:
            return pltpu.make_async_copy(
                pair.at[tile], grad_tokens.at[core, :, cols], store_sem.at[tile]
            )
        target = grad_tokens.at[1 - core if kind else core, :, cols]
        return exchange(
            target if kind else pair.at[tile], target, join_send, join_recv, tile, twin
        )

    def add_far(tile):
        slot = tile % 2
        hidden_copy(tile, slot).wait()
        if tile + 1 < blocks:
            hidden_copy(tile + 1, 1 - slot).start()
        far_copy(tile).wait()

        @pl.loop(0, half // 32)
        def _(row):
            span = pl.ds(pl.multiple_of(row * 32, 32), 32)
            total = (
                pair[tile, span, :].astype(jnp.float32)
                + far_in[tile, span, :].astype(jnp.float32)
                + hidden_tile[slot, span, :]
            )
            pair[tile, span, :] = total.astype(jnp.bfloat16)

        join(tile, 0).start()
        join(tile, 2).start()

    def stage_copy(tile):
        return pltpu.make_async_copy(
            stage.at[tile % 2],
            grad_attn.at[pl.ds(tile * TILE, TILE), pl.ds(0, 3 * local)],
            stage_sem.at[1, tile % 2],
        )

    def weight_grad(tile):
        if tile >= 2:
            stage_copy(tile - 2).wait()
        stage[tile % 2] = lax.dot_general(
            wide[:, tile * TILE : (tile + 1) * TILE],
            d_projected[...],
            left_side,
            preferred_element_type=jnp.float32,
        ).astype(jnp.bfloat16)
        stage_copy(tile).start()

    hidden_copy(0, 0).start()
    for tile in range(blocks):
        token_tile(tile)
        if tile >= 1:
            add_twin(tile - 1)
        if tile == blocks // 2 - 1:
            serve()
    add_twin(blocks - 1)
    serve()
    token_load.wait()
    for tile in range(blocks):
        weight_grad(tile)
        add_far(tile)
        if tile % 2 == 1:
            serve()
    for tile in (blocks - 2, blocks - 1):
        output_copy(tile).wait()
        stage_copy(tile).wait()
    while events:
        serve()
    out_copy(1).wait()
    for tile in range(blocks):
        join(tile, 1).wait_recv()
        join(tile, 0).wait_send()
        join(tile, 2).wait()
    for step in range(1, n):
        for unit in range(2):
            for way in range(2):
                ring(way, unit, step).wait_send()


def kernel_detach(
    d_branch,
    attn_full,
    attended,
    query_rot,
    key_rot,
    value,
    query_raw,
    key_raw,
    tokens,
    d_hidden,
    grad_gate,
    grad_up,
    totals,
    inverses,
    cosine,
    sine,
    doc_ids,
    query_gain,
    key_gain,
    n,
):
    count, width = tokens.shape
    local = query_gain.shape[0]
    units = grad_gate.shape[1]
    half = count // 2
    chunk = width // n // 2
    blocks = width // TILE
    low = jnp.bfloat16
    full = jnp.float32
    hbm = pl.BlockSpec(memory_space=pl.ANY)
    vmem = pl.BlockSpec(memory_space=pltpu.VMEM)
    dma = pltpu.SemaphoreType.DMA
    shape = jax.ShapeDtypeStruct
    outs = pl.pallas_call(
        functools.partial(detach_kernel, n),
        out_shape=(
            shape((2, chunk, units), full),
            shape((2, chunk, units), full),
            shape((width, 4 * local), low),
            shape((2, half, width), low),
            shape((1, local), full),
            shape((1, local), full),
        ),
        in_specs=[hbm] * 12 + [vmem] * 8,
        out_specs=(hbm,) * 4 + (vmem,) * 2,
        scratch_shapes=[
            pltpu.VMEM((count, width), low),
            pltpu.VMEM((width, local), low),
            pltpu.VMEM((2, TILE, 3 * local), low),
            pltpu.VMEM((count, local), low),
            pltpu.VMEM((count, local), low),
            pltpu.VMEM((count, local), low),
            pltpu.VMEM((count, local), low),
            pltpu.VMEM((count, local), full),
            pltpu.VMEM((count, local), full),
            pltpu.VMEM((count, local), low),
            pltpu.VMEM((count, local), full),
            pltpu.VMEM((count, local), full),
            pltpu.VMEM((count, HEAD_CHANNELS), full),
            pltpu.VMEM((count, HEAD_CHANNELS), full),
            pltpu.VMEM((count, 3 * local), low),
            pltpu.VMEM((2, 2, chunk, units), low),
            pltpu.VMEM((n - 1, 2, 2, chunk, units), low),
            pltpu.VMEM((2, chunk, units), full),
            pltpu.VMEM((4, count, TILE), low),
            pltpu.VMEM((4, half, TILE), low),
            pltpu.VMEM((blocks, half, TILE), low),
            pltpu.VMEM((blocks, half, TILE), low),
            pltpu.VMEM((2, half, TILE), full),
            pltpu.VMEM((2, TILE, local), low),
            pltpu.VMEM((2, TILE, 3 * local), low),
            pltpu.VMEM((4, 8, count), full),
            pltpu.VMEM((count, 128), full),
            dma((2, 2, n - 1)),
            dma((2, 2, n - 1)),
            dma((2,)),
            dma((2,)),
            dma((blocks,)),
            dma((blocks,)),
            dma((blocks,)),
            dma((blocks,)),
            dma((blocks,)),
            dma((blocks,)),
            dma((2, 2)),
            dma((8,)),
            dma((2,)),
            dma((2,)),
            dma((2, 2)),
            dma((blocks,)),
            dma((2,)),
        ],
        compiler_params=pltpu.CompilerParams(
            collective_id=5, has_side_effects=True, vmem_limit_bytes=60 * 2**20
        ),
    )(
        d_branch,
        attn_full,
        attended,
        query_rot,
        key_rot,
        value,
        query_raw,
        key_raw,
        tokens,
        d_hidden,
        grad_gate.reshape(n, 2, chunk, units),
        grad_up.reshape(n, 2, chunk, units),
        totals,
        inverses,
        cosine,
        sine,
        doc_ids.reshape(count, 1),
        doc_ids.reshape(1, count),
        query_gain.astype(full).reshape(1, local),
        key_gain.astype(full).reshape(1, local),
    )
    return (
        outs[0].reshape(2 * chunk, units),
        outs[1].reshape(2 * chunk, units),
        outs[2],
        outs[3].reshape(count, width),
        outs[4][0],
        outs[5][0],
    )


def half_of(full, core):
    rows = full.shape[0] // 2
    return lax.dynamic_index_in_dim(full.reshape(2, rows, -1), core, 0, keepdims=False)


def join_halves(half, core):
    got = lax.ppermute(half, "mp", ((0, 1), (1, 0), (2, 3), (3, 2)))
    first = jnp.where(core == 0, half, got)
    second = jnp.where(core == 0, got, half)
    return jnp.concatenate([first, second], axis=0)


def fused_layer(
    n,
    tokens,
    doc_ids,
    q_weight,
    k_weight,
    v_weight,
    o_weight,
    q_gain,
    k_gain,
    attn_gain,
    gate_weight,
    up_weight,
    down_weight,
    mlp_gain,
    cotangent,
):
    core = lax.axis_index("mp") % 2
    heads = q_gain.shape[0]
    width = heads * HEAD_CHANNELS
    head_part = q_gain.size
    col_part = attn_gain.size
    packed = jnp.concatenate(
        [q_gain.reshape(-1), k_gain.reshape(-1), attn_gain, mlp_gain], axis=0
    )
    size = packed.shape[0]
    shard = jnp.concatenate([q_weight, k_weight, v_weight, o_weight.T], axis=1)
    attn_full, gains = kernel_gather(
        shard, jnp.pad(packed, (0, 2048 - size)).reshape(16, 128), n
    )
    gains = gains.reshape(n, -1)[:, :size]

    def whole(part):
        return part.reshape(n, heads, -1).transpose(1, 0, 2).reshape(-1)

    query_scale = whole(gains[:, :head_part])
    key_scale = whole(gains[:, head_part : 2 * head_part])
    attn_gains = gains[:, 2 * head_part : 2 * head_part + col_part].reshape(-1)
    mlp_gains = gains[:, 2 * head_part + col_part :].reshape(-1)
    angles = angles_of(doc_ids, SEQ_LEN, HEAD_CHANNELS)
    cosine = jnp.cos(angles)
    sine_wave = jnp.sin(angles)
    cosine = jnp.concatenate([cosine, cosine], axis=1)
    sine_wave = jnp.concatenate([-sine_wave, sine_wave], axis=1)
    upstream = half_of(cotangent, core)

    (
        gate_full,
        up_full,
        query_raw,
        key_raw,
        query_rot,
        key_rot,
        value,
        attended,
        totals,
        inverses,
        branch,
        hidden_state,
        hidden_low,
    ) = kernel_attend(
        tokens,
        attn_full,
        gate_weight,
        up_weight,
        half_of(tokens, core),
        cosine,
        sine_wave,
        doc_ids,
        query_scale,
        key_scale,
        attn_gains,
        n,
    )
    product, gate_slope, silu, down_full, d_mlp, block_half, mlp_gain_rows = kernel_feed(
        hidden_low, gate_full, up_full, down_weight.T, hidden_state, upstream, mlp_gains, n
    )
    block_out = join_halves(block_half, core)
    out_down, d_hidden, d_branch, grad_gate, grad_up, attn_gain_rows = kernel_back(
        d_mlp,
        product,
        down_full,
        gate_slope,
        silu,
        gate_full,
        up_full,
        hidden_low,
        upstream,
        branch,
        attn_gains,
        n,
    )
    out_gate, out_up, grad_attn, grad_tokens, query_gain_row, key_gain_row = kernel_detach(
        d_branch,
        attn_full,
        attended,
        query_rot,
        key_rot,
        value,
        query_raw,
        key_raw,
        tokens,
        d_hidden,
        grad_gate,
        grad_up,
        totals,
        inverses,
        cosine,
        sine_wave,
        doc_ids,
        query_scale,
        key_scale,
        n,
    )

    def by_owner(flat):
        return flat.reshape(heads, n, -1).transpose(1, 0, 2).reshape(n, -1)

    rows = jnp.concatenate(
        [
            by_owner(query_gain_row),
            by_owner(key_gain_row),
            attn_gain_rows.reshape(n, -1),
            mlp_gain_rows.reshape(n, -1),
        ],
        axis=1,
    )
    rows = jnp.pad(rows, ((0, 0), (0, 1024 - size))).reshape(n, 8, 128)
    out_attn, summed = kernel_scatter(grad_attn, rows, n)
    summed = summed.reshape(-1)
    return (
        block_out,
        grad_tokens,
        out_attn[:, :width],
        out_attn[:, width : 2 * width],
        out_attn[:, 2 * width : 3 * width],
        out_attn[:, 3 * width :].T,
        summed[:head_part].reshape(q_gain.shape),
        summed[head_part : 2 * head_part].reshape(k_gain.shape),
        summed[2 * head_part : 2 * head_part + col_part],
        out_gate,
        out_up,
        out_down.T,
        summed[2 * head_part + col_part : size],
    )


def solution(mesh):
    in_specs = (
        P("dp", None),
        P("dp"),
        P("dp", "mp"),
        P("dp", "mp"),
        P("dp", "mp"),
        P("mp", "dp"),
        P("mp", "dp"),
        P("mp", "dp"),
        P("dp"),
        P("dp", "mp"),
        P("dp", "mp"),
        P("mp", "dp"),
        P("dp"),
        P("dp", None),
    )
    out_specs = (
        P("dp", None),
        P("dp", None),
        P("dp", "mp"),
        P("dp", "mp"),
        P("dp", "mp"),
        P("mp", "dp"),
        P("mp", "dp"),
        P("mp", "dp"),
        P("dp"),
        P("dp", "mp"),
        P("dp", "mp"),
        P("mp", "dp"),
        P("dp"),
    )
    n, m = mesh.shape["dp"], mesh.shape["mp"]

    def on_device(*arrays):
        if (n, m, arrays[0].shape[0]) == (RING, 4, SEQ_LEN):
            return fused_layer(n, *arrays)
        return plain_layer(*arrays)

    return jax.shard_map(
        on_device, mesh=mesh, in_specs=in_specs, out_specs=out_specs, check_vma=False
    )
```

```python
import functools
import math

import jax
import jax.numpy as jnp
from jax import lax
from jax.experimental import pallas as pl
from jax.experimental.pallas import tpu as pltpu
from jax.sharding import PartitionSpec as P

D = 2048
HEAD_CHANNELS = 128
SEQ_LEN = 1024
RING = 8


EPSILON = 1e-06
ROPE_BASE = 500000.0
MASKED = -1e30
ROW_LIMIT = 512


def matmul(left_side, right_side):
    return jnp.dot(left_side, right_side, preferred_element_type=jnp.float32)


def transposed_left(left_side, right_side):
    return lax.dot_general(
        left_side, right_side, (((0,), (0,)), ((), ())), preferred_element_type=jnp.float32
    )


def transposed_right(left_side, right_side):
    return lax.dot_general(
        left_side, right_side, (((1,), (1,)), ((), ())), preferred_element_type=jnp.float32
    )


def angles_of(doc_rows, seq_len, head_dim):
    shaped = doc_rows.reshape(-1, seq_len)
    leading = jnp.sum(1 - shaped, axis=1, keepdims=True, dtype=jnp.int32)
    places = jnp.arange(seq_len, dtype=jnp.int32)[None, :] - shaped * leading
    frequency = jnp.exp(
        jnp.arange(head_dim // 2, dtype=jnp.float32) * (-2.0 * math.log(ROPE_BASE) / head_dim)
    )
    return places.reshape(-1).astype(jnp.float32)[:, None] * frequency[None, :]


def rotate(vectors, angles):
    halfway = vectors.shape[-1] // 2
    cosine = jnp.cos(angles)[:, None, :]
    sine_wave = jnp.sin(angles)[:, None, :]
    former = vectors[..., :halfway]
    latter = vectors[..., halfway:]
    return jnp.concatenate(
        [former * cosine - latter * sine_wave, latter * cosine + former * sine_wave], axis=-1
    )


def rotate_back(vectors, angles):
    halfway = vectors.shape[-1] // 2
    cosine = jnp.cos(angles)[:, None, :]
    sine_wave = jnp.sin(angles)[:, None, :]
    former = vectors[..., :halfway]
    latter = vectors[..., halfway:]
    return jnp.concatenate(
        [former * cosine + latter * sine_wave, latter * cosine - former * sine_wave], axis=-1
    )


def block_scores(query_block, key_seq, doc_seq, offset):
    factor = 1.0 / math.sqrt(query_block.shape[-1])
    scores = (
        jnp.einsum("qhd,khd->hqk", query_block, key_seq, preferred_element_type=jnp.float32)
        * factor
    )
    row_places = offset + jnp.arange(query_block.shape[0], dtype=jnp.int32)
    key_places = jnp.arange(key_seq.shape[0], dtype=jnp.int32)
    row_docs = doc_seq[offset : offset + query_block.shape[0]]
    allowed = (key_places[None, :] <= row_places[:, None]) & (doc_seq[None, :] == row_docs[:, None])
    return jnp.where(allowed[None], scores, MASKED)


def attend_sequence(inputs):
    query_seq, key_seq, value_seq, doc_seq = inputs
    row_block = math.gcd(query_seq.shape[0], ROW_LIMIT)
    outputs = []
    totals = []
    for offset in range(0, query_seq.shape[0], row_block):
        scores = block_scores(query_seq[offset : offset + row_block], key_seq, doc_seq, offset)
        maximum = jnp.max(scores, axis=-1, keepdims=True)
        weights = jnp.exp(scores - maximum)
        denominator = jnp.sum(weights, axis=-1, keepdims=True)
        rounded = (weights / denominator).astype(jnp.bfloat16)
        outputs.append(
            jnp.einsum(
                "hqk,khd->qhd", rounded, value_seq, preferred_element_type=jnp.float32
            ).astype(jnp.bfloat16)
        )
        totals.append((maximum + jnp.log(denominator))[..., 0])
    return (jnp.concatenate(outputs, axis=0), jnp.concatenate(totals, axis=1))


def attend_backward(inputs):
    query_seq, key_seq, value_seq, doc_seq, grad_seq, lse_seq = inputs
    row_block = math.gcd(query_seq.shape[0], ROW_LIMIT)
    factor = 1.0 / math.sqrt(query_seq.shape[-1])
    grad_keys = jnp.zeros(key_seq.shape, jnp.float32)
    grad_values = jnp.zeros(value_seq.shape, jnp.float32)
    grad_rows = []
    for offset in range(0, query_seq.shape[0], row_block):
        query_block = query_seq[offset : offset + row_block]
        grad_block = grad_seq[offset : offset + row_block]
        scores = block_scores(query_block, key_seq, doc_seq, offset)
        weights = jnp.exp(scores - lse_seq[:, offset : offset + row_block, None])
        d_weights = jnp.einsum(
            "qhd,khd->hqk", grad_block, value_seq, preferred_element_type=jnp.float32
        )
        correction = jnp.sum(d_weights * weights, axis=-1, keepdims=True)
        d_scores = (weights * (d_weights - correction)).astype(jnp.bfloat16)
        grad_rows.append(
            jnp.einsum("hqk,khd->qhd", d_scores, key_seq, preferred_element_type=jnp.float32)
            * factor
        )
        grad_keys = (
            grad_keys
            + jnp.einsum("hqk,qhd->khd", d_scores, query_block, preferred_element_type=jnp.float32)
            * factor
        )
        grad_values = grad_values + jnp.einsum(
            "hqk,qhd->khd",
            weights.astype(jnp.bfloat16),
            grad_block,
            preferred_element_type=jnp.float32,
        )
    return (jnp.concatenate(grad_rows, axis=0), grad_keys, grad_values)


def plain_layer(
    tokens,
    doc_ids,
    q_weight,
    k_weight,
    v_weight,
    o_weight,
    q_gain,
    k_gain,
    attn_gain,
    gate_weight,
    up_weight,
    down_weight,
    mlp_gain,
    cotangent,
):
    query_full, key_complete, value_full, output_full, query_gains, key_gains, attn_gains = (
        lax.all_gather(q_weight, "dp", axis=0, tiled=True),
        lax.all_gather(k_weight, "dp", axis=0, tiled=True),
        lax.all_gather(v_weight, "dp", axis=0, tiled=True),
        lax.all_gather(o_weight, "dp", axis=1, tiled=True),
        lax.all_gather(q_gain, "dp", axis=1, tiled=True),
        lax.all_gather(k_gain, "dp", axis=1, tiled=True),
        lax.all_gather(attn_gain, "dp", axis=0, tiled=True),
    )
    gate_full, up_full, down_full, mlp_gains = (
        lax.all_gather(gate_weight, "dp", axis=0, tiled=True),
        lax.all_gather(up_weight, "dp", axis=0, tiled=True),
        lax.all_gather(down_weight, "dp", axis=1, tiled=True),
        lax.all_gather(mlp_gain, "dp", axis=0, tiled=True),
    )
    row_count = tokens.shape[0]
    heads_on_device = q_gain.shape[0]
    local_width = heads_on_device * HEAD_CHANNELS
    sequences = row_count // SEQ_LEN
    seq_shape = (sequences, SEQ_LEN, heads_on_device, HEAD_CHANNELS)
    angles = angles_of(doc_ids, SEQ_LEN, HEAD_CHANNELS)
    doc_seqs = doc_ids.reshape(sequences, SEQ_LEN)
    query_raw = matmul(tokens, query_full)
    key_unnormed = matmul(tokens, key_complete)
    values = matmul(tokens, value_full).astype(jnp.bfloat16)
    query_sq, key_sq = lax.psum(
        (jnp.sum(query_raw * query_raw, axis=1), jnp.sum(key_unnormed * key_unnormed, axis=1)), "mp"
    )
    query_inv = lax.rsqrt(query_sq / D + EPSILON)[:, None]
    key_inverse_norm = lax.rsqrt(key_sq / D + EPSILON)[:, None]
    query_scale = query_gains.reshape(-1)
    key_scale = key_gains.reshape(-1)
    query_rot = rotate(
        (query_raw * query_inv * query_scale).reshape(row_count, heads_on_device, HEAD_CHANNELS),
        angles,
    ).astype(jnp.bfloat16)
    key_rot = rotate(
        (key_unnormed * key_inverse_norm * key_scale).reshape(
            row_count, heads_on_device, HEAD_CHANNELS
        ),
        angles,
    ).astype(jnp.bfloat16)
    query_seqs = query_rot.reshape(seq_shape)
    key_seqs = key_rot.reshape(seq_shape)
    value_seqs = values.reshape(seq_shape)
    attended, lse_all = lax.map(attend_sequence, (query_seqs, key_seqs, value_seqs, doc_seqs))
    attended = attended.reshape(row_count, local_width)
    branch = lax.psum(matmul(attended, output_full), "mp")
    branch_inv = lax.rsqrt(jnp.mean(branch * branch, axis=1, keepdims=True) + EPSILON)
    hidden_state = tokens.astype(jnp.float32) + branch * branch_inv * attn_gains
    hidden_low = hidden_state.astype(jnp.bfloat16)
    gate_act = matmul(hidden_low, gate_full)
    up_part = matmul(hidden_low, up_full)
    product = (jax.nn.silu(gate_act) * up_part).astype(jnp.bfloat16)
    mlp_branch = lax.psum(matmul(product, down_full).astype(jnp.bfloat16), "mp").astype(jnp.float32)
    mlp_inv = lax.rsqrt(jnp.mean(mlp_branch * mlp_branch, axis=1, keepdims=True) + EPSILON)
    block_out = (hidden_state + mlp_branch * mlp_inv * mlp_gains).astype(jnp.bfloat16)
    gate_full, up_full, down_full, mlp_gains = (
        lax.all_gather(gate_weight, "dp", axis=0, tiled=True),
        lax.all_gather(up_weight, "dp", axis=0, tiled=True),
        lax.all_gather(down_weight, "dp", axis=1, tiled=True),
        lax.all_gather(mlp_gain, "dp", axis=0, tiled=True),
    )
    upstream = cotangent.astype(jnp.float32)
    grad_mlp_scale = jnp.sum(upstream * mlp_branch * mlp_inv, axis=0)
    mlp_scaled = mlp_gains * upstream
    mlp_cube = mlp_inv * mlp_inv * mlp_inv
    d_mlp = (
        mlp_inv * mlp_scaled
        - mlp_branch * mlp_cube * jnp.mean(mlp_scaled * mlp_branch, axis=1, keepdims=True)
    ).astype(jnp.bfloat16)
    grad_down = transposed_left(product, d_mlp)
    d_product = transposed_right(d_mlp, down_full)
    sigmoid = jax.nn.sigmoid(gate_act)
    d_gate = (d_product * up_part * sigmoid * (1.0 + gate_act * (1.0 - sigmoid))).astype(
        jnp.bfloat16
    )
    d_up = (d_product * gate_act * sigmoid).astype(jnp.bfloat16)
    grad_gate = transposed_left(hidden_low, d_gate)
    grad_up = transposed_left(hidden_low, d_up)
    mlp_input = transposed_right(d_gate, gate_full) + transposed_right(d_up, up_full)
    d_hidden = upstream + lax.psum(mlp_input.astype(jnp.bfloat16), "mp").astype(jnp.float32)
    mlp_grads = (
        lax.psum_scatter(
            grad_gate.astype(jnp.bfloat16), "dp", scatter_dimension=0, tiled=True
        ).astype(jnp.float32),
        lax.psum_scatter(
            grad_up.astype(jnp.bfloat16), "dp", scatter_dimension=0, tiled=True
        ).astype(jnp.float32),
        lax.psum_scatter(
            grad_down.astype(jnp.bfloat16), "dp", scatter_dimension=1, tiled=True
        ).astype(jnp.float32),
        lax.psum_scatter(
            grad_mlp_scale.astype(jnp.bfloat16), "dp", scatter_dimension=0, tiled=True
        ).astype(jnp.float32),
    )
    query_full, key_complete, value_full, output_full, query_gains, key_gains, attn_gains = (
        lax.all_gather(q_weight, "dp", axis=0, tiled=True),
        lax.all_gather(k_weight, "dp", axis=0, tiled=True),
        lax.all_gather(v_weight, "dp", axis=0, tiled=True),
        lax.all_gather(o_weight, "dp", axis=1, tiled=True),
        lax.all_gather(q_gain, "dp", axis=1, tiled=True),
        lax.all_gather(k_gain, "dp", axis=1, tiled=True),
        lax.all_gather(attn_gain, "dp", axis=0, tiled=True),
    )
    query_scale = query_gains.reshape(-1)
    key_scale = key_gains.reshape(-1)
    grad_attn_scale = jnp.sum(d_hidden * branch * branch_inv, axis=0)
    attn_scaled = attn_gains * d_hidden
    branch_cube = branch_inv * branch_inv * branch_inv
    d_branch = (
        branch_inv * attn_scaled
        - branch * branch_cube * jnp.mean(attn_scaled * branch, axis=1, keepdims=True)
    ).astype(jnp.bfloat16)
    grad_output = transposed_left(attended, d_branch)
    d_attended = transposed_right(d_branch, output_full).astype(jnp.bfloat16)
    grad_qrot, grad_krot, grad_vals = lax.map(
        attend_backward,
        (query_seqs, key_seqs, value_seqs, doc_seqs, d_attended.reshape(seq_shape), lse_all),
    )
    d_values = grad_vals.reshape(row_count, local_width).astype(jnp.bfloat16)
    d_qnorm = rotate_back(
        grad_qrot.reshape(row_count, heads_on_device, HEAD_CHANNELS), angles
    ).reshape(row_count, local_width)
    grad_key_normed = rotate_back(
        grad_krot.reshape(row_count, heads_on_device, HEAD_CHANNELS), angles
    ).reshape(row_count, local_width)
    grad_qscale = jnp.sum(d_qnorm * query_raw * query_inv, axis=0).reshape(
        heads_on_device, HEAD_CHANNELS
    )
    grad_key_rms_factor = jnp.sum(
        grad_key_normed * key_unnormed * key_inverse_norm, axis=0
    ).reshape(heads_on_device, HEAD_CHANNELS)
    query_scaled = query_scale * d_qnorm
    key_scaled = key_scale * grad_key_normed
    query_inner, key_inner = lax.psum(
        (jnp.sum(query_scaled * query_raw, axis=1), jnp.sum(key_scaled * key_unnormed, axis=1)),
        "mp",
    )
    query_cube = query_inv * query_inv * query_inv
    key_cube = key_inverse_norm * key_inverse_norm * key_inverse_norm
    d_query = (
        query_inv * query_scaled - query_raw * query_cube * (query_inner / D)[:, None]
    ).astype(jnp.bfloat16)
    d_key = (
        key_inverse_norm * key_scaled - key_unnormed * key_cube * (key_inner / D)[:, None]
    ).astype(jnp.bfloat16)
    grad_query = transposed_left(tokens, d_query)
    grad_key = transposed_left(tokens, d_key)
    grad_value = transposed_left(tokens, d_values)
    token_back = (
        transposed_right(d_query, query_full)
        + transposed_right(d_key, key_complete)
        + transposed_right(d_values, value_full)
    )
    grad_tokens = (
        d_hidden + lax.psum(token_back.astype(jnp.bfloat16), "mp").astype(jnp.float32)
    ).astype(jnp.bfloat16)
    attn_grads = (
        lax.psum_scatter(
            grad_query.astype(jnp.bfloat16), "dp", scatter_dimension=0, tiled=True
        ).astype(jnp.float32),
        lax.psum_scatter(
            grad_key.astype(jnp.bfloat16), "dp", scatter_dimension=0, tiled=True
        ).astype(jnp.float32),
        lax.psum_scatter(
            grad_value.astype(jnp.bfloat16), "dp", scatter_dimension=0, tiled=True
        ).astype(jnp.float32),
        lax.psum_scatter(
            grad_output.astype(jnp.bfloat16), "dp", scatter_dimension=1, tiled=True
        ).astype(jnp.float32),
        lax.psum_scatter(
            grad_qscale.astype(jnp.bfloat16), "dp", scatter_dimension=1, tiled=True
        ).astype(jnp.float32),
        lax.psum_scatter(
            grad_key_rms_factor.astype(jnp.bfloat16), "dp", scatter_dimension=1, tiled=True
        ).astype(jnp.float32),
        lax.psum_scatter(
            grad_attn_scale.astype(jnp.bfloat16), "dp", scatter_dimension=0, tiled=True
        ).astype(jnp.float32),
    )
    return (
        block_out,
        grad_tokens,
        attn_grads[0],
        attn_grads[1],
        attn_grads[2],
        attn_grads[3],
        attn_grads[4],
        attn_grads[5],
        attn_grads[6],
        mlp_grads[0],
        mlp_grads[1],
        mlp_grads[2],
        mlp_grads[3],
    )


MESH = pl.DeviceIdType.MESH
SUBS = 2
TILE = 256
BLOCK = 256
SMALL = 16


def place_of(index, n):
    odd = lax.rem(index, 2)
    half = lax.div(index, 2)
    return (1 - odd) * half + odd * (n - 1 - half)


def device_at(place, n):
    late = lax.div(place, n // 2)
    return (1 - late) * (2 * place) + late * (2 * (n - 1 - place) + 1)


def holder_of(index, steps, n):
    return device_at(lax.rem(place_of(index, n) + (steps + 2 * n), n), n)


def neighbours(n):
    index = lax.axis_index("dp")
    rank = lax.axis_index("mp")
    core = lax.rem(rank, 2)
    right = {"dp": holder_of(index, 1, n)}
    left = {"dp": holder_of(index, -1, n)}
    twin = {"mp": rank + 1 - 2 * core}
    far = {"mp": lax.rem(rank + 2, 4)}
    return index, core, right, left, twin, far


def greet(targets):
    barrier = pltpu.get_barrier_semaphore()
    for target in targets:
        pl.semaphore_signal(barrier, inc=1, device_id=target, device_id_type=MESH)
    pl.semaphore_wait(barrier, len(targets))


def exchange(source, target, send, recv, slot, device):
    return pltpu.make_async_remote_copy(
        src_ref=source,
        dst_ref=target,
        send_sem=send.at[slot],
        recv_sem=recv.at[slot],
        device_id=device,
        device_id_type=MESH,
    )


def columns_to_rows(pieces, count):
    lane = lax.broadcasted_iota(jnp.int32, (count, 128), 1)
    spread = jnp.zeros((count, 128), jnp.float32)
    for place, piece in enumerate(pieces):
        spread = jnp.where(lane == place, piece, spread)
    return spread.T[:8]


def rows_to_columns(rows):
    padded = jnp.concatenate([rows] + [jnp.zeros_like(rows)] * 15, axis=0)
    return padded.T


def gather_kernel(
    n,
    query,
    key,
    value,
    output,
    small,
    doc_row,
    frequency,
    down,
    full,
    query_gain,
    key_gain,
    attn_gain,
    mlp_gain,
    cosine,
    sine,
    doc_col,
    down_shard,
    mine,
    turned_output,
    down_buf,
    turned_down,
    small_full,
    send,
    recv,
    small_send,
    small_recv,
    load,
    store,
):
    index, core, right, left, twin, far = neighbours(n)
    chunk = query.shape[1]
    local = query.shape[2]
    rows = chunk // SUBS
    count = cosine.shape[0]
    heads = local // HEAD_CHANNELS
    units = down.shape[0]

    loads = [
        pltpu.make_async_copy(
            source, mine.at[:, :, pl.ds(place * local, local)], load.at[place]
        )
        for place, source in enumerate((query, key, value, turned_output))
    ]
    for copy in loads[:3]:
        copy.start()
    flipped = output[...].T
    turned_output[0] = flipped[:chunk]
    turned_output[1] = flipped[chunk:]
    loads[3].start()

    def hop(way, sub, step, incoming):
        owner = holder_of(index, (step - 1 + incoming) * (2 * way - 1), n)
        span = pl.ds(sub * rows, rows)
        target = full.at[owner, way, span]
        return pltpu.make_async_remote_copy(
            src_ref=mine.at[way, span] if step == 1 and not incoming else target,
            dst_ref=target,
            send_sem=send.at[way, sub, step - 1],
            recv_sem=recv.at[way, sub, step - 1],
            device_id=left if way else right,
            device_id_type=MESH,
        )

    def small_hop(step, incoming):
        target = small_full.at[holder_of(index, 1 - incoming - step, n)]
        source = small if step == 1 and not incoming else target
        return exchange(source, target, small_send, small_recv, step - 1, right)

    greet((right, left))
    small_hop(1, 0).start()
    for copy in loads:
        copy.wait()
    for sub in range(SUBS):
        for way in range(2):
            hop(way, sub, 1, 0).start()
    own = pltpu.make_async_copy(mine, full.at[index], store.at[0])
    own.start()
    down_load = pltpu.make_async_copy(down, down_buf, store.at[1])
    down_load.start()
    small_full[index] = small[...]
    docs = doc_row[...].astype(jnp.float32)
    leading = jnp.sum(1.0 - docs, axis=1, keepdims=True)
    doc_col[...] = rows_to_columns(jnp.broadcast_to(docs, (8, count)))

    def table(tile):
        span = pl.ds(pl.multiple_of(tile * 64, 64), 64)
        spot = lax.broadcasted_iota(jnp.int32, (64, HEAD_CHANNELS), 0) + tile * 64
        lane = lax.broadcasted_iota(jnp.int32, (64, HEAD_CHANNELS), 1)
        angles = (spot.astype(jnp.float32) - doc_col[span, 0:1] * leading) * frequency[...]
        cosine[span, :] = jnp.cos(angles)
        wave = jnp.sin(angles)
        sine[span, :] = jnp.where(lane < HEAD_CHANNELS // 2, -wave, wave)

    tiles = count // 64
    for step in range(1, n):
        for sub in range(SUBS):
            for way in range(2):
                hop(way, sub, step, 1).wait_recv()
                if step < n - 1:
                    hop(way, sub, step + 1, 0).start()
        small_hop(step, 1).wait_recv()
        if step < n - 1:
            small_hop(step + 1, 0).start()
        if step <= 4:
            pl.loop((step - 1) * tiles // 4, step * tiles // 4)(table)
        if step == 5:
            down_load.wait()
            for part in range(4):
                span = slice(part * (units // 4), (part + 1) * (units // 4))
                flipped = down_buf[span, :].T
                turned_down[0, :, span] = flipped[:chunk]
                turned_down[1, :, span] = flipped[chunk:]
            down_store = pltpu.make_async_copy(turned_down, down_shard, store.at[2])
            down_store.start()
    lanes = jnp.zeros(small.shape, jnp.float32)
    for owner in range(n):
        part = small_full[owner].astype(jnp.float32)
        lanes = lanes + part
        for row in range(2):
            spot = (2 * owner + row) * 128
            attn_gain[:, spot : spot + 128] = part[8 + row : 9 + row]
            mlp_gain[:, spot : spot + 128] = part[10 + row : 11 + row]
    for head in range(heads):
        spot = head * HEAD_CHANNELS
        query_gain[:, spot : spot + HEAD_CHANNELS] = lanes[head : head + 1]
        key_gain[:, spot : spot + HEAD_CHANNELS] = lanes[4 + head : 5 + head]
    own.wait()
    down_store.wait()
    for step in range(1, n):
        for sub in range(SUBS):
            for way in range(2):
                hop(way, sub, step, 0).wait_send()
        small_hop(step, 0).wait_send()


def kernel_gather(query, key, value, output, small, doc_ids, frequency, down, n):
    rows, local = query.shape
    chunk = rows // 2
    count = doc_ids.shape[0]
    units = down.shape[0]
    low = query.dtype
    full = jnp.float32
    hbm = pl.BlockSpec(memory_space=pl.ANY)
    vmem = pl.BlockSpec(memory_space=pltpu.VMEM)
    dma = pltpu.SemaphoreType.DMA
    shape = jax.ShapeDtypeStruct
    split = [part.reshape(2, chunk, local) for part in (query, key, value)]
    outs = pl.pallas_call(
        functools.partial(gather_kernel, n),
        out_shape=(
            shape((n, 2, chunk, 4 * local), low),
            shape((1, local), full),
            shape((1, local), full),
            shape((1, n * rows), full),
            shape((1, n * rows), full),
            shape((count, HEAD_CHANNELS), full),
            shape((count, HEAD_CHANNELS), full),
            shape((count, 128), full),
            shape((2, chunk, units), low),
        ),
        in_specs=[hbm] * 3 + [vmem] * 4 + [hbm],
        out_specs=(hbm,) + (vmem,) * 7 + (hbm,),
        scratch_shapes=[
            pltpu.VMEM((2, chunk, 4 * local), low),
            pltpu.VMEM((2, chunk, local), low),
            pltpu.VMEM((units, rows), low),
            pltpu.VMEM((2, chunk, units), low),
            pltpu.VMEM((n, SMALL, 128), low),
            dma((2, SUBS, n - 1)),
            dma((2, SUBS, n - 1)),
            dma((n - 1,)),
            dma((n - 1,)),
            dma((4,)),
            dma((3,)),
        ],
        compiler_params=pltpu.CompilerParams(
            collective_id=0, has_side_effects=True, vmem_limit_bytes=60 * 2**20
        ),
    )(*split, output, small, doc_ids.reshape(1, count), frequency, down)
    return outs[0].reshape(n * rows, 4 * local), *outs[1:]


def scatter_kernel(
    n,
    grads,
    query_row,
    key_row,
    attn_row,
    mlp_row,
    out_query,
    out_key,
    out_value,
    out_output,
    small_out,
    own,
    inbox,
    tail,
    parts,
    small_inbox,
    small_outbox,
    send,
    recv,
    small_send,
    small_recv,
    own_sem,
):
    index, core, right, left, twin, far = neighbours(n)
    chunk = out_query.shape[1]
    local = out_query.shape[2]
    rows = chunk // SUBS
    heads = local // HEAD_CHANNELS

    def hop(way, sub, step):
        first = grads.at[holder_of(index, 2 * way - 1, n), way, pl.ds(sub * rows, rows)]
        return pltpu.make_async_remote_copy(
            src_ref=first if step == 1 else inbox.at[step - 2, way, sub],
            dst_ref=inbox.at[step - 1, way, sub],
            send_sem=send.at[way, sub, step - 1],
            recv_sem=recv.at[way, sub, step - 1],
            device_id=left if way else right,
            device_id_type=MESH,
        )

    def own_copy(way, sub, step):
        owner = holder_of(index, (1 + step) * (2 * way - 1), n)
        return pltpu.make_async_copy(
            grads.at[owner, way, pl.ds(sub * rows, rows)],
            own.at[way, sub],
            own_sem.at[way, sub],
        )

    def small_hop(step):
        first = parts.at[holder_of(index, -1, n)]
        return exchange(
            first if step == 1 else small_outbox.at[step - 2],
            small_inbox.at[step - 1],
            small_send,
            small_recv,
            step - 1,
            twin if step == n else right,
        )

    greet((right, left, twin))
    for sub in range(SUBS):
        for way in range(2):
            hop(way, sub, 1).start()
            own_copy(way, sub, 1).start()
    for owner in range(n):
        for head in range(heads):
            spot = head * HEAD_CHANNELS
            parts[owner, head : head + 1, :] = query_row[:, spot : spot + HEAD_CHANNELS]
            parts[owner, 4 + head : 5 + head, :] = key_row[:, spot : spot + HEAD_CHANNELS]
        for row in range(2):
            spot = (2 * owner + row) * 128
            parts[owner, 8 + row : 9 + row, :] = attn_row[:, spot : spot + 128]
            parts[owner, 10 + row : 11 + row, :] = mlp_row[:, spot : spot + 128]
        parts[owner, 12:16, :] = jnp.zeros((4, 128), jnp.float32)
    small_hop(1).start()
    for step in range(1, n):
        for sub in range(SUBS):
            for way in range(2):
                own_copy(way, sub, step).wait()
                hop(way, sub, step).wait_recv()

                @pl.loop(0, rows // 16)
                def _(tile, way=way, sub=sub, step=step):
                    near = pl.ds(pl.multiple_of(tile * 16, 16), 16)
                    total = inbox[step - 1, way, sub, near, :].astype(jnp.float32) + own[
                        way, sub, near, :
                    ].astype(jnp.float32)
                    if step < n - 1:
                        inbox[step - 1, way, sub, near, :] = total.astype(inbox.dtype)
                    else:
                        wide = pl.ds(pl.multiple_of(sub * rows + tile * 16, 16), 16)
                        out_query[way, wide, :] = total[:, :local]
                        out_key[way, wide, :] = total[:, local : 2 * local]
                        out_value[way, wide, :] = total[:, 2 * local : 3 * local]
                        deep = pl.ds(
                            pl.multiple_of(way * chunk + sub * rows + tile * 16, 16), 16
                        )
                        tail[deep, :] = total[:, 3 * local :]

                if step < n - 1:
                    hop(way, sub, step + 1).start()
                    own_copy(way, sub, step + 1).start()
        if step < n - 1:
            small_hop(step).wait_recv()
            owner = holder_of(index, -1 - step, n)
            small_outbox[step - 1] = small_inbox[step - 1] + parts[owner]
            small_hop(step + 1).start()
    small_hop(n - 1).wait_recv()
    small_outbox[n - 2] = small_inbox[n - 2] + parts[index]
    small_hop(n).start()
    out_output[...] = tail[...].T
    small_hop(n).wait_recv()
    line = lax.broadcasted_iota(jnp.int32, small_out.shape, 0)
    small_out[...] = small_outbox[n - 2] + jnp.where(line >= 8, small_inbox[n - 1], 0.0)
    for step in range(1, n):
        for sub in range(SUBS):
            for way in range(2):
                hop(way, sub, step).wait_send()
        small_hop(step).wait_send()
    small_hop(n).wait_send()


def kernel_scatter(grads, query_row, key_row, attn_row, mlp_row, n):
    rows, width = grads.shape[0] // n, grads.shape[1]
    chunk, local = rows // 2, width // 4
    deep = chunk // SUBS
    full = jnp.float32
    vmem = pl.BlockSpec(memory_space=pltpu.VMEM)
    dma = pltpu.SemaphoreType.DMA
    shape = jax.ShapeDtypeStruct
    outs = pl.pallas_call(
        functools.partial(scatter_kernel, n),
        out_shape=(shape((2, chunk, local), full),) * 3
        + (shape((local, rows), full), shape((SMALL, 128), full)),
        in_specs=[pl.BlockSpec(memory_space=pl.ANY)] + [vmem] * 4,
        out_specs=(vmem,) * 5,
        scratch_shapes=[
            pltpu.VMEM((2, SUBS, deep, width), grads.dtype),
            pltpu.VMEM((n - 1, 2, SUBS, deep, width), grads.dtype),
            pltpu.VMEM((rows, local), full),
            pltpu.VMEM((n, SMALL, 128), full),
            pltpu.VMEM((n, SMALL, 128), full),
            pltpu.VMEM((n - 1, SMALL, 128), full),
            dma((2, SUBS, n - 1)),
            dma((2, SUBS, n - 1)),
            dma((n,)),
            dma((n,)),
            dma((2, SUBS)),
        ],
        compiler_params=pltpu.CompilerParams(
            collective_id=1, has_side_effects=True, vmem_limit_bytes=60 * 2**20
        ),
    )(grads.reshape(n, 2, chunk, width), query_row, key_row, attn_row, mlp_row)
    return tuple(part.reshape(rows, local) for part in outs[:3]) + outs[3:]


def turned(vectors, cosine, sine):
    return vectors * cosine + pltpu.roll(vectors, HEAD_CHANNELS // 2, 1) * sine


def masked_scores(query, key, doc_col, doc_row, block):
    length = key.shape[0]
    scores = lax.dot_general(
        query, key, (((1,), (1,)), ((), ())), preferred_element_type=jnp.float32
    ) * (1.0 / math.sqrt(HEAD_CHANNELS))
    row = lax.broadcasted_iota(jnp.int32, scores.shape, 0) + block * BLOCK
    col = lax.broadcasted_iota(jnp.int32, scores.shape, 1)
    own = doc_col[block * BLOCK : (block + 1) * BLOCK, 0:1]
    same = own == doc_row[:, :length].astype(jnp.float32)
    return jnp.where((col <= row) & same, scores, MASKED)


def attend_kernel(
    n,
    tokens,
    attn_full,
    gate_shard,
    up_shard,
    cosine,
    sine,
    doc_col,
    doc_row,
    query_gain,
    key_gain,
    attn_gain,
    gate_full,
    up_full,
    query_raw_out,
    key_raw_out,
    query_rot_out,
    key_rot_out,
    value_out,
    attended_out,
    totals,
    inverses,
    branch_out,
    hidden_out,
    hidden_low,
    lhs,
    weights,
    query_raw,
    key_raw,
    query_rot,
    key_rot,
    value,
    attended,
    mixed,
    twin_in,
    pair,
    far_in,
    branch,
    half_buf,
    low_buf,
    stat,
    ring_send,
    ring_recv,
    stat_send,
    stat_recv,
    twin_send,
    twin_recv,
    far_send,
    far_recv,
    join_send,
    join_recv,
    load_sem,
    store_sem,
):
    index, core, right, left, twin, far = neighbours(n)
    count, width = lhs.shape
    half = count // 2
    local = query_raw.shape[1]
    heads = local // HEAD_CHANNELS
    blocks = width // TILE
    shards = (gate_shard, up_shard)
    fulls = (gate_full, up_full)
    right_side = (((1,), (1,)), ((), ()))

    def ring(way, unit, step, incoming):
        owner = holder_of(index, (step - 1 + incoming) * (2 * way - 1), n)
        target = fulls[unit].at[owner, way]
        return pltpu.make_async_remote_copy(
            src_ref=shards[unit].at[way] if step == 1 and not incoming else target,
            dst_ref=target,
            send_sem=ring_send.at[way, unit, step - 1],
            recv_sem=ring_recv.at[way, unit, step - 1],
            device_id=left if way else right,
            device_id_type=MESH,
        )

    events = [(step, unit) for step in range(1, n) for unit in range(2)]

    def serve():
        step, unit = events.pop(0)
        for way in range(2):
            ring(way, unit, step, 1).wait_recv()
            if step < n - 1:
                ring(way, unit, step + 1, 0).start()

    greet((right, left, twin, far))
    for unit in range(2):
        for way in range(2):
            ring(way, unit, 1, 0).start()
    loads = [
        pltpu.make_async_copy(tokens, lhs, load_sem.at[0]),
        pltpu.make_async_copy(attn_full, weights, load_sem.at[1]),
        pltpu.make_async_copy(
            tokens.at[pl.ds(pl.multiple_of(core * half, half), half)], half_buf, load_sem.at[2]
        ),
        pltpu.make_async_copy(gate_shard, gate_full.at[index], load_sem.at[3]),
        pltpu.make_async_copy(up_shard, up_full.at[index], load_sem.at[4]),
    ]
    for copy in loads:
        copy.start()
    loads[0].wait()
    loads[1].wait()

    def project(target, start):
        for tile in range(local // TILE):
            cols = slice(start + tile * TILE, start + (tile + 1) * TILE)
            target[:, tile * TILE : (tile + 1) * TILE] = jnp.dot(
                lhs[...], weights[:, cols], preferred_element_type=jnp.float32
            ).astype(target.dtype)

    project(query_raw, 0)
    project(key_raw, local)
    squares = [
        jnp.sum(raw[...] * raw[...], axis=1, keepdims=True) for raw in (query_raw, key_raw)
    ]
    stat[0] = columns_to_rows(squares, count)
    first = exchange(stat.at[0], stat.at[1], stat_send, stat_recv, 0, twin)
    first.start()
    project(value, 2 * local)
    first.wait()
    stat[2] = stat[0] + stat[1]
    second = exchange(stat.at[2], stat.at[3], stat_send, stat_recv, 1, far)
    second.start()
    serve()
    second.wait()
    inverses[...] = lax.rsqrt(rows_to_columns(stat[2] + stat[3]) / width + EPSILON)

    @pl.loop(0, heads)
    def _(head):
        cols = pl.ds(pl.multiple_of(head * HEAD_CHANNELS, HEAD_CHANNELS), HEAD_CHANNELS)
        for place, (raw, gain, out) in enumerate(
            ((query_raw, query_gain, query_rot), (key_raw, key_gain, key_rot))
        ):
            normed = raw[:, cols] * inverses[:, place : place + 1] * gain[:, cols]
            out[:, cols] = turned(normed, cosine[...], sine[...]).astype(jnp.bfloat16)

    stores = [
        pltpu.make_async_copy(source, target, store_sem.at[place])
        for place, (source, target) in enumerate(
            (
                (query_raw, query_raw_out),
                (key_raw, key_raw_out),
                (query_rot, query_rot_out),
                (key_rot, key_rot_out),
                (value, value_out),
            )
        )
    ]
    for copy in stores:
        copy.start()
    serve()
    totals[...] = jnp.zeros_like(totals)

    @pl.loop(0, heads)
    def _(head):
        cols = pl.ds(pl.multiple_of(head * HEAD_CHANNELS, HEAD_CHANNELS), HEAD_CHANNELS)
        lane = lax.broadcasted_iota(jnp.int32, (BLOCK, 128), 1)
        for block in range(count // BLOCK):
            span = slice(block * BLOCK, (block + 1) * BLOCK)
            length = (block + 1) * BLOCK
            scores = masked_scores(
                query_rot[span, cols], key_rot[:length, cols], doc_col, doc_row, block
            )
            maximum = jnp.max(scores, axis=1, keepdims=True)
            powers = jnp.exp(scores - maximum)
            denominator = jnp.sum(powers, axis=1, keepdims=True)
            rounded = (powers * (1.0 / denominator)).astype(jnp.bfloat16)
            attended[span, cols] = jnp.dot(
                rounded, value[:length, cols], preferred_element_type=jnp.float32
            ).astype(jnp.bfloat16)
            totals[span, :] = jnp.where(
                lane == head, maximum + jnp.log(denominator), totals[span, :]
            )

    stores.append(pltpu.make_async_copy(attended, attended_out, store_sem.at[5]))
    stores[5].start()
    serve()

    def twin_copy(tile):
        span = pl.ds(pl.multiple_of((1 - core) * half, half), half)
        return exchange(
            mixed.at[tile % 4, span], twin_in.at[tile % 4], twin_send, twin_recv, tile, twin
        )

    def far_copy(tile):
        return exchange(pair.at[tile], far_in.at[tile], far_send, far_recv, tile, far)

    def output_tile(tile):
        span = slice(tile * TILE, (tile + 1) * TILE)
        mixed[tile % 4] = lax.dot_general(
            attended[...],
            weights[span, 3 * local :],
            right_side,
            preferred_element_type=jnp.float32,
        ).astype(jnp.bfloat16)
        twin_copy(tile).start()

    def add_twin(tile):
        twin_copy(tile).wait_recv()

        @pl.loop(0, half // 32)
        def _(row):
            span = pl.ds(pl.multiple_of(row * 32, 32), 32)
            mine = pl.ds(pl.multiple_of(core * half + row * 32, 32), 32)
            total = mixed[tile % 4, mine, :].astype(jnp.float32) + twin_in[
                tile % 4, span, :
            ].astype(jnp.float32)
            pair[tile, span, :] = total.astype(jnp.bfloat16)

        far_copy(tile).start()
        twin_copy(tile).wait_send()

    def add_far(tile):
        far_copy(tile).wait_recv()

        @pl.loop(0, half // 32)
        def _(row):
            span = pl.ds(pl.multiple_of(row * 32, 32), 32)
            branch[span, tile * TILE : (tile + 1) * TILE] = pair[tile, span, :].astype(
                jnp.float32
            ) + far_in[tile, span, :].astype(jnp.float32)

    for tile in range(blocks):
        output_tile(tile)
        if tile >= 1:
            add_twin(tile - 1)
    add_twin(blocks - 1)
    serve()
    for tile in range(blocks):
        add_far(tile)
        if tile % 2 == 1:
            serve()
    loads[2].wait()

    def finish(tile):
        span = pl.ds(pl.multiple_of(tile * 16, 16), 16)
        mix = branch[span, :]
        inverse = lax.rsqrt(jnp.sum(mix * mix, axis=1, keepdims=True) / width + EPSILON)
        state = half_buf[span, :].astype(jnp.float32) + mix * inverse * attn_gain[...]
        low_buf[span, :] = state.astype(jnp.bfloat16)
        hidden_out[span, :] = state

    def join(part, kind):
        span = pl.ds(part * (half // 4), half // 4)
        if kind == 2:
            return pltpu.make_async_copy(
                low_buf.at[span], hidden_low.at[core, span], store_sem.at[6 + part]
            )
        target = hidden_low.at[1 - core if kind else core, span]
        return exchange(
            target if kind else low_buf.at[span], target, join_send, join_recv, part, twin
        )

    for part in range(4):
        pl.loop(part * (half // 64), (part + 1) * (half // 64))(finish)
        join(part, 0).start()
        join(part, 2).start()
    stores.append(pltpu.make_async_copy(branch, branch_out, store_sem.at[10]))
    stores[6].start()
    while events:
        serve()
    for part in range(4):
        join(part, 1).wait_recv()
        join(part, 0).wait_send()
        join(part, 2).wait()
    for copy in stores + loads[3:]:
        copy.wait()
    for tile in range(blocks):
        far_copy(tile).wait_send()
    for step in range(1, n):
        for unit in range(2):
            for way in range(2):
                ring(way, unit, step, 0).wait_send()


def kernel_attend(
    tokens,
    attn_full,
    gate_shard,
    up_shard,
    cosine,
    sine,
    doc_col,
    doc_ids,
    query_gain,
    key_gain,
    attn_gain,
    n,
):
    count, width = tokens.shape
    local = query_gain.shape[1]
    units = gate_shard.shape[1]
    half = count // 2
    chunk = width // n // 2
    blocks = width // TILE
    low = jnp.bfloat16
    full = jnp.float32
    hbm = pl.BlockSpec(memory_space=pl.ANY)
    vmem = pl.BlockSpec(memory_space=pltpu.VMEM)
    dma = pltpu.SemaphoreType.DMA
    shape = jax.ShapeDtypeStruct
    outs = pl.pallas_call(
        functools.partial(attend_kernel, n),
        out_shape=(
            shape((n, 2, chunk, units), low),
            shape((n, 2, chunk, units), low),
            shape((count, local), full),
            shape((count, local), full),
            shape((count, local), low),
            shape((count, local), low),
            shape((count, local), low),
            shape((count, local), low),
            shape((count, 128), full),
            shape((count, 128), full),
            shape((half, width), full),
            shape((half, width), full),
            shape((2, half, width), low),
        ),
        in_specs=[hbm] * 4 + [vmem] * 7,
        out_specs=(hbm,) * 8 + (vmem,) * 2 + (hbm, vmem, hbm),
        scratch_shapes=[
            pltpu.VMEM((count, width), low),
            pltpu.VMEM((width, 4 * local), low),
            pltpu.VMEM((count, local), full),
            pltpu.VMEM((count, local), full),
            pltpu.VMEM((count, local), low),
            pltpu.VMEM((count, local), low),
            pltpu.VMEM((count, local), low),
            pltpu.VMEM((count, local), low),
            pltpu.VMEM((4, count, TILE), low),
            pltpu.VMEM((4, half, TILE), low),
            pltpu.VMEM((blocks, half, TILE), low),
            pltpu.VMEM((blocks, half, TILE), low),
            pltpu.VMEM((half, width), full),
            pltpu.VMEM((half, width), low),
            pltpu.VMEM((half, width), low),
            pltpu.VMEM((4, 8, count), full),
            dma((2, 2, n - 1)),
            dma((2, 2, n - 1)),
            dma((2,)),
            dma((2,)),
            dma((blocks,)),
            dma((blocks,)),
            dma((blocks,)),
            dma((blocks,)),
            dma((4,)),
            dma((4,)),
            dma((5,)),
            dma((11,)),
        ],
        compiler_params=pltpu.CompilerParams(
            collective_id=4, has_side_effects=True, vmem_limit_bytes=58 * 2**20
        ),
    )(
        tokens,
        attn_full,
        gate_shard.reshape(2, chunk, units),
        up_shard.reshape(2, chunk, units),
        cosine,
        sine,
        doc_col,
        doc_ids.reshape(1, count),
        query_gain,
        key_gain,
        attn_gain,
    )
    return (
        outs[0].reshape(width, units),
        outs[1].reshape(width, units),
        *outs[2:12],
        outs[12].reshape(count, width),
    )


def feed_kernel(
    n,
    hidden_low,
    gate_full,
    up_full,
    down_shard,
    hidden,
    upstream,
    gains,
    product_out,
    gate_slope,
    silu_out,
    down_full,
    d_mlp,
    block_half,
    gain_grad,
    lhs,
    product,
    held,
    gate_tile,
    up_tile,
    slope_tile,
    silu_tile,
    twin_out,
    twin_in,
    pair,
    far_in,
    branch,
    hidden_buf,
    upstream_buf,
    d_buf,
    block_buf,
    gain_sum,
    ring_send,
    ring_recv,
    twin_send,
    twin_recv,
    far_send,
    far_recv,
    join_send,
    join_recv,
    load_sem,
    tile_sem,
    stage_sem,
    store_sem,
):
    index, core, right, left, twin, far = neighbours(n)
    half = hidden.shape[0]
    chunk = held.shape[2]
    rows = chunk // SUBS
    tiles = product.shape[1] // TILE
    width = branch.shape[1]

    loads = [
        pltpu.make_async_copy(hidden_low, lhs, load_sem.at[0]),
        pltpu.make_async_copy(down_shard, held.at[index], load_sem.at[1]),
        pltpu.make_async_copy(hidden, hidden_buf, load_sem.at[2]),
        pltpu.make_async_copy(
            upstream.at[pl.ds(pl.multiple_of(core * half, half), half)],
            upstream_buf,
            load_sem.at[3],
        ),
    ]

    def weight_copies(tile, slot):
        cols = pl.ds(pl.multiple_of(tile * TILE, TILE), TILE)
        return (
            pltpu.make_async_copy(gate_full.at[:, cols], gate_tile.at[slot], tile_sem.at[slot, 0]),
            pltpu.make_async_copy(up_full.at[:, cols], up_tile.at[slot], tile_sem.at[slot, 1]),
        )

    def stage_copies(tile, slot):
        cols = pl.ds(pl.multiple_of(tile * TILE, TILE), TILE)
        return (
            pltpu.make_async_copy(slope_tile.at[slot], gate_slope.at[:, cols], stage_sem.at[slot, 0]),
            pltpu.make_async_copy(silu_tile.at[slot], silu_out.at[:, cols], stage_sem.at[slot, 1]),
        )

    def ring(way, sub, step, incoming):
        owner = holder_of(index, (step - 1 + incoming) * (2 * way - 1), n)
        span = pl.ds(sub * rows, rows)
        target = held.at[owner, way, span]
        return pltpu.make_async_remote_copy(
            src_ref=down_shard.at[way, span] if step == 1 and not incoming else target,
            dst_ref=target,
            send_sem=ring_send.at[way, sub, step - 1],
            recv_sem=ring_recv.at[way, sub, step - 1],
            device_id=left if way else right,
            device_id_type=MESH,
        )

    def serve(step, sub):
        for way in range(2):
            ring(way, sub, step, 1).wait_recv()
            if step < n - 1:
                ring(way, sub, step + 1, 0).start()

    def columns(sub):
        return pl.ds(0, 2 * chunk) if sub is None else pl.ds(sub * 2 * rows, 2 * rows)

    def twin_copy(step, sub=None):
        return exchange(
            twin_out.at[step, :, columns(sub)],
            twin_in.at[step, :, columns(sub)],
            twin_send,
            twin_recv,
            step + (sub or 0),
            twin,
        )

    def far_copy(step, sub=None):
        return exchange(
            pair.at[step, :, columns(sub)],
            far_in.at[step, :, columns(sub)],
            far_send,
            far_recv,
            step + (sub or 0),
            far,
        )

    greet((right, left, twin, far))
    for sub in range(SUBS):
        for way in range(2):
            ring(way, sub, 1, 0).start()
    for copy in loads:
        copy.start()
    for copy in weight_copies(0, 0):
        copy.start()
    loads[0].wait()

    def feed_tile(tile):
        slot = lax.rem(tile, 2)
        for copy in weight_copies(tile, slot):
            copy.wait()

        @pl.when(tile + 1 < tiles)
        def _():
            for copy in weight_copies(tile + 1, 1 - slot):
                copy.start()

        @pl.when(tile >= 2)
        def _():
            for copy in stage_copies(tile - 2, slot):
                copy.wait()

        cols = pl.ds(pl.multiple_of(tile * TILE, TILE), TILE)

        gate = jnp.dot(lhs[...], gate_tile[slot], preferred_element_type=jnp.float32)
        up = jnp.dot(lhs[...], up_tile[slot], preferred_element_type=jnp.float32)
        sigmoid = jax.nn.sigmoid(gate)
        silu = gate * sigmoid
        product[:, cols] = (silu * up).astype(jnp.bfloat16)
        slope_tile[slot] = (up * sigmoid * (1.0 + gate * (1.0 - sigmoid))).astype(jnp.bfloat16)
        silu_tile[slot] = silu.astype(jnp.bfloat16)

        for copy in stage_copies(tile, slot):
            copy.start()

    events = [(step, sub) for step in range(1, n) for sub in range(SUBS)]
    groups = 4
    for group in range(groups):
        pl.loop(group * tiles // groups, (group + 1) * tiles // groups)(feed_tile)
        serve(*events.pop(0))
    stores = [pltpu.make_async_copy(product, product_out, store_sem.at[0])]
    stores[0].start()
    loads[1].wait()

    def multiply(step, sub=None):
        part = slice(None) if sub is None else slice(sub * rows, (sub + 1) * rows)
        first = held[holder_of(index, -step, n), 0, part]
        second = held[holder_of(index, step, n), 1, part]
        rhs = jnp.concatenate([first, second], axis=0)
        contract = (((1,), (1,)), ((), ()))
        span = pl.ds(pl.multiple_of((1 - core) * half, half), half)
        twin_out[step, :, columns(sub)] = lax.dot_general(
            product[span, :], rhs, contract, preferred_element_type=jnp.float32
        ).astype(jnp.bfloat16)
        twin_copy(step, sub).start()
        span = pl.ds(pl.multiple_of(core * half, half), half)
        pair[step, :, columns(sub)] = lax.dot_general(
            product[span, :], rhs, contract, preferred_element_type=jnp.float32
        ).astype(jnp.bfloat16)

    def add_twin(step, sub=None):
        twin_copy(step, sub).wait_recv()
        cols = columns(sub)

        @pl.loop(0, half // 32)
        def _(tile):
            span = pl.ds(pl.multiple_of(tile * 32, 32), 32)
            total = pair[step, span, cols].astype(jnp.float32) + twin_in[
                step, span, cols
            ].astype(jnp.float32)
            pair[step, span, cols] = total.astype(jnp.bfloat16)

        far_copy(step, sub).start()

    def add_far(step):
        if step < n - 1:
            far_copy(step).wait_recv()
        else:
            for sub in range(SUBS):
                far_copy(step, sub).wait_recv()
        first = pl.multiple_of(holder_of(index, -step, n) * 2 * chunk, chunk)
        second = pl.multiple_of(holder_of(index, step, n) * 2 * chunk + chunk, chunk)

        @pl.loop(0, half // 32)
        def _(tile):
            span = pl.ds(pl.multiple_of(tile * 32, 32), 32)
            total = pair[step, span, :].astype(jnp.float32) + far_in[step, span, :].astype(
                jnp.float32
            )
            if step < n - 1:
                sides = total[:, :chunk], total[:, chunk:]
            else:
                sides = [
                    jnp.concatenate(
                        [
                            total[:, (2 * sub + way) * rows : (2 * sub + way + 1) * rows]
                            for sub in range(SUBS)
                        ],
                        axis=1,
                    )
                    for way in range(2)
                ]
            branch[span, pl.ds(first, chunk)] = sides[0]
            branch[span, pl.ds(second, chunk)] = sides[1]

    def serve_until(step, sub):
        while events and events[0] <= (step, sub):
            serve(*events.pop(0))

    for step in range(n - 1):
        serve_until(step, SUBS - 1)
        multiply(step)
        if step >= 1:
            if step <= 3:
                add_twin(step - 1)
            if step >= 3:
                add_twin(step)
            if step >= 2:
                add_far(step - 2)
        if step < 2 and events:
            serve(*events.pop(0))
    for sub in range(SUBS):
        serve_until(n - 1, sub)
        multiply(n - 1, sub)
        add_twin(n - 1, sub)
        if sub == 0:
            add_far(n - 3)
    stores.append(pltpu.make_async_copy(held, down_full, store_sem.at[1]))
    stores[1].start()
    add_far(n - 2)
    loads[2].wait()
    loads[3].wait()
    gain_sum[...] = jnp.zeros_like(gain_sum)
    add_far(n - 1)

    def finish(tile):
        span = pl.ds(pl.multiple_of(tile * 16, 16), 16)
        mixed = branch[span, :]
        scale = gains[...]
        inverse = lax.rsqrt(jnp.sum(mixed * mixed, axis=1, keepdims=True) / width + EPSILON)
        grad = upstream_buf[span, :].astype(jnp.float32)
        scaled = scale * grad
        mean = jnp.sum(scaled * mixed, axis=1, keepdims=True) / width
        normed = mixed * inverse
        d_buf[span, :] = (
            inverse * scaled - mixed * (inverse * inverse * inverse * mean)
        ).astype(jnp.bfloat16)
        block_buf[span, :] = (hidden_buf[span, :] + normed * scale).astype(jnp.bfloat16)
        terms = grad * normed
        gain_sum[...] += terms[:8] + terms[8:]

    def join(part, own):
        span = pl.ds(part * (half // 4), half // 4)
        if own:
            return pltpu.make_async_copy(d_buf.at[span], d_mlp.at[core, span], store_sem.at[3 + part])
        return pltpu.make_async_remote_copy(
            src_ref=d_buf.at[span],
            dst_ref=d_mlp.at[core, span],
            send_sem=join_send.at[part],
            recv_sem=join_recv.at[part],
            device_id=twin,
            device_id_type=MESH,
        )

    def joined(part):
        span = pl.ds(part * (half // 4), half // 4)
        target = d_mlp.at[1 - core, span]
        return pltpu.make_async_remote_copy(
            src_ref=target,
            dst_ref=target,
            send_sem=join_send.at[part],
            recv_sem=join_recv.at[part],
            device_id=twin,
            device_id_type=MESH,
        )

    for part in range(4):
        pl.loop(part * (half // 64), (part + 1) * (half // 64))(finish)
        join(part, False).start()
        join(part, True).start()
    stores.append(pltpu.make_async_copy(block_buf, block_half, store_sem.at[2]))
    stores[2].start()
    gain_grad[...] = jnp.sum(gain_sum[...], axis=0, keepdims=True)
    for part in range(4):
        joined(part).wait_recv()
        join(part, False).wait_send()
        join(part, True).wait()
    for copy in stores:
        copy.wait()
    for tile in (tiles - 2, tiles - 1):
        for copy in stage_copies(tile, tile % 2):
            copy.wait()
    for step in range(n + 1):
        name = (step, None) if step < n - 1 else (n - 1, step - n + 1)
        twin_copy(*name).wait_send()
        far_copy(*name).wait_send()
    for step in range(1, n):
        for sub in range(SUBS):
            for way in range(2):
                ring(way, sub, step, 0).wait_send()


def kernel_feed(hidden_low, gate_full, up_full, down_shard, hidden, upstream, gains, n):
    count, width = hidden_low.shape
    units = gate_full.shape[1]
    half = count // 2
    chunk = width // n // 2
    rows = chunk // SUBS
    low = jnp.bfloat16
    hbm = pl.BlockSpec(memory_space=pl.ANY)
    vmem = pl.BlockSpec(memory_space=pltpu.VMEM)
    dma = pltpu.SemaphoreType.DMA
    product, slope, silu, down_full, d_mlp, block, gain_grad = pl.pallas_call(
        functools.partial(feed_kernel, n),
        out_shape=(
            jax.ShapeDtypeStruct((count, units), low),
            jax.ShapeDtypeStruct((count, units), low),
            jax.ShapeDtypeStruct((count, units), low),
            jax.ShapeDtypeStruct((n, 2, chunk, units), low),
            jax.ShapeDtypeStruct((2, half, width), low),
            jax.ShapeDtypeStruct((half, width), low),
            jax.ShapeDtypeStruct((1, width), jnp.float32),
        ),
        in_specs=[hbm] * 6 + [vmem],
        out_specs=(hbm,) * 6 + (vmem,),
        scratch_shapes=[
            pltpu.VMEM((count, width), low),
            pltpu.VMEM((count, units), low),
            pltpu.VMEM((n, 2, chunk, units), low),
            pltpu.VMEM((2, width, TILE), low),
            pltpu.VMEM((2, width, TILE), low),
            pltpu.VMEM((2, count, TILE), low),
            pltpu.VMEM((2, count, TILE), low),
            pltpu.VMEM((n, half, 2 * chunk), low),
            pltpu.VMEM((n, half, 2 * chunk), low),
            pltpu.VMEM((n, half, 2 * chunk), low),
            pltpu.VMEM((n, half, 2 * chunk), low),
            pltpu.VMEM((half, width), jnp.float32),
            pltpu.VMEM((half, width), jnp.float32),
            pltpu.VMEM((half, width), low),
            pltpu.VMEM((half, width), low),
            pltpu.VMEM((half, width), low),
            pltpu.VMEM((8, width), jnp.float32),
            dma((2, SUBS, n - 1)),
            dma((2, SUBS, n - 1)),
            dma((n + 1,)),
            dma((n + 1,)),
            dma((n + 1,)),
            dma((n + 1,)),
            dma((4,)),
            dma((4,)),
            dma((4,)),
            dma((2, 2)),
            dma((2, 2)),
            dma((7,)),
        ],
        compiler_params=pltpu.CompilerParams(
            collective_id=2, has_side_effects=True, vmem_limit_bytes=58 * 2**20
        ),
    )(
        hidden_low,
        gate_full,
        up_full,
        down_shard,
        hidden,
        upstream,
        gains,
    )
    return (
        product,
        slope,
        silu,
        down_full.reshape(width, units),
        d_mlp.reshape(count, width),
        block,
        gain_grad,
    )


def back_kernel(
    n,
    d_mlp,
    product,
    down_full,
    gate_slope,
    silu_in,
    gate_full,
    up_full,
    hidden_low,
    upstream,
    branch,
    block_half,
    gains,
    out_down,
    d_hidden_out,
    d_branch,
    d_gate_out,
    d_up_out,
    head_grads,
    block_out,
    gain_grad,
    d_out,
    prod,
    d_gate,
    d_up,
    down_tile,
    slope_tile,
    silu_tile,
    gate_tile,
    up_tile,
    hidden_tile,
    first,
    own,
    inbox,
    mixed,
    twin_in,
    pair,
    far_in,
    d_hidden,
    branch_tile,
    upstream_tile,
    d_buf,
    stage,
    gain_sum,
    ring_send,
    ring_recv,
    twin_send,
    twin_recv,
    far_send,
    far_recv,
    join_send,
    join_recv,
    load_sem,
    down_sem,
    weight_sem,
    hidden_sem,
    row_sem,
    stage_sem,
    store_sem,
):
    index, core, right, left, twin, far = neighbours(n)
    side = d_out.shape[2]
    width, units = d_out.shape[3], prod.shape[3]
    pack = 2 * side
    half = d_hidden.shape[0]
    chunk = inbox.shape[3] * SUBS
    rows = chunk // SUBS
    tiles = units // TILE
    blocks = width // TILE
    quarter = half // 4
    left_side = (((0,), (0,)), ((), ()))
    right_side = (((1,), (1,)), ((), ()))

    def tile_span(tile):
        return pl.ds(pl.multiple_of(tile * TILE, TILE), TILE)

    def down_copies(group, tile, slot):
        cols = tile_span(tile)
        return (
            pltpu.make_async_copy(down_full.at[:, cols], down_tile.at[slot], down_sem.at[slot, 0]),
            pltpu.make_async_copy(
                gate_slope.at[:, group, :, cols], slope_tile.at[slot], down_sem.at[slot, 1]
            ),
            pltpu.make_async_copy(
                silu_in.at[:, group, :, cols], silu_tile.at[slot], down_sem.at[slot, 2]
            ),
        )

    def weight_copies(tile, slot):
        span = tile_span(tile)
        return (
            pltpu.make_async_copy(gate_full.at[span], gate_tile.at[slot], weight_sem.at[slot, 0]),
            pltpu.make_async_copy(up_full.at[span], up_tile.at[slot], weight_sem.at[slot, 1]),
        )

    def hidden_copy(group, way):
        owner = holder_of(index, 2 * way - 1, n)
        start = pl.multiple_of(owner * 2 * chunk + way * chunk, chunk)
        return pltpu.make_async_copy(
            hidden_low.at[:, group, :, pl.ds(start, chunk)],
            hidden_tile.at[group, :, :, pl.ds(way * chunk, chunk)],
            hidden_sem.at[group, way],
        )

    def row_copies(part, slot):
        span = pl.ds(part * quarter, quarter)
        mine = pl.ds(pl.multiple_of(core * half + part * quarter, quarter), quarter)
        return (
            pltpu.make_async_copy(branch.at[span], branch_tile.at[slot], row_sem.at[slot, 0]),
            pltpu.make_async_copy(upstream.at[mine], upstream_tile.at[slot], row_sem.at[slot, 1]),
        )

    def stage_copy(which):
        return pltpu.make_async_copy(stage.at[which], head_grads.at[which], stage_sem.at[which])

    def block_copy(kind):
        if kind == 2:
            return pltpu.make_async_copy(block_half, block_out.at[core], store_sem.at[5])
        target = block_out.at[1 - core if kind else core]
        return exchange(target if kind else block_half, target, join_send, join_recv, 4, twin)

    def ring(way, sub, step):
        return pltpu.make_async_remote_copy(
            src_ref=first.at[way, pl.ds(sub * rows, rows)]
            if step == 1
            else inbox.at[step - 2, way, sub],
            dst_ref=inbox.at[step - 1, way, sub],
            send_sem=ring_send.at[way, sub, step - 1],
            recv_sem=ring_recv.at[way, sub, step - 1],
            device_id=left if way else right,
            device_id_type=MESH,
        )

    def grad_block(step):
        cols = []
        for way in range(2):
            owner = holder_of(index, (1 + step) * (2 * way - 1), n)
            start = pl.multiple_of(owner * 2 * chunk + way * chunk, chunk)
            cols.append(d_out[:, :, :, pl.ds(start, chunk)].reshape(2 * pack, chunk))
        block = lax.dot_general(
            jnp.concatenate(cols, axis=1),
            prod[...].reshape(2 * pack, units),
            left_side,
            preferred_element_type=jnp.float32,
        ).astype(jnp.bfloat16)
        target = first if step == 0 else own.at[step % 2]
        target[0] = block[:chunk]
        target[1] = block[chunk:]

    def serve(step, sub):
        for way in range(2):
            ring(way, sub, step).wait_recv()

            @pl.loop(0, rows // 16)
            def _(tile, way=way):
                near = pl.ds(pl.multiple_of(tile * 16, 16), 16)
                mine = pl.ds(pl.multiple_of(sub * rows + tile * 16, 16), 16)
                total = inbox[step - 1, way, sub, near, :].astype(jnp.float32) + own[
                    step % 2, way, mine, :
                ].astype(jnp.float32)
                if step < n - 1:
                    inbox[step - 1, way, sub, near, :] = total.astype(jnp.bfloat16)
                else:
                    out_down[way, mine, :] = total

            if step < n - 1:
                ring(way, sub, step + 1).start()

    def twin_copy(turn):
        return exchange(
            mixed.at[turn % 4, 1 - core], twin_in.at[turn % 4], twin_send, twin_recv, turn, twin
        )

    def far_copy(turn):
        return exchange(pair.at[turn], far_in.at[turn], far_send, far_recv, turn, far)

    greet((right, left, twin, far))
    loads = []
    for group in range(2):
        loads += [
            pltpu.make_async_copy(d_mlp.at[:, group], d_out.at[group], load_sem.at[0, group]),
            pltpu.make_async_copy(product.at[:, group], prod.at[group], load_sem.at[1, group]),
        ]
    for copy in loads:
        copy.start()
    for turn in range(2):
        for copy in down_copies(0, turn, turn):
            copy.start()
        for copy in weight_copies(turn, turn):
            copy.start()
    for copy in loads:
        copy.wait()
    grad_block(0)
    for sub in range(SUBS):
        for way in range(2):
            ring(way, sub, 1).start()
    block_copy(0).start()
    block_copy(2).start()
    for group in range(2):
        for way in range(2):
            hidden_copy(group, way).start()
    grad_block(1)

    def product_tile(group, tile):
        turn = group * tiles + tile
        slot = lax.rem(turn, 3)
        for copy in down_copies(group, tile, slot):
            copy.wait()

        @pl.when(turn + 2 < 2 * tiles)
        def _():
            later = turn + 2
            for copy in down_copies(
                lax.div(later, tiles), lax.rem(later, tiles), lax.rem(later, 3)
            ):
                copy.start()

        cols = tile_span(tile)
        grad = jnp.dot(
            d_out[group].reshape(pack, width), down_tile[slot], preferred_element_type=jnp.float32
        )
        for target, factor in ((d_gate, slope_tile), (d_up, silu_tile)):
            scaled = grad * factor[slot].reshape(pack, TILE).astype(jnp.float32)
            target[group, :, :, cols] = scaled.astype(jnp.bfloat16).reshape(2, side, TILE)

    def input_tile(turn):
        group, tile = divmod(turn, blocks)
        slot = turn % 3
        for copy in weight_copies(tile, slot):
            copy.wait()
        if turn + 2 < 2 * blocks:
            for copy in weight_copies((tile + 2) % blocks, (turn + 2) % 3):
                copy.start()
        total = lax.dot_general(
            d_gate[group].reshape(pack, units),
            gate_tile[slot],
            right_side,
            preferred_element_type=jnp.float32,
        ) + lax.dot_general(
            d_up[group].reshape(pack, units),
            up_tile[slot],
            right_side,
            preferred_element_type=jnp.float32,
        )
        mixed[turn % 4] = total.astype(jnp.bfloat16).reshape(2, side, TILE)
        twin_copy(turn).start()

    def add_twin(turn):
        twin_copy(turn).wait_recv()

        @pl.loop(0, side // 32)
        def _(row):
            span = pl.ds(pl.multiple_of(row * 32, 32), 32)
            total = mixed[turn % 4, core, span, :].astype(jnp.float32) + twin_in[
                turn % 4, span, :
            ].astype(jnp.float32)
            pair[turn, span, :] = total.astype(jnp.bfloat16)

        far_copy(turn).start()
        twin_copy(turn).wait_send()

    def add_far(turn):
        group, tile = divmod(turn, blocks)
        far_copy(turn).wait_recv()

        @pl.loop(0, side // 32)
        def _(row):
            span = pl.ds(pl.multiple_of(row * 32, 32), 32)
            wide = pl.ds(pl.multiple_of(group * side + row * 32, 32), 32)
            d_hidden[wide, tile * TILE : (tile + 1) * TILE] = pair[turn, span, :].astype(
                jnp.float32
            ) + far_in[turn, span, :].astype(jnp.float32)

    def weight_block(which, source):
        block = lax.dot_general(
            hidden_tile[...].reshape(2 * pack, TILE),
            source[...].reshape(2 * pack, units),
            left_side,
            preferred_element_type=jnp.float32,
        ).astype(jnp.bfloat16)
        stage[which, 0] = block[:chunk]
        stage[which, 1] = block[chunk:]
        stage_copy(which).start()

    def finish(part, slot, tile):
        near = pl.ds(pl.multiple_of(tile * 16, 16), 16)
        span = pl.ds(pl.multiple_of(part * quarter + tile * 16, 16), 16)
        total = d_hidden[span, :] + upstream_tile[slot, near, :].astype(jnp.float32)
        d_hidden[span, :] = total
        mix = branch_tile[slot, near, :]
        inverse = lax.rsqrt(jnp.sum(mix * mix, axis=1, keepdims=True) / width + EPSILON)
        scaled = gains[...] * total
        mean = jnp.sum(scaled * mix, axis=1, keepdims=True) / width
        d_buf[span, :] = (inverse * scaled - mix * (inverse * inverse * inverse * mean)).astype(
            jnp.bfloat16
        )
        terms = total * mix * inverse
        gain_sum[...] += terms[:8] + terms[8:]

    def join(part, kind):
        span = pl.ds(part * quarter, quarter)
        if kind == 2:
            return pltpu.make_async_copy(
                d_buf.at[span], d_branch.at[core, span], store_sem.at[part]
            )
        target = d_branch.at[1 - core if kind else core, span]
        return exchange(
            target if kind else d_buf.at[span], target, join_send, join_recv, part, twin
        )

    def finish_group(group):
        for part in (2 * group, 2 * group + 1):
            slot = part % 2
            for copy in row_copies(part, slot):
                copy.wait()
            pl.loop(0, quarter // 16)(functools.partial(finish, part, slot))
            if part < 2:
                for copy in row_copies(part + 2, slot):
                    copy.start()
            join(part, 0).start()
            join(part, 2).start()

    events = [(step, sub) for step in range(1, n) for sub in range(SUBS)]

    def next_event():
        if events:
            step, sub = events.pop(0)
            serve(step, sub)
            if sub == SUBS - 1 and step < n - 1:
                grad_block(step + 1)

    def product_group(group):
        pl.loop(0, tiles // 2)(functools.partial(product_tile, group))
        next_event()
        pl.loop(tiles // 2, tiles)(functools.partial(product_tile, group))
        next_event()

    def grad_store(group):
        return [
            pltpu.make_async_copy(
                source.at[group], target.at[:, group], store_sem.at[6 + 2 * place + group]
            )
            for place, (source, target) in enumerate(((d_gate, d_gate_out), (d_up, d_up_out)))
        ]

    gain_sum[...] = jnp.zeros_like(gain_sum)
    for part in range(2):
        for copy in row_copies(part, part):
            copy.start()
    for group in range(2):
        product_group(group)
        for copy in grad_store(group):
            copy.start()
        if group == 1:
            for turn in range(blocks - 3, blocks):
                add_far(turn)
        for turn in range(group * blocks, (group + 1) * blocks):
            input_tile(turn)
            if turn % blocks >= 1:
                add_twin(turn - 1)
            if turn % blocks >= 3:
                add_far(turn - 3)
            if turn % blocks in (2, 5):
                next_event()
        add_twin((group + 1) * blocks - 1)
        next_event()
        if group == 1:
            finish_group(0)
    for group in range(2):
        for way in range(2):
            hidden_copy(group, way).wait()
    weight_block(0, d_gate)
    add_far(2 * blocks - 3)
    next_event()
    weight_block(1, d_up)
    add_far(2 * blocks - 2)
    next_event()
    add_far(2 * blocks - 1)
    finish_group(1)
    stores = pltpu.make_async_copy(d_hidden, d_hidden_out, store_sem.at[4])
    stores.start()
    while events:
        next_event()
    for part in range(4):
        join(part, 1).wait_recv()
        join(part, 0).wait_send()
        join(part, 2).wait()
    stores.wait()
    gain_grad[...] = jnp.sum(gain_sum[...], axis=0, keepdims=True)
    for which in range(2):
        stage_copy(which).wait()
        for copy in grad_store(which):
            copy.wait()
    block_copy(0).wait_send()
    block_copy(1).wait_recv()
    block_copy(2).wait()
    for turn in range(2 * blocks):
        far_copy(turn).wait_send()
    for step in range(1, n):
        for sub in range(SUBS):
            for way in range(2):
                ring(way, sub, step).wait_send()


def kernel_back(
    d_mlp,
    product,
    down_full,
    gate_slope,
    silu,
    gate_full,
    up_full,
    hidden_low,
    upstream,
    branch,
    block_half,
    gains,
    n,
):
    count, width = d_mlp.shape
    units = product.shape[1]
    half = count // 2
    side = count // 4
    chunk = width // n // 2
    rows = chunk // SUBS
    blocks = width // TILE
    low = jnp.bfloat16
    full = jnp.float32
    hbm = pl.BlockSpec(memory_space=pl.ANY)
    vmem = pl.BlockSpec(memory_space=pltpu.VMEM)
    dma = pltpu.SemaphoreType.DMA
    shape = jax.ShapeDtypeStruct

    def cut(array):
        return array.reshape(2, 2, side, array.shape[1])

    outs = pl.pallas_call(
        functools.partial(back_kernel, n),
        out_shape=(
            shape((2, chunk, units), full),
            shape((half, width), full),
            shape((2, half, width), low),
            shape((2, 2, side, units), low),
            shape((2, 2, side, units), low),
            shape((2, 2, chunk, units), low),
            shape((2, half, width), low),
            shape((1, width), full),
        ),
        in_specs=[hbm] * 11 + [vmem],
        out_specs=(vmem,) + (hbm,) * 6 + (vmem,),
        scratch_shapes=[
            pltpu.VMEM((2, 2, side, width), low),
            pltpu.VMEM((2, 2, side, units), low),
            pltpu.VMEM((2, 2, side, units), low),
            pltpu.VMEM((2, 2, side, units), low),
            pltpu.VMEM((3, width, TILE), low),
            pltpu.VMEM((3, 2, side, TILE), low),
            pltpu.VMEM((3, 2, side, TILE), low),
            pltpu.VMEM((3, TILE, units), low),
            pltpu.VMEM((3, TILE, units), low),
            pltpu.VMEM((2, 2, side, TILE), low),
            pltpu.VMEM((2, chunk, units), low),
            pltpu.VMEM((2, 2, chunk, units), low),
            pltpu.VMEM((n - 1, 2, SUBS, rows, units), low),
            pltpu.VMEM((4, 2, side, TILE), low),
            pltpu.VMEM((4, side, TILE), low),
            pltpu.VMEM((2 * blocks, side, TILE), low),
            pltpu.VMEM((2 * blocks, side, TILE), low),
            pltpu.VMEM((half, width), full),
            pltpu.VMEM((2, half // 4, width), full),
            pltpu.VMEM((2, half // 4, width), low),
            pltpu.VMEM((half, width), low),
            pltpu.VMEM((2, 2, chunk, units), low),
            pltpu.VMEM((8, width), full),
            dma((2, SUBS, n - 1)),
            dma((2, SUBS, n - 1)),
            dma((2 * blocks,)),
            dma((2 * blocks,)),
            dma((2 * blocks,)),
            dma((2 * blocks,)),
            dma((5,)),
            dma((5,)),
            dma((2, 2)),
            dma((3, 3)),
            dma((3, 2)),
            dma((2, 2)),
            dma((2, 2)),
            dma((2,)),
            dma((10,)),
        ],
        compiler_params=pltpu.CompilerParams(
            collective_id=3, has_side_effects=True, vmem_limit_bytes=60 * 2**20
        ),
    )(
        cut(d_mlp),
        cut(product),
        down_full,
        cut(gate_slope),
        cut(silu),
        gate_full,
        up_full,
        cut(hidden_low),
        upstream,
        branch,
        block_half,
        gains,
    )
    out_down, d_hidden, d_branch, d_gate, d_up, head_grads, block_out, gain_grad = outs
    return (
        out_down.reshape(2 * chunk, units),
        d_hidden,
        d_branch.reshape(count, width),
        d_gate.reshape(count, units),
        d_up.reshape(count, units),
        head_grads,
        block_out.reshape(count, width),
        gain_grad,
    )


def detach_kernel(
    n,
    d_branch,
    attn_full,
    attended_in,
    query_rot_in,
    key_rot_in,
    value_in,
    query_raw_in,
    key_raw_in,
    tokens,
    d_hidden,
    head_grads,
    d_gate,
    d_up,
    hidden_low,
    totals,
    inverses,
    cosine,
    sine,
    doc_col,
    doc_row,
    query_gain,
    key_gain,
    out_gate,
    out_up,
    grad_attn,
    grad_tokens,
    query_gain_grad,
    key_gain_grad,
    branch_tile,
    output_tile,
    grad_tile,
    unit_tile,
    weight_tile,
    attended,
    query_rot,
    key_rot,
    value,
    query_raw,
    key_raw,
    d_attended,
    d_query_norm,
    d_key_norm,
    d_key_sum,
    d_value_sum,
    d_projected,
    own,
    inbox,
    total_buf,
    mixed,
    twin_in,
    pair,
    far_in,
    hidden_tile,
    stage_output,
    stage,
    stat,
    inner,
    ring_send,
    ring_recv,
    stat_send,
    stat_recv,
    twin_send,
    twin_recv,
    far_send,
    far_recv,
    join_send,
    join_recv,
    unit_sem,
    grad_sem,
    branch_sem,
    load_sem,
    weight_sem,
    hidden_sem,
    stage_sem,
    store_sem,
    out_sem,
):
    index, core, right, left, twin, far = neighbours(n)
    count, width = tokens.shape
    half = count // 2
    local = query_raw.shape[1]
    heads = local // HEAD_CHANNELS
    blocks = width // TILE
    chunk = inbox.shape[3]
    grads = (d_gate, d_up)
    part_cols = grad_tile.shape[2]
    parts_in = d_gate.shape[1] // part_cols
    outs = (out_gate, out_up)
    left_side = (((0,), (0,)), ((), ()))
    right_side = (((1,), (1,)), ((), ()))
    factor = 1.0 / math.sqrt(HEAD_CHANNELS)

    def ring(way, unit, step):
        first = head_grads.at[unit, way]
        return pltpu.make_async_remote_copy(
            src_ref=first if step == 1 else inbox.at[step - 2, way, unit],
            dst_ref=inbox.at[step - 1, way, unit],
            send_sem=ring_send.at[way, unit, step - 1],
            recv_sem=ring_recv.at[way, unit, step - 1],
            device_id=left if way else right,
            device_id_type=MESH,
        )

    events = [(step, unit) for step in range(1, n) for unit in range(2)]

    def unit_copy(step, way):
        owner = holder_of(index, (1 + step) * (2 * way - 1), n)
        start = pl.multiple_of(owner * 2 * chunk + way * chunk, chunk)
        return pltpu.make_async_copy(
            hidden_low.at[:, pl.ds(start, chunk)],
            unit_tile.at[step % 2, :, pl.ds(way * chunk, chunk)],
            unit_sem.at[step % 2, way],
        )

    def grad_copy(unit, part, slot):
        cols = pl.ds(pl.multiple_of(part * part_cols, part_cols), part_cols)
        return pltpu.make_async_copy(
            grads[unit].at[:, cols], grad_tile.at[slot], grad_sem.at[slot]
        )

    def grad_block(step, unit):
        if unit == 0:
            for way in range(2):
                unit_copy(step, way).wait()
                if step < n - 1:
                    unit_copy(step + 1, way).start()

        base = 2 * (step - 1) + unit
        final = base == 2 * n - 3

        @pl.loop(0, parts_in)
        def _(part):
            slot = lax.rem(base * parts_in + part, 3)
            spare = lax.rem(slot + 2, 3)
            grad_copy(unit, part, slot).wait()

            @pl.when(part + 2 < parts_in)
            def _():
                grad_copy(unit, part + 2, spare).start()

            if not final:

                @pl.when(part + 2 >= parts_in)
                def _():
                    grad_copy(1 - unit, part + 2 - parts_in, spare).start()

            cols = pl.ds(pl.multiple_of(part * part_cols, part_cols), part_cols)
            block = lax.dot_general(
                unit_tile[step % 2],
                grad_tile[slot],
                left_side,
                preferred_element_type=jnp.float32,
            ).astype(jnp.bfloat16)
            own[unit, 0, :, cols] = block[:chunk]
            own[unit, 1, :, cols] = block[chunk:]

    def out_copy(unit):
        return pltpu.make_async_copy(total_buf, outs[unit], out_sem.at[unit])

    def serve():
        step, unit = events.pop(0)
        if step == n - 1 and unit == 1:
            out_copy(0).wait()
        for way in range(2):
            ring(way, unit, step).wait_recv()

            @pl.loop(0, chunk // 16)
            def _(tile, way=way):
                span = pl.ds(pl.multiple_of(tile * 16, 16), 16)
                total = inbox[step - 1, way, unit, span, :].astype(jnp.float32) + own[
                    unit, way, span, :
                ].astype(jnp.float32)
                if step < n - 1:
                    inbox[step - 1, way, unit, span, :] = total.astype(jnp.bfloat16)
                else:
                    total_buf[way, span, :] = total

            if step < n - 1:
                ring(way, unit, step + 1).start()
        if step < n - 1:
            grad_block(step + 1, unit)
        else:
            out_copy(unit).start()

    greet((right, left, twin, far))
    for unit in range(2):
        for way in range(2):
            ring(way, unit, 1).start()
    for way in range(2):
        unit_copy(1, way).start()
    for part in range(2):
        grad_copy(0, part, part).start()

    def weight_copy(tile, slot):
        return pltpu.make_async_copy(
            attn_full.at[pl.ds(tile * TILE, TILE), pl.ds(0, 3 * local)],
            weight_tile.at[slot],
            weight_sem.at[slot],
        )

    def hidden_copy(tile, slot):
        return pltpu.make_async_copy(
            d_hidden.at[:, pl.ds(tile * TILE, TILE)], hidden_tile.at[slot], hidden_sem.at[slot]
        )

    loads = [
        pltpu.make_async_copy(source, target, load_sem.at[place])
        for place, (source, target) in enumerate(
            (
                (attended_in, attended),
                (query_rot_in, query_rot),
                (key_rot_in, key_rot),
                (value_in, value),
                (query_raw_in, query_raw),
                (key_raw_in, key_raw),
            )
        )
    ]

    def branch_copies(tile, source):
        cols = pl.ds(tile * TILE, TILE)
        slot = tile % 2
        copies = [
            pltpu.make_async_copy(source.at[:, cols], branch_tile.at[slot], branch_sem.at[slot, 0])
        ]
        if source is d_branch:
            copies.append(
                pltpu.make_async_copy(
                    attn_full.at[cols, pl.ds(3 * local, local)],
                    output_tile.at[slot],
                    branch_sem.at[slot, 1],
                )
            )
        return copies

    def output_copy(tile):
        return pltpu.make_async_copy(
            stage_output.at[tile % 2],
            grad_attn.at[pl.ds(tile * TILE, TILE), pl.ds(3 * local, local)],
            stage_sem.at[0, tile % 2],
        )

    for copy in branch_copies(0, d_branch) + loads:
        copy.start()
    grad_block(1, 0)
    grad_block(1, 1)
    loads[0].wait()
    for tile in range(blocks):
        for copy in branch_copies(tile, d_branch):
            copy.wait()
        if tile + 1 < blocks:
            for copy in branch_copies(tile + 1, d_branch):
                copy.start()
        product = jnp.dot(
            branch_tile[tile % 2], output_tile[tile % 2], preferred_element_type=jnp.float32
        )
        if tile == 0:
            d_query_norm[...] = product
        else:
            d_query_norm[...] += product
        if tile >= 2:
            output_copy(tile - 2).wait()
        stage_output[tile % 2] = lax.dot_general(
            branch_tile[tile % 2],
            attended[...],
            left_side,
            preferred_element_type=jnp.float32,
        ).astype(jnp.bfloat16)
        output_copy(tile).start()
    d_attended[...] = d_query_norm[...].astype(jnp.bfloat16)
    branch_copies(0, tokens)[0].start()
    weight_copy(0, 0).start()
    for copy in loads[1:]:
        copy.wait()
    serve()

    def unturned(vectors, span):
        return vectors * cosine[span, :] - pltpu.roll(vectors, HEAD_CHANNELS // 2, 1) * sine[span, :]

    def head_backward(head):
        cols = pl.ds(pl.multiple_of(head * HEAD_CHANNELS, HEAD_CHANNELS), HEAD_CHANNELS)
        lane = lax.broadcasted_iota(jnp.int32, (BLOCK, 128), 1)
        for block in reversed(range(count // BLOCK)):
            span = slice(block * BLOCK, (block + 1) * BLOCK)
            length = (block + 1) * BLOCK
            query = query_rot[span, cols]
            key = key_rot[:length, cols]
            grad = d_attended[span, cols]
            scores = masked_scores(query, key, doc_col, doc_row, block)
            total = jnp.sum(jnp.where(lane == head, totals[span, :], 0.0), axis=1, keepdims=True)
            powers = jnp.exp(scores - total)
            d_powers = lax.dot_general(
                grad, value[:length, cols], right_side, preferred_element_type=jnp.float32
            )
            correction = jnp.sum(d_powers * powers, axis=1, keepdims=True)
            d_scores = (powers * (d_powers - correction)).astype(jnp.bfloat16)
            rounded = powers.astype(jnp.bfloat16)
            d_query = jnp.dot(d_scores, key, preferred_element_type=jnp.float32) * factor
            d_query_norm[span, cols] = unturned(d_query, span)
            d_key = lax.dot_general(
                d_scores, query, left_side, preferred_element_type=jnp.float32
            )
            d_value = lax.dot_general(
                rounded, grad, left_side, preferred_element_type=jnp.float32
            )
            if length == count:
                d_key_sum[...] = d_key
                d_value_sum[...] = d_value
            else:
                d_key_sum[:length, :] += d_key
                d_value_sum[:length, :] += d_value
        d_key_norm[:, cols] = unturned(d_key_sum[...] * factor, slice(None))
        start = pl.multiple_of(2 * local + head * HEAD_CHANNELS, HEAD_CHANNELS)
        d_projected[:, pl.ds(start, HEAD_CHANNELS)] = d_value_sum[...].astype(jnp.bfloat16)

    pl.loop(0, heads // 2)(head_backward)
    serve()
    pl.loop(heads // 2, heads)(head_backward)
    serve()
    parts = []
    for place, (norm, raw, gain, gain_grad) in enumerate(
        (
            (d_query_norm, query_raw, query_gain, query_gain_grad),
            (d_key_norm, key_raw, key_gain, key_gain_grad),
        )
    ):
        dots = jnp.zeros((count, HEAD_CHANNELS), jnp.float32)
        for head in range(heads):
            cols = slice(head * HEAD_CHANNELS, (head + 1) * HEAD_CHANNELS)
            both = norm[:, cols] * raw[:, cols]
            gain_grad[:, cols] = jnp.sum(
                both * inverses[:, place : place + 1], axis=0, keepdims=True
            )
            dots = dots + both * gain[:, cols]
        parts.append(jnp.sum(dots, axis=1, keepdims=True))
    stat[0] = columns_to_rows(parts, count)
    first = exchange(stat.at[0], stat.at[1], stat_send, stat_recv, 0, twin)
    first.start()
    first.wait()
    stat[2] = stat[0] + stat[1]
    second = exchange(stat.at[2], stat.at[3], stat_send, stat_recv, 1, far)
    second.start()
    serve()
    second.wait()
    inner[...] = rows_to_columns(stat[2] + stat[3]) / width

    @pl.loop(0, heads)
    def _(head):
        cols = pl.ds(pl.multiple_of(head * HEAD_CHANNELS, HEAD_CHANNELS), HEAD_CHANNELS)
        for place, (norm, raw, gain) in enumerate(
            ((d_query_norm, query_raw, query_gain), (d_key_norm, key_raw, key_gain))
        ):
            inverse = inverses[:, place : place + 1]
            cube = inverse * inverse * inverse * inner[:, place : place + 1]
            start = pl.multiple_of(place * local + head * HEAD_CHANNELS, HEAD_CHANNELS)
            d_projected[:, pl.ds(start, HEAD_CHANNELS)] = (
                norm[:, cols] * inverse * gain[:, cols] - raw[:, cols] * cube
            ).astype(jnp.bfloat16)

    def twin_copy(tile):
        span = pl.ds(pl.multiple_of((1 - core) * half, half), half)
        return exchange(
            mixed.at[tile % 4, span], twin_in.at[tile % 4], twin_send, twin_recv, tile, twin
        )

    def far_copy(tile):
        return exchange(pair.at[tile], far_in.at[tile], far_send, far_recv, tile, far)

    def token_tile(tile):
        slot = tile % 2
        weight_copy(tile, slot).wait()
        if tile + 1 < blocks:
            weight_copy(tile + 1, 1 - slot).start()
        mixed[tile % 4] = lax.dot_general(
            d_projected[...], weight_tile[slot], right_side, preferred_element_type=jnp.float32
        ).astype(jnp.bfloat16)
        twin_copy(tile).start()

    def add_twin(tile):
        twin_copy(tile).wait_recv()

        @pl.loop(0, half // 32)
        def _(row):
            span = pl.ds(pl.multiple_of(row * 32, 32), 32)
            mine = pl.ds(pl.multiple_of(core * half + row * 32, 32), 32)
            total = mixed[tile % 4, mine, :].astype(jnp.float32) + twin_in[
                tile % 4, span, :
            ].astype(jnp.float32)
            pair[tile, span, :] = total.astype(jnp.bfloat16)

        far_copy(tile).start()
        twin_copy(tile).wait_send()

    def join(tile, kind):
        cols = pl.ds(tile * TILE, TILE)
        if kind == 2:
            return pltpu.make_async_copy(
                pair.at[tile], grad_tokens.at[core, :, cols], store_sem.at[tile]
            )
        target = grad_tokens.at[1 - core if kind else core, :, cols]
        return exchange(
            target if kind else pair.at[tile], target, join_send, join_recv, tile, twin
        )

    def add_far(tile):
        slot = tile % 2
        hidden_copy(tile, slot).wait()
        if tile + 1 < blocks:
            hidden_copy(tile + 1, 1 - slot).start()
        far_copy(tile).wait()

        @pl.loop(0, half // 32)
        def _(row):
            span = pl.ds(pl.multiple_of(row * 32, 32), 32)
            total = (
                pair[tile, span, :].astype(jnp.float32)
                + far_in[tile, span, :].astype(jnp.float32)
                + hidden_tile[slot, span, :]
            )
            pair[tile, span, :] = total.astype(jnp.bfloat16)

        join(tile, 0).start()
        join(tile, 2).start()

    def stage_copy(tile):
        return pltpu.make_async_copy(
            stage.at[tile % 2],
            grad_attn.at[pl.ds(tile * TILE, TILE), pl.ds(0, 3 * local)],
            stage_sem.at[1, tile % 2],
        )

    def weight_grad(tile):
        if tile >= 2:
            stage_copy(tile - 2).wait()
        branch_copies(tile, tokens)[0].wait()
        if tile + 1 < blocks:
            branch_copies(tile + 1, tokens)[0].start()
        stage[tile % 2] = lax.dot_general(
            branch_tile[tile % 2],
            d_projected[...],
            left_side,
            preferred_element_type=jnp.float32,
        ).astype(jnp.bfloat16)
        stage_copy(tile).start()

    hidden_copy(0, 0).start()
    for tile in range(blocks):
        token_tile(tile)
        if tile >= 1:
            add_twin(tile - 1)
        if tile == blocks // 2 - 1:
            serve()
    add_twin(blocks - 1)
    serve()
    for tile in range(blocks):
        weight_grad(tile)
        add_far(tile)
        if tile % 2 == 1:
            serve()
    for tile in (blocks - 2, blocks - 1):
        output_copy(tile).wait()
        stage_copy(tile).wait()
    while events:
        serve()
    out_copy(1).wait()
    for tile in range(blocks):
        join(tile, 1).wait_recv()
        join(tile, 0).wait_send()
        join(tile, 2).wait()
    for step in range(1, n):
        for unit in range(2):
            for way in range(2):
                ring(way, unit, step).wait_send()


def kernel_detach(
    d_branch,
    attn_full,
    attended,
    query_rot,
    key_rot,
    value,
    query_raw,
    key_raw,
    tokens,
    d_hidden,
    head_grads,
    d_gate,
    d_up,
    hidden_low,
    totals,
    inverses,
    cosine,
    sine,
    doc_col,
    doc_ids,
    query_gain,
    key_gain,
    n,
):
    count, width = tokens.shape
    local = query_gain.shape[1]
    units = d_gate.shape[1]
    half = count // 2
    chunk = width // n // 2
    blocks = width // TILE
    low = jnp.bfloat16
    full = jnp.float32
    hbm = pl.BlockSpec(memory_space=pl.ANY)
    vmem = pl.BlockSpec(memory_space=pltpu.VMEM)
    dma = pltpu.SemaphoreType.DMA
    shape = jax.ShapeDtypeStruct
    outs = pl.pallas_call(
        functools.partial(detach_kernel, n),
        out_shape=(
            shape((2, chunk, units), full),
            shape((2, chunk, units), full),
            shape((width, 4 * local), low),
            shape((2, half, width), low),
            shape((1, local), full),
            shape((1, local), full),
        ),
        in_specs=[hbm] * 14 + [vmem] * 8,
        out_specs=(hbm,) * 4 + (vmem,) * 2,
        scratch_shapes=[
            pltpu.VMEM((2, count, TILE), low),
            pltpu.VMEM((2, TILE, local), low),
            pltpu.VMEM((3, count, 2 * TILE), low),
            pltpu.VMEM((2, count, TILE), low),
            pltpu.VMEM((2, TILE, 3 * local), low),
            pltpu.VMEM((count, local), low),
            pltpu.VMEM((count, local), low),
            pltpu.VMEM((count, local), low),
            pltpu.VMEM((count, local), low),
            pltpu.VMEM((count, local), full),
            pltpu.VMEM((count, local), full),
            pltpu.VMEM((count, local), low),
            pltpu.VMEM((count, local), full),
            pltpu.VMEM((count, local), full),
            pltpu.VMEM((count, HEAD_CHANNELS), full),
            pltpu.VMEM((count, HEAD_CHANNELS), full),
            pltpu.VMEM((count, 3 * local), low),
            pltpu.VMEM((2, 2, chunk, units), low),
            pltpu.VMEM((n - 1, 2, 2, chunk, units), low),
            pltpu.VMEM((2, chunk, units), full),
            pltpu.VMEM((4, count, TILE), low),
            pltpu.VMEM((4, half, TILE), low),
            pltpu.VMEM((blocks, half, TILE), low),
            pltpu.VMEM((blocks, half, TILE), low),
            pltpu.VMEM((2, half, TILE), full),
            pltpu.VMEM((2, TILE, local), low),
            pltpu.VMEM((2, TILE, 3 * local), low),
            pltpu.VMEM((4, 8, count), full),
            pltpu.VMEM((count, 128), full),
            dma((2, 2, n - 1)),
            dma((2, 2, n - 1)),
            dma((2,)),
            dma((2,)),
            dma((blocks,)),
            dma((blocks,)),
            dma((blocks,)),
            dma((blocks,)),
            dma((blocks,)),
            dma((blocks,)),
            dma((2, 2)),
            dma((3,)),
            dma((2, 2)),
            dma((6,)),
            dma((2,)),
            dma((2,)),
            dma((2, 2)),
            dma((blocks,)),
            dma((2,)),
        ],
        compiler_params=pltpu.CompilerParams(
            collective_id=5, has_side_effects=True, vmem_limit_bytes=60 * 2**20
        ),
    )(
        d_branch,
        attn_full,
        attended,
        query_rot,
        key_rot,
        value,
        query_raw,
        key_raw,
        tokens,
        d_hidden,
        head_grads,
        d_gate,
        d_up,
        hidden_low,
        totals,
        inverses,
        cosine,
        sine,
        doc_col,
        doc_ids.reshape(1, count),
        query_gain,
        key_gain,
    )
    return (
        outs[0].reshape(2 * chunk, units),
        outs[1].reshape(2 * chunk, units),
        outs[2],
        outs[3].reshape(count, width),
        outs[4],
        outs[5],
    )


def fused_layer(
    n,
    tokens,
    doc_ids,
    q_weight,
    k_weight,
    v_weight,
    o_weight,
    q_gain,
    k_gain,
    attn_gain,
    gate_weight,
    up_weight,
    down_weight,
    mlp_gain,
    cotangent,
):
    index = lax.axis_index("dp")
    heads, channels = q_gain.shape
    small = jnp.concatenate(
        [
            q_gain,
            k_gain,
            jnp.zeros((SMALL - 2 * heads, channels), q_gain.dtype),
        ],
        axis=0,
    )
    small = lax.dynamic_update_slice(
        jnp.zeros((SMALL, HEAD_CHANNELS), q_gain.dtype), small, (0, index * channels)
    )
    small = lax.dynamic_update_slice(
        small, jnp.concatenate([attn_gain, mlp_gain]).reshape(4, 128), (2 * heads, 0)
    )
    frequency = jnp.exp(
        jnp.arange(HEAD_CHANNELS // 2, dtype=jnp.float32)
        * (-2.0 * math.log(ROPE_BASE) / HEAD_CHANNELS)
    )
    frequency = jnp.concatenate([frequency, frequency])[None, :]
    (
        attn_full,
        query_gain,
        key_gain,
        attn_gains,
        mlp_gains,
        cosine,
        sine,
        doc_col,
        down_shard,
    ) = kernel_gather(
        q_weight, k_weight, v_weight, o_weight, small, doc_ids, frequency, down_weight, n
    )
    (
        gate_full,
        up_full,
        query_raw,
        key_raw,
        query_rot,
        key_rot,
        value,
        attended,
        totals,
        inverses,
        branch,
        hidden_state,
        hidden_low,
    ) = kernel_attend(
        tokens,
        attn_full,
        gate_weight,
        up_weight,
        cosine,
        sine,
        doc_col,
        doc_ids,
        query_gain,
        key_gain,
        attn_gains,
        n,
    )
    product, gate_slope, silu, down_full, d_mlp, block_half, mlp_row = kernel_feed(
        hidden_low, gate_full, up_full, down_shard, hidden_state, cotangent, mlp_gains, n
    )
    out_down, d_hidden, d_branch, d_gate, d_up, head_grads, block_out, attn_row = kernel_back(
        d_mlp,
        product,
        down_full,
        gate_slope,
        silu,
        gate_full,
        up_full,
        hidden_low,
        cotangent,
        branch,
        block_half,
        attn_gains,
        n,
    )
    out_gate, out_up, grad_attn, grad_tokens, query_row, key_row = kernel_detach(
        d_branch,
        attn_full,
        attended,
        query_rot,
        key_rot,
        value,
        query_raw,
        key_raw,
        tokens,
        d_hidden,
        head_grads,
        d_gate,
        d_up,
        hidden_low,
        totals,
        inverses,
        cosine,
        sine,
        doc_col,
        doc_ids,
        query_gain,
        key_gain,
        n,
    )
    out_query, out_key, out_value, out_output, summed = kernel_scatter(
        grad_attn, query_row, key_row, attn_row, mlp_row, n
    )
    lanes = lax.dynamic_slice(summed, (0, index * channels), (2 * heads, channels))
    return (
        block_out,
        grad_tokens,
        out_query,
        out_key,
        out_value,
        out_output,
        lanes[:heads],
        lanes[heads:],
        summed[2 * heads : 2 * heads + 2].reshape(-1),
        out_gate,
        out_up,
        out_down.T,
        summed[2 * heads + 2 : 2 * heads + 4].reshape(-1),
    )


def solution(mesh):
    in_specs = (
        P("dp", None),
        P("dp"),
        P("dp", "mp"),
        P("dp", "mp"),
        P("dp", "mp"),
        P("mp", "dp"),
        P("mp", "dp"),
        P("mp", "dp"),
        P("dp"),
        P("dp", "mp"),
        P("dp", "mp"),
        P("mp", "dp"),
        P("dp"),
        P("dp", None),
    )
    out_specs = (
        P("dp", None),
        P("dp", None),
        P("dp", "mp"),
        P("dp", "mp"),
        P("dp", "mp"),
        P("mp", "dp"),
        P("mp", "dp"),
        P("mp", "dp"),
        P("dp"),
        P("dp", "mp"),
        P("dp", "mp"),
        P("mp", "dp"),
        P("dp"),
    )
    n, m = mesh.shape["dp"], mesh.shape["mp"]

    def on_device(*arrays):
        if (n, m, arrays[0].shape[0]) == (RING, 4, SEQ_LEN):
            return fused_layer(n, *arrays)
        return plain_layer(*arrays)

    return jax.shard_map(
        on_device, mesh=mesh, in_specs=in_specs, out_specs=out_specs, check_vma=False
    )
```

```python
import functools
import math

import jax
import jax.numpy as jnp
from jax import lax
from jax.experimental import pallas as pl
from jax.experimental.pallas import tpu as pltpu
from jax.sharding import PartitionSpec as P

D = 2048
HEAD_CHANNELS = 128
SEQ_LEN = 1024
RING = 8


EPSILON = 1e-06
ROPE_BASE = 500000.0
MASKED = -1e30
ROW_LIMIT = 512


def matmul(left_side, right_side):
    return jnp.dot(left_side, right_side, preferred_element_type=jnp.float32)


def transposed_left(left_side, right_side):
    return lax.dot_general(
        left_side, right_side, (((0,), (0,)), ((), ())), preferred_element_type=jnp.float32
    )


def transposed_right(left_side, right_side):
    return lax.dot_general(
        left_side, right_side, (((1,), (1,)), ((), ())), preferred_element_type=jnp.float32
    )


def angles_of(doc_rows, seq_len, head_dim):
    shaped = doc_rows.reshape(-1, seq_len)
    leading = jnp.sum(1 - shaped, axis=1, keepdims=True, dtype=jnp.int32)
    places = jnp.arange(seq_len, dtype=jnp.int32)[None, :] - shaped * leading
    frequency = jnp.exp(
        jnp.arange(head_dim // 2, dtype=jnp.float32) * (-2.0 * math.log(ROPE_BASE) / head_dim)
    )
    return places.reshape(-1).astype(jnp.float32)[:, None] * frequency[None, :]


def rotate(vectors, angles):
    halfway = vectors.shape[-1] // 2
    cosine = jnp.cos(angles)[:, None, :]
    sine_wave = jnp.sin(angles)[:, None, :]
    former = vectors[..., :halfway]
    latter = vectors[..., halfway:]
    return jnp.concatenate(
        [former * cosine - latter * sine_wave, latter * cosine + former * sine_wave], axis=-1
    )


def rotate_back(vectors, angles):
    halfway = vectors.shape[-1] // 2
    cosine = jnp.cos(angles)[:, None, :]
    sine_wave = jnp.sin(angles)[:, None, :]
    former = vectors[..., :halfway]
    latter = vectors[..., halfway:]
    return jnp.concatenate(
        [former * cosine + latter * sine_wave, latter * cosine - former * sine_wave], axis=-1
    )


def block_scores(query_block, key_seq, doc_seq, offset):
    factor = 1.0 / math.sqrt(query_block.shape[-1])
    scores = (
        jnp.einsum("qhd,khd->hqk", query_block, key_seq, preferred_element_type=jnp.float32)
        * factor
    )
    row_places = offset + jnp.arange(query_block.shape[0], dtype=jnp.int32)
    key_places = jnp.arange(key_seq.shape[0], dtype=jnp.int32)
    row_docs = doc_seq[offset : offset + query_block.shape[0]]
    allowed = (key_places[None, :] <= row_places[:, None]) & (doc_seq[None, :] == row_docs[:, None])
    return jnp.where(allowed[None], scores, MASKED)


def attend_sequence(inputs):
    query_seq, key_seq, value_seq, doc_seq = inputs
    row_block = math.gcd(query_seq.shape[0], ROW_LIMIT)
    outputs = []
    totals = []
    for offset in range(0, query_seq.shape[0], row_block):
        scores = block_scores(query_seq[offset : offset + row_block], key_seq, doc_seq, offset)
        maximum = jnp.max(scores, axis=-1, keepdims=True)
        weights = jnp.exp(scores - maximum)
        denominator = jnp.sum(weights, axis=-1, keepdims=True)
        rounded = (weights / denominator).astype(jnp.bfloat16)
        outputs.append(
            jnp.einsum(
                "hqk,khd->qhd", rounded, value_seq, preferred_element_type=jnp.float32
            ).astype(jnp.bfloat16)
        )
        totals.append((maximum + jnp.log(denominator))[..., 0])
    return (jnp.concatenate(outputs, axis=0), jnp.concatenate(totals, axis=1))


def attend_backward(inputs):
    query_seq, key_seq, value_seq, doc_seq, grad_seq, lse_seq = inputs
    row_block = math.gcd(query_seq.shape[0], ROW_LIMIT)
    factor = 1.0 / math.sqrt(query_seq.shape[-1])
    grad_keys = jnp.zeros(key_seq.shape, jnp.float32)
    grad_values = jnp.zeros(value_seq.shape, jnp.float32)
    grad_rows = []
    for offset in range(0, query_seq.shape[0], row_block):
        query_block = query_seq[offset : offset + row_block]
        grad_block = grad_seq[offset : offset + row_block]
        scores = block_scores(query_block, key_seq, doc_seq, offset)
        weights = jnp.exp(scores - lse_seq[:, offset : offset + row_block, None])
        d_weights = jnp.einsum(
            "qhd,khd->hqk", grad_block, value_seq, preferred_element_type=jnp.float32
        )
        correction = jnp.sum(d_weights * weights, axis=-1, keepdims=True)
        d_scores = (weights * (d_weights - correction)).astype(jnp.bfloat16)
        grad_rows.append(
            jnp.einsum("hqk,khd->qhd", d_scores, key_seq, preferred_element_type=jnp.float32)
            * factor
        )
        grad_keys = (
            grad_keys
            + jnp.einsum("hqk,qhd->khd", d_scores, query_block, preferred_element_type=jnp.float32)
            * factor
        )
        grad_values = grad_values + jnp.einsum(
            "hqk,qhd->khd",
            weights.astype(jnp.bfloat16),
            grad_block,
            preferred_element_type=jnp.float32,
        )
    return (jnp.concatenate(grad_rows, axis=0), grad_keys, grad_values)


def plain_layer(
    tokens,
    doc_ids,
    q_weight,
    k_weight,
    v_weight,
    o_weight,
    q_gain,
    k_gain,
    attn_gain,
    gate_weight,
    up_weight,
    down_weight,
    mlp_gain,
    cotangent,
):
    query_full, key_complete, value_full, output_full, query_gains, key_gains, attn_gains = (
        lax.all_gather(q_weight, "dp", axis=0, tiled=True),
        lax.all_gather(k_weight, "dp", axis=0, tiled=True),
        lax.all_gather(v_weight, "dp", axis=0, tiled=True),
        lax.all_gather(o_weight, "dp", axis=1, tiled=True),
        lax.all_gather(q_gain, "dp", axis=1, tiled=True),
        lax.all_gather(k_gain, "dp", axis=1, tiled=True),
        lax.all_gather(attn_gain, "dp", axis=0, tiled=True),
    )
    gate_full, up_full, down_full, mlp_gains = (
        lax.all_gather(gate_weight, "dp", axis=0, tiled=True),
        lax.all_gather(up_weight, "dp", axis=0, tiled=True),
        lax.all_gather(down_weight, "dp", axis=1, tiled=True),
        lax.all_gather(mlp_gain, "dp", axis=0, tiled=True),
    )
    row_count = tokens.shape[0]
    heads_on_device = q_gain.shape[0]
    local_width = heads_on_device * HEAD_CHANNELS
    sequences = row_count // SEQ_LEN
    seq_shape = (sequences, SEQ_LEN, heads_on_device, HEAD_CHANNELS)
    angles = angles_of(doc_ids, SEQ_LEN, HEAD_CHANNELS)
    doc_seqs = doc_ids.reshape(sequences, SEQ_LEN)
    query_raw = matmul(tokens, query_full)
    key_unnormed = matmul(tokens, key_complete)
    values = matmul(tokens, value_full).astype(jnp.bfloat16)
    query_sq, key_sq = lax.psum(
        (jnp.sum(query_raw * query_raw, axis=1), jnp.sum(key_unnormed * key_unnormed, axis=1)), "mp"
    )
    query_inv = lax.rsqrt(query_sq / D + EPSILON)[:, None]
    key_inverse_norm = lax.rsqrt(key_sq / D + EPSILON)[:, None]
    query_scale = query_gains.reshape(-1)
    key_scale = key_gains.reshape(-1)
    query_rot = rotate(
        (query_raw * query_inv * query_scale).reshape(row_count, heads_on_device, HEAD_CHANNELS),
        angles,
    ).astype(jnp.bfloat16)
    key_rot = rotate(
        (key_unnormed * key_inverse_norm * key_scale).reshape(
            row_count, heads_on_device, HEAD_CHANNELS
        ),
        angles,
    ).astype(jnp.bfloat16)
    query_seqs = query_rot.reshape(seq_shape)
    key_seqs = key_rot.reshape(seq_shape)
    value_seqs = values.reshape(seq_shape)
    attended, lse_all = lax.map(attend_sequence, (query_seqs, key_seqs, value_seqs, doc_seqs))
    attended = attended.reshape(row_count, local_width)
    branch = lax.psum(matmul(attended, output_full), "mp")
    branch_inv = lax.rsqrt(jnp.mean(branch * branch, axis=1, keepdims=True) + EPSILON)
    hidden_state = tokens.astype(jnp.float32) + branch * branch_inv * attn_gains
    hidden_low = hidden_state.astype(jnp.bfloat16)
    gate_act = matmul(hidden_low, gate_full)
    up_part = matmul(hidden_low, up_full)
    product = (jax.nn.silu(gate_act) * up_part).astype(jnp.bfloat16)
    mlp_branch = lax.psum(matmul(product, down_full).astype(jnp.bfloat16), "mp").astype(jnp.float32)
    mlp_inv = lax.rsqrt(jnp.mean(mlp_branch * mlp_branch, axis=1, keepdims=True) + EPSILON)
    block_out = (hidden_state + mlp_branch * mlp_inv * mlp_gains).astype(jnp.bfloat16)
    gate_full, up_full, down_full, mlp_gains = (
        lax.all_gather(gate_weight, "dp", axis=0, tiled=True),
        lax.all_gather(up_weight, "dp", axis=0, tiled=True),
        lax.all_gather(down_weight, "dp", axis=1, tiled=True),
        lax.all_gather(mlp_gain, "dp", axis=0, tiled=True),
    )
    upstream = cotangent.astype(jnp.float32)
    grad_mlp_scale = jnp.sum(upstream * mlp_branch * mlp_inv, axis=0)
    mlp_scaled = mlp_gains * upstream
    mlp_cube = mlp_inv * mlp_inv * mlp_inv
    d_mlp = (
        mlp_inv * mlp_scaled
        - mlp_branch * mlp_cube * jnp.mean(mlp_scaled * mlp_branch, axis=1, keepdims=True)
    ).astype(jnp.bfloat16)
    grad_down = transposed_left(product, d_mlp)
    d_product = transposed_right(d_mlp, down_full)
    sigmoid = jax.nn.sigmoid(gate_act)
    d_gate = (d_product * up_part * sigmoid * (1.0 + gate_act * (1.0 - sigmoid))).astype(
        jnp.bfloat16
    )
    d_up = (d_product * gate_act * sigmoid).astype(jnp.bfloat16)
    grad_gate = transposed_left(hidden_low, d_gate)
    grad_up = transposed_left(hidden_low, d_up)
    mlp_input = transposed_right(d_gate, gate_full) + transposed_right(d_up, up_full)
    d_hidden = upstream + lax.psum(mlp_input.astype(jnp.bfloat16), "mp").astype(jnp.float32)
    mlp_grads = (
        lax.psum_scatter(
            grad_gate.astype(jnp.bfloat16), "dp", scatter_dimension=0, tiled=True
        ).astype(jnp.float32),
        lax.psum_scatter(
            grad_up.astype(jnp.bfloat16), "dp", scatter_dimension=0, tiled=True
        ).astype(jnp.float32),
        lax.psum_scatter(
            grad_down.astype(jnp.bfloat16), "dp", scatter_dimension=1, tiled=True
        ).astype(jnp.float32),
        lax.psum_scatter(
            grad_mlp_scale.astype(jnp.bfloat16), "dp", scatter_dimension=0, tiled=True
        ).astype(jnp.float32),
    )
    query_full, key_complete, value_full, output_full, query_gains, key_gains, attn_gains = (
        lax.all_gather(q_weight, "dp", axis=0, tiled=True),
        lax.all_gather(k_weight, "dp", axis=0, tiled=True),
        lax.all_gather(v_weight, "dp", axis=0, tiled=True),
        lax.all_gather(o_weight, "dp", axis=1, tiled=True),
        lax.all_gather(q_gain, "dp", axis=1, tiled=True),
        lax.all_gather(k_gain, "dp", axis=1, tiled=True),
        lax.all_gather(attn_gain, "dp", axis=0, tiled=True),
    )
    query_scale = query_gains.reshape(-1)
    key_scale = key_gains.reshape(-1)
    grad_attn_scale = jnp.sum(d_hidden * branch * branch_inv, axis=0)
    attn_scaled = attn_gains * d_hidden
    branch_cube = branch_inv * branch_inv * branch_inv
    d_branch = (
        branch_inv * attn_scaled
        - branch * branch_cube * jnp.mean(attn_scaled * branch, axis=1, keepdims=True)
    ).astype(jnp.bfloat16)
    grad_output = transposed_left(attended, d_branch)
    d_attended = transposed_right(d_branch, output_full).astype(jnp.bfloat16)
    grad_qrot, grad_krot, grad_vals = lax.map(
        attend_backward,
        (query_seqs, key_seqs, value_seqs, doc_seqs, d_attended.reshape(seq_shape), lse_all),
    )
    d_values = grad_vals.reshape(row_count, local_width).astype(jnp.bfloat16)
    d_qnorm = rotate_back(
        grad_qrot.reshape(row_count, heads_on_device, HEAD_CHANNELS), angles
    ).reshape(row_count, local_width)
    grad_key_normed = rotate_back(
        grad_krot.reshape(row_count, heads_on_device, HEAD_CHANNELS), angles
    ).reshape(row_count, local_width)
    grad_qscale = jnp.sum(d_qnorm * query_raw * query_inv, axis=0).reshape(
        heads_on_device, HEAD_CHANNELS
    )
    grad_key_rms_factor = jnp.sum(
        grad_key_normed * key_unnormed * key_inverse_norm, axis=0
    ).reshape(heads_on_device, HEAD_CHANNELS)
    query_scaled = query_scale * d_qnorm
    key_scaled = key_scale * grad_key_normed
    query_inner, key_inner = lax.psum(
        (jnp.sum(query_scaled * query_raw, axis=1), jnp.sum(key_scaled * key_unnormed, axis=1)),
        "mp",
    )
    query_cube = query_inv * query_inv * query_inv
    key_cube = key_inverse_norm * key_inverse_norm * key_inverse_norm
    d_query = (
        query_inv * query_scaled - query_raw * query_cube * (query_inner / D)[:, None]
    ).astype(jnp.bfloat16)
    d_key = (
        key_inverse_norm * key_scaled - key_unnormed * key_cube * (key_inner / D)[:, None]
    ).astype(jnp.bfloat16)
    grad_query = transposed_left(tokens, d_query)
    grad_key = transposed_left(tokens, d_key)
    grad_value = transposed_left(tokens, d_values)
    token_back = (
        transposed_right(d_query, query_full)
        + transposed_right(d_key, key_complete)
        + transposed_right(d_values, value_full)
    )
    grad_tokens = (
        d_hidden + lax.psum(token_back.astype(jnp.bfloat16), "mp").astype(jnp.float32)
    ).astype(jnp.bfloat16)
    attn_grads = (
        lax.psum_scatter(
            grad_query.astype(jnp.bfloat16), "dp", scatter_dimension=0, tiled=True
        ).astype(jnp.float32),
        lax.psum_scatter(
            grad_key.astype(jnp.bfloat16), "dp", scatter_dimension=0, tiled=True
        ).astype(jnp.float32),
        lax.psum_scatter(
            grad_value.astype(jnp.bfloat16), "dp", scatter_dimension=0, tiled=True
        ).astype(jnp.float32),
        lax.psum_scatter(
            grad_output.astype(jnp.bfloat16), "dp", scatter_dimension=1, tiled=True
        ).astype(jnp.float32),
        lax.psum_scatter(
            grad_qscale.astype(jnp.bfloat16), "dp", scatter_dimension=1, tiled=True
        ).astype(jnp.float32),
        lax.psum_scatter(
            grad_key_rms_factor.astype(jnp.bfloat16), "dp", scatter_dimension=1, tiled=True
        ).astype(jnp.float32),
        lax.psum_scatter(
            grad_attn_scale.astype(jnp.bfloat16), "dp", scatter_dimension=0, tiled=True
        ).astype(jnp.float32),
    )
    return (
        block_out,
        grad_tokens,
        attn_grads[0],
        attn_grads[1],
        attn_grads[2],
        attn_grads[3],
        attn_grads[4],
        attn_grads[5],
        attn_grads[6],
        mlp_grads[0],
        mlp_grads[1],
        mlp_grads[2],
        mlp_grads[3],
    )


MESH = pl.DeviceIdType.MESH
SUBS = 2
TILE = 256
BLOCK = 256
SMALL = 16


def place_of(index, n):
    odd = lax.rem(index, 2)
    half = lax.div(index, 2)
    return (1 - odd) * half + odd * (n - 1 - half)


def device_at(place, n):
    late = lax.div(place, n // 2)
    return (1 - late) * (2 * place) + late * (2 * (n - 1 - place) + 1)


def holder_of(index, steps, n):
    return device_at(lax.rem(place_of(index, n) + (steps + 2 * n), n), n)


def neighbours(n):
    index = lax.axis_index("dp")
    rank = lax.axis_index("mp")
    core = lax.rem(rank, 2)
    right = {"dp": holder_of(index, 1, n)}
    left = {"dp": holder_of(index, -1, n)}
    twin = {"mp": rank + 1 - 2 * core}
    far = {"mp": lax.rem(rank + 2, 4)}
    return index, core, right, left, twin, far


def greet(targets):
    barrier = pltpu.get_barrier_semaphore()
    for target in targets:
        pl.semaphore_signal(barrier, inc=1, device_id=target, device_id_type=MESH)
    pl.semaphore_wait(barrier, len(targets))


def exchange(source, target, send, recv, slot, device):
    return pltpu.make_async_remote_copy(
        src_ref=source,
        dst_ref=target,
        send_sem=send.at[slot],
        recv_sem=recv.at[slot],
        device_id=device,
        device_id_type=MESH,
    )


def columns_to_rows(pieces, count):
    lane = lax.broadcasted_iota(jnp.int32, (count, 128), 1)
    spread = jnp.zeros((count, 128), jnp.float32)
    for place, piece in enumerate(pieces):
        spread = jnp.where(lane == place, piece, spread)
    return spread.T[:8]


def rows_to_columns(rows):
    padded = jnp.concatenate([rows] + [jnp.zeros_like(rows)] * 15, axis=0)
    return padded.T


def gather_kernel(
    n,
    query,
    key,
    value,
    output,
    small,
    doc_row,
    frequency,
    down,
    full,
    query_gain,
    key_gain,
    attn_gain,
    mlp_gain,
    cosine,
    sine,
    doc_col,
    down_shard,
    mine,
    turned_output,
    down_buf,
    turned_down,
    small_full,
    send,
    recv,
    small_send,
    small_recv,
    load,
    store,
):
    index, core, right, left, twin, far = neighbours(n)
    chunk = query.shape[1]
    local = query.shape[2]
    rows = chunk // SUBS
    count = cosine.shape[0]
    heads = local // HEAD_CHANNELS
    units = down.shape[0]

    loads = [
        pltpu.make_async_copy(
            source, mine.at[:, :, pl.ds(place * local, local)], load.at[place]
        )
        for place, source in enumerate((query, key, value, turned_output))
    ]
    for copy in loads[:3]:
        copy.start()
    flipped = output[...].T
    turned_output[0] = flipped[:chunk]
    turned_output[1] = flipped[chunk:]
    loads[3].start()

    def hop(way, sub, step, incoming):
        owner = holder_of(index, (step - 1 + incoming) * (2 * way - 1), n)
        span = pl.ds(sub * rows, rows)
        target = full.at[owner, way, span]
        return pltpu.make_async_remote_copy(
            src_ref=mine.at[way, span] if step == 1 and not incoming else target,
            dst_ref=target,
            send_sem=send.at[way, sub, step - 1],
            recv_sem=recv.at[way, sub, step - 1],
            device_id=left if way else right,
            device_id_type=MESH,
        )

    def small_hop(step, incoming):
        target = small_full.at[holder_of(index, 1 - incoming - step, n)]
        source = small if step == 1 and not incoming else target
        return exchange(source, target, small_send, small_recv, step - 1, right)

    greet((right, left))
    small_hop(1, 0).start()
    for copy in loads:
        copy.wait()
    for sub in range(SUBS):
        for way in range(2):
            hop(way, sub, 1, 0).start()
    own = pltpu.make_async_copy(mine, full.at[index], store.at[0])
    own.start()
    down_load = pltpu.make_async_copy(down, down_buf, store.at[1])
    down_load.start()
    small_full[index] = small[...]
    docs = doc_row[...].astype(jnp.float32)
    leading = jnp.sum(1.0 - docs, axis=1, keepdims=True)
    doc_col[...] = rows_to_columns(jnp.broadcast_to(docs, (8, count)))

    def table(tile):
        span = pl.ds(pl.multiple_of(tile * 64, 64), 64)
        spot = lax.broadcasted_iota(jnp.int32, (64, HEAD_CHANNELS), 0) + tile * 64
        lane = lax.broadcasted_iota(jnp.int32, (64, HEAD_CHANNELS), 1)
        angles = (spot.astype(jnp.float32) - doc_col[span, 0:1] * leading) * frequency[...]
        cosine[span, :] = jnp.cos(angles)
        wave = jnp.sin(angles)
        sine[span, :] = jnp.where(lane < HEAD_CHANNELS // 2, -wave, wave)

    tiles = count // 64
    for step in range(1, n):
        for sub in range(SUBS):
            for way in range(2):
                hop(way, sub, step, 1).wait_recv()
                if step < n - 1:
                    hop(way, sub, step + 1, 0).start()
        small_hop(step, 1).wait_recv()
        if step < n - 1:
            small_hop(step + 1, 0).start()
        if step <= 4:
            pl.loop((step - 1) * tiles // 4, step * tiles // 4)(table)
        if step == 5:
            down_load.wait()
            for part in range(4):
                span = slice(part * (units // 4), (part + 1) * (units // 4))
                flipped = down_buf[span, :].T
                turned_down[0, :, span] = flipped[:chunk]
                turned_down[1, :, span] = flipped[chunk:]
            down_store = pltpu.make_async_copy(turned_down, down_shard, store.at[2])
            down_store.start()
    lanes = jnp.zeros(small.shape, jnp.float32)
    for owner in range(n):
        part = small_full[owner].astype(jnp.float32)
        lanes = lanes + part
        for row in range(2):
            spot = (2 * owner + row) * 128
            attn_gain[:, spot : spot + 128] = part[8 + row : 9 + row]
            mlp_gain[:, spot : spot + 128] = part[10 + row : 11 + row]
    for head in range(heads):
        spot = head * HEAD_CHANNELS
        query_gain[:, spot : spot + HEAD_CHANNELS] = lanes[head : head + 1]
        key_gain[:, spot : spot + HEAD_CHANNELS] = lanes[4 + head : 5 + head]
    own.wait()
    down_store.wait()
    for step in range(1, n):
        for sub in range(SUBS):
            for way in range(2):
                hop(way, sub, step, 0).wait_send()
        small_hop(step, 0).wait_send()


def kernel_gather(query, key, value, output, small, doc_ids, frequency, down, n):
    rows, local = query.shape
    chunk = rows // 2
    count = doc_ids.shape[0]
    units = down.shape[0]
    low = query.dtype
    full = jnp.float32
    hbm = pl.BlockSpec(memory_space=pl.ANY)
    vmem = pl.BlockSpec(memory_space=pltpu.VMEM)
    dma = pltpu.SemaphoreType.DMA
    shape = jax.ShapeDtypeStruct
    split = [part.reshape(2, chunk, local) for part in (query, key, value)]
    outs = pl.pallas_call(
        functools.partial(gather_kernel, n),
        out_shape=(
            shape((n, 2, chunk, 4 * local), low),
            shape((1, local), full),
            shape((1, local), full),
            shape((1, n * rows), full),
            shape((1, n * rows), full),
            shape((count, HEAD_CHANNELS), full),
            shape((count, HEAD_CHANNELS), full),
            shape((count, 128), full),
            shape((2, chunk, units), low),
        ),
        in_specs=[hbm] * 3 + [vmem] * 4 + [hbm],
        out_specs=(hbm,) + (vmem,) * 7 + (hbm,),
        scratch_shapes=[
            pltpu.VMEM((2, chunk, 4 * local), low),
            pltpu.VMEM((2, chunk, local), low),
            pltpu.VMEM((units, rows), low),
            pltpu.VMEM((2, chunk, units), low),
            pltpu.VMEM((n, SMALL, 128), low),
            dma((2, SUBS, n - 1)),
            dma((2, SUBS, n - 1)),
            dma((n - 1,)),
            dma((n - 1,)),
            dma((4,)),
            dma((3,)),
        ],
        compiler_params=pltpu.CompilerParams(
            collective_id=0, has_side_effects=True, vmem_limit_bytes=60 * 2**20
        ),
    )(*split, output, small, doc_ids.reshape(1, count), frequency, down)
    return outs[0].reshape(n * rows, 4 * local), *outs[1:]


def scatter_kernel(
    n,
    grads,
    query_row,
    key_row,
    attn_row,
    mlp_row,
    out_query,
    out_key,
    out_value,
    out_output,
    small_out,
    own,
    inbox,
    tail,
    parts,
    small_inbox,
    small_outbox,
    send,
    recv,
    small_send,
    small_recv,
    own_sem,
):
    index, core, right, left, twin, far = neighbours(n)
    chunk = out_query.shape[1]
    local = out_query.shape[2]
    rows = chunk // SUBS
    heads = local // HEAD_CHANNELS

    def hop(way, sub, step):
        first = grads.at[holder_of(index, 2 * way - 1, n), way, pl.ds(sub * rows, rows)]
        return pltpu.make_async_remote_copy(
            src_ref=first if step == 1 else inbox.at[step - 2, way, sub],
            dst_ref=inbox.at[step - 1, way, sub],
            send_sem=send.at[way, sub, step - 1],
            recv_sem=recv.at[way, sub, step - 1],
            device_id=left if way else right,
            device_id_type=MESH,
        )

    def own_copy(way, sub, step):
        owner = holder_of(index, (1 + step) * (2 * way - 1), n)
        return pltpu.make_async_copy(
            grads.at[owner, way, pl.ds(sub * rows, rows)],
            own.at[way, sub],
            own_sem.at[way, sub],
        )

    def small_hop(step):
        first = parts.at[holder_of(index, -1, n)]
        return exchange(
            first if step == 1 else small_outbox.at[step - 2],
            small_inbox.at[step - 1],
            small_send,
            small_recv,
            step - 1,
            twin if step == n else right,
        )

    greet((right, left, twin))
    for sub in range(SUBS):
        for way in range(2):
            hop(way, sub, 1).start()
            own_copy(way, sub, 1).start()
    for owner in range(n):
        for head in range(heads):
            spot = head * HEAD_CHANNELS
            parts[owner, head : head + 1, :] = query_row[:, spot : spot + HEAD_CHANNELS]
            parts[owner, 4 + head : 5 + head, :] = key_row[:, spot : spot + HEAD_CHANNELS]
        for row in range(2):
            spot = (2 * owner + row) * 128
            parts[owner, 8 + row : 9 + row, :] = attn_row[:, spot : spot + 128]
            parts[owner, 10 + row : 11 + row, :] = mlp_row[:, spot : spot + 128]
        parts[owner, 12:16, :] = jnp.zeros((4, 128), jnp.float32)
    small_hop(1).start()
    for step in range(1, n):
        for sub in range(SUBS):
            for way in range(2):
                own_copy(way, sub, step).wait()
                hop(way, sub, step).wait_recv()

                @pl.loop(0, rows // 16)
                def _(tile, way=way, sub=sub, step=step):
                    near = pl.ds(pl.multiple_of(tile * 16, 16), 16)
                    got = inbox[step - 1, way, sub, near, :]
                    held = own[way, sub, near, :]
                    if step < n - 1:
                        inbox[step - 1, way, sub, near, :] = got + held
                    else:
                        total = got.astype(jnp.float32) + held.astype(jnp.float32)
                        wide = pl.ds(pl.multiple_of(sub * rows + tile * 16, 16), 16)
                        out_query[way, wide, :] = total[:, :local]
                        out_key[way, wide, :] = total[:, local : 2 * local]
                        out_value[way, wide, :] = total[:, 2 * local : 3 * local]
                        deep = pl.ds(
                            pl.multiple_of(way * chunk + sub * rows + tile * 16, 16), 16
                        )
                        tail[deep, :] = total[:, 3 * local :]

                if step < n - 1:
                    hop(way, sub, step + 1).start()
                    own_copy(way, sub, step + 1).start()
        if step < n - 1:
            small_hop(step).wait_recv()
            owner = holder_of(index, -1 - step, n)
            small_outbox[step - 1] = small_inbox[step - 1] + parts[owner]
            small_hop(step + 1).start()
    small_hop(n - 1).wait_recv()
    small_outbox[n - 2] = small_inbox[n - 2] + parts[index]
    small_hop(n).start()
    out_output[...] = tail[...].T
    small_hop(n).wait_recv()
    line = lax.broadcasted_iota(jnp.int32, small_out.shape, 0)
    small_out[...] = small_outbox[n - 2] + jnp.where(line >= 8, small_inbox[n - 1], 0.0)
    for step in range(1, n):
        for sub in range(SUBS):
            for way in range(2):
                hop(way, sub, step).wait_send()
        small_hop(step).wait_send()
    small_hop(n).wait_send()


def kernel_scatter(grads, query_row, key_row, attn_row, mlp_row, n):
    rows, width = grads.shape[0] // n, grads.shape[1]
    chunk, local = rows // 2, width // 4
    deep = chunk // SUBS
    full = jnp.float32
    vmem = pl.BlockSpec(memory_space=pltpu.VMEM)
    dma = pltpu.SemaphoreType.DMA
    shape = jax.ShapeDtypeStruct
    outs = pl.pallas_call(
        functools.partial(scatter_kernel, n),
        out_shape=(shape((2, chunk, local), full),) * 3
        + (shape((local, rows), full), shape((SMALL, 128), full)),
        in_specs=[pl.BlockSpec(memory_space=pl.ANY)] + [vmem] * 4,
        out_specs=(vmem,) * 5,
        scratch_shapes=[
            pltpu.VMEM((2, SUBS, deep, width), grads.dtype),
            pltpu.VMEM((n - 1, 2, SUBS, deep, width), grads.dtype),
            pltpu.VMEM((rows, local), full),
            pltpu.VMEM((n, SMALL, 128), full),
            pltpu.VMEM((n, SMALL, 128), full),
            pltpu.VMEM((n - 1, SMALL, 128), full),
            dma((2, SUBS, n - 1)),
            dma((2, SUBS, n - 1)),
            dma((n,)),
            dma((n,)),
            dma((2, SUBS)),
        ],
        compiler_params=pltpu.CompilerParams(
            collective_id=1, has_side_effects=True, vmem_limit_bytes=60 * 2**20
        ),
    )(grads.reshape(n, 2, chunk, width), query_row, key_row, attn_row, mlp_row)
    return tuple(part.reshape(rows, local) for part in outs[:3]) + outs[3:]


def turned(vectors, cosine, sine):
    return vectors * cosine + pltpu.roll(vectors, HEAD_CHANNELS // 2, 1) * sine


def masked_scores(query, key, doc_col, doc_row, block):
    length = key.shape[0]
    scores = lax.dot_general(
        query, key, (((1,), (1,)), ((), ())), preferred_element_type=jnp.float32
    ) * (1.0 / math.sqrt(HEAD_CHANNELS))
    row = lax.broadcasted_iota(jnp.int32, scores.shape, 0) + block * BLOCK
    col = lax.broadcasted_iota(jnp.int32, scores.shape, 1)
    own = doc_col[block * BLOCK : (block + 1) * BLOCK, 0:1]
    same = own == doc_row[:, :length].astype(jnp.float32)
    return jnp.where((col <= row) & same, scores, MASKED)


def attend_kernel(
    n,
    tokens,
    attn_full,
    gate_shard,
    up_shard,
    cosine,
    sine,
    doc_col,
    doc_row,
    query_gain,
    key_gain,
    attn_gain,
    gate_full,
    up_full,
    query_raw_out,
    key_raw_out,
    query_rot_out,
    key_rot_out,
    value_out,
    attended_out,
    totals,
    inverses,
    branch_out,
    hidden_out,
    hidden_low,
    lhs,
    weights,
    query_raw,
    key_raw,
    query_rot,
    key_rot,
    value,
    attended,
    mixed,
    twin_in,
    pair,
    far_in,
    branch,
    half_buf,
    low_buf,
    stat,
    ring_send,
    ring_recv,
    stat_send,
    stat_recv,
    twin_send,
    twin_recv,
    far_send,
    far_recv,
    join_send,
    join_recv,
    load_sem,
    store_sem,
):
    index, core, right, left, twin, far = neighbours(n)
    count, width = lhs.shape
    half = count // 2
    local = query_raw.shape[1]
    heads = local // HEAD_CHANNELS
    blocks = width // TILE
    shards = (gate_shard, up_shard)
    fulls = (gate_full, up_full)
    right_side = (((1,), (1,)), ((), ()))

    def ring(way, unit, step, incoming):
        owner = holder_of(index, (step - 1 + incoming) * (2 * way - 1), n)
        target = fulls[unit].at[owner, way]
        return pltpu.make_async_remote_copy(
            src_ref=shards[unit].at[way] if step == 1 and not incoming else target,
            dst_ref=target,
            send_sem=ring_send.at[way, unit, step - 1],
            recv_sem=ring_recv.at[way, unit, step - 1],
            device_id=left if way else right,
            device_id_type=MESH,
        )

    events = [(step, unit) for step in range(1, n) for unit in range(2)]

    def serve():
        step, unit = events.pop(0)
        for way in range(2):
            ring(way, unit, step, 1).wait_recv()
            if step < n - 1:
                ring(way, unit, step + 1, 0).start()

    greet((right, left, twin, far))
    for unit in range(2):
        for way in range(2):
            ring(way, unit, 1, 0).start()
    loads = [
        pltpu.make_async_copy(tokens, lhs, load_sem.at[0]),
        pltpu.make_async_copy(attn_full, weights, load_sem.at[1]),
        pltpu.make_async_copy(
            tokens.at[pl.ds(pl.multiple_of(core * half, half), half)], half_buf, load_sem.at[2]
        ),
        pltpu.make_async_copy(gate_shard, gate_full.at[index], load_sem.at[3]),
        pltpu.make_async_copy(up_shard, up_full.at[index], load_sem.at[4]),
    ]
    for copy in loads:
        copy.start()
    loads[0].wait()
    loads[1].wait()

    def project(target, start):
        for tile in range(local // TILE):
            cols = slice(start + tile * TILE, start + (tile + 1) * TILE)
            target[:, tile * TILE : (tile + 1) * TILE] = jnp.dot(
                lhs[...], weights[:, cols], preferred_element_type=jnp.float32
            ).astype(target.dtype)

    project(query_raw, 0)
    project(key_raw, local)
    squares = [
        jnp.sum(raw[...] * raw[...], axis=1, keepdims=True) for raw in (query_raw, key_raw)
    ]
    stat[0] = columns_to_rows(squares, count)
    first = exchange(stat.at[0], stat.at[1], stat_send, stat_recv, 0, twin)
    first.start()
    project(value, 2 * local)
    first.wait()
    stat[2] = stat[0] + stat[1]
    second = exchange(stat.at[2], stat.at[3], stat_send, stat_recv, 1, far)
    second.start()
    serve()
    second.wait()
    inverses[...] = lax.rsqrt(rows_to_columns(stat[2] + stat[3]) / width + EPSILON)

    @pl.loop(0, heads)
    def _(head):
        cols = pl.ds(pl.multiple_of(head * HEAD_CHANNELS, HEAD_CHANNELS), HEAD_CHANNELS)
        for place, (raw, gain, out) in enumerate(
            ((query_raw, query_gain, query_rot), (key_raw, key_gain, key_rot))
        ):
            normed = raw[:, cols] * inverses[:, place : place + 1] * gain[:, cols]
            out[:, cols] = turned(normed, cosine[...], sine[...]).astype(jnp.bfloat16)

    stores = [
        pltpu.make_async_copy(source, target, store_sem.at[place])
        for place, (source, target) in enumerate(
            (
                (query_raw, query_raw_out),
                (key_raw, key_raw_out),
                (query_rot, query_rot_out),
                (key_rot, key_rot_out),
                (value, value_out),
            )
        )
    ]
    for copy in stores:
        copy.start()
    serve()
    totals[...] = jnp.zeros_like(totals)

    @pl.loop(0, heads)
    def _(head):
        cols = pl.ds(pl.multiple_of(head * HEAD_CHANNELS, HEAD_CHANNELS), HEAD_CHANNELS)
        lane = lax.broadcasted_iota(jnp.int32, (BLOCK, 128), 1)
        for block in range(count // BLOCK):
            span = slice(block * BLOCK, (block + 1) * BLOCK)
            length = (block + 1) * BLOCK
            scores = masked_scores(
                query_rot[span, cols], key_rot[:length, cols], doc_col, doc_row, block
            )
            maximum = jnp.max(scores, axis=1, keepdims=True)
            powers = jnp.exp(scores - maximum)
            denominator = jnp.sum(powers, axis=1, keepdims=True)
            rounded = (powers * (1.0 / denominator)).astype(jnp.bfloat16)
            attended[span, cols] = jnp.dot(
                rounded, value[:length, cols], preferred_element_type=jnp.float32
            ).astype(jnp.bfloat16)
            totals[span, :] = jnp.where(
                lane == head, maximum + jnp.log(denominator), totals[span, :]
            )

    stores.append(pltpu.make_async_copy(attended, attended_out, store_sem.at[5]))
    stores[5].start()
    serve()

    def twin_copy(tile):
        span = pl.ds(pl.multiple_of((1 - core) * half, half), half)
        return exchange(
            mixed.at[tile % 4, span], twin_in.at[tile % 4], twin_send, twin_recv, tile, twin
        )

    def far_copy(tile):
        return exchange(pair.at[tile], far_in.at[tile], far_send, far_recv, tile, far)

    def output_tile(tile):
        span = slice(tile * TILE, (tile + 1) * TILE)
        mixed[tile % 4] = lax.dot_general(
            attended[...],
            weights[span, 3 * local :],
            right_side,
            preferred_element_type=jnp.float32,
        ).astype(jnp.bfloat16)
        twin_copy(tile).start()

    def add_twin(tile):
        twin_copy(tile).wait_recv()

        @pl.loop(0, half // 32)
        def _(row):
            span = pl.ds(pl.multiple_of(row * 32, 32), 32)
            mine = pl.ds(pl.multiple_of(core * half + row * 32, 32), 32)
            total = mixed[tile % 4, mine, :].astype(jnp.float32) + twin_in[
                tile % 4, span, :
            ].astype(jnp.float32)
            pair[tile, span, :] = total.astype(jnp.bfloat16)

        far_copy(tile).start()
        twin_copy(tile).wait_send()

    def add_far(tile):
        far_copy(tile).wait_recv()

        @pl.loop(0, half // 32)
        def _(row):
            span = pl.ds(pl.multiple_of(row * 32, 32), 32)
            branch[span, tile * TILE : (tile + 1) * TILE] = pair[tile, span, :].astype(
                jnp.float32
            ) + far_in[tile, span, :].astype(jnp.float32)

    for tile in range(blocks):
        output_tile(tile)
        if tile >= 1:
            add_twin(tile - 1)
    add_twin(blocks - 1)
    serve()
    for tile in range(blocks):
        add_far(tile)
        if tile % 2 == 1:
            serve()
    loads[2].wait()

    def finish(tile):
        span = pl.ds(pl.multiple_of(tile * 16, 16), 16)
        mix = branch[span, :]
        inverse = lax.rsqrt(jnp.sum(mix * mix, axis=1, keepdims=True) / width + EPSILON)
        state = half_buf[span, :].astype(jnp.float32) + mix * inverse * attn_gain[...]
        low_buf[span, :] = state.astype(jnp.bfloat16)
        hidden_out[span, :] = state

    def join(part, kind):
        span = pl.ds(part * (half // 4), half // 4)
        if kind == 2:
            return pltpu.make_async_copy(
                low_buf.at[span], hidden_low.at[core, span], store_sem.at[6 + part]
            )
        target = hidden_low.at[1 - core if kind else core, span]
        return exchange(
            target if kind else low_buf.at[span], target, join_send, join_recv, part, twin
        )

    for part in range(4):
        pl.loop(part * (half // 64), (part + 1) * (half // 64))(finish)
        join(part, 0).start()
        join(part, 2).start()
    stores.append(pltpu.make_async_copy(branch, branch_out, store_sem.at[10]))
    stores[6].start()
    while events:
        serve()
    for part in range(4):
        join(part, 1).wait_recv()
        join(part, 0).wait_send()
        join(part, 2).wait()
    for copy in stores + loads[3:]:
        copy.wait()
    for tile in range(blocks):
        far_copy(tile).wait_send()
    for step in range(1, n):
        for unit in range(2):
            for way in range(2):
                ring(way, unit, step, 0).wait_send()


def kernel_attend(
    tokens,
    attn_full,
    gate_shard,
    up_shard,
    cosine,
    sine,
    doc_col,
    doc_ids,
    query_gain,
    key_gain,
    attn_gain,
    n,
):
    count, width = tokens.shape
    local = query_gain.shape[1]
    units = gate_shard.shape[1]
    half = count // 2
    chunk = width // n // 2
    blocks = width // TILE
    low = jnp.bfloat16
    full = jnp.float32
    hbm = pl.BlockSpec(memory_space=pl.ANY)
    vmem = pl.BlockSpec(memory_space=pltpu.VMEM)
    dma = pltpu.SemaphoreType.DMA
    shape = jax.ShapeDtypeStruct
    outs = pl.pallas_call(
        functools.partial(attend_kernel, n),
        out_shape=(
            shape((n, 2, chunk, units), low),
            shape((n, 2, chunk, units), low),
            shape((count, local), full),
            shape((count, local), full),
            shape((count, local), low),
            shape((count, local), low),
            shape((count, local), low),
            shape((count, local), low),
            shape((count, 128), full),
            shape((count, 128), full),
            shape((half, width), full),
            shape((half, width), full),
            shape((2, half, width), low),
        ),
        in_specs=[hbm] * 4 + [vmem] * 7,
        out_specs=(hbm,) * 8 + (vmem,) * 2 + (hbm, vmem, hbm),
        scratch_shapes=[
            pltpu.VMEM((count, width), low),
            pltpu.VMEM((width, 4 * local), low),
            pltpu.VMEM((count, local), full),
            pltpu.VMEM((count, local), full),
            pltpu.VMEM((count, local), low),
            pltpu.VMEM((count, local), low),
            pltpu.VMEM((count, local), low),
            pltpu.VMEM((count, local), low),
            pltpu.VMEM((4, count, TILE), low),
            pltpu.VMEM((4, half, TILE), low),
            pltpu.VMEM((blocks, half, TILE), low),
            pltpu.VMEM((blocks, half, TILE), low),
            pltpu.VMEM((half, width), full),
            pltpu.VMEM((half, width), low),
            pltpu.VMEM((half, width), low),
            pltpu.VMEM((4, 8, count), full),
            dma((2, 2, n - 1)),
            dma((2, 2, n - 1)),
            dma((2,)),
            dma((2,)),
            dma((blocks,)),
            dma((blocks,)),
            dma((blocks,)),
            dma((blocks,)),
            dma((4,)),
            dma((4,)),
            dma((5,)),
            dma((11,)),
        ],
        compiler_params=pltpu.CompilerParams(
            collective_id=4, has_side_effects=True, vmem_limit_bytes=58 * 2**20
        ),
    )(
        tokens,
        attn_full,
        gate_shard.reshape(2, chunk, units),
        up_shard.reshape(2, chunk, units),
        cosine,
        sine,
        doc_col,
        doc_ids.reshape(1, count),
        query_gain,
        key_gain,
        attn_gain,
    )
    return (
        outs[0].reshape(width, units),
        outs[1].reshape(width, units),
        *outs[2:12],
        outs[12].reshape(count, width),
    )


def feed_kernel(
    n,
    hidden_low,
    gate_full,
    up_full,
    down_shard,
    hidden,
    upstream,
    gains,
    product_out,
    gate_slope,
    silu_out,
    down_full,
    d_mlp,
    block_half,
    gain_grad,
    lhs,
    product,
    held,
    gate_tile,
    up_tile,
    slope_tile,
    silu_tile,
    twin_out,
    twin_in,
    pair,
    far_in,
    branch,
    hidden_buf,
    upstream_buf,
    d_buf,
    block_buf,
    gain_sum,
    ring_send,
    ring_recv,
    twin_send,
    twin_recv,
    far_send,
    far_recv,
    join_send,
    join_recv,
    load_sem,
    tile_sem,
    stage_sem,
    store_sem,
):
    index, core, right, left, twin, far = neighbours(n)
    half = hidden.shape[0]
    chunk = held.shape[2]
    rows = chunk // SUBS
    tiles = product.shape[1] // TILE
    width = branch.shape[1]

    loads = [
        pltpu.make_async_copy(hidden_low, lhs, load_sem.at[0]),
        pltpu.make_async_copy(down_shard, held.at[index], load_sem.at[1]),
        pltpu.make_async_copy(hidden, hidden_buf, load_sem.at[2]),
        pltpu.make_async_copy(
            upstream.at[pl.ds(pl.multiple_of(core * half, half), half)],
            upstream_buf,
            load_sem.at[3],
        ),
    ]

    def weight_copies(tile, slot):
        cols = pl.ds(pl.multiple_of(tile * TILE, TILE), TILE)
        return (
            pltpu.make_async_copy(gate_full.at[:, cols], gate_tile.at[slot], tile_sem.at[slot, 0]),
            pltpu.make_async_copy(up_full.at[:, cols], up_tile.at[slot], tile_sem.at[slot, 1]),
        )

    def stage_copies(tile, slot):
        cols = pl.ds(pl.multiple_of(tile * TILE, TILE), TILE)
        return (
            pltpu.make_async_copy(slope_tile.at[slot], gate_slope.at[:, cols], stage_sem.at[slot, 0]),
            pltpu.make_async_copy(silu_tile.at[slot], silu_out.at[:, cols], stage_sem.at[slot, 1]),
        )

    def ring(way, sub, step, incoming):
        owner = holder_of(index, (step - 1 + incoming) * (2 * way - 1), n)
        span = pl.ds(sub * rows, rows)
        target = held.at[owner, way, span]
        return pltpu.make_async_remote_copy(
            src_ref=down_shard.at[way, span] if step == 1 and not incoming else target,
            dst_ref=target,
            send_sem=ring_send.at[way, sub, step - 1],
            recv_sem=ring_recv.at[way, sub, step - 1],
            device_id=left if way else right,
            device_id_type=MESH,
        )

    def serve(step, sub):
        for way in range(2):
            ring(way, sub, step, 1).wait_recv()
            if step < n - 1:
                ring(way, sub, step + 1, 0).start()

    def columns(sub):
        return pl.ds(0, 2 * chunk) if sub is None else pl.ds(sub * 2 * rows, 2 * rows)

    def twin_copy(step, sub=None):
        return exchange(
            twin_out.at[step, :, columns(sub)],
            twin_in.at[step, :, columns(sub)],
            twin_send,
            twin_recv,
            step + (sub or 0),
            twin,
        )

    def far_copy(step, sub=None):
        return exchange(
            pair.at[step, :, columns(sub)],
            far_in.at[step, :, columns(sub)],
            far_send,
            far_recv,
            step + (sub or 0),
            far,
        )

    greet((right, left, twin, far))
    for sub in range(SUBS):
        for way in range(2):
            ring(way, sub, 1, 0).start()
    for copy in loads:
        copy.start()
    for copy in weight_copies(0, 0):
        copy.start()
    loads[0].wait()

    def feed_tile(tile):
        slot = lax.rem(tile, 2)
        for copy in weight_copies(tile, slot):
            copy.wait()

        @pl.when(tile + 1 < tiles)
        def _():
            for copy in weight_copies(tile + 1, 1 - slot):
                copy.start()

        @pl.when(tile >= 2)
        def _():
            for copy in stage_copies(tile - 2, slot):
                copy.wait()

        cols = pl.ds(pl.multiple_of(tile * TILE, TILE), TILE)

        gate = jnp.dot(lhs[...], gate_tile[slot], preferred_element_type=jnp.float32)
        up = jnp.dot(lhs[...], up_tile[slot], preferred_element_type=jnp.float32)
        sigmoid = jax.nn.sigmoid(gate)
        silu = gate * sigmoid
        product[:, cols] = (silu * up).astype(jnp.bfloat16)
        slope_tile[slot] = (up * sigmoid * (1.0 + gate * (1.0 - sigmoid))).astype(jnp.bfloat16)
        silu_tile[slot] = silu.astype(jnp.bfloat16)

        for copy in stage_copies(tile, slot):
            copy.start()

    events = [(step, sub) for step in range(1, n) for sub in range(SUBS)]
    groups = 4
    for group in range(groups):
        pl.loop(group * tiles // groups, (group + 1) * tiles // groups)(feed_tile)
        serve(*events.pop(0))
    stores = [pltpu.make_async_copy(product, product_out, store_sem.at[0])]
    stores[0].start()
    loads[1].wait()

    def multiply(step, sub=None):
        part = slice(None) if sub is None else slice(sub * rows, (sub + 1) * rows)
        first = held[holder_of(index, -step, n), 0, part]
        second = held[holder_of(index, step, n), 1, part]
        rhs = jnp.concatenate([first, second], axis=0)
        contract = (((1,), (1,)), ((), ()))
        span = pl.ds(pl.multiple_of((1 - core) * half, half), half)
        twin_out[step, :, columns(sub)] = lax.dot_general(
            product[span, :], rhs, contract, preferred_element_type=jnp.float32
        ).astype(jnp.bfloat16)
        twin_copy(step, sub).start()
        span = pl.ds(pl.multiple_of(core * half, half), half)
        pair[step, :, columns(sub)] = lax.dot_general(
            product[span, :], rhs, contract, preferred_element_type=jnp.float32
        ).astype(jnp.bfloat16)

    def add_twin(step, sub=None):
        twin_copy(step, sub).wait_recv()
        cols = columns(sub)

        @pl.loop(0, half // 32)
        def _(tile):
            span = pl.ds(pl.multiple_of(tile * 32, 32), 32)
            total = pair[step, span, cols].astype(jnp.float32) + twin_in[
                step, span, cols
            ].astype(jnp.float32)
            pair[step, span, cols] = total.astype(jnp.bfloat16)

        far_copy(step, sub).start()

    def add_far(step):
        if step < n - 1:
            far_copy(step).wait_recv()
        else:
            for sub in range(SUBS):
                far_copy(step, sub).wait_recv()
        first = pl.multiple_of(holder_of(index, -step, n) * 2 * chunk, chunk)
        second = pl.multiple_of(holder_of(index, step, n) * 2 * chunk + chunk, chunk)

        @pl.loop(0, half // 32)
        def _(tile):
            span = pl.ds(pl.multiple_of(tile * 32, 32), 32)
            total = pair[step, span, :].astype(jnp.float32) + far_in[step, span, :].astype(
                jnp.float32
            )
            if step < n - 1:
                sides = total[:, :chunk], total[:, chunk:]
            else:
                sides = [
                    jnp.concatenate(
                        [
                            total[:, (2 * sub + way) * rows : (2 * sub + way + 1) * rows]
                            for sub in range(SUBS)
                        ],
                        axis=1,
                    )
                    for way in range(2)
                ]
            branch[span, pl.ds(first, chunk)] = sides[0]
            branch[span, pl.ds(second, chunk)] = sides[1]

    def serve_until(step, sub):
        while events and events[0] <= (step, sub):
            serve(*events.pop(0))

    for step in range(n - 1):
        serve_until(step, SUBS - 1)
        multiply(step)
        if step >= 1:
            if step <= 3:
                add_twin(step - 1)
            if step >= 3:
                add_twin(step)
            if step >= 2:
                add_far(step - 2)
        if step < 2 and events:
            serve(*events.pop(0))
    for sub in range(SUBS):
        serve_until(n - 1, sub)
        multiply(n - 1, sub)
        add_twin(n - 1, sub)
        if sub == 0:
            add_far(n - 3)
    stores.append(pltpu.make_async_copy(held, down_full, store_sem.at[1]))
    stores[1].start()
    add_far(n - 2)
    loads[2].wait()
    loads[3].wait()
    gain_sum[...] = jnp.zeros_like(gain_sum)
    add_far(n - 1)

    def finish(tile):
        span = pl.ds(pl.multiple_of(tile * 16, 16), 16)
        mixed = branch[span, :]
        scale = gains[...]
        inverse = lax.rsqrt(jnp.sum(mixed * mixed, axis=1, keepdims=True) / width + EPSILON)
        grad = upstream_buf[span, :].astype(jnp.float32)
        scaled = scale * grad
        mean = jnp.sum(scaled * mixed, axis=1, keepdims=True) / width
        normed = mixed * inverse
        d_buf[span, :] = (
            inverse * scaled - mixed * (inverse * inverse * inverse * mean)
        ).astype(jnp.bfloat16)
        block_buf[span, :] = (hidden_buf[span, :] + normed * scale).astype(jnp.bfloat16)
        terms = grad * normed
        gain_sum[...] += terms[:8] + terms[8:]

    def join(part, own):
        span = pl.ds(part * (half // 4), half // 4)
        if own:
            return pltpu.make_async_copy(d_buf.at[span], d_mlp.at[core, span], store_sem.at[3 + part])
        return pltpu.make_async_remote_copy(
            src_ref=d_buf.at[span],
            dst_ref=d_mlp.at[core, span],
            send_sem=join_send.at[part],
            recv_sem=join_recv.at[part],
            device_id=twin,
            device_id_type=MESH,
        )

    def joined(part):
        span = pl.ds(part * (half // 4), half // 4)
        target = d_mlp.at[1 - core, span]
        return pltpu.make_async_remote_copy(
            src_ref=target,
            dst_ref=target,
            send_sem=join_send.at[part],
            recv_sem=join_recv.at[part],
            device_id=twin,
            device_id_type=MESH,
        )

    for part in range(4):
        pl.loop(part * (half // 64), (part + 1) * (half // 64))(finish)
        join(part, False).start()
        join(part, True).start()
    stores.append(pltpu.make_async_copy(block_buf, block_half, store_sem.at[2]))
    stores[2].start()
    gain_grad[...] = jnp.sum(gain_sum[...], axis=0, keepdims=True)
    for part in range(4):
        joined(part).wait_recv()
        join(part, False).wait_send()
        join(part, True).wait()
    for copy in stores:
        copy.wait()
    for tile in (tiles - 2, tiles - 1):
        for copy in stage_copies(tile, tile % 2):
            copy.wait()
    for step in range(n + 1):
        name = (step, None) if step < n - 1 else (n - 1, step - n + 1)
        twin_copy(*name).wait_send()
        far_copy(*name).wait_send()
    for step in range(1, n):
        for sub in range(SUBS):
            for way in range(2):
                ring(way, sub, step, 0).wait_send()


def kernel_feed(hidden_low, gate_full, up_full, down_shard, hidden, upstream, gains, n):
    count, width = hidden_low.shape
    units = gate_full.shape[1]
    half = count // 2
    chunk = width // n // 2
    rows = chunk // SUBS
    low = jnp.bfloat16
    hbm = pl.BlockSpec(memory_space=pl.ANY)
    vmem = pl.BlockSpec(memory_space=pltpu.VMEM)
    dma = pltpu.SemaphoreType.DMA
    product, slope, silu, down_full, d_mlp, block, gain_grad = pl.pallas_call(
        functools.partial(feed_kernel, n),
        out_shape=(
            jax.ShapeDtypeStruct((count, units), low),
            jax.ShapeDtypeStruct((count, units), low),
            jax.ShapeDtypeStruct((count, units), low),
            jax.ShapeDtypeStruct((n, 2, chunk, units), low),
            jax.ShapeDtypeStruct((2, half, width), low),
            jax.ShapeDtypeStruct((half, width), low),
            jax.ShapeDtypeStruct((1, width), jnp.float32),
        ),
        in_specs=[hbm] * 6 + [vmem],
        out_specs=(hbm,) * 6 + (vmem,),
        scratch_shapes=[
            pltpu.VMEM((count, width), low),
            pltpu.VMEM((count, units), low),
            pltpu.VMEM((n, 2, chunk, units), low),
            pltpu.VMEM((2, width, TILE), low),
            pltpu.VMEM((2, width, TILE), low),
            pltpu.VMEM((2, count, TILE), low),
            pltpu.VMEM((2, count, TILE), low),
            pltpu.VMEM((n, half, 2 * chunk), low),
            pltpu.VMEM((n, half, 2 * chunk), low),
            pltpu.VMEM((n, half, 2 * chunk), low),
            pltpu.VMEM((n, half, 2 * chunk), low),
            pltpu.VMEM((half, width), jnp.float32),
            pltpu.VMEM((half, width), jnp.float32),
            pltpu.VMEM((half, width), low),
            pltpu.VMEM((half, width), low),
            pltpu.VMEM((half, width), low),
            pltpu.VMEM((8, width), jnp.float32),
            dma((2, SUBS, n - 1)),
            dma((2, SUBS, n - 1)),
            dma((n + 1,)),
            dma((n + 1,)),
            dma((n + 1,)),
            dma((n + 1,)),
            dma((4,)),
            dma((4,)),
            dma((4,)),
            dma((2, 2)),
            dma((2, 2)),
            dma((7,)),
        ],
        compiler_params=pltpu.CompilerParams(
            collective_id=2, has_side_effects=True, vmem_limit_bytes=58 * 2**20
        ),
    )(
        hidden_low,
        gate_full,
        up_full,
        down_shard,
        hidden,
        upstream,
        gains,
    )
    return (
        product,
        slope,
        silu,
        down_full.reshape(width, units),
        d_mlp.reshape(count, width),
        block,
        gain_grad,
    )


def back_kernel(
    n,
    d_mlp,
    product,
    down_full,
    gate_slope,
    silu_in,
    gate_full,
    up_full,
    hidden_low,
    block_half,
    out_down,
    d_hidden_out,
    d_gate_out,
    d_up_out,
    head_grads,
    block_out,
    d_out,
    prod,
    d_gate,
    d_up,
    down_tile,
    slope_tile,
    silu_tile,
    gate_tile,
    up_tile,
    hidden_tile,
    first,
    own,
    inbox,
    mixed,
    twin_in,
    pair,
    far_in,
    d_hidden,
    stage,
    ring_send,
    ring_recv,
    twin_send,
    twin_recv,
    far_send,
    far_recv,
    join_send,
    join_recv,
    load_sem,
    down_sem,
    weight_sem,
    hidden_sem,
    stage_sem,
    store_sem,
):
    index, core, right, left, twin, far = neighbours(n)
    side = d_out.shape[2]
    width, units = d_out.shape[3], prod.shape[3]
    pack = 2 * side
    half = d_hidden.shape[0]
    chunk = inbox.shape[3] * SUBS
    rows = chunk // SUBS
    tiles = units // TILE
    blocks = width // TILE
    left_side = (((0,), (0,)), ((), ()))
    right_side = (((1,), (1,)), ((), ()))

    def tile_span(tile):
        return pl.ds(pl.multiple_of(tile * TILE, TILE), TILE)

    def down_copies(group, tile, slot):
        cols = tile_span(tile)
        return (
            pltpu.make_async_copy(down_full.at[:, cols], down_tile.at[slot], down_sem.at[slot, 0]),
            pltpu.make_async_copy(
                gate_slope.at[:, group, :, cols], slope_tile.at[slot], down_sem.at[slot, 1]
            ),
            pltpu.make_async_copy(
                silu_in.at[:, group, :, cols], silu_tile.at[slot], down_sem.at[slot, 2]
            ),
        )

    def weight_copies(tile, slot):
        span = tile_span(tile)
        return (
            pltpu.make_async_copy(gate_full.at[span], gate_tile.at[slot], weight_sem.at[slot, 0]),
            pltpu.make_async_copy(up_full.at[span], up_tile.at[slot], weight_sem.at[slot, 1]),
        )

    def hidden_copy(group, way):
        owner = holder_of(index, 2 * way - 1, n)
        start = pl.multiple_of(owner * 2 * chunk + way * chunk, chunk)
        return pltpu.make_async_copy(
            hidden_low.at[:, group, :, pl.ds(start, chunk)],
            hidden_tile.at[group, :, :, pl.ds(way * chunk, chunk)],
            hidden_sem.at[group, way],
        )

    def stage_copy(which):
        return pltpu.make_async_copy(stage.at[which], head_grads.at[which], stage_sem.at[which])

    def block_copy(kind):
        if kind == 2:
            return pltpu.make_async_copy(block_half, block_out.at[core], store_sem.at[5])
        target = block_out.at[1 - core if kind else core]
        return exchange(target if kind else block_half, target, join_send, join_recv, 0, twin)

    def ring(way, sub, step):
        return pltpu.make_async_remote_copy(
            src_ref=first.at[way, pl.ds(sub * rows, rows)]
            if step == 1
            else inbox.at[step - 2, way, sub],
            dst_ref=inbox.at[step - 1, way, sub],
            send_sem=ring_send.at[way, sub, step - 1],
            recv_sem=ring_recv.at[way, sub, step - 1],
            device_id=left if way else right,
            device_id_type=MESH,
        )

    def grad_block(step):
        cols = []
        for way in range(2):
            owner = holder_of(index, (1 + step) * (2 * way - 1), n)
            start = pl.multiple_of(owner * 2 * chunk + way * chunk, chunk)
            cols.append(d_out[:, :, :, pl.ds(start, chunk)].reshape(2 * pack, chunk))
        block = lax.dot_general(
            jnp.concatenate(cols, axis=1),
            prod[...].reshape(2 * pack, units),
            left_side,
            preferred_element_type=jnp.float32,
        ).astype(jnp.bfloat16)
        target = first if step == 0 else own.at[step % 2]
        target[0] = block[:chunk]
        target[1] = block[chunk:]

    def serve(step, sub):
        for way in range(2):
            ring(way, sub, step).wait_recv()

            @pl.loop(0, rows // 16)
            def _(tile, way=way):
                near = pl.ds(pl.multiple_of(tile * 16, 16), 16)
                mine = pl.ds(pl.multiple_of(sub * rows + tile * 16, 16), 16)
                got = inbox[step - 1, way, sub, near, :]
                held = own[step % 2, way, mine, :]
                if step < n - 1:
                    inbox[step - 1, way, sub, near, :] = got + held
                else:
                    out_down[way, mine, :] = got.astype(jnp.float32) + held.astype(jnp.float32)

            if step < n - 1:
                ring(way, sub, step + 1).start()

    def twin_copy(turn):
        return exchange(
            mixed.at[turn % 4, 1 - core], twin_in.at[turn % 4], twin_send, twin_recv, turn, twin
        )

    def far_copy(turn):
        return exchange(pair.at[turn], far_in.at[turn], far_send, far_recv, turn, far)

    greet((right, left, twin, far))
    loads = []
    for group in range(2):
        loads += [
            pltpu.make_async_copy(d_mlp.at[:, group], d_out.at[group], load_sem.at[0, group]),
            pltpu.make_async_copy(product.at[:, group], prod.at[group], load_sem.at[1, group]),
        ]
    for copy in loads:
        copy.start()
    for turn in range(2):
        for copy in down_copies(0, turn, turn):
            copy.start()
        for copy in weight_copies(turn, turn):
            copy.start()
    for copy in loads:
        copy.wait()
    grad_block(0)
    for sub in range(SUBS):
        for way in range(2):
            ring(way, sub, 1).start()
    block_copy(0).start()
    block_copy(2).start()
    for group in range(2):
        for way in range(2):
            hidden_copy(group, way).start()
    grad_block(1)

    def product_tile(group, tile):
        turn = group * tiles + tile
        slot = lax.rem(turn, 3)
        for copy in down_copies(group, tile, slot):
            copy.wait()

        @pl.when(turn + 2 < 2 * tiles)
        def _():
            later = turn + 2
            for copy in down_copies(
                lax.div(later, tiles), lax.rem(later, tiles), lax.rem(later, 3)
            ):
                copy.start()

        cols = tile_span(tile)
        grad = jnp.dot(
            d_out[group].reshape(pack, width), down_tile[slot], preferred_element_type=jnp.float32
        )
        for target, factor in ((d_gate, slope_tile), (d_up, silu_tile)):
            scaled = grad * factor[slot].reshape(pack, TILE).astype(jnp.float32)
            target[group, :, :, cols] = scaled.astype(jnp.bfloat16).reshape(2, side, TILE)

    def input_tile(turn):
        group, tile = divmod(turn, blocks)
        slot = turn % 3
        for copy in weight_copies(tile, slot):
            copy.wait()
        if turn + 2 < 2 * blocks:
            for copy in weight_copies((tile + 2) % blocks, (turn + 2) % 3):
                copy.start()
        total = lax.dot_general(
            d_gate[group].reshape(pack, units),
            gate_tile[slot],
            right_side,
            preferred_element_type=jnp.float32,
        ) + lax.dot_general(
            d_up[group].reshape(pack, units),
            up_tile[slot],
            right_side,
            preferred_element_type=jnp.float32,
        )
        mixed[turn % 4] = total.astype(jnp.bfloat16).reshape(2, side, TILE)
        twin_copy(turn).start()

    def add_twin(turn):
        twin_copy(turn).wait_recv()

        @pl.loop(0, side // 32)
        def _(row):
            span = pl.ds(pl.multiple_of(row * 32, 32), 32)
            pair[turn, span, :] = mixed[turn % 4, core, span, :] + twin_in[turn % 4, span, :]

        far_copy(turn).start()
        twin_copy(turn).wait_send()

    def add_far(turn):
        group, tile = divmod(turn, blocks)
        far_copy(turn).wait_recv()

        @pl.loop(0, side // 32)
        def _(row):
            span = pl.ds(pl.multiple_of(row * 32, 32), 32)
            wide = pl.ds(pl.multiple_of(group * side + row * 32, 32), 32)
            d_hidden[wide, tile * TILE : (tile + 1) * TILE] = pair[turn, span, :].astype(
                jnp.float32
            ) + far_in[turn, span, :].astype(jnp.float32)

    def weight_block(which, source):
        block = lax.dot_general(
            hidden_tile[...].reshape(2 * pack, TILE),
            source[...].reshape(2 * pack, units),
            left_side,
            preferred_element_type=jnp.float32,
        ).astype(jnp.bfloat16)
        stage[which, 0] = block[:chunk]
        stage[which, 1] = block[chunk:]
        stage_copy(which).start()

    events = [(step, sub) for step in range(1, n) for sub in range(SUBS)]

    def next_event():
        if events:
            step, sub = events.pop(0)
            serve(step, sub)
            if sub == SUBS - 1 and step < n - 1:
                grad_block(step + 1)

    def product_group(group):
        pl.loop(0, tiles // 2)(functools.partial(product_tile, group))
        next_event()
        pl.loop(tiles // 2, tiles)(functools.partial(product_tile, group))
        next_event()

    def grad_store(group):
        return [
            pltpu.make_async_copy(
                source.at[group], target.at[:, group], store_sem.at[6 + 2 * place + group]
            )
            for place, (source, target) in enumerate(((d_gate, d_gate_out), (d_up, d_up_out)))
        ]

    def hidden_store(group):
        span = pl.ds(group * side, side)
        return pltpu.make_async_copy(
            d_hidden.at[span], d_hidden_out.at[span], store_sem.at[group]
        )

    for group in range(2):
        product_group(group)
        for copy in grad_store(group):
            copy.start()
        if group == 1:
            for turn in range(blocks - 3, blocks):
                add_far(turn)
        for turn in range(group * blocks, (group + 1) * blocks):
            input_tile(turn)
            if turn % blocks >= 1:
                add_twin(turn - 1)
            if turn % blocks >= 3:
                add_far(turn - 3)
            if turn % 2 == 1:
                next_event()
        add_twin((group + 1) * blocks - 1)
        if group == 1:
            hidden_store(0).start()
    for group in range(2):
        for way in range(2):
            hidden_copy(group, way).wait()
    weight_block(0, d_gate)
    add_far(2 * blocks - 3)
    next_event()
    weight_block(1, d_up)
    add_far(2 * blocks - 2)
    next_event()
    add_far(2 * blocks - 1)
    hidden_store(1).start()
    while events:
        next_event()
    for group in range(2):
        hidden_store(group).wait()
    for which in range(2):
        stage_copy(which).wait()
        for copy in grad_store(which):
            copy.wait()
    block_copy(0).wait_send()
    block_copy(1).wait_recv()
    block_copy(2).wait()
    for turn in range(2 * blocks):
        far_copy(turn).wait_send()
    for step in range(1, n):
        for sub in range(SUBS):
            for way in range(2):
                ring(way, sub, step).wait_send()


def kernel_back(
    d_mlp,
    product,
    down_full,
    gate_slope,
    silu,
    gate_full,
    up_full,
    hidden_low,
    block_half,
    n,
):
    count, width = d_mlp.shape
    units = product.shape[1]
    half = count // 2
    side = count // 4
    chunk = width // n // 2
    rows = chunk // SUBS
    blocks = width // TILE
    low = jnp.bfloat16
    full = jnp.float32
    hbm = pl.BlockSpec(memory_space=pl.ANY)
    vmem = pl.BlockSpec(memory_space=pltpu.VMEM)
    dma = pltpu.SemaphoreType.DMA
    shape = jax.ShapeDtypeStruct

    def cut(array):
        return array.reshape(2, 2, side, array.shape[1])

    outs = pl.pallas_call(
        functools.partial(back_kernel, n),
        out_shape=(
            shape((2, chunk, units), full),
            shape((half, width), full),
            shape((2, 2, side, units), low),
            shape((2, 2, side, units), low),
            shape((2, 2, chunk, units), low),
            shape((2, half, width), low),
        ),
        in_specs=[hbm] * 9,
        out_specs=(vmem,) + (hbm,) * 5,
        scratch_shapes=[
            pltpu.VMEM((2, 2, side, width), low),
            pltpu.VMEM((2, 2, side, units), low),
            pltpu.VMEM((2, 2, side, units), low),
            pltpu.VMEM((2, 2, side, units), low),
            pltpu.VMEM((3, width, TILE), low),
            pltpu.VMEM((3, 2, side, TILE), low),
            pltpu.VMEM((3, 2, side, TILE), low),
            pltpu.VMEM((3, TILE, units), low),
            pltpu.VMEM((3, TILE, units), low),
            pltpu.VMEM((2, 2, side, TILE), low),
            pltpu.VMEM((2, chunk, units), low),
            pltpu.VMEM((2, 2, chunk, units), low),
            pltpu.VMEM((n - 1, 2, SUBS, rows, units), low),
            pltpu.VMEM((4, 2, side, TILE), low),
            pltpu.VMEM((4, side, TILE), low),
            pltpu.VMEM((2 * blocks, side, TILE), low),
            pltpu.VMEM((2 * blocks, side, TILE), low),
            pltpu.VMEM((half, width), full),
            pltpu.VMEM((2, 2, chunk, units), low),
            dma((2, SUBS, n - 1)),
            dma((2, SUBS, n - 1)),
            dma((2 * blocks,)),
            dma((2 * blocks,)),
            dma((2 * blocks,)),
            dma((2 * blocks,)),
            dma((1,)),
            dma((1,)),
            dma((2, 2)),
            dma((3, 3)),
            dma((3, 2)),
            dma((2, 2)),
            dma((2,)),
            dma((10,)),
        ],
        compiler_params=pltpu.CompilerParams(
            collective_id=3, has_side_effects=True, vmem_limit_bytes=60 * 2**20
        ),
    )(
        cut(d_mlp),
        cut(product),
        down_full,
        cut(gate_slope),
        cut(silu),
        gate_full,
        up_full,
        cut(hidden_low),
        block_half,
    )
    out_down, d_hidden, d_gate, d_up, head_grads, block_out = outs
    return (
        out_down.reshape(2 * chunk, units),
        d_hidden,
        d_gate.reshape(count, units),
        d_up.reshape(count, units),
        head_grads,
        block_out.reshape(count, width),
    )


def detach_kernel(
    n,
    branch,
    upstream,
    attn_gain,
    attn_full,
    attended_in,
    query_rot_in,
    key_rot_in,
    value_in,
    query_raw_in,
    key_raw_in,
    tokens,
    d_hidden,
    head_grads,
    d_gate,
    d_up,
    hidden_low,
    totals,
    inverses,
    cosine,
    sine,
    doc_col,
    doc_row,
    query_gain,
    key_gain,
    out_gate,
    out_up,
    grad_attn,
    grad_tokens,
    query_gain_grad,
    key_gain_grad,
    attn_gain_grad,
    d_branch,
    branch_tile,
    output_tile,
    grad_tile,
    unit_tile,
    weight_tile,
    attended,
    query_rot,
    key_rot,
    value,
    query_raw,
    key_raw,
    d_attended,
    d_query_norm,
    d_key_norm,
    d_key_sum,
    d_value_sum,
    d_projected,
    own,
    inbox,
    total_buf,
    mixed,
    twin_in,
    pair,
    far_in,
    hidden_tile,
    upstream_tile,
    upstream_rows,
    gain_sum,
    stage_output,
    stage,
    stat,
    ring_send,
    ring_recv,
    stat_send,
    stat_recv,
    twin_send,
    twin_recv,
    far_send,
    far_recv,
    join_send,
    join_recv,
    whole_send,
    whole_recv,
    whole_sem,
    row_sem,
    unit_sem,
    grad_sem,
    branch_sem,
    load_sem,
    weight_sem,
    hidden_sem,
    upstream_sem,
    stage_sem,
    store_sem,
    out_sem,
):
    index, core, right, left, twin, far = neighbours(n)
    count, width = tokens.shape
    half = count // 2
    local = query_raw.shape[1]
    heads = local // HEAD_CHANNELS
    blocks = width // TILE
    chunk = inbox.shape[3]
    grads = (d_gate, d_up)
    part_cols = grad_tile.shape[2]
    parts_in = d_gate.shape[1] // part_cols
    outs = (out_gate, out_up)
    left_side = (((0,), (0,)), ((), ()))
    right_side = (((1,), (1,)), ((), ()))
    factor = 1.0 / math.sqrt(HEAD_CHANNELS)

    def ring(way, unit, step):
        first = head_grads.at[unit, way]
        return pltpu.make_async_remote_copy(
            src_ref=first if step == 1 else inbox.at[step - 2, way, unit],
            dst_ref=inbox.at[step - 1, way, unit],
            send_sem=ring_send.at[way, unit, step - 1],
            recv_sem=ring_recv.at[way, unit, step - 1],
            device_id=left if way else right,
            device_id_type=MESH,
        )

    events = [(step, unit) for step in range(1, n) for unit in range(2)]

    def unit_copy(step, way):
        owner = holder_of(index, (1 + step) * (2 * way - 1), n)
        start = pl.multiple_of(owner * 2 * chunk + way * chunk, chunk)
        return pltpu.make_async_copy(
            hidden_low.at[:, pl.ds(start, chunk)],
            unit_tile.at[step % 2, :, pl.ds(way * chunk, chunk)],
            unit_sem.at[step % 2, way],
        )

    def grad_copy(unit, part, slot):
        cols = pl.ds(pl.multiple_of(part * part_cols, part_cols), part_cols)
        return pltpu.make_async_copy(
            grads[unit].at[:, cols], grad_tile.at[slot], grad_sem.at[slot]
        )

    def grad_block(step, unit):
        if unit == 0:
            for way in range(2):
                unit_copy(step, way).wait()
                if step < n - 1:
                    unit_copy(step + 1, way).start()

        base = 2 * (step - 1) + unit
        final = base == 2 * n - 3

        @pl.loop(0, parts_in)
        def _(part):
            slot = lax.rem(base * parts_in + part, 3)
            spare = lax.rem(slot + 2, 3)
            grad_copy(unit, part, slot).wait()

            @pl.when(part + 2 < parts_in)
            def _():
                grad_copy(unit, part + 2, spare).start()

            if not final:

                @pl.when(part + 2 >= parts_in)
                def _():
                    grad_copy(1 - unit, part + 2 - parts_in, spare).start()

            cols = pl.ds(pl.multiple_of(part * part_cols, part_cols), part_cols)
            block = lax.dot_general(
                unit_tile[step % 2],
                grad_tile[slot],
                left_side,
                preferred_element_type=jnp.float32,
            ).astype(jnp.bfloat16)
            own[unit, 0, :, cols] = block[:chunk]
            own[unit, 1, :, cols] = block[chunk:]

    def out_copy(unit):
        return pltpu.make_async_copy(total_buf, outs[unit], out_sem.at[unit])

    def serve():
        step, unit = events.pop(0)
        if step == n - 1 and unit == 1:
            out_copy(0).wait()
        for way in range(2):
            ring(way, unit, step).wait_recv()

            @pl.loop(0, chunk // 16)
            def _(tile, way=way):
                span = pl.ds(pl.multiple_of(tile * 16, 16), 16)
                got = inbox[step - 1, way, unit, span, :]
                held = own[unit, way, span, :]
                if step < n - 1:
                    inbox[step - 1, way, unit, span, :] = got + held
                else:
                    total_buf[way, span, :] = got.astype(jnp.float32) + held.astype(jnp.float32)

            if step < n - 1:
                ring(way, unit, step + 1).start()
        if step < n - 1:
            grad_block(step + 1, unit)
        else:
            out_copy(unit).start()

    greet((right, left, twin, far))
    for unit in range(2):
        for way in range(2):
            ring(way, unit, 1).start()
    for way in range(2):
        unit_copy(1, way).start()
    for part in range(2):
        grad_copy(0, part, part).start()

    def weight_copy(tile, slot):
        return pltpu.make_async_copy(
            attn_full.at[pl.ds(tile * TILE, TILE), pl.ds(0, 3 * local)],
            weight_tile.at[slot],
            weight_sem.at[slot],
        )

    def hidden_copies(tile, slot):
        cols = pl.ds(tile * TILE, TILE)
        mine = pl.ds(pl.multiple_of(core * half, half), half)
        return (
            pltpu.make_async_copy(
                d_hidden.at[:, cols], hidden_tile.at[slot], hidden_sem.at[slot]
            ),
            pltpu.make_async_copy(
                upstream.at[mine, cols], upstream_tile.at[slot], upstream_sem.at[slot]
            ),
        )

    loads = [
        pltpu.make_async_copy(source, target, load_sem.at[place])
        for place, (source, target) in enumerate(
            (
                (attended_in, attended),
                (query_rot_in, query_rot),
                (key_rot_in, key_rot),
                (value_in, value),
                (query_raw_in, query_raw),
                (key_raw_in, key_raw),
            )
        )
    ]

    def branch_copies(tile, source):
        cols = pl.ds(tile * TILE, TILE)
        slot = tile % 2
        copies = [
            pltpu.make_async_copy(source.at[:, cols], branch_tile.at[slot], branch_sem.at[slot, 0])
        ]
        if source is d_branch:
            copies.append(
                pltpu.make_async_copy(
                    attn_full.at[cols, pl.ds(3 * local, local)],
                    output_tile.at[slot],
                    branch_sem.at[slot, 1],
                )
            )
        return copies

    def output_copy(tile):
        return pltpu.make_async_copy(
            stage_output.at[tile % 2],
            grad_attn.at[pl.ds(tile * TILE, TILE), pl.ds(3 * local, local)],
            stage_sem.at[0, tile % 2],
        )

    deep = half // 4

    def row_copies(part):
        span = pl.ds(part * deep, deep)
        mine = pl.ds(pl.multiple_of(core * half + part * deep, deep), deep)
        return [
            pltpu.make_async_copy(d_hidden.at[span], total_buf.at[0], row_sem.at[0]),
            pltpu.make_async_copy(branch.at[span], total_buf.at[1], row_sem.at[1]),
            pltpu.make_async_copy(upstream.at[mine], upstream_rows, row_sem.at[2]),
        ]

    def finish(part, tile):
        near = pl.ds(pl.multiple_of(tile * 16, 16), 16)
        total = total_buf[0, near, :] + upstream_rows[near, :].astype(jnp.float32)
        mix = total_buf[1, near, :]
        inverse = lax.rsqrt(jnp.sum(mix * mix, axis=1, keepdims=True) / width + EPSILON)
        scaled = attn_gain[...] * total
        mean = jnp.sum(scaled * mix, axis=1, keepdims=True) / width
        grad = (inverse * scaled - mix * (inverse * inverse * inverse * mean)).astype(
            jnp.bfloat16
        )
        for block in range(blocks):
            spot = pl.multiple_of((block % 2) * half + part * deep + tile * 16, 16)
            mixed[block // 2, pl.ds(spot, 16), :] = grad[:, block * TILE : (block + 1) * TILE]
        terms = total * mix * inverse
        gain_sum[...] += terms[:8] + terms[8:]

    def whole_copy(block, kind):
        cols = pl.ds(block * TILE, TILE)
        source = mixed.at[block // 2, pl.ds((block % 2) * half, half)]
        keeper = 1 - core if kind == 1 else core
        target = d_branch.at[pl.ds(pl.multiple_of(keeper * half, half), half), cols]
        if kind == 2:
            return pltpu.make_async_copy(source, target, whole_sem.at[block])
        return exchange(
            target if kind else source, target, whole_send, whole_recv, block, twin
        )

    for copy in row_copies(0) + loads:
        copy.start()
    gain_sum[...] = jnp.zeros_like(gain_sum)
    grad_block(1, 0)
    grad_block(1, 1)
    for part in range(4):
        for copy in row_copies(part):
            copy.wait()
        pl.loop(0, deep // 16)(functools.partial(finish, part))
        if part < 3:
            for copy in row_copies(part + 1):
                copy.start()
        if part == 1:
            serve()
    for block in range(blocks):
        whole_copy(block, 0).start()
        whole_copy(block, 2).start()
    attn_gain_grad[...] = jnp.sum(gain_sum[...], axis=0, keepdims=True)
    for block in range(blocks):
        whole_copy(block, 1).wait_recv()
        whole_copy(block, 0).wait_send()
        whole_copy(block, 2).wait()
    for copy in branch_copies(0, d_branch):
        copy.start()
    loads[0].wait()
    for tile in range(blocks):
        for copy in branch_copies(tile, d_branch):
            copy.wait()
        if tile + 1 < blocks:
            for copy in branch_copies(tile + 1, d_branch):
                copy.start()
        product = jnp.dot(
            branch_tile[tile % 2], output_tile[tile % 2], preferred_element_type=jnp.float32
        )
        if tile == 0:
            d_query_norm[...] = product
        else:
            d_query_norm[...] += product
        if tile >= 2:
            output_copy(tile - 2).wait()
        stage_output[tile % 2] = lax.dot_general(
            branch_tile[tile % 2],
            attended[...],
            left_side,
            preferred_element_type=jnp.float32,
        ).astype(jnp.bfloat16)
        output_copy(tile).start()
    d_attended[...] = d_query_norm[...].astype(jnp.bfloat16)
    branch_copies(0, tokens)[0].start()
    weight_copy(0, 0).start()
    for copy in loads[1:]:
        copy.wait()
    serve()

    def unturned(vectors, span):
        return vectors * cosine[span, :] - pltpu.roll(vectors, HEAD_CHANNELS // 2, 1) * sine[span, :]

    def head_backward(head):
        cols = pl.ds(pl.multiple_of(head * HEAD_CHANNELS, HEAD_CHANNELS), HEAD_CHANNELS)
        lane = lax.broadcasted_iota(jnp.int32, (BLOCK, 128), 1)
        for block in reversed(range(count // BLOCK)):
            span = slice(block * BLOCK, (block + 1) * BLOCK)
            length = (block + 1) * BLOCK
            query = query_rot[span, cols]
            key = key_rot[:length, cols]
            grad = d_attended[span, cols]
            scores = masked_scores(query, key, doc_col, doc_row, block)
            total = jnp.sum(jnp.where(lane == head, totals[span, :], 0.0), axis=1, keepdims=True)
            powers = jnp.exp(scores - total)
            d_powers = lax.dot_general(
                grad, value[:length, cols], right_side, preferred_element_type=jnp.float32
            )
            correction = jnp.sum(d_powers * powers, axis=1, keepdims=True)
            d_scores = (powers * (d_powers - correction)).astype(jnp.bfloat16)
            rounded = powers.astype(jnp.bfloat16)
            d_query = jnp.dot(d_scores, key, preferred_element_type=jnp.float32) * factor
            d_query_norm[span, cols] = unturned(d_query, span)
            d_key = lax.dot_general(
                d_scores, query, left_side, preferred_element_type=jnp.float32
            )
            d_value = lax.dot_general(
                rounded, grad, left_side, preferred_element_type=jnp.float32
            )
            if length == count:
                d_key_sum[...] = d_key
                d_value_sum[...] = d_value
            else:
                d_key_sum[:length, :] += d_key
                d_value_sum[:length, :] += d_value
        d_key_norm[:, cols] = unturned(d_key_sum[...] * factor, slice(None))
        start = pl.multiple_of(2 * local + head * HEAD_CHANNELS, HEAD_CHANNELS)
        d_projected[:, pl.ds(start, HEAD_CHANNELS)] = d_value_sum[...].astype(jnp.bfloat16)

    pl.loop(0, heads // 2)(head_backward)
    serve()
    pl.loop(heads // 2, heads)(head_backward)
    serve()
    parts = []
    for place, (norm, raw, gain, gain_grad) in enumerate(
        (
            (d_query_norm, query_raw, query_gain, query_gain_grad),
            (d_key_norm, key_raw, key_gain, key_gain_grad),
        )
    ):
        dots = jnp.zeros((count, HEAD_CHANNELS), jnp.float32)
        for head in range(heads):
            cols = slice(head * HEAD_CHANNELS, (head + 1) * HEAD_CHANNELS)
            both = norm[:, cols] * raw[:, cols]
            gain_grad[:, cols] = jnp.sum(
                both * inverses[:, place : place + 1], axis=0, keepdims=True
            )
            dots = dots + both * gain[:, cols]
        parts.append(jnp.sum(dots, axis=1, keepdims=True))
    stat[0] = columns_to_rows(parts, count)
    first = exchange(stat.at[0], stat.at[1], stat_send, stat_recv, 0, twin)
    first.start()
    first.wait()
    stat[2] = stat[0] + stat[1]
    second = exchange(stat.at[2], stat.at[3], stat_send, stat_recv, 1, far)
    second.start()
    serve()
    second.wait()
    inner = d_key_sum
    inner[...] = rows_to_columns(stat[2] + stat[3]) / width

    @pl.loop(0, heads)
    def _(head):
        cols = pl.ds(pl.multiple_of(head * HEAD_CHANNELS, HEAD_CHANNELS), HEAD_CHANNELS)
        for place, (norm, raw, gain) in enumerate(
            ((d_query_norm, query_raw, query_gain), (d_key_norm, key_raw, key_gain))
        ):
            inverse = inverses[:, place : place + 1]
            cube = inverse * inverse * inverse * inner[:, place : place + 1]
            start = pl.multiple_of(place * local + head * HEAD_CHANNELS, HEAD_CHANNELS)
            d_projected[:, pl.ds(start, HEAD_CHANNELS)] = (
                norm[:, cols] * inverse * gain[:, cols] - raw[:, cols] * cube
            ).astype(jnp.bfloat16)

    def twin_copy(tile):
        span = pl.ds(pl.multiple_of((1 - core) * half, half), half)
        return exchange(
            mixed.at[tile % 4, span], twin_in.at[tile % 4], twin_send, twin_recv, tile, twin
        )

    def far_copy(tile):
        return exchange(pair.at[tile], far_in.at[tile], far_send, far_recv, tile, far)

    def token_tile(tile):
        slot = tile % 2
        weight_copy(tile, slot).wait()
        if tile + 1 < blocks:
            weight_copy(tile + 1, 1 - slot).start()
        mixed[tile % 4] = lax.dot_general(
            d_projected[...], weight_tile[slot], right_side, preferred_element_type=jnp.float32
        ).astype(jnp.bfloat16)
        twin_copy(tile).start()

    def add_twin(tile):
        twin_copy(tile).wait_recv()

        @pl.loop(0, half // 32)
        def _(row):
            span = pl.ds(pl.multiple_of(row * 32, 32), 32)
            mine = pl.ds(pl.multiple_of(core * half + row * 32, 32), 32)
            pair[tile, span, :] = mixed[tile % 4, mine, :] + twin_in[tile % 4, span, :]

        far_copy(tile).start()
        twin_copy(tile).wait_send()

    def join(tile, kind):
        cols = pl.ds(tile * TILE, TILE)
        if kind == 2:
            return pltpu.make_async_copy(
                pair.at[tile], grad_tokens.at[core, :, cols], store_sem.at[tile]
            )
        target = grad_tokens.at[1 - core if kind else core, :, cols]
        return exchange(
            target if kind else pair.at[tile], target, join_send, join_recv, tile, twin
        )

    def add_far(tile):
        slot = tile % 2
        for copy in hidden_copies(tile, slot):
            copy.wait()
        if tile + 1 < blocks:
            for copy in hidden_copies(tile + 1, 1 - slot):
                copy.start()
        far_copy(tile).wait()

        @pl.loop(0, half // 32)
        def _(row):
            span = pl.ds(pl.multiple_of(row * 32, 32), 32)
            total = (
                pair[tile, span, :].astype(jnp.float32)
                + far_in[tile, span, :].astype(jnp.float32)
                + hidden_tile[slot, span, :]
                + upstream_tile[slot, span, :].astype(jnp.float32)
            )
            pair[tile, span, :] = total.astype(jnp.bfloat16)

        join(tile, 0).start()
        join(tile, 2).start()

    def stage_copy(tile):
        return pltpu.make_async_copy(
            stage.at[tile % 2],
            grad_attn.at[pl.ds(tile * TILE, TILE), pl.ds(0, 3 * local)],
            stage_sem.at[1, tile % 2],
        )

    def weight_grad(tile):
        if tile >= 2:
            stage_copy(tile - 2).wait()
        branch_copies(tile, tokens)[0].wait()
        if tile + 1 < blocks:
            branch_copies(tile + 1, tokens)[0].start()
        stage[tile % 2] = lax.dot_general(
            branch_tile[tile % 2],
            d_projected[...],
            left_side,
            preferred_element_type=jnp.float32,
        ).astype(jnp.bfloat16)
        stage_copy(tile).start()

    for copy in hidden_copies(0, 0):
        copy.start()
    for tile in range(blocks):
        token_tile(tile)
        if tile >= 1:
            add_twin(tile - 1)
        if tile == blocks // 2 - 1:
            serve()
    add_twin(blocks - 1)
    serve()
    for tile in range(blocks):
        weight_grad(tile)
        add_far(tile)
        if tile % 2 == 1:
            serve()
    for tile in (blocks - 2, blocks - 1):
        output_copy(tile).wait()
        stage_copy(tile).wait()
    while events:
        serve()
    out_copy(1).wait()
    for tile in range(blocks):
        join(tile, 1).wait_recv()
        join(tile, 0).wait_send()
        join(tile, 2).wait()
    for step in range(1, n):
        for unit in range(2):
            for way in range(2):
                ring(way, unit, step).wait_send()


def kernel_detach(
    branch,
    upstream,
    attn_gain,
    attn_full,
    attended,
    query_rot,
    key_rot,
    value,
    query_raw,
    key_raw,
    tokens,
    d_hidden,
    head_grads,
    d_gate,
    d_up,
    hidden_low,
    totals,
    inverses,
    cosine,
    sine,
    doc_col,
    doc_ids,
    query_gain,
    key_gain,
    n,
):
    count, width = tokens.shape
    local = query_gain.shape[1]
    units = d_gate.shape[1]
    half = count // 2
    chunk = width // n // 2
    blocks = width // TILE
    low = jnp.bfloat16
    full = jnp.float32
    hbm = pl.BlockSpec(memory_space=pl.ANY)
    vmem = pl.BlockSpec(memory_space=pltpu.VMEM)
    dma = pltpu.SemaphoreType.DMA
    shape = jax.ShapeDtypeStruct
    outs = pl.pallas_call(
        functools.partial(detach_kernel, n),
        out_shape=(
            shape((2, chunk, units), full),
            shape((2, chunk, units), full),
            shape((width, 4 * local), low),
            shape((2, half, width), low),
            shape((1, local), full),
            shape((1, local), full),
            shape((1, width), full),
            shape((count, width), low),
        ),
        in_specs=[hbm] * 2 + [vmem] + [hbm] * 13 + [vmem] * 8,
        out_specs=(hbm,) * 4 + (vmem,) * 3 + (hbm,),
        scratch_shapes=[
            pltpu.VMEM((2, count, TILE), low),
            pltpu.VMEM((2, TILE, local), low),
            pltpu.VMEM((3, count, 2 * TILE), low),
            pltpu.VMEM((2, count, TILE), low),
            pltpu.VMEM((2, TILE, 3 * local), low),
            pltpu.VMEM((count, local), low),
            pltpu.VMEM((count, local), low),
            pltpu.VMEM((count, local), low),
            pltpu.VMEM((count, local), low),
            pltpu.VMEM((count, local), full),
            pltpu.VMEM((count, local), full),
            pltpu.VMEM((count, local), low),
            pltpu.VMEM((count, local), full),
            pltpu.VMEM((count, local), full),
            pltpu.VMEM((count, HEAD_CHANNELS), full),
            pltpu.VMEM((count, HEAD_CHANNELS), full),
            pltpu.VMEM((count, 3 * local), low),
            pltpu.VMEM((2, 2, chunk, units), low),
            pltpu.VMEM((n - 1, 2, 2, chunk, units), low),
            pltpu.VMEM((2, chunk, units), full),
            pltpu.VMEM((4, count, TILE), low),
            pltpu.VMEM((4, half, TILE), low),
            pltpu.VMEM((blocks, half, TILE), low),
            pltpu.VMEM((blocks, half, TILE), low),
            pltpu.VMEM((2, half, TILE), full),
            pltpu.VMEM((2, half, TILE), low),
            pltpu.VMEM((half // 4, width), low),
            pltpu.VMEM((8, width), full),
            pltpu.VMEM((2, TILE, local), low),
            pltpu.VMEM((2, TILE, 3 * local), low),
            pltpu.VMEM((4, 8, count), full),
            dma((2, 2, n - 1)),
            dma((2, 2, n - 1)),
            dma((2,)),
            dma((2,)),
            dma((blocks,)),
            dma((blocks,)),
            dma((blocks,)),
            dma((blocks,)),
            dma((blocks,)),
            dma((blocks,)),
            dma((blocks,)),
            dma((blocks,)),
            dma((blocks,)),
            dma((3,)),
            dma((2, 2)),
            dma((3,)),
            dma((2, 2)),
            dma((6,)),
            dma((2,)),
            dma((2,)),
            dma((2,)),
            dma((2, 2)),
            dma((blocks,)),
            dma((2,)),
        ],
        compiler_params=pltpu.CompilerParams(
            collective_id=5, has_side_effects=True, vmem_limit_bytes=60 * 2**20
        ),
    )(
        branch,
        upstream,
        attn_gain,
        attn_full,
        attended,
        query_rot,
        key_rot,
        value,
        query_raw,
        key_raw,
        tokens,
        d_hidden,
        head_grads,
        d_gate,
        d_up,
        hidden_low,
        totals,
        inverses,
        cosine,
        sine,
        doc_col,
        doc_ids.reshape(1, count),
        query_gain,
        key_gain,
    )
    return (
        outs[0].reshape(2 * chunk, units),
        outs[1].reshape(2 * chunk, units),
        outs[2],
        outs[3].reshape(count, width),
        outs[4],
        outs[5],
        outs[6],
    )


def fused_layer(
    n,
    tokens,
    doc_ids,
    q_weight,
    k_weight,
    v_weight,
    o_weight,
    q_gain,
    k_gain,
    attn_gain,
    gate_weight,
    up_weight,
    down_weight,
    mlp_gain,
    cotangent,
):
    index = lax.axis_index("dp")
    heads, channels = q_gain.shape
    small = jnp.concatenate(
        [
            q_gain,
            k_gain,
            jnp.zeros((SMALL - 2 * heads, channels), q_gain.dtype),
        ],
        axis=0,
    )
    small = lax.dynamic_update_slice(
        jnp.zeros((SMALL, HEAD_CHANNELS), q_gain.dtype), small, (0, index * channels)
    )
    small = lax.dynamic_update_slice(
        small, jnp.concatenate([attn_gain, mlp_gain]).reshape(4, 128), (2 * heads, 0)
    )
    frequency = jnp.exp(
        jnp.arange(HEAD_CHANNELS // 2, dtype=jnp.float32)
        * (-2.0 * math.log(ROPE_BASE) / HEAD_CHANNELS)
    )
    frequency = jnp.concatenate([frequency, frequency])[None, :]
    (
        attn_full,
        query_gain,
        key_gain,
        attn_gains,
        mlp_gains,
        cosine,
        sine,
        doc_col,
        down_shard,
    ) = kernel_gather(
        q_weight, k_weight, v_weight, o_weight, small, doc_ids, frequency, down_weight, n
    )
    (
        gate_full,
        up_full,
        query_raw,
        key_raw,
        query_rot,
        key_rot,
        value,
        attended,
        totals,
        inverses,
        branch,
        hidden_state,
        hidden_low,
    ) = kernel_attend(
        tokens,
        attn_full,
        gate_weight,
        up_weight,
        cosine,
        sine,
        doc_col,
        doc_ids,
        query_gain,
        key_gain,
        attn_gains,
        n,
    )
    product, gate_slope, silu, down_full, d_mlp, block_half, mlp_row = kernel_feed(
        hidden_low, gate_full, up_full, down_shard, hidden_state, cotangent, mlp_gains, n
    )
    out_down, d_hidden, d_gate, d_up, head_grads, block_out = kernel_back(
        d_mlp,
        product,
        down_full,
        gate_slope,
        silu,
        gate_full,
        up_full,
        hidden_low,
        block_half,
        n,
    )
    out_gate, out_up, grad_attn, grad_tokens, query_row, key_row, attn_row = kernel_detach(
        branch,
        cotangent,
        attn_gains,
        attn_full,
        attended,
        query_rot,
        key_rot,
        value,
        query_raw,
        key_raw,
        tokens,
        d_hidden,
        head_grads,
        d_gate,
        d_up,
        hidden_low,
        totals,
        inverses,
        cosine,
        sine,
        doc_col,
        doc_ids,
        query_gain,
        key_gain,
        n,
    )
    out_query, out_key, out_value, out_output, summed = kernel_scatter(
        grad_attn, query_row, key_row, attn_row, mlp_row, n
    )
    lanes = lax.dynamic_slice(summed, (0, index * channels), (2 * heads, channels))
    return (
        block_out,
        grad_tokens,
        out_query,
        out_key,
        out_value,
        out_output,
        lanes[:heads],
        lanes[heads:],
        summed[2 * heads : 2 * heads + 2].reshape(-1),
        out_gate,
        out_up,
        out_down.T,
        summed[2 * heads + 2 : 2 * heads + 4].reshape(-1),
    )


def solution(mesh):
    in_specs = (
        P("dp", None),
        P("dp"),
        P("dp", "mp"),
        P("dp", "mp"),
        P("dp", "mp"),
        P("mp", "dp"),
        P("mp", "dp"),
        P("mp", "dp"),
        P("dp"),
        P("dp", "mp"),
        P("dp", "mp"),
        P("mp", "dp"),
        P("dp"),
        P("dp", None),
    )
    out_specs = (
        P("dp", None),
        P("dp", None),
        P("dp", "mp"),
        P("dp", "mp"),
        P("dp", "mp"),
        P("mp", "dp"),
        P("mp", "dp"),
        P("mp", "dp"),
        P("dp"),
        P("dp", "mp"),
        P("dp", "mp"),
        P("mp", "dp"),
        P("dp"),
    )
    n, m = mesh.shape["dp"], mesh.shape["mp"]

    def on_device(*arrays):
        if (n, m, arrays[0].shape[0]) == (RING, 4, SEQ_LEN):
            return fused_layer(n, *arrays)
        return plain_layer(*arrays)

    return jax.shard_map(
        on_device, mesh=mesh, in_specs=in_specs, out_specs=out_specs, check_vma=False
    )
```

```python
import functools
import math

import jax
import jax.numpy as jnp
from jax import lax
from jax.experimental import pallas as pl
from jax.experimental.pallas import tpu as pltpu
from jax.sharding import PartitionSpec as P

D = 2048
HEAD_CHANNELS = 128
SEQ_LEN = 1024
RING = 8


EPSILON = 1e-06
ROPE_BASE = 500000.0
MASKED = -1e30
ROW_LIMIT = 512


def matmul(left_side, right_side):
    return jnp.dot(left_side, right_side, preferred_element_type=jnp.float32)


def transposed_left(left_side, right_side):
    return lax.dot_general(
        left_side, right_side, (((0,), (0,)), ((), ())), preferred_element_type=jnp.float32
    )


def transposed_right(left_side, right_side):
    return lax.dot_general(
        left_side, right_side, (((1,), (1,)), ((), ())), preferred_element_type=jnp.float32
    )


def angles_of(doc_rows, seq_len, head_dim):
    shaped = doc_rows.reshape(-1, seq_len)
    leading = jnp.sum(1 - shaped, axis=1, keepdims=True, dtype=jnp.int32)
    places = jnp.arange(seq_len, dtype=jnp.int32)[None, :] - shaped * leading
    frequency = jnp.exp(
        jnp.arange(head_dim // 2, dtype=jnp.float32) * (-2.0 * math.log(ROPE_BASE) / head_dim)
    )
    return places.reshape(-1).astype(jnp.float32)[:, None] * frequency[None, :]


def rotate(vectors, angles):
    halfway = vectors.shape[-1] // 2
    cosine = jnp.cos(angles)[:, None, :]
    sine_wave = jnp.sin(angles)[:, None, :]
    former = vectors[..., :halfway]
    latter = vectors[..., halfway:]
    return jnp.concatenate(
        [former * cosine - latter * sine_wave, latter * cosine + former * sine_wave], axis=-1
    )


def rotate_back(vectors, angles):
    halfway = vectors.shape[-1] // 2
    cosine = jnp.cos(angles)[:, None, :]
    sine_wave = jnp.sin(angles)[:, None, :]
    former = vectors[..., :halfway]
    latter = vectors[..., halfway:]
    return jnp.concatenate(
        [former * cosine + latter * sine_wave, latter * cosine - former * sine_wave], axis=-1
    )


def block_scores(query_block, key_seq, doc_seq, offset):
    factor = 1.0 / math.sqrt(query_block.shape[-1])
    scores = (
        jnp.einsum("qhd,khd->hqk", query_block, key_seq, preferred_element_type=jnp.float32)
        * factor
    )
    row_places = offset + jnp.arange(query_block.shape[0], dtype=jnp.int32)
    key_places = jnp.arange(key_seq.shape[0], dtype=jnp.int32)
    row_docs = doc_seq[offset : offset + query_block.shape[0]]
    allowed = (key_places[None, :] <= row_places[:, None]) & (doc_seq[None, :] == row_docs[:, None])
    return jnp.where(allowed[None], scores, MASKED)


def attend_sequence(inputs):
    query_seq, key_seq, value_seq, doc_seq = inputs
    row_block = math.gcd(query_seq.shape[0], ROW_LIMIT)
    outputs = []
    totals = []
    for offset in range(0, query_seq.shape[0], row_block):
        scores = block_scores(query_seq[offset : offset + row_block], key_seq, doc_seq, offset)
        maximum = jnp.max(scores, axis=-1, keepdims=True)
        weights = jnp.exp(scores - maximum)
        denominator = jnp.sum(weights, axis=-1, keepdims=True)
        rounded = (weights / denominator).astype(jnp.bfloat16)
        outputs.append(
            jnp.einsum(
                "hqk,khd->qhd", rounded, value_seq, preferred_element_type=jnp.float32
            ).astype(jnp.bfloat16)
        )
        totals.append((maximum + jnp.log(denominator))[..., 0])
    return (jnp.concatenate(outputs, axis=0), jnp.concatenate(totals, axis=1))


def attend_backward(inputs):
    query_seq, key_seq, value_seq, doc_seq, grad_seq, lse_seq = inputs
    row_block = math.gcd(query_seq.shape[0], ROW_LIMIT)
    factor = 1.0 / math.sqrt(query_seq.shape[-1])
    grad_keys = jnp.zeros(key_seq.shape, jnp.float32)
    grad_values = jnp.zeros(value_seq.shape, jnp.float32)
    grad_rows = []
    for offset in range(0, query_seq.shape[0], row_block):
        query_block = query_seq[offset : offset + row_block]
        grad_block = grad_seq[offset : offset + row_block]
        scores = block_scores(query_block, key_seq, doc_seq, offset)
        weights = jnp.exp(scores - lse_seq[:, offset : offset + row_block, None])
        d_weights = jnp.einsum(
            "qhd,khd->hqk", grad_block, value_seq, preferred_element_type=jnp.float32
        )
        correction = jnp.sum(d_weights * weights, axis=-1, keepdims=True)
        d_scores = (weights * (d_weights - correction)).astype(jnp.bfloat16)
        grad_rows.append(
            jnp.einsum("hqk,khd->qhd", d_scores, key_seq, preferred_element_type=jnp.float32)
            * factor
        )
        grad_keys = (
            grad_keys
            + jnp.einsum("hqk,qhd->khd", d_scores, query_block, preferred_element_type=jnp.float32)
            * factor
        )
        grad_values = grad_values + jnp.einsum(
            "hqk,qhd->khd",
            weights.astype(jnp.bfloat16),
            grad_block,
            preferred_element_type=jnp.float32,
        )
    return (jnp.concatenate(grad_rows, axis=0), grad_keys, grad_values)


def plain_layer(
    tokens,
    doc_ids,
    q_weight,
    k_weight,
    v_weight,
    o_weight,
    q_gain,
    k_gain,
    attn_gain,
    gate_weight,
    up_weight,
    down_weight,
    mlp_gain,
    cotangent,
):
    query_full, key_complete, value_full, output_full, query_gains, key_gains, attn_gains = (
        lax.all_gather(q_weight, "dp", axis=0, tiled=True),
        lax.all_gather(k_weight, "dp", axis=0, tiled=True),
        lax.all_gather(v_weight, "dp", axis=0, tiled=True),
        lax.all_gather(o_weight, "dp", axis=1, tiled=True),
        lax.all_gather(q_gain, "dp", axis=1, tiled=True),
        lax.all_gather(k_gain, "dp", axis=1, tiled=True),
        lax.all_gather(attn_gain, "dp", axis=0, tiled=True),
    )
    gate_full, up_full, down_full, mlp_gains = (
        lax.all_gather(gate_weight, "dp", axis=0, tiled=True),
        lax.all_gather(up_weight, "dp", axis=0, tiled=True),
        lax.all_gather(down_weight, "dp", axis=1, tiled=True),
        lax.all_gather(mlp_gain, "dp", axis=0, tiled=True),
    )
    row_count = tokens.shape[0]
    heads_on_device = q_gain.shape[0]
    local_width = heads_on_device * HEAD_CHANNELS
    sequences = row_count // SEQ_LEN
    seq_shape = (sequences, SEQ_LEN, heads_on_device, HEAD_CHANNELS)
    angles = angles_of(doc_ids, SEQ_LEN, HEAD_CHANNELS)
    doc_seqs = doc_ids.reshape(sequences, SEQ_LEN)
    query_raw = matmul(tokens, query_full)
    key_unnormed = matmul(tokens, key_complete)
    values = matmul(tokens, value_full).astype(jnp.bfloat16)
    query_sq, key_sq = lax.psum(
        (jnp.sum(query_raw * query_raw, axis=1), jnp.sum(key_unnormed * key_unnormed, axis=1)), "mp"
    )
    query_inv = lax.rsqrt(query_sq / D + EPSILON)[:, None]
    key_inverse_norm = lax.rsqrt(key_sq / D + EPSILON)[:, None]
    query_scale = query_gains.reshape(-1)
    key_scale = key_gains.reshape(-1)
    query_rot = rotate(
        (query_raw * query_inv * query_scale).reshape(row_count, heads_on_device, HEAD_CHANNELS),
        angles,
    ).astype(jnp.bfloat16)
    key_rot = rotate(
        (key_unnormed * key_inverse_norm * key_scale).reshape(
            row_count, heads_on_device, HEAD_CHANNELS
        ),
        angles,
    ).astype(jnp.bfloat16)
    query_seqs = query_rot.reshape(seq_shape)
    key_seqs = key_rot.reshape(seq_shape)
    value_seqs = values.reshape(seq_shape)
    attended, lse_all = lax.map(attend_sequence, (query_seqs, key_seqs, value_seqs, doc_seqs))
    attended = attended.reshape(row_count, local_width)
    branch = lax.psum(matmul(attended, output_full), "mp")
    branch_inv = lax.rsqrt(jnp.mean(branch * branch, axis=1, keepdims=True) + EPSILON)
    hidden_state = tokens.astype(jnp.float32) + branch * branch_inv * attn_gains
    hidden_low = hidden_state.astype(jnp.bfloat16)
    gate_act = matmul(hidden_low, gate_full)
    up_part = matmul(hidden_low, up_full)
    product = (jax.nn.silu(gate_act) * up_part).astype(jnp.bfloat16)
    mlp_branch = lax.psum(matmul(product, down_full).astype(jnp.bfloat16), "mp").astype(jnp.float32)
    mlp_inv = lax.rsqrt(jnp.mean(mlp_branch * mlp_branch, axis=1, keepdims=True) + EPSILON)
    block_out = (hidden_state + mlp_branch * mlp_inv * mlp_gains).astype(jnp.bfloat16)
    gate_full, up_full, down_full, mlp_gains = (
        lax.all_gather(gate_weight, "dp", axis=0, tiled=True),
        lax.all_gather(up_weight, "dp", axis=0, tiled=True),
        lax.all_gather(down_weight, "dp", axis=1, tiled=True),
        lax.all_gather(mlp_gain, "dp", axis=0, tiled=True),
    )
    upstream = cotangent.astype(jnp.float32)
    grad_mlp_scale = jnp.sum(upstream * mlp_branch * mlp_inv, axis=0)
    mlp_scaled = mlp_gains * upstream
    mlp_cube = mlp_inv * mlp_inv * mlp_inv
    d_mlp = (
        mlp_inv * mlp_scaled
        - mlp_branch * mlp_cube * jnp.mean(mlp_scaled * mlp_branch, axis=1, keepdims=True)
    ).astype(jnp.bfloat16)
    grad_down = transposed_left(product, d_mlp)
    d_product = transposed_right(d_mlp, down_full)
    sigmoid = jax.nn.sigmoid(gate_act)
    d_gate = (d_product * up_part * sigmoid * (1.0 + gate_act * (1.0 - sigmoid))).astype(
        jnp.bfloat16
    )
    d_up = (d_product * gate_act * sigmoid).astype(jnp.bfloat16)
    grad_gate = transposed_left(hidden_low, d_gate)
    grad_up = transposed_left(hidden_low, d_up)
    mlp_input = transposed_right(d_gate, gate_full) + transposed_right(d_up, up_full)
    d_hidden = upstream + lax.psum(mlp_input.astype(jnp.bfloat16), "mp").astype(jnp.float32)
    mlp_grads = (
        lax.psum_scatter(
            grad_gate.astype(jnp.bfloat16), "dp", scatter_dimension=0, tiled=True
        ).astype(jnp.float32),
        lax.psum_scatter(
            grad_up.astype(jnp.bfloat16), "dp", scatter_dimension=0, tiled=True
        ).astype(jnp.float32),
        lax.psum_scatter(
            grad_down.astype(jnp.bfloat16), "dp", scatter_dimension=1, tiled=True
        ).astype(jnp.float32),
        lax.psum_scatter(
            grad_mlp_scale.astype(jnp.bfloat16), "dp", scatter_dimension=0, tiled=True
        ).astype(jnp.float32),
    )
    query_full, key_complete, value_full, output_full, query_gains, key_gains, attn_gains = (
        lax.all_gather(q_weight, "dp", axis=0, tiled=True),
        lax.all_gather(k_weight, "dp", axis=0, tiled=True),
        lax.all_gather(v_weight, "dp", axis=0, tiled=True),
        lax.all_gather(o_weight, "dp", axis=1, tiled=True),
        lax.all_gather(q_gain, "dp", axis=1, tiled=True),
        lax.all_gather(k_gain, "dp", axis=1, tiled=True),
        lax.all_gather(attn_gain, "dp", axis=0, tiled=True),
    )
    query_scale = query_gains.reshape(-1)
    key_scale = key_gains.reshape(-1)
    grad_attn_scale = jnp.sum(d_hidden * branch * branch_inv, axis=0)
    attn_scaled = attn_gains * d_hidden
    branch_cube = branch_inv * branch_inv * branch_inv
    d_branch = (
        branch_inv * attn_scaled
        - branch * branch_cube * jnp.mean(attn_scaled * branch, axis=1, keepdims=True)
    ).astype(jnp.bfloat16)
    grad_output = transposed_left(attended, d_branch)
    d_attended = transposed_right(d_branch, output_full).astype(jnp.bfloat16)
    grad_qrot, grad_krot, grad_vals = lax.map(
        attend_backward,
        (query_seqs, key_seqs, value_seqs, doc_seqs, d_attended.reshape(seq_shape), lse_all),
    )
    d_values = grad_vals.reshape(row_count, local_width).astype(jnp.bfloat16)
    d_qnorm = rotate_back(
        grad_qrot.reshape(row_count, heads_on_device, HEAD_CHANNELS), angles
    ).reshape(row_count, local_width)
    grad_key_normed = rotate_back(
        grad_krot.reshape(row_count, heads_on_device, HEAD_CHANNELS), angles
    ).reshape(row_count, local_width)
    grad_qscale = jnp.sum(d_qnorm * query_raw * query_inv, axis=0).reshape(
        heads_on_device, HEAD_CHANNELS
    )
    grad_key_rms_factor = jnp.sum(
        grad_key_normed * key_unnormed * key_inverse_norm, axis=0
    ).reshape(heads_on_device, HEAD_CHANNELS)
    query_scaled = query_scale * d_qnorm
    key_scaled = key_scale * grad_key_normed
    query_inner, key_inner = lax.psum(
        (jnp.sum(query_scaled * query_raw, axis=1), jnp.sum(key_scaled * key_unnormed, axis=1)),
        "mp",
    )
    query_cube = query_inv * query_inv * query_inv
    key_cube = key_inverse_norm * key_inverse_norm * key_inverse_norm
    d_query = (
        query_inv * query_scaled - query_raw * query_cube * (query_inner / D)[:, None]
    ).astype(jnp.bfloat16)
    d_key = (
        key_inverse_norm * key_scaled - key_unnormed * key_cube * (key_inner / D)[:, None]
    ).astype(jnp.bfloat16)
    grad_query = transposed_left(tokens, d_query)
    grad_key = transposed_left(tokens, d_key)
    grad_value = transposed_left(tokens, d_values)
    token_back = (
        transposed_right(d_query, query_full)
        + transposed_right(d_key, key_complete)
        + transposed_right(d_values, value_full)
    )
    grad_tokens = (
        d_hidden + lax.psum(token_back.astype(jnp.bfloat16), "mp").astype(jnp.float32)
    ).astype(jnp.bfloat16)
    attn_grads = (
        lax.psum_scatter(
            grad_query.astype(jnp.bfloat16), "dp", scatter_dimension=0, tiled=True
        ).astype(jnp.float32),
        lax.psum_scatter(
            grad_key.astype(jnp.bfloat16), "dp", scatter_dimension=0, tiled=True
        ).astype(jnp.float32),
        lax.psum_scatter(
            grad_value.astype(jnp.bfloat16), "dp", scatter_dimension=0, tiled=True
        ).astype(jnp.float32),
        lax.psum_scatter(
            grad_output.astype(jnp.bfloat16), "dp", scatter_dimension=1, tiled=True
        ).astype(jnp.float32),
        lax.psum_scatter(
            grad_qscale.astype(jnp.bfloat16), "dp", scatter_dimension=1, tiled=True
        ).astype(jnp.float32),
        lax.psum_scatter(
            grad_key_rms_factor.astype(jnp.bfloat16), "dp", scatter_dimension=1, tiled=True
        ).astype(jnp.float32),
        lax.psum_scatter(
            grad_attn_scale.astype(jnp.bfloat16), "dp", scatter_dimension=0, tiled=True
        ).astype(jnp.float32),
    )
    return (
        block_out,
        grad_tokens,
        attn_grads[0],
        attn_grads[1],
        attn_grads[2],
        attn_grads[3],
        attn_grads[4],
        attn_grads[5],
        attn_grads[6],
        mlp_grads[0],
        mlp_grads[1],
        mlp_grads[2],
        mlp_grads[3],
    )


MESH = pl.DeviceIdType.MESH
SUBS = 2
TILE = 256
BLOCK = 256
SMALL = 16


def place_of(index, n):
    odd = lax.rem(index, 2)
    half = lax.div(index, 2)
    return (1 - odd) * half + odd * (n - 1 - half)


def device_at(place, n):
    late = lax.div(place, n // 2)
    return (1 - late) * (2 * place) + late * (2 * (n - 1 - place) + 1)


def holder_of(index, steps, n):
    return device_at(lax.rem(place_of(index, n) + (steps + 2 * n), n), n)


def neighbours(n):
    index = lax.axis_index("dp")
    rank = lax.axis_index("mp")
    core = lax.rem(rank, 2)
    right = {"dp": holder_of(index, 1, n)}
    left = {"dp": holder_of(index, -1, n)}
    twin = {"mp": rank + 1 - 2 * core}
    far = {"mp": lax.rem(rank + 2, 4)}
    return index, core, right, left, twin, far


def greet(targets, meanwhile=None):
    barrier = pltpu.get_barrier_semaphore()
    for target in targets:
        pl.semaphore_signal(barrier, inc=1, device_id=target, device_id_type=MESH)
    if meanwhile is not None:
        meanwhile()
    pl.semaphore_wait(barrier, len(targets))


def exchange(source, target, send, recv, slot, device):
    return pltpu.make_async_remote_copy(
        src_ref=source,
        dst_ref=target,
        send_sem=send.at[slot],
        recv_sem=recv.at[slot],
        device_id=device,
        device_id_type=MESH,
    )


def columns_to_rows(pieces, count):
    lane = lax.broadcasted_iota(jnp.int32, (count, 128), 1)
    spread = jnp.zeros((count, 128), jnp.float32)
    for place, piece in enumerate(pieces):
        spread = jnp.where(lane == place, piece, spread)
    return spread.T[:8]


def rows_to_columns(rows):
    padded = jnp.concatenate([rows] + [jnp.zeros_like(rows)] * 15, axis=0)
    return padded.T


def gather_kernel(
    n,
    query,
    key,
    value,
    output,
    small,
    doc_row,
    frequency,
    down,
    full,
    query_gain,
    key_gain,
    attn_gain,
    mlp_gain,
    cosine,
    sine,
    doc_col,
    down_shard,
    mine,
    down_buf,
    turned_down,
    small_full,
    send,
    recv,
    small_send,
    small_recv,
    load,
    store,
):
    index, core, right, left, twin, far = neighbours(n)
    chunk = query.shape[1]
    local = query.shape[2]
    rows = chunk // SUBS
    count = cosine.shape[0]
    heads = local // HEAD_CHANNELS
    units = down.shape[0]

    loads = [
        pltpu.make_async_copy(
            source, mine.at[:, :, pl.ds(place * local, local)], load.at[place]
        )
        for place, source in enumerate((query, key, value))
    ]
    for copy in loads:
        copy.start()

    def turn_output():
        flipped = output[...].T
        mine[0, :, 3 * local :] = flipped[:chunk]
        mine[1, :, 3 * local :] = flipped[chunk:]

    def hop(way, sub, step, incoming):
        owner = holder_of(index, (step - 1 + incoming) * (2 * way - 1), n)
        span = pl.ds(sub * rows, rows)
        target = full.at[owner, way, span]
        return pltpu.make_async_remote_copy(
            src_ref=mine.at[way, span] if step == 1 and not incoming else target,
            dst_ref=target,
            send_sem=send.at[way, sub, step - 1],
            recv_sem=recv.at[way, sub, step - 1],
            device_id=left if way else right,
            device_id_type=MESH,
        )

    def small_hop(step, incoming):
        target = small_full.at[holder_of(index, 1 - incoming - step, n)]
        source = small if step == 1 and not incoming else target
        return exchange(source, target, small_send, small_recv, step - 1, right)

    greet((right, left), turn_output)
    small_hop(1, 0).start()
    for copy in loads:
        copy.wait()
    for sub in range(SUBS):
        for way in range(2):
            hop(way, sub, 1, 0).start()
    own = pltpu.make_async_copy(mine, full.at[index], store.at[0])
    own.start()
    down_load = pltpu.make_async_copy(down, down_buf, store.at[1])
    down_load.start()
    small_full[index] = small[...]
    docs = doc_row[...].astype(jnp.float32)
    leading = jnp.sum(1.0 - docs, axis=1, keepdims=True)
    doc_col[...] = rows_to_columns(jnp.broadcast_to(docs, (8, count)))

    def table(tile):
        span = pl.ds(pl.multiple_of(tile * 64, 64), 64)
        spot = lax.broadcasted_iota(jnp.int32, (64, HEAD_CHANNELS), 0) + tile * 64
        lane = lax.broadcasted_iota(jnp.int32, (64, HEAD_CHANNELS), 1)
        angles = (spot.astype(jnp.float32) - doc_col[span, 0:1] * leading) * frequency[...]
        cosine[span, :] = jnp.cos(angles)
        wave = jnp.sin(angles)
        sine[span, :] = jnp.where(lane < HEAD_CHANNELS // 2, -wave, wave)

    tiles = count // 64
    for step in range(1, n):
        for sub in range(SUBS):
            for way in range(2):
                hop(way, sub, step, 1).wait_recv()
                if step < n - 1:
                    hop(way, sub, step + 1, 0).start()
        small_hop(step, 1).wait_recv()
        if step < n - 1:
            small_hop(step + 1, 0).start()
        if step <= 4:
            pl.loop((step - 1) * tiles // 4, step * tiles // 4)(table)
        if step == 5:
            down_load.wait()
            for part in range(4):
                span = slice(part * (units // 4), (part + 1) * (units // 4))
                flipped = down_buf[span, :].T
                turned_down[0, :, span] = flipped[:chunk]
                turned_down[1, :, span] = flipped[chunk:]
            down_store = pltpu.make_async_copy(turned_down, down_shard, store.at[2])
            down_store.start()
    lanes = jnp.zeros(small.shape, jnp.float32)
    for owner in range(n):
        part = small_full[owner].astype(jnp.float32)
        lanes = lanes + part
        for row in range(2):
            spot = (2 * owner + row) * 128
            attn_gain[:, spot : spot + 128] = part[8 + row : 9 + row]
            mlp_gain[:, spot : spot + 128] = part[10 + row : 11 + row]
    for head in range(heads):
        spot = head * HEAD_CHANNELS
        query_gain[:, spot : spot + HEAD_CHANNELS] = lanes[head : head + 1]
        key_gain[:, spot : spot + HEAD_CHANNELS] = lanes[4 + head : 5 + head]
    own.wait()
    down_store.wait()
    for step in range(1, n):
        for sub in range(SUBS):
            for way in range(2):
                hop(way, sub, step, 0).wait_send()
        small_hop(step, 0).wait_send()


def kernel_gather(query, key, value, output, small, doc_ids, frequency, down, n):
    rows, local = query.shape
    chunk = rows // 2
    count = doc_ids.shape[0]
    units = down.shape[0]
    low = query.dtype
    full = jnp.float32
    hbm = pl.BlockSpec(memory_space=pl.ANY)
    vmem = pl.BlockSpec(memory_space=pltpu.VMEM)
    dma = pltpu.SemaphoreType.DMA
    shape = jax.ShapeDtypeStruct
    split = [part.reshape(2, chunk, local) for part in (query, key, value)]
    outs = pl.pallas_call(
        functools.partial(gather_kernel, n),
        out_shape=(
            shape((n, 2, chunk, 4 * local), low),
            shape((1, local), full),
            shape((1, local), full),
            shape((1, n * rows), full),
            shape((1, n * rows), full),
            shape((count, HEAD_CHANNELS), full),
            shape((count, HEAD_CHANNELS), full),
            shape((count, 128), full),
            shape((2, chunk, units), low),
        ),
        in_specs=[hbm] * 3 + [vmem] * 4 + [hbm],
        out_specs=(hbm,) + (vmem,) * 7 + (hbm,),
        scratch_shapes=[
            pltpu.VMEM((2, chunk, 4 * local), low),
            pltpu.VMEM((units, rows), low),
            pltpu.VMEM((2, chunk, units), low),
            pltpu.VMEM((n, SMALL, 128), low),
            dma((2, SUBS, n - 1)),
            dma((2, SUBS, n - 1)),
            dma((n - 1,)),
            dma((n - 1,)),
            dma((3,)),
            dma((3,)),
        ],
        compiler_params=pltpu.CompilerParams(
            collective_id=0, has_side_effects=True, vmem_limit_bytes=60 * 2**20
        ),
    )(*split, output, small, doc_ids.reshape(1, count), frequency, down)
    return outs[0].reshape(n * rows, 4 * local), *outs[1:]


def scatter_kernel(
    n,
    grads,
    query_row,
    key_row,
    attn_row,
    mlp_row,
    out_query,
    out_key,
    out_value,
    out_output,
    small_out,
    own,
    inbox,
    tail,
    parts,
    small_inbox,
    small_outbox,
    send,
    recv,
    small_send,
    small_recv,
    own_sem,
):
    index, core, right, left, twin, far = neighbours(n)
    chunk = out_query.shape[1]
    local = out_query.shape[2]
    rows = chunk // SUBS
    heads = local // HEAD_CHANNELS

    def hop(way, sub, step):
        first = grads.at[holder_of(index, 2 * way - 1, n), way, pl.ds(sub * rows, rows)]
        return pltpu.make_async_remote_copy(
            src_ref=first if step == 1 else inbox.at[step - 2, way, sub],
            dst_ref=inbox.at[step - 1, way, sub],
            send_sem=send.at[way, sub, step - 1],
            recv_sem=recv.at[way, sub, step - 1],
            device_id=left if way else right,
            device_id_type=MESH,
        )

    def own_copy(way, sub, step):
        owner = holder_of(index, (1 + step) * (2 * way - 1), n)
        return pltpu.make_async_copy(
            grads.at[owner, way, pl.ds(sub * rows, rows)],
            own.at[way, sub],
            own_sem.at[way, sub],
        )

    def small_hop(step):
        first = parts.at[holder_of(index, -1, n)]
        return exchange(
            first if step == 1 else small_outbox.at[step - 2],
            small_inbox.at[step - 1],
            small_send,
            small_recv,
            step - 1,
            twin if step == n else right,
        )

    greet((right, left, twin))
    for sub in range(SUBS):
        for way in range(2):
            hop(way, sub, 1).start()
            own_copy(way, sub, 1).start()
    for owner in range(n):
        for head in range(heads):
            spot = head * HEAD_CHANNELS
            parts[owner, head : head + 1, :] = query_row[:, spot : spot + HEAD_CHANNELS]
            parts[owner, 4 + head : 5 + head, :] = key_row[:, spot : spot + HEAD_CHANNELS]
        for row in range(2):
            spot = (2 * owner + row) * 128
            parts[owner, 8 + row : 9 + row, :] = attn_row[:, spot : spot + 128]
            parts[owner, 10 + row : 11 + row, :] = mlp_row[:, spot : spot + 128]
        parts[owner, 12:16, :] = jnp.zeros((4, 128), jnp.float32)
    small_hop(1).start()
    for step in range(1, n):
        for sub in range(SUBS):
            for way in range(2):
                own_copy(way, sub, step).wait()
                hop(way, sub, step).wait_recv()

                @pl.loop(0, rows // 16)
                def _(tile, way=way, sub=sub, step=step):
                    near = pl.ds(pl.multiple_of(tile * 16, 16), 16)
                    got = inbox[step - 1, way, sub, near, :]
                    held = own[way, sub, near, :]
                    if step < n - 1:
                        inbox[step - 1, way, sub, near, :] = got + held
                    else:
                        total = got.astype(jnp.float32) + held.astype(jnp.float32)
                        wide = pl.ds(pl.multiple_of(sub * rows + tile * 16, 16), 16)
                        out_query[way, wide, :] = total[:, :local]
                        out_key[way, wide, :] = total[:, local : 2 * local]
                        out_value[way, wide, :] = total[:, 2 * local : 3 * local]
                        deep = pl.ds(
                            pl.multiple_of(way * chunk + sub * rows + tile * 16, 16), 16
                        )
                        tail[deep, :] = total[:, 3 * local :]

                if step < n - 1:
                    hop(way, sub, step + 1).start()
                    own_copy(way, sub, step + 1).start()
        if step < n - 1:
            small_hop(step).wait_recv()
            owner = holder_of(index, -1 - step, n)
            small_outbox[step - 1] = small_inbox[step - 1] + parts[owner]
            small_hop(step + 1).start()
    small_hop(n - 1).wait_recv()
    small_outbox[n - 2] = small_inbox[n - 2] + parts[index]
    small_hop(n).start()
    out_output[...] = tail[...].T
    small_hop(n).wait_recv()
    line = lax.broadcasted_iota(jnp.int32, small_out.shape, 0)
    small_out[...] = small_outbox[n - 2] + jnp.where(line >= 8, small_inbox[n - 1], 0.0)
    for step in range(1, n):
        for sub in range(SUBS):
            for way in range(2):
                hop(way, sub, step).wait_send()
        small_hop(step).wait_send()
    small_hop(n).wait_send()


def kernel_scatter(grads, query_row, key_row, attn_row, mlp_row, n):
    rows, width = grads.shape[0] // n, grads.shape[1]
    chunk, local = rows // 2, width // 4
    deep = chunk // SUBS
    full = jnp.float32
    vmem = pl.BlockSpec(memory_space=pltpu.VMEM)
    dma = pltpu.SemaphoreType.DMA
    shape = jax.ShapeDtypeStruct
    outs = pl.pallas_call(
        functools.partial(scatter_kernel, n),
        out_shape=(shape((2, chunk, local), full),) * 3
        + (shape((local, rows), full), shape((SMALL, 128), full)),
        in_specs=[pl.BlockSpec(memory_space=pl.ANY)] + [vmem] * 4,
        out_specs=(vmem,) * 5,
        scratch_shapes=[
            pltpu.VMEM((2, SUBS, deep, width), grads.dtype),
            pltpu.VMEM((n - 1, 2, SUBS, deep, width), grads.dtype),
            pltpu.VMEM((rows, local), full),
            pltpu.VMEM((n, SMALL, 128), full),
            pltpu.VMEM((n, SMALL, 128), full),
            pltpu.VMEM((n - 1, SMALL, 128), full),
            dma((2, SUBS, n - 1)),
            dma((2, SUBS, n - 1)),
            dma((n,)),
            dma((n,)),
            dma((2, SUBS)),
        ],
        compiler_params=pltpu.CompilerParams(
            collective_id=1, has_side_effects=True, vmem_limit_bytes=60 * 2**20
        ),
    )(grads.reshape(n, 2, chunk, width), query_row, key_row, attn_row, mlp_row)
    return tuple(part.reshape(rows, local) for part in outs[:3]) + outs[3:]


def turned(vectors, cosine, sine):
    return vectors * cosine + pltpu.roll(vectors, HEAD_CHANNELS // 2, 1) * sine


def masked_scores(query, key, doc_col, doc_row, block):
    length = key.shape[0]
    scores = lax.dot_general(
        query, key, (((1,), (1,)), ((), ())), preferred_element_type=jnp.float32
    ) * (1.0 / math.sqrt(HEAD_CHANNELS))
    row = lax.broadcasted_iota(jnp.int32, scores.shape, 0) + block * BLOCK
    col = lax.broadcasted_iota(jnp.int32, scores.shape, 1)
    own = doc_col[block * BLOCK : (block + 1) * BLOCK, 0:1]
    same = own == doc_row[:, :length].astype(jnp.float32)
    return jnp.where((col <= row) & same, scores, MASKED)


def attend_kernel(
    n,
    tokens,
    attn_full,
    gate_shard,
    up_shard,
    cosine,
    sine,
    doc_col,
    doc_row,
    query_gain,
    key_gain,
    attn_gain,
    gate_full,
    up_full,
    query_raw_out,
    key_raw_out,
    query_rot_out,
    key_rot_out,
    value_out,
    attended_out,
    totals,
    inverses,
    branch_out,
    hidden_out,
    hidden_low,
    lhs,
    weights,
    query_raw,
    key_raw,
    query_rot,
    key_rot,
    value,
    attended,
    mixed,
    twin_in,
    pair,
    far_in,
    branch,
    half_buf,
    low_buf,
    stat,
    ring_send,
    ring_recv,
    stat_send,
    stat_recv,
    twin_send,
    twin_recv,
    far_send,
    far_recv,
    join_send,
    join_recv,
    load_sem,
    store_sem,
):
    index, core, right, left, twin, far = neighbours(n)
    count, width = lhs.shape
    half = count // 2
    local = query_raw.shape[1]
    heads = local // HEAD_CHANNELS
    blocks = width // TILE
    shards = (gate_shard, up_shard)
    fulls = (gate_full, up_full)
    right_side = (((1,), (1,)), ((), ()))

    def ring(way, unit, step, incoming):
        owner = holder_of(index, (step - 1 + incoming) * (2 * way - 1), n)
        target = fulls[unit].at[owner, way]
        return pltpu.make_async_remote_copy(
            src_ref=shards[unit].at[way] if step == 1 and not incoming else target,
            dst_ref=target,
            send_sem=ring_send.at[way, unit, step - 1],
            recv_sem=ring_recv.at[way, unit, step - 1],
            device_id=left if way else right,
            device_id_type=MESH,
        )

    events = [(step, unit) for step in range(1, n) for unit in range(2)]

    def serve():
        step, unit = events.pop(0)
        for way in range(2):
            ring(way, unit, step, 1).wait_recv()
            if step < n - 1:
                ring(way, unit, step + 1, 0).start()

    greet((right, left, twin, far))
    for unit in range(2):
        for way in range(2):
            ring(way, unit, 1, 0).start()
    loads = [
        pltpu.make_async_copy(tokens, lhs, load_sem.at[0]),
        pltpu.make_async_copy(attn_full, weights, load_sem.at[1]),
        pltpu.make_async_copy(
            tokens.at[pl.ds(pl.multiple_of(core * half, half), half)], half_buf, load_sem.at[2]
        ),
        pltpu.make_async_copy(gate_shard, gate_full.at[index], load_sem.at[3]),
        pltpu.make_async_copy(up_shard, up_full.at[index], load_sem.at[4]),
    ]
    for copy in loads:
        copy.start()
    loads[0].wait()
    loads[1].wait()

    def project(target, start):
        for tile in range(local // TILE):
            cols = slice(start + tile * TILE, start + (tile + 1) * TILE)
            target[:, tile * TILE : (tile + 1) * TILE] = jnp.dot(
                lhs[...], weights[:, cols], preferred_element_type=jnp.float32
            ).astype(target.dtype)

    project(query_raw, 0)
    project(key_raw, local)
    squares = [
        jnp.sum(raw[...] * raw[...], axis=1, keepdims=True) for raw in (query_raw, key_raw)
    ]
    stat[0] = columns_to_rows(squares, count)
    first = exchange(stat.at[0], stat.at[1], stat_send, stat_recv, 0, twin)
    first.start()
    project(value, 2 * local)
    first.wait()
    stat[2] = stat[0] + stat[1]
    second = exchange(stat.at[2], stat.at[3], stat_send, stat_recv, 1, far)
    second.start()
    serve()
    second.wait()
    inverses[...] = lax.rsqrt(rows_to_columns(stat[2] + stat[3]) / width + EPSILON)

    @pl.loop(0, heads)
    def _(head):
        cols = pl.ds(pl.multiple_of(head * HEAD_CHANNELS, HEAD_CHANNELS), HEAD_CHANNELS)
        for place, (raw, gain, out) in enumerate(
            ((query_raw, query_gain, query_rot), (key_raw, key_gain, key_rot))
        ):
            normed = raw[:, cols] * inverses[:, place : place + 1] * gain[:, cols]
            out[:, cols] = turned(normed, cosine[...], sine[...]).astype(jnp.bfloat16)

    stores = [
        pltpu.make_async_copy(source, target, store_sem.at[place])
        for place, (source, target) in enumerate(
            (
                (query_raw, query_raw_out),
                (key_raw, key_raw_out),
                (query_rot, query_rot_out),
                (key_rot, key_rot_out),
                (value, value_out),
            )
        )
    ]
    for copy in stores:
        copy.start()
    serve()
    totals[...] = jnp.zeros_like(totals)

    @pl.loop(0, heads)
    def _(head):
        cols = pl.ds(pl.multiple_of(head * HEAD_CHANNELS, HEAD_CHANNELS), HEAD_CHANNELS)
        lane = lax.broadcasted_iota(jnp.int32, (BLOCK, 128), 1)
        for block in range(count // BLOCK):
            span = slice(block * BLOCK, (block + 1) * BLOCK)
            length = (block + 1) * BLOCK
            scores = masked_scores(
                query_rot[span, cols], key_rot[:length, cols], doc_col, doc_row, block
            )
            maximum = jnp.max(scores, axis=1, keepdims=True)
            powers = jnp.exp(scores - maximum)
            denominator = jnp.sum(powers, axis=1, keepdims=True)
            rounded = (powers * (1.0 / denominator)).astype(jnp.bfloat16)
            attended[span, cols] = jnp.dot(
                rounded, value[:length, cols], preferred_element_type=jnp.float32
            ).astype(jnp.bfloat16)
            totals[span, :] = jnp.where(
                lane == head, maximum + jnp.log(denominator), totals[span, :]
            )

    stores.append(pltpu.make_async_copy(attended, attended_out, store_sem.at[5]))
    stores[5].start()
    serve()

    def twin_copy(tile):
        span = pl.ds(pl.multiple_of((1 - core) * half, half), half)
        return exchange(
            mixed.at[tile % 4, span], twin_in.at[tile % 4], twin_send, twin_recv, tile, twin
        )

    def far_copy(tile):
        return exchange(pair.at[tile], far_in.at[tile], far_send, far_recv, tile, far)

    def output_tile(tile):
        span = slice(tile * TILE, (tile + 1) * TILE)
        mixed[tile % 4] = lax.dot_general(
            attended[...],
            weights[span, 3 * local :],
            right_side,
            preferred_element_type=jnp.float32,
        ).astype(jnp.bfloat16)
        twin_copy(tile).start()

    def add_twin(tile):
        twin_copy(tile).wait_recv()

        @pl.loop(0, half // 32)
        def _(row):
            span = pl.ds(pl.multiple_of(row * 32, 32), 32)
            mine = pl.ds(pl.multiple_of(core * half + row * 32, 32), 32)
            total = mixed[tile % 4, mine, :].astype(jnp.float32) + twin_in[
                tile % 4, span, :
            ].astype(jnp.float32)
            pair[tile, span, :] = total.astype(jnp.bfloat16)

        far_copy(tile).start()
        twin_copy(tile).wait_send()

    def add_far(tile):
        far_copy(tile).wait_recv()

        @pl.loop(0, half // 32)
        def _(row):
            span = pl.ds(pl.multiple_of(row * 32, 32), 32)
            branch[span, tile * TILE : (tile + 1) * TILE] = pair[tile, span, :].astype(
                jnp.float32
            ) + far_in[tile, span, :].astype(jnp.float32)

    for tile in range(blocks):
        output_tile(tile)
        if tile >= 1:
            add_twin(tile - 1)
    add_twin(blocks - 1)
    serve()
    for tile in range(blocks):
        add_far(tile)
        if tile % 2 == 1:
            serve()
    loads[2].wait()

    def finish(tile):
        span = pl.ds(pl.multiple_of(tile * 16, 16), 16)
        mix = branch[span, :]
        inverse = lax.rsqrt(jnp.sum(mix * mix, axis=1, keepdims=True) / width + EPSILON)
        state = half_buf[span, :].astype(jnp.float32) + mix * inverse * attn_gain[...]
        low_buf[span, :] = state.astype(jnp.bfloat16)
        hidden_out[span, :] = state

    def join(part, kind):
        span = pl.ds(part * (half // 4), half // 4)
        if kind == 2:
            return pltpu.make_async_copy(
                low_buf.at[span], hidden_low.at[core, span], store_sem.at[6 + part]
            )
        target = hidden_low.at[1 - core if kind else core, span]
        return exchange(
            target if kind else low_buf.at[span], target, join_send, join_recv, part, twin
        )

    for part in range(4):
        pl.loop(part * (half // 64), (part + 1) * (half // 64))(finish)
        join(part, 0).start()
        join(part, 2).start()
    stores.append(pltpu.make_async_copy(branch, branch_out, store_sem.at[10]))
    stores[6].start()
    while events:
        serve()
    for part in range(4):
        join(part, 1).wait_recv()
        join(part, 0).wait_send()
        join(part, 2).wait()
    for copy in stores + loads[3:]:
        copy.wait()
    for tile in range(blocks):
        far_copy(tile).wait_send()
    for step in range(1, n):
        for unit in range(2):
            for way in range(2):
                ring(way, unit, step, 0).wait_send()


def kernel_attend(
    tokens,
    attn_full,
    gate_shard,
    up_shard,
    cosine,
    sine,
    doc_col,
    doc_ids,
    query_gain,
    key_gain,
    attn_gain,
    n,
):
    count, width = tokens.shape
    local = query_gain.shape[1]
    units = gate_shard.shape[1]
    half = count // 2
    chunk = width // n // 2
    blocks = width // TILE
    low = jnp.bfloat16
    full = jnp.float32
    hbm = pl.BlockSpec(memory_space=pl.ANY)
    vmem = pl.BlockSpec(memory_space=pltpu.VMEM)
    dma = pltpu.SemaphoreType.DMA
    shape = jax.ShapeDtypeStruct
    outs = pl.pallas_call(
        functools.partial(attend_kernel, n),
        out_shape=(
            shape((n, 2, chunk, units), low),
            shape((n, 2, chunk, units), low),
            shape((count, local), full),
            shape((count, local), full),
            shape((count, local), low),
            shape((count, local), low),
            shape((count, local), low),
            shape((count, local), low),
            shape((count, 128), full),
            shape((count, 128), full),
            shape((half, width), full),
            shape((half, width), full),
            shape((2, half, width), low),
        ),
        in_specs=[hbm] * 4 + [vmem] * 7,
        out_specs=(hbm,) * 8 + (vmem,) * 2 + (hbm, vmem, hbm),
        scratch_shapes=[
            pltpu.VMEM((count, width), low),
            pltpu.VMEM((width, 4 * local), low),
            pltpu.VMEM((count, local), full),
            pltpu.VMEM((count, local), full),
            pltpu.VMEM((count, local), low),
            pltpu.VMEM((count, local), low),
            pltpu.VMEM((count, local), low),
            pltpu.VMEM((count, local), low),
            pltpu.VMEM((4, count, TILE), low),
            pltpu.VMEM((4, half, TILE), low),
            pltpu.VMEM((blocks, half, TILE), low),
            pltpu.VMEM((blocks, half, TILE), low),
            pltpu.VMEM((half, width), full),
            pltpu.VMEM((half, width), low),
            pltpu.VMEM((half, width), low),
            pltpu.VMEM((4, 8, count), full),
            dma((2, 2, n - 1)),
            dma((2, 2, n - 1)),
            dma((2,)),
            dma((2,)),
            dma((blocks,)),
            dma((blocks,)),
            dma((blocks,)),
            dma((blocks,)),
            dma((4,)),
            dma((4,)),
            dma((5,)),
            dma((11,)),
        ],
        compiler_params=pltpu.CompilerParams(
            collective_id=4, has_side_effects=True, vmem_limit_bytes=58 * 2**20
        ),
    )(
        tokens,
        attn_full,
        gate_shard.reshape(2, chunk, units),
        up_shard.reshape(2, chunk, units),
        cosine,
        sine,
        doc_col,
        doc_ids.reshape(1, count),
        query_gain,
        key_gain,
        attn_gain,
    )
    return (
        outs[0].reshape(width, units),
        outs[1].reshape(width, units),
        *outs[2:12],
        outs[12].reshape(count, width),
    )


def feed_kernel(
    n,
    hidden_low,
    gate_full,
    up_full,
    down_shard,
    hidden,
    upstream,
    gains,
    product_out,
    gate_slope,
    silu_out,
    down_full,
    d_mlp,
    block_half,
    gain_grad,
    lhs,
    product,
    held,
    gate_tile,
    up_tile,
    slope_tile,
    silu_tile,
    twin_out,
    twin_in,
    pair,
    far_in,
    branch,
    hidden_buf,
    upstream_buf,
    d_buf,
    block_buf,
    gain_sum,
    ring_send,
    ring_recv,
    twin_send,
    twin_recv,
    far_send,
    far_recv,
    join_send,
    join_recv,
    load_sem,
    tile_sem,
    stage_sem,
    store_sem,
):
    index, core, right, left, twin, far = neighbours(n)
    half = hidden.shape[0]
    chunk = held.shape[2]
    rows = chunk // SUBS
    tiles = product.shape[1] // TILE
    width = branch.shape[1]

    loads = [
        pltpu.make_async_copy(hidden_low, lhs, load_sem.at[0]),
        pltpu.make_async_copy(down_shard, held.at[index], load_sem.at[1]),
        pltpu.make_async_copy(hidden, hidden_buf, load_sem.at[2]),
        pltpu.make_async_copy(
            upstream.at[pl.ds(pl.multiple_of(core * half, half), half)],
            upstream_buf,
            load_sem.at[3],
        ),
    ]

    def weight_copies(tile, slot):
        cols = pl.ds(pl.multiple_of(tile * TILE, TILE), TILE)
        return (
            pltpu.make_async_copy(gate_full.at[:, cols], gate_tile.at[slot], tile_sem.at[slot, 0]),
            pltpu.make_async_copy(up_full.at[:, cols], up_tile.at[slot], tile_sem.at[slot, 1]),
        )

    def stage_copies(tile, slot):
        cols = pl.ds(pl.multiple_of(tile * TILE, TILE), TILE)
        return (
            pltpu.make_async_copy(slope_tile.at[slot], gate_slope.at[:, cols], stage_sem.at[slot, 0]),
            pltpu.make_async_copy(silu_tile.at[slot], silu_out.at[:, cols], stage_sem.at[slot, 1]),
        )

    def ring(way, sub, step, incoming):
        owner = holder_of(index, (step - 1 + incoming) * (2 * way - 1), n)
        span = pl.ds(sub * rows, rows)
        target = held.at[owner, way, span]
        return pltpu.make_async_remote_copy(
            src_ref=down_shard.at[way, span] if step == 1 and not incoming else target,
            dst_ref=target,
            send_sem=ring_send.at[way, sub, step - 1],
            recv_sem=ring_recv.at[way, sub, step - 1],
            device_id=left if way else right,
            device_id_type=MESH,
        )

    def serve(step, sub):
        for way in range(2):
            ring(way, sub, step, 1).wait_recv()
            if step < n - 1:
                ring(way, sub, step + 1, 0).start()

    def columns(sub):
        return pl.ds(0, 2 * chunk) if sub is None else pl.ds(sub * 2 * rows, 2 * rows)

    def twin_copy(step, sub=None):
        return exchange(
            twin_out.at[step, :, columns(sub)],
            twin_in.at[step, :, columns(sub)],
            twin_send,
            twin_recv,
            step + (sub or 0),
            twin,
        )

    def far_copy(step, sub=None):
        return exchange(
            pair.at[step, :, columns(sub)],
            far_in.at[step, :, columns(sub)],
            far_send,
            far_recv,
            step + (sub or 0),
            far,
        )

    for copy in loads:
        copy.start()
    for copy in weight_copies(0, 0):
        copy.start()
    greet((right, left, twin, far))
    for sub in range(SUBS):
        for way in range(2):
            ring(way, sub, 1, 0).start()
    loads[0].wait()

    def feed_tile(tile):
        slot = lax.rem(tile, 2)
        for copy in weight_copies(tile, slot):
            copy.wait()

        @pl.when(tile + 1 < tiles)
        def _():
            for copy in weight_copies(tile + 1, 1 - slot):
                copy.start()

        @pl.when(tile >= 2)
        def _():
            for copy in stage_copies(tile - 2, slot):
                copy.wait()

        cols = pl.ds(pl.multiple_of(tile * TILE, TILE), TILE)

        gate = jnp.dot(lhs[...], gate_tile[slot], preferred_element_type=jnp.float32)
        up = jnp.dot(lhs[...], up_tile[slot], preferred_element_type=jnp.float32)
        sigmoid = jax.nn.sigmoid(gate)
        silu = gate * sigmoid
        product[:, cols] = (silu * up).astype(jnp.bfloat16)
        slope_tile[slot] = (up * sigmoid * (1.0 + gate * (1.0 - sigmoid))).astype(jnp.bfloat16)
        silu_tile[slot] = silu.astype(jnp.bfloat16)

        for copy in stage_copies(tile, slot):
            copy.start()

    events = [(step, sub) for step in range(1, n) for sub in range(SUBS)]
    groups = 4
    for group in range(groups):
        pl.loop(group * tiles // groups, (group + 1) * tiles // groups)(feed_tile)
        serve(*events.pop(0))
    stores = [pltpu.make_async_copy(product, product_out, store_sem.at[0])]
    stores[0].start()
    loads[1].wait()

    def multiply(step, sub=None):
        part = slice(None) if sub is None else slice(sub * rows, (sub + 1) * rows)
        first = held[holder_of(index, -step, n), 0, part]
        second = held[holder_of(index, step, n), 1, part]
        rhs = jnp.concatenate([first, second], axis=0)
        contract = (((1,), (1,)), ((), ()))
        span = pl.ds(pl.multiple_of((1 - core) * half, half), half)
        twin_out[step, :, columns(sub)] = lax.dot_general(
            product[span, :], rhs, contract, preferred_element_type=jnp.float32
        ).astype(jnp.bfloat16)
        twin_copy(step, sub).start()
        span = pl.ds(pl.multiple_of(core * half, half), half)
        pair[step, :, columns(sub)] = lax.dot_general(
            product[span, :], rhs, contract, preferred_element_type=jnp.float32
        ).astype(jnp.bfloat16)

    def add_twin(step, sub=None):
        twin_copy(step, sub).wait_recv()
        cols = columns(sub)

        @pl.loop(0, half // 32, unroll=4)
        def _(tile):
            span = pl.ds(pl.multiple_of(tile * 32, 32), 32)
            total = pair[step, span, cols].astype(jnp.float32) + twin_in[
                step, span, cols
            ].astype(jnp.float32)
            pair[step, span, cols] = total.astype(jnp.bfloat16)

        far_copy(step, sub).start()

    def add_far(step):
        if step < n - 1:
            far_copy(step).wait_recv()
        else:
            for sub in range(SUBS):
                far_copy(step, sub).wait_recv()
        first = pl.multiple_of(holder_of(index, -step, n) * 2 * chunk, chunk)
        second = pl.multiple_of(holder_of(index, step, n) * 2 * chunk + chunk, chunk)

        @pl.loop(0, half // 32, unroll=4)
        def _(tile):
            span = pl.ds(pl.multiple_of(tile * 32, 32), 32)
            total = pair[step, span, :].astype(jnp.float32) + far_in[step, span, :].astype(
                jnp.float32
            )
            if step < n - 1:
                sides = total[:, :chunk], total[:, chunk:]
            else:
                sides = [
                    jnp.concatenate(
                        [
                            total[:, (2 * sub + way) * rows : (2 * sub + way + 1) * rows]
                            for sub in range(SUBS)
                        ],
                        axis=1,
                    )
                    for way in range(2)
                ]
            branch[span, pl.ds(first, chunk)] = sides[0]
            branch[span, pl.ds(second, chunk)] = sides[1]

    def serve_until(step, sub):
        while events and events[0] <= (step, sub):
            serve(*events.pop(0))

    for step in range(n - 1):
        serve_until(step, SUBS - 1)
        multiply(step)
        if step >= 1:
            if step <= 3:
                add_twin(step - 1)
            if step >= 3:
                add_twin(step)
            if step >= 2:
                add_far(step - 2)
        if step < 2 and events:
            serve(*events.pop(0))
    for sub in range(SUBS):
        serve_until(n - 1, sub)
        multiply(n - 1, sub)
        add_twin(n - 1, sub)
        if sub == 0:
            add_far(n - 3)
    stores.append(pltpu.make_async_copy(held, down_full, store_sem.at[1]))
    stores[1].start()
    add_far(n - 2)
    loads[2].wait()
    loads[3].wait()
    gain_sum[...] = jnp.zeros_like(gain_sum)
    add_far(n - 1)

    def finish(tile):
        span = pl.ds(pl.multiple_of(tile * 16, 16), 16)
        mixed = branch[span, :]
        scale = gains[...]
        inverse = lax.rsqrt(jnp.sum(mixed * mixed, axis=1, keepdims=True) / width + EPSILON)
        grad = upstream_buf[span, :].astype(jnp.float32)
        scaled = scale * grad
        mean = jnp.sum(scaled * mixed, axis=1, keepdims=True) / width
        normed = mixed * inverse
        d_buf[span, :] = (
            inverse * scaled - mixed * (inverse * inverse * inverse * mean)
        ).astype(jnp.bfloat16)
        block_buf[span, :] = (hidden_buf[span, :] + normed * scale).astype(jnp.bfloat16)
        terms = grad * normed
        gain_sum[...] += terms[:8] + terms[8:]

    def join(part, own):
        span = pl.ds(part * (half // 4), half // 4)
        if own:
            return pltpu.make_async_copy(d_buf.at[span], d_mlp.at[core, span], store_sem.at[3 + part])
        return pltpu.make_async_remote_copy(
            src_ref=d_buf.at[span],
            dst_ref=d_mlp.at[core, span],
            send_sem=join_send.at[part],
            recv_sem=join_recv.at[part],
            device_id=twin,
            device_id_type=MESH,
        )

    def joined(part):
        span = pl.ds(part * (half // 4), half // 4)
        target = d_mlp.at[1 - core, span]
        return pltpu.make_async_remote_copy(
            src_ref=target,
            dst_ref=target,
            send_sem=join_send.at[part],
            recv_sem=join_recv.at[part],
            device_id=twin,
            device_id_type=MESH,
        )

    for part in range(4):
        pl.loop(part * (half // 64), (part + 1) * (half // 64), unroll=2)(finish)
        join(part, False).start()
        join(part, True).start()
    stores.append(pltpu.make_async_copy(block_buf, block_half, store_sem.at[2]))
    stores[2].start()
    gain_grad[...] = jnp.sum(gain_sum[...], axis=0, keepdims=True)
    for part in range(4):
        joined(part).wait_recv()
        join(part, False).wait_send()
        join(part, True).wait()
    for copy in stores:
        copy.wait()
    for tile in (tiles - 2, tiles - 1):
        for copy in stage_copies(tile, tile % 2):
            copy.wait()
    for step in range(n + 1):
        name = (step, None) if step < n - 1 else (n - 1, step - n + 1)
        twin_copy(*name).wait_send()
        far_copy(*name).wait_send()
    for step in range(1, n):
        for sub in range(SUBS):
            for way in range(2):
                ring(way, sub, step, 0).wait_send()


def kernel_feed(hidden_low, gate_full, up_full, down_shard, hidden, upstream, gains, n):
    count, width = hidden_low.shape
    units = gate_full.shape[1]
    half = count // 2
    chunk = width // n // 2
    rows = chunk // SUBS
    low = jnp.bfloat16
    hbm = pl.BlockSpec(memory_space=pl.ANY)
    vmem = pl.BlockSpec(memory_space=pltpu.VMEM)
    dma = pltpu.SemaphoreType.DMA
    product, slope, silu, down_full, d_mlp, block, gain_grad = pl.pallas_call(
        functools.partial(feed_kernel, n),
        out_shape=(
            jax.ShapeDtypeStruct((count, units), low),
            jax.ShapeDtypeStruct((count, units), low),
            jax.ShapeDtypeStruct((count, units), low),
            jax.ShapeDtypeStruct((n, 2, chunk, units), low),
            jax.ShapeDtypeStruct((2, half, width), low),
            jax.ShapeDtypeStruct((half, width), low),
            jax.ShapeDtypeStruct((1, width), jnp.float32),
        ),
        in_specs=[hbm] * 6 + [vmem],
        out_specs=(hbm,) * 6 + (vmem,),
        scratch_shapes=[
            pltpu.VMEM((count, width), low),
            pltpu.VMEM((count, units), low),
            pltpu.VMEM((n, 2, chunk, units), low),
            pltpu.VMEM((2, width, TILE), low),
            pltpu.VMEM((2, width, TILE), low),
            pltpu.VMEM((2, count, TILE), low),
            pltpu.VMEM((2, count, TILE), low),
            pltpu.VMEM((n, half, 2 * chunk), low),
            pltpu.VMEM((n, half, 2 * chunk), low),
            pltpu.VMEM((n, half, 2 * chunk), low),
            pltpu.VMEM((n, half, 2 * chunk), low),
            pltpu.VMEM((half, width), jnp.float32),
            pltpu.VMEM((half, width), jnp.float32),
            pltpu.VMEM((half, width), low),
            pltpu.VMEM((half, width), low),
            pltpu.VMEM((half, width), low),
            pltpu.VMEM((8, width), jnp.float32),
            dma((2, SUBS, n - 1)),
            dma((2, SUBS, n - 1)),
            dma((n + 1,)),
            dma((n + 1,)),
            dma((n + 1,)),
            dma((n + 1,)),
            dma((4,)),
            dma((4,)),
            dma((4,)),
            dma((2, 2)),
            dma((2, 2)),
            dma((7,)),
        ],
        compiler_params=pltpu.CompilerParams(
            collective_id=2, has_side_effects=True, vmem_limit_bytes=58 * 2**20
        ),
    )(
        hidden_low,
        gate_full,
        up_full,
        down_shard,
        hidden,
        upstream,
        gains,
    )
    return (
        product,
        slope,
        silu,
        down_full.reshape(width, units),
        d_mlp.reshape(count, width),
        block,
        gain_grad,
    )


def back_kernel(
    n,
    d_mlp,
    product,
    down_full,
    gate_slope,
    silu_in,
    gate_full,
    up_full,
    hidden_low,
    block_half,
    out_down,
    d_hidden_out,
    d_gate_out,
    d_up_out,
    head_grads,
    block_out,
    d_out,
    prod,
    d_gate,
    d_up,
    down_tile,
    slope_tile,
    silu_tile,
    gate_tile,
    up_tile,
    hidden_tile,
    first,
    own,
    inbox,
    mixed,
    twin_in,
    pair,
    far_in,
    d_hidden,
    stage,
    ring_send,
    ring_recv,
    twin_send,
    twin_recv,
    far_send,
    far_recv,
    join_send,
    join_recv,
    load_sem,
    down_sem,
    weight_sem,
    hidden_sem,
    stage_sem,
    store_sem,
):
    index, core, right, left, twin, far = neighbours(n)
    side = d_out.shape[2]
    width, units = d_out.shape[3], prod.shape[3]
    pack = 2 * side
    half = d_hidden.shape[0]
    chunk = inbox.shape[3] * SUBS
    rows = chunk // SUBS
    tiles = units // TILE
    blocks = width // TILE
    left_side = (((0,), (0,)), ((), ()))
    right_side = (((1,), (1,)), ((), ()))

    def tile_span(tile):
        return pl.ds(pl.multiple_of(tile * TILE, TILE), TILE)

    def down_copies(group, tile, slot):
        cols = tile_span(tile)
        return (
            pltpu.make_async_copy(down_full.at[:, cols], down_tile.at[slot], down_sem.at[slot, 0]),
            pltpu.make_async_copy(
                gate_slope.at[:, group, :, cols], slope_tile.at[slot], down_sem.at[slot, 1]
            ),
            pltpu.make_async_copy(
                silu_in.at[:, group, :, cols], silu_tile.at[slot], down_sem.at[slot, 2]
            ),
        )

    def weight_copies(tile, slot):
        span = tile_span(tile)
        return (
            pltpu.make_async_copy(gate_full.at[span], gate_tile.at[slot], weight_sem.at[slot, 0]),
            pltpu.make_async_copy(up_full.at[span], up_tile.at[slot], weight_sem.at[slot, 1]),
        )

    def hidden_copy(group, way):
        owner = holder_of(index, 2 * way - 1, n)
        start = pl.multiple_of(owner * 2 * chunk + way * chunk, chunk)
        return pltpu.make_async_copy(
            hidden_low.at[:, group, :, pl.ds(start, chunk)],
            hidden_tile.at[group, :, :, pl.ds(way * chunk, chunk)],
            hidden_sem.at[group, way],
        )

    def stage_copy(which):
        return pltpu.make_async_copy(stage.at[which], head_grads.at[which], stage_sem.at[which])

    def block_copy(kind):
        if kind == 2:
            return pltpu.make_async_copy(block_half, block_out.at[core], store_sem.at[5])
        target = block_out.at[1 - core if kind else core]
        return exchange(target if kind else block_half, target, join_send, join_recv, 0, twin)

    def ring(way, sub, step):
        return pltpu.make_async_remote_copy(
            src_ref=first.at[way, pl.ds(sub * rows, rows)]
            if step == 1
            else inbox.at[step - 2, way, sub],
            dst_ref=inbox.at[step - 1, way, sub],
            send_sem=ring_send.at[way, sub, step - 1],
            recv_sem=ring_recv.at[way, sub, step - 1],
            device_id=left if way else right,
            device_id_type=MESH,
        )

    def grad_block(step):
        cols = []
        for way in range(2):
            owner = holder_of(index, (1 + step) * (2 * way - 1), n)
            start = pl.multiple_of(owner * 2 * chunk + way * chunk, chunk)
            cols.append(d_out[:, :, :, pl.ds(start, chunk)].reshape(2 * pack, chunk))
        block = lax.dot_general(
            jnp.concatenate(cols, axis=1),
            prod[...].reshape(2 * pack, units),
            left_side,
            preferred_element_type=jnp.float32,
        ).astype(jnp.bfloat16)
        target = first if step == 0 else own.at[step % 2]
        target[0] = block[:chunk]
        target[1] = block[chunk:]

    def serve(step, sub):
        for way in range(2):
            ring(way, sub, step).wait_recv()

            @pl.loop(0, rows // 16)
            def _(tile, way=way):
                near = pl.ds(pl.multiple_of(tile * 16, 16), 16)
                mine = pl.ds(pl.multiple_of(sub * rows + tile * 16, 16), 16)
                got = inbox[step - 1, way, sub, near, :]
                held = own[step % 2, way, mine, :]
                if step < n - 1:
                    inbox[step - 1, way, sub, near, :] = got + held
                else:
                    out_down[way, mine, :] = got.astype(jnp.float32) + held.astype(jnp.float32)

            if step < n - 1:
                ring(way, sub, step + 1).start()

    def twin_copy(turn):
        return exchange(
            mixed.at[turn % 4, 1 - core], twin_in.at[turn % 4], twin_send, twin_recv, turn, twin
        )

    def far_copy(turn):
        return exchange(pair.at[turn], far_in.at[turn], far_send, far_recv, turn, far)

    loads = []
    for group in range(2):
        loads += [
            pltpu.make_async_copy(d_mlp.at[:, group], d_out.at[group], load_sem.at[0, group]),
            pltpu.make_async_copy(product.at[:, group], prod.at[group], load_sem.at[1, group]),
        ]
    for copy in loads:
        copy.start()
    for turn in range(2):
        for copy in down_copies(0, turn, turn):
            copy.start()
        for copy in weight_copies(turn, turn):
            copy.start()
    greet((right, left, twin, far))
    for copy in loads:
        copy.wait()
    grad_block(0)
    for sub in range(SUBS):
        for way in range(2):
            ring(way, sub, 1).start()
    block_copy(0).start()
    block_copy(2).start()
    for group in range(2):
        for way in range(2):
            hidden_copy(group, way).start()
    grad_block(1)

    def product_tile(group, tile):
        turn = group * tiles + tile
        slot = lax.rem(turn, 3)
        for copy in down_copies(group, tile, slot):
            copy.wait()

        @pl.when(turn + 2 < 2 * tiles)
        def _():
            later = turn + 2
            for copy in down_copies(
                lax.div(later, tiles), lax.rem(later, tiles), lax.rem(later, 3)
            ):
                copy.start()

        cols = tile_span(tile)
        grad = jnp.dot(
            d_out[group].reshape(pack, width), down_tile[slot], preferred_element_type=jnp.float32
        )
        for target, factor in ((d_gate, slope_tile), (d_up, silu_tile)):
            scaled = grad * factor[slot].reshape(pack, TILE).astype(jnp.float32)
            target[group, :, :, cols] = scaled.astype(jnp.bfloat16).reshape(2, side, TILE)

    def input_tile(turn):
        group, tile = divmod(turn, blocks)
        slot = turn % 3
        for copy in weight_copies(tile, slot):
            copy.wait()
        if turn + 2 < 2 * blocks:
            for copy in weight_copies((tile + 2) % blocks, (turn + 2) % 3):
                copy.start()
        total = lax.dot_general(
            d_gate[group].reshape(pack, units),
            gate_tile[slot],
            right_side,
            preferred_element_type=jnp.float32,
        ) + lax.dot_general(
            d_up[group].reshape(pack, units),
            up_tile[slot],
            right_side,
            preferred_element_type=jnp.float32,
        )
        mixed[turn % 4] = total.astype(jnp.bfloat16).reshape(2, side, TILE)
        twin_copy(turn).start()

    def add_twin(turn):
        twin_copy(turn).wait_recv()

        @pl.loop(0, side // 32)
        def _(row):
            span = pl.ds(pl.multiple_of(row * 32, 32), 32)
            pair[turn, span, :] = mixed[turn % 4, core, span, :] + twin_in[turn % 4, span, :]

        far_copy(turn).start()
        twin_copy(turn).wait_send()

    def add_far(turn):
        group, tile = divmod(turn, blocks)
        far_copy(turn).wait_recv()

        @pl.loop(0, side // 32)
        def _(row):
            span = pl.ds(pl.multiple_of(row * 32, 32), 32)
            wide = pl.ds(pl.multiple_of(group * side + row * 32, 32), 32)
            d_hidden[wide, tile * TILE : (tile + 1) * TILE] = pair[turn, span, :].astype(
                jnp.float32
            ) + far_in[turn, span, :].astype(jnp.float32)

    def weight_block(which, source):
        block = lax.dot_general(
            hidden_tile[...].reshape(2 * pack, TILE),
            source[...].reshape(2 * pack, units),
            left_side,
            preferred_element_type=jnp.float32,
        ).astype(jnp.bfloat16)
        stage[which, 0] = block[:chunk]
        stage[which, 1] = block[chunk:]
        stage_copy(which).start()

    events = [(step, sub) for step in range(1, n) for sub in range(SUBS)]

    def next_event():
        if events:
            step, sub = events.pop(0)
            serve(step, sub)
            if sub == SUBS - 1 and step < n - 1:
                grad_block(step + 1)

    def product_group(group):
        pl.loop(0, tiles // 2)(functools.partial(product_tile, group))
        next_event()
        pl.loop(tiles // 2, tiles)(functools.partial(product_tile, group))
        next_event()

    def grad_store(group):
        return [
            pltpu.make_async_copy(
                source.at[group], target.at[:, group], store_sem.at[6 + 2 * place + group]
            )
            for place, (source, target) in enumerate(((d_gate, d_gate_out), (d_up, d_up_out)))
        ]

    def hidden_store(group):
        span = pl.ds(group * side, side)
        return pltpu.make_async_copy(
            d_hidden.at[span], d_hidden_out.at[span], store_sem.at[group]
        )

    for group in range(2):
        product_group(group)
        for copy in grad_store(group):
            copy.start()
        if group == 1:
            for turn in range(blocks - 3, blocks):
                add_far(turn)
        for turn in range(group * blocks, (group + 1) * blocks):
            input_tile(turn)
            if turn % blocks >= 1:
                add_twin(turn - 1)
            if turn % blocks >= 3:
                add_far(turn - 3)
            if turn % 2 == 1:
                next_event()
        add_twin((group + 1) * blocks - 1)
        if group == 1:
            hidden_store(0).start()
    for group in range(2):
        for way in range(2):
            hidden_copy(group, way).wait()
    weight_block(0, d_gate)
    add_far(2 * blocks - 3)
    next_event()
    weight_block(1, d_up)
    add_far(2 * blocks - 2)
    next_event()
    add_far(2 * blocks - 1)
    hidden_store(1).start()
    while events:
        next_event()
    for group in range(2):
        hidden_store(group).wait()
    for which in range(2):
        stage_copy(which).wait()
        for copy in grad_store(which):
            copy.wait()
    block_copy(0).wait_send()
    block_copy(1).wait_recv()
    block_copy(2).wait()
    for turn in range(2 * blocks):
        far_copy(turn).wait_send()
    for step in range(1, n):
        for sub in range(SUBS):
            for way in range(2):
                ring(way, sub, step).wait_send()


def kernel_back(
    d_mlp,
    product,
    down_full,
    gate_slope,
    silu,
    gate_full,
    up_full,
    hidden_low,
    block_half,
    n,
):
    count, width = d_mlp.shape
    units = product.shape[1]
    half = count // 2
    side = count // 4
    chunk = width // n // 2
    rows = chunk // SUBS
    blocks = width // TILE
    low = jnp.bfloat16
    full = jnp.float32
    hbm = pl.BlockSpec(memory_space=pl.ANY)
    vmem = pl.BlockSpec(memory_space=pltpu.VMEM)
    dma = pltpu.SemaphoreType.DMA
    shape = jax.ShapeDtypeStruct

    def cut(array):
        return array.reshape(2, 2, side, array.shape[1])

    outs = pl.pallas_call(
        functools.partial(back_kernel, n),
        out_shape=(
            shape((2, chunk, units), full),
            shape((half, width), full),
            shape((2, 2, side, units), low),
            shape((2, 2, side, units), low),
            shape((2, 2, chunk, units), low),
            shape((2, half, width), low),
        ),
        in_specs=[hbm] * 9,
        out_specs=(vmem,) + (hbm,) * 5,
        scratch_shapes=[
            pltpu.VMEM((2, 2, side, width), low),
            pltpu.VMEM((2, 2, side, units), low),
            pltpu.VMEM((2, 2, side, units), low),
            pltpu.VMEM((2, 2, side, units), low),
            pltpu.VMEM((3, width, TILE), low),
            pltpu.VMEM((3, 2, side, TILE), low),
            pltpu.VMEM((3, 2, side, TILE), low),
            pltpu.VMEM((3, TILE, units), low),
            pltpu.VMEM((3, TILE, units), low),
            pltpu.VMEM((2, 2, side, TILE), low),
            pltpu.VMEM((2, chunk, units), low),
            pltpu.VMEM((2, 2, chunk, units), low),
            pltpu.VMEM((n - 1, 2, SUBS, rows, units), low),
            pltpu.VMEM((4, 2, side, TILE), low),
            pltpu.VMEM((4, side, TILE), low),
            pltpu.VMEM((2 * blocks, side, TILE), low),
            pltpu.VMEM((2 * blocks, side, TILE), low),
            pltpu.VMEM((half, width), full),
            pltpu.VMEM((2, 2, chunk, units), low),
            dma((2, SUBS, n - 1)),
            dma((2, SUBS, n - 1)),
            dma((2 * blocks,)),
            dma((2 * blocks,)),
            dma((2 * blocks,)),
            dma((2 * blocks,)),
            dma((1,)),
            dma((1,)),
            dma((2, 2)),
            dma((3, 3)),
            dma((3, 2)),
            dma((2, 2)),
            dma((2,)),
            dma((10,)),
        ],
        compiler_params=pltpu.CompilerParams(
            collective_id=3, has_side_effects=True, vmem_limit_bytes=60 * 2**20
        ),
    )(
        cut(d_mlp),
        cut(product),
        down_full,
        cut(gate_slope),
        cut(silu),
        gate_full,
        up_full,
        cut(hidden_low),
        block_half,
    )
    out_down, d_hidden, d_gate, d_up, head_grads, block_out = outs
    return (
        out_down.reshape(2 * chunk, units),
        d_hidden,
        d_gate.reshape(count, units),
        d_up.reshape(count, units),
        head_grads,
        block_out.reshape(count, width),
    )


def detach_kernel(
    n,
    branch,
    upstream,
    attn_gain,
    attn_full,
    attended_in,
    query_rot_in,
    key_rot_in,
    value_in,
    query_raw_in,
    key_raw_in,
    tokens,
    d_hidden,
    head_grads,
    d_gate,
    d_up,
    hidden_low,
    totals,
    inverses,
    cosine,
    sine,
    doc_col,
    doc_row,
    query_gain,
    key_gain,
    out_gate,
    out_up,
    grad_attn,
    grad_tokens,
    query_gain_grad,
    key_gain_grad,
    attn_gain_grad,
    d_branch,
    branch_tile,
    output_tile,
    grad_tile,
    unit_tile,
    weight_tile,
    attended,
    query_rot,
    key_rot,
    value,
    query_raw,
    key_raw,
    d_attended,
    d_query_norm,
    d_key_norm,
    d_key_sum,
    d_value_sum,
    d_projected,
    own,
    inbox,
    total_buf,
    mixed,
    twin_in,
    pair,
    far_in,
    hidden_tile,
    upstream_tile,
    upstream_rows,
    gain_sum,
    stage_output,
    stage,
    stat,
    ring_send,
    ring_recv,
    stat_send,
    stat_recv,
    twin_send,
    twin_recv,
    far_send,
    far_recv,
    join_send,
    join_recv,
    whole_send,
    whole_recv,
    whole_sem,
    row_sem,
    unit_sem,
    grad_sem,
    branch_sem,
    load_sem,
    weight_sem,
    hidden_sem,
    upstream_sem,
    stage_sem,
    store_sem,
    out_sem,
):
    index, core, right, left, twin, far = neighbours(n)
    count, width = tokens.shape
    half = count // 2
    local = query_raw.shape[1]
    heads = local // HEAD_CHANNELS
    blocks = width // TILE
    chunk = inbox.shape[3]
    grads = (d_gate, d_up)
    part_cols = grad_tile.shape[2]
    parts_in = d_gate.shape[1] // part_cols
    outs = (out_gate, out_up)
    left_side = (((0,), (0,)), ((), ()))
    right_side = (((1,), (1,)), ((), ()))
    factor = 1.0 / math.sqrt(HEAD_CHANNELS)

    def ring(way, unit, step):
        first = head_grads.at[unit, way]
        return pltpu.make_async_remote_copy(
            src_ref=first if step == 1 else inbox.at[step - 2, way, unit],
            dst_ref=inbox.at[step - 1, way, unit],
            send_sem=ring_send.at[way, unit, step - 1],
            recv_sem=ring_recv.at[way, unit, step - 1],
            device_id=left if way else right,
            device_id_type=MESH,
        )

    events = [(step, unit) for step in range(1, n) for unit in range(2)]

    def unit_copy(step, way):
        owner = holder_of(index, (1 + step) * (2 * way - 1), n)
        start = pl.multiple_of(owner * 2 * chunk + way * chunk, chunk)
        return pltpu.make_async_copy(
            hidden_low.at[:, pl.ds(start, chunk)],
            unit_tile.at[step % 2, :, pl.ds(way * chunk, chunk)],
            unit_sem.at[step % 2, way],
        )

    def grad_copy(unit, part, slot):
        cols = pl.ds(pl.multiple_of(part * part_cols, part_cols), part_cols)
        return pltpu.make_async_copy(
            grads[unit].at[:, cols], grad_tile.at[slot], grad_sem.at[slot]
        )

    def grad_block(step, unit):
        if unit == 0:
            for way in range(2):
                unit_copy(step, way).wait()
                if step < n - 1:
                    unit_copy(step + 1, way).start()

        base = 2 * (step - 1) + unit
        final = base == 2 * n - 3

        @pl.loop(0, parts_in)
        def _(part):
            slot = lax.rem(base * parts_in + part, 3)
            spare = lax.rem(slot + 2, 3)
            grad_copy(unit, part, slot).wait()

            @pl.when(part + 2 < parts_in)
            def _():
                grad_copy(unit, part + 2, spare).start()

            if not final:

                @pl.when(part + 2 >= parts_in)
                def _():
                    grad_copy(1 - unit, part + 2 - parts_in, spare).start()

            cols = pl.ds(pl.multiple_of(part * part_cols, part_cols), part_cols)
            block = lax.dot_general(
                unit_tile[step % 2],
                grad_tile[slot],
                left_side,
                preferred_element_type=jnp.float32,
            ).astype(jnp.bfloat16)
            own[unit, 0, :, cols] = block[:chunk]
            own[unit, 1, :, cols] = block[chunk:]

    def out_copy(unit):
        return pltpu.make_async_copy(total_buf, outs[unit], out_sem.at[unit])

    def serve():
        step, unit = events.pop(0)
        if step == n - 1 and unit == 1:
            out_copy(0).wait()
        for way in range(2):
            ring(way, unit, step).wait_recv()

            @pl.loop(0, chunk // 16)
            def _(tile, way=way):
                span = pl.ds(pl.multiple_of(tile * 16, 16), 16)
                got = inbox[step - 1, way, unit, span, :]
                held = own[unit, way, span, :]
                if step < n - 1:
                    inbox[step - 1, way, unit, span, :] = got + held
                else:
                    total_buf[way, span, :] = got.astype(jnp.float32) + held.astype(jnp.float32)

            if step < n - 1:
                ring(way, unit, step + 1).start()
        if step < n - 1:
            grad_block(step + 1, unit)
        else:
            out_copy(unit).start()

    greet((right, left, twin, far))
    for unit in range(2):
        for way in range(2):
            ring(way, unit, 1).start()
    for way in range(2):
        unit_copy(1, way).start()
    for part in range(2):
        grad_copy(0, part, part).start()

    def weight_copy(tile, slot):
        return pltpu.make_async_copy(
            attn_full.at[pl.ds(tile * TILE, TILE), pl.ds(0, 3 * local)],
            weight_tile.at[slot],
            weight_sem.at[slot],
        )

    def hidden_copies(tile, slot):
        cols = pl.ds(tile * TILE, TILE)
        mine = pl.ds(pl.multiple_of(core * half, half), half)
        return (
            pltpu.make_async_copy(
                d_hidden.at[:, cols], hidden_tile.at[slot], hidden_sem.at[slot]
            ),
            pltpu.make_async_copy(
                upstream.at[mine, cols], upstream_tile.at[slot], upstream_sem.at[slot]
            ),
        )

    loads = [
        pltpu.make_async_copy(source, target, load_sem.at[place])
        for place, (source, target) in enumerate(
            (
                (attended_in, attended),
                (query_rot_in, query_rot),
                (key_rot_in, key_rot),
                (value_in, value),
                (query_raw_in, query_raw),
                (key_raw_in, key_raw),
            )
        )
    ]

    def branch_copies(tile, source):
        cols = pl.ds(tile * TILE, TILE)
        slot = tile % 2
        copies = [
            pltpu.make_async_copy(source.at[:, cols], branch_tile.at[slot], branch_sem.at[slot, 0])
        ]
        if source is d_branch:
            copies.append(
                pltpu.make_async_copy(
                    attn_full.at[cols, pl.ds(3 * local, local)],
                    output_tile.at[slot],
                    branch_sem.at[slot, 1],
                )
            )
        return copies

    def output_copy(tile):
        return pltpu.make_async_copy(
            stage_output.at[tile % 2],
            grad_attn.at[pl.ds(tile * TILE, TILE), pl.ds(3 * local, local)],
            stage_sem.at[0, tile % 2],
        )

    deep = half // 4

    def row_copies(part):
        span = pl.ds(part * deep, deep)
        mine = pl.ds(pl.multiple_of(core * half + part * deep, deep), deep)
        return [
            pltpu.make_async_copy(d_hidden.at[span], total_buf.at[0], row_sem.at[0]),
            pltpu.make_async_copy(branch.at[span], total_buf.at[1], row_sem.at[1]),
            pltpu.make_async_copy(upstream.at[mine], upstream_rows, row_sem.at[2]),
        ]

    def finish(part, tile):
        near = pl.ds(pl.multiple_of(tile * 16, 16), 16)
        total = total_buf[0, near, :] + upstream_rows[near, :].astype(jnp.float32)
        mix = total_buf[1, near, :]
        inverse = lax.rsqrt(jnp.sum(mix * mix, axis=1, keepdims=True) / width + EPSILON)
        scaled = attn_gain[...] * total
        mean = jnp.sum(scaled * mix, axis=1, keepdims=True) / width
        grad = (inverse * scaled - mix * (inverse * inverse * inverse * mean)).astype(
            jnp.bfloat16
        )
        for block in range(blocks):
            spot = pl.multiple_of((block % 2) * half + part * deep + tile * 16, 16)
            mixed[block // 2, pl.ds(spot, 16), :] = grad[:, block * TILE : (block + 1) * TILE]
        terms = total * mix * inverse
        gain_sum[...] += terms[:8] + terms[8:]

    def whole_copy(block, kind):
        cols = pl.ds(block * TILE, TILE)
        source = mixed.at[block // 2, pl.ds((block % 2) * half, half)]
        keeper = 1 - core if kind == 1 else core
        target = d_branch.at[pl.ds(pl.multiple_of(keeper * half, half), half), cols]
        if kind == 2:
            return pltpu.make_async_copy(source, target, whole_sem.at[block])
        return exchange(
            target if kind else source, target, whole_send, whole_recv, block, twin
        )

    for copy in row_copies(0) + loads:
        copy.start()
    gain_sum[...] = jnp.zeros_like(gain_sum)
    grad_block(1, 0)
    grad_block(1, 1)
    for part in range(4):
        for copy in row_copies(part):
            copy.wait()
        pl.loop(0, deep // 16)(functools.partial(finish, part))
        if part < 3:
            for copy in row_copies(part + 1):
                copy.start()
        if part == 1:
            serve()
    for block in range(blocks):
        whole_copy(block, 0).start()
        whole_copy(block, 2).start()
    attn_gain_grad[...] = jnp.sum(gain_sum[...], axis=0, keepdims=True)
    for block in range(blocks):
        whole_copy(block, 1).wait_recv()
        whole_copy(block, 0).wait_send()
        whole_copy(block, 2).wait()
    for copy in branch_copies(0, d_branch):
        copy.start()
    loads[0].wait()
    for tile in range(blocks):
        for copy in branch_copies(tile, d_branch):
            copy.wait()
        if tile + 1 < blocks:
            for copy in branch_copies(tile + 1, d_branch):
                copy.start()
        product = jnp.dot(
            branch_tile[tile % 2], output_tile[tile % 2], preferred_element_type=jnp.float32
        )
        if tile == 0:
            d_query_norm[...] = product
        else:
            d_query_norm[...] += product
        if tile >= 2:
            output_copy(tile - 2).wait()
        stage_output[tile % 2] = lax.dot_general(
            branch_tile[tile % 2],
            attended[...],
            left_side,
            preferred_element_type=jnp.float32,
        ).astype(jnp.bfloat16)
        output_copy(tile).start()
    d_attended[...] = d_query_norm[...].astype(jnp.bfloat16)
    branch_copies(0, tokens)[0].start()
    weight_copy(0, 0).start()
    for copy in loads[1:]:
        copy.wait()
    serve()

    def unturned(vectors, span):
        return vectors * cosine[span, :] - pltpu.roll(vectors, HEAD_CHANNELS // 2, 1) * sine[span, :]

    def head_backward(head):
        cols = pl.ds(pl.multiple_of(head * HEAD_CHANNELS, HEAD_CHANNELS), HEAD_CHANNELS)
        lane = lax.broadcasted_iota(jnp.int32, (BLOCK, 128), 1)
        for block in reversed(range(count // BLOCK)):
            span = slice(block * BLOCK, (block + 1) * BLOCK)
            length = (block + 1) * BLOCK
            query = query_rot[span, cols]
            key = key_rot[:length, cols]
            grad = d_attended[span, cols]
            scores = masked_scores(query, key, doc_col, doc_row, block)
            total = jnp.sum(jnp.where(lane == head, totals[span, :], 0.0), axis=1, keepdims=True)
            powers = jnp.exp(scores - total)
            d_powers = lax.dot_general(
                grad, value[:length, cols], right_side, preferred_element_type=jnp.float32
            )
            correction = jnp.sum(d_powers * powers, axis=1, keepdims=True)
            d_scores = (powers * (d_powers - correction)).astype(jnp.bfloat16)
            rounded = powers.astype(jnp.bfloat16)
            d_query = jnp.dot(d_scores, key, preferred_element_type=jnp.float32) * factor
            d_query_norm[span, cols] = unturned(d_query, span)
            d_key = lax.dot_general(
                d_scores, query, left_side, preferred_element_type=jnp.float32
            )
            d_value = lax.dot_general(
                rounded, grad, left_side, preferred_element_type=jnp.float32
            )
            if length == count:
                d_key_sum[...] = d_key
                d_value_sum[...] = d_value
            else:
                d_key_sum[:length, :] += d_key
                d_value_sum[:length, :] += d_value
        d_key_norm[:, cols] = unturned(d_key_sum[...] * factor, slice(None))
        start = pl.multiple_of(2 * local + head * HEAD_CHANNELS, HEAD_CHANNELS)
        d_projected[:, pl.ds(start, HEAD_CHANNELS)] = d_value_sum[...].astype(jnp.bfloat16)

    pl.loop(0, heads // 2)(head_backward)
    serve()
    pl.loop(heads // 2, heads)(head_backward)
    serve()
    parts = []
    for place, (norm, raw, gain, gain_grad) in enumerate(
        (
            (d_query_norm, query_raw, query_gain, query_gain_grad),
            (d_key_norm, key_raw, key_gain, key_gain_grad),
        )
    ):
        dots = jnp.zeros((count, HEAD_CHANNELS), jnp.float32)
        for head in range(heads):
            cols = slice(head * HEAD_CHANNELS, (head + 1) * HEAD_CHANNELS)
            both = norm[:, cols] * raw[:, cols]
            gain_grad[:, cols] = jnp.sum(
                both * inverses[:, place : place + 1], axis=0, keepdims=True
            )
            dots = dots + both * gain[:, cols]
        parts.append(jnp.sum(dots, axis=1, keepdims=True))
    stat[0] = columns_to_rows(parts, count)
    first = exchange(stat.at[0], stat.at[1], stat_send, stat_recv, 0, twin)
    first.start()
    first.wait()
    stat[2] = stat[0] + stat[1]
    second = exchange(stat.at[2], stat.at[3], stat_send, stat_recv, 1, far)
    second.start()
    serve()
    second.wait()
    inner = d_key_sum
    inner[...] = rows_to_columns(stat[2] + stat[3]) / width

    @pl.loop(0, heads)
    def _(head):
        cols = pl.ds(pl.multiple_of(head * HEAD_CHANNELS, HEAD_CHANNELS), HEAD_CHANNELS)
        for place, (norm, raw, gain) in enumerate(
            ((d_query_norm, query_raw, query_gain), (d_key_norm, key_raw, key_gain))
        ):
            inverse = inverses[:, place : place + 1]
            cube = inverse * inverse * inverse * inner[:, place : place + 1]
            start = pl.multiple_of(place * local + head * HEAD_CHANNELS, HEAD_CHANNELS)
            d_projected[:, pl.ds(start, HEAD_CHANNELS)] = (
                norm[:, cols] * inverse * gain[:, cols] - raw[:, cols] * cube
            ).astype(jnp.bfloat16)

    def twin_copy(tile):
        span = pl.ds(pl.multiple_of((1 - core) * half, half), half)
        return exchange(
            mixed.at[tile % 4, span], twin_in.at[tile % 4], twin_send, twin_recv, tile, twin
        )

    def far_copy(tile):
        return exchange(pair.at[tile], far_in.at[tile], far_send, far_recv, tile, far)

    def token_tile(tile):
        slot = tile % 2
        weight_copy(tile, slot).wait()
        if tile + 1 < blocks:
            weight_copy(tile + 1, 1 - slot).start()
        mixed[tile % 4] = lax.dot_general(
            d_projected[...], weight_tile[slot], right_side, preferred_element_type=jnp.float32
        ).astype(jnp.bfloat16)
        twin_copy(tile).start()

    def add_twin(tile):
        twin_copy(tile).wait_recv()

        @pl.loop(0, half // 32)
        def _(row):
            span = pl.ds(pl.multiple_of(row * 32, 32), 32)
            mine = pl.ds(pl.multiple_of(core * half + row * 32, 32), 32)
            pair[tile, span, :] = mixed[tile % 4, mine, :] + twin_in[tile % 4, span, :]

        far_copy(tile).start()
        twin_copy(tile).wait_send()

    def join(tile, kind):
        cols = pl.ds(tile * TILE, TILE)
        if kind == 2:
            return pltpu.make_async_copy(
                pair.at[tile], grad_tokens.at[core, :, cols], store_sem.at[tile]
            )
        target = grad_tokens.at[1 - core if kind else core, :, cols]
        return exchange(
            target if kind else pair.at[tile], target, join_send, join_recv, tile, twin
        )

    def add_far(tile):
        slot = tile % 2
        for copy in hidden_copies(tile, slot):
            copy.wait()
        if tile + 1 < blocks:
            for copy in hidden_copies(tile + 1, 1 - slot):
                copy.start()
        far_copy(tile).wait()

        @pl.loop(0, half // 32)
        def _(row):
            span = pl.ds(pl.multiple_of(row * 32, 32), 32)
            total = (
                pair[tile, span, :].astype(jnp.float32)
                + far_in[tile, span, :].astype(jnp.float32)
                + hidden_tile[slot, span, :]
                + upstream_tile[slot, span, :].astype(jnp.float32)
            )
            pair[tile, span, :] = total.astype(jnp.bfloat16)

        join(tile, 0).start()
        join(tile, 2).start()

    def stage_copy(tile):
        return pltpu.make_async_copy(
            stage.at[tile % 2],
            grad_attn.at[pl.ds(tile * TILE, TILE), pl.ds(0, 3 * local)],
            stage_sem.at[1, tile % 2],
        )

    def weight_grad(tile):
        if tile >= 2:
            stage_copy(tile - 2).wait()
        branch_copies(tile, tokens)[0].wait()
        if tile + 1 < blocks:
            branch_copies(tile + 1, tokens)[0].start()
        stage[tile % 2] = lax.dot_general(
            branch_tile[tile % 2],
            d_projected[...],
            left_side,
            preferred_element_type=jnp.float32,
        ).astype(jnp.bfloat16)
        stage_copy(tile).start()

    for copy in hidden_copies(0, 0):
        copy.start()
    for tile in range(blocks):
        token_tile(tile)
        if tile >= 1:
            add_twin(tile - 1)
        if tile == blocks // 2 - 1:
            serve()
    add_twin(blocks - 1)
    serve()
    for tile in range(blocks):
        weight_grad(tile)
        add_far(tile)
        if tile % 2 == 1:
            serve()
    for tile in (blocks - 2, blocks - 1):
        output_copy(tile).wait()
        stage_copy(tile).wait()
    while events:
        serve()
    out_copy(1).wait()
    for tile in range(blocks):
        join(tile, 1).wait_recv()
        join(tile, 0).wait_send()
        join(tile, 2).wait()
    for step in range(1, n):
        for unit in range(2):
            for way in range(2):
                ring(way, unit, step).wait_send()


def kernel_detach(
    branch,
    upstream,
    attn_gain,
    attn_full,
    attended,
    query_rot,
    key_rot,
    value,
    query_raw,
    key_raw,
    tokens,
    d_hidden,
    head_grads,
    d_gate,
    d_up,
    hidden_low,
    totals,
    inverses,
    cosine,
    sine,
    doc_col,
    doc_ids,
    query_gain,
    key_gain,
    n,
):
    count, width = tokens.shape
    local = query_gain.shape[1]
    units = d_gate.shape[1]
    half = count // 2
    chunk = width // n // 2
    blocks = width // TILE
    low = jnp.bfloat16
    full = jnp.float32
    hbm = pl.BlockSpec(memory_space=pl.ANY)
    vmem = pl.BlockSpec(memory_space=pltpu.VMEM)
    dma = pltpu.SemaphoreType.DMA
    shape = jax.ShapeDtypeStruct
    outs = pl.pallas_call(
        functools.partial(detach_kernel, n),
        out_shape=(
            shape((2, chunk, units), full),
            shape((2, chunk, units), full),
            shape((width, 4 * local), low),
            shape((2, half, width), low),
            shape((1, local), full),
            shape((1, local), full),
            shape((1, width), full),
            shape((count, width), low),
        ),
        in_specs=[hbm] * 2 + [vmem] + [hbm] * 13 + [vmem] * 8,
        out_specs=(hbm,) * 4 + (vmem,) * 3 + (hbm,),
        scratch_shapes=[
            pltpu.VMEM((2, count, TILE), low),
            pltpu.VMEM((2, TILE, local), low),
            pltpu.VMEM((3, count, 2 * TILE), low),
            pltpu.VMEM((2, count, TILE), low),
            pltpu.VMEM((2, TILE, 3 * local), low),
            pltpu.VMEM((count, local), low),
            pltpu.VMEM((count, local), low),
            pltpu.VMEM((count, local), low),
            pltpu.VMEM((count, local), low),
            pltpu.VMEM((count, local), full),
            pltpu.VMEM((count, local), full),
            pltpu.VMEM((count, local), low),
            pltpu.VMEM((count, local), full),
            pltpu.VMEM((count, local), full),
            pltpu.VMEM((count, HEAD_CHANNELS), full),
            pltpu.VMEM((count, HEAD_CHANNELS), full),
            pltpu.VMEM((count, 3 * local), low),
            pltpu.VMEM((2, 2, chunk, units), low),
            pltpu.VMEM((n - 1, 2, 2, chunk, units), low),
            pltpu.VMEM((2, chunk, units), full),
            pltpu.VMEM((4, count, TILE), low),
            pltpu.VMEM((4, half, TILE), low),
            pltpu.VMEM((blocks, half, TILE), low),
            pltpu.VMEM((blocks, half, TILE), low),
            pltpu.VMEM((2, half, TILE), full),
            pltpu.VMEM((2, half, TILE), low),
            pltpu.VMEM((half // 4, width), low),
            pltpu.VMEM((8, width), full),
            pltpu.VMEM((2, TILE, local), low),
            pltpu.VMEM((2, TILE, 3 * local), low),
            pltpu.VMEM((4, 8, count), full),
            dma((2, 2, n - 1)),
            dma((2, 2, n - 1)),
            dma((2,)),
            dma((2,)),
            dma((blocks,)),
            dma((blocks,)),
            dma((blocks,)),
            dma((blocks,)),
            dma((blocks,)),
            dma((blocks,)),
            dma((blocks,)),
            dma((blocks,)),
            dma((blocks,)),
            dma((3,)),
            dma((2, 2)),
            dma((3,)),
            dma((2, 2)),
            dma((6,)),
            dma((2,)),
            dma((2,)),
            dma((2,)),
            dma((2, 2)),
            dma((blocks,)),
            dma((2,)),
        ],
        compiler_params=pltpu.CompilerParams(
            collective_id=5, has_side_effects=True, vmem_limit_bytes=60 * 2**20
        ),
    )(
        branch,
        upstream,
        attn_gain,
        attn_full,
        attended,
        query_rot,
        key_rot,
        value,
        query_raw,
        key_raw,
        tokens,
        d_hidden,
        head_grads,
        d_gate,
        d_up,
        hidden_low,
        totals,
        inverses,
        cosine,
        sine,
        doc_col,
        doc_ids.reshape(1, count),
        query_gain,
        key_gain,
    )
    return (
        outs[0].reshape(2 * chunk, units),
        outs[1].reshape(2 * chunk, units),
        outs[2],
        outs[3].reshape(count, width),
        outs[4],
        outs[5],
        outs[6],
    )


def fused_layer(
    n,
    tokens,
    doc_ids,
    q_weight,
    k_weight,
    v_weight,
    o_weight,
    q_gain,
    k_gain,
    attn_gain,
    gate_weight,
    up_weight,
    down_weight,
    mlp_gain,
    cotangent,
):
    index = lax.axis_index("dp")
    heads, channels = q_gain.shape
    small = jnp.concatenate(
        [
            q_gain,
            k_gain,
            jnp.zeros((SMALL - 2 * heads, channels), q_gain.dtype),
        ],
        axis=0,
    )
    small = lax.dynamic_update_slice(
        jnp.zeros((SMALL, HEAD_CHANNELS), q_gain.dtype), small, (0, index * channels)
    )
    small = lax.dynamic_update_slice(
        small, jnp.concatenate([attn_gain, mlp_gain]).reshape(4, 128), (2 * heads, 0)
    )
    frequency = jnp.exp(
        jnp.arange(HEAD_CHANNELS // 2, dtype=jnp.float32)
        * (-2.0 * math.log(ROPE_BASE) / HEAD_CHANNELS)
    )
    frequency = jnp.concatenate([frequency, frequency])[None, :]
    (
        attn_full,
        query_gain,
        key_gain,
        attn_gains,
        mlp_gains,
        cosine,
        sine,
        doc_col,
        down_shard,
    ) = kernel_gather(
        q_weight, k_weight, v_weight, o_weight, small, doc_ids, frequency, down_weight, n
    )
    (
        gate_full,
        up_full,
        query_raw,
        key_raw,
        query_rot,
        key_rot,
        value,
        attended,
        totals,
        inverses,
        branch,
        hidden_state,
        hidden_low,
    ) = kernel_attend(
        tokens,
        attn_full,
        gate_weight,
        up_weight,
        cosine,
        sine,
        doc_col,
        doc_ids,
        query_gain,
        key_gain,
        attn_gains,
        n,
    )
    product, gate_slope, silu, down_full, d_mlp, block_half, mlp_row = kernel_feed(
        hidden_low, gate_full, up_full, down_shard, hidden_state, cotangent, mlp_gains, n
    )
    out_down, d_hidden, d_gate, d_up, head_grads, block_out = kernel_back(
        d_mlp,
        product,
        down_full,
        gate_slope,
        silu,
        gate_full,
        up_full,
        hidden_low,
        block_half,
        n,
    )
    out_gate, out_up, grad_attn, grad_tokens, query_row, key_row, attn_row = kernel_detach(
        branch,
        cotangent,
        attn_gains,
        attn_full,
        attended,
        query_rot,
        key_rot,
        value,
        query_raw,
        key_raw,
        tokens,
        d_hidden,
        head_grads,
        d_gate,
        d_up,
        hidden_low,
        totals,
        inverses,
        cosine,
        sine,
        doc_col,
        doc_ids,
        query_gain,
        key_gain,
        n,
    )
    out_query, out_key, out_value, out_output, summed = kernel_scatter(
        grad_attn, query_row, key_row, attn_row, mlp_row, n
    )
    lanes = lax.dynamic_slice(summed, (0, index * channels), (2 * heads, channels))
    return (
        block_out,
        grad_tokens,
        out_query,
        out_key,
        out_value,
        out_output,
        lanes[:heads],
        lanes[heads:],
        summed[2 * heads : 2 * heads + 2].reshape(-1),
        out_gate,
        out_up,
        out_down.T,
        summed[2 * heads + 2 : 2 * heads + 4].reshape(-1),
    )


def solution(mesh):
    in_specs = (
        P("dp", None),
        P("dp"),
        P("dp", "mp"),
        P("dp", "mp"),
        P("dp", "mp"),
        P("mp", "dp"),
        P("mp", "dp"),
        P("mp", "dp"),
        P("dp"),
        P("dp", "mp"),
        P("dp", "mp"),
        P("mp", "dp"),
        P("dp"),
        P("dp", None),
    )
    out_specs = (
        P("dp", None),
        P("dp", None),
        P("dp", "mp"),
        P("dp", "mp"),
        P("dp", "mp"),
        P("mp", "dp"),
        P("mp", "dp"),
        P("mp", "dp"),
        P("dp"),
        P("dp", "mp"),
        P("dp", "mp"),
        P("mp", "dp"),
        P("dp"),
    )
    n, m = mesh.shape["dp"], mesh.shape["mp"]

    def on_device(*arrays):
        if (n, m, arrays[0].shape[0]) == (RING, 4, SEQ_LEN):
            return fused_layer(n, *arrays)
        return plain_layer(*arrays)

    return jax.shard_map(
        on_device, mesh=mesh, in_specs=in_specs, out_specs=out_specs, check_vma=False
    )
```

```python
import functools
import math

import jax
import jax.numpy as jnp
from jax import lax
from jax.experimental import pallas as pl
from jax.experimental.pallas import tpu as pltpu
from jax.sharding import PartitionSpec as P

D = 2048
HEAD_CHANNELS = 128
SEQ_LEN = 1024
RING = 8


EPSILON = 1e-06
ROPE_BASE = 500000.0
MASKED = -1e30
ROW_LIMIT = 512


def matmul(left_side, right_side):
    return jnp.dot(left_side, right_side, preferred_element_type=jnp.float32)


def transposed_left(left_side, right_side):
    return lax.dot_general(
        left_side, right_side, (((0,), (0,)), ((), ())), preferred_element_type=jnp.float32
    )


def transposed_right(left_side, right_side):
    return lax.dot_general(
        left_side, right_side, (((1,), (1,)), ((), ())), preferred_element_type=jnp.float32
    )


def angles_of(doc_rows, seq_len, head_dim):
    shaped = doc_rows.reshape(-1, seq_len)
    leading = jnp.sum(1 - shaped, axis=1, keepdims=True, dtype=jnp.int32)
    places = jnp.arange(seq_len, dtype=jnp.int32)[None, :] - shaped * leading
    frequency = jnp.exp(
        jnp.arange(head_dim // 2, dtype=jnp.float32) * (-2.0 * math.log(ROPE_BASE) / head_dim)
    )
    return places.reshape(-1).astype(jnp.float32)[:, None] * frequency[None, :]


def rotate(vectors, angles):
    halfway = vectors.shape[-1] // 2
    cosine = jnp.cos(angles)[:, None, :]
    sine_wave = jnp.sin(angles)[:, None, :]
    former = vectors[..., :halfway]
    latter = vectors[..., halfway:]
    return jnp.concatenate(
        [former * cosine - latter * sine_wave, latter * cosine + former * sine_wave], axis=-1
    )


def rotate_back(vectors, angles):
    halfway = vectors.shape[-1] // 2
    cosine = jnp.cos(angles)[:, None, :]
    sine_wave = jnp.sin(angles)[:, None, :]
    former = vectors[..., :halfway]
    latter = vectors[..., halfway:]
    return jnp.concatenate(
        [former * cosine + latter * sine_wave, latter * cosine - former * sine_wave], axis=-1
    )


def block_scores(query_block, key_seq, doc_seq, offset):
    factor = 1.0 / math.sqrt(query_block.shape[-1])
    scores = (
        jnp.einsum("qhd,khd->hqk", query_block, key_seq, preferred_element_type=jnp.float32)
        * factor
    )
    row_places = offset + jnp.arange(query_block.shape[0], dtype=jnp.int32)
    key_places = jnp.arange(key_seq.shape[0], dtype=jnp.int32)
    row_docs = doc_seq[offset : offset + query_block.shape[0]]
    allowed = (key_places[None, :] <= row_places[:, None]) & (doc_seq[None, :] == row_docs[:, None])
    return jnp.where(allowed[None], scores, MASKED)


def attend_sequence(inputs):
    query_seq, key_seq, value_seq, doc_seq = inputs
    row_block = math.gcd(query_seq.shape[0], ROW_LIMIT)
    outputs = []
    totals = []
    for offset in range(0, query_seq.shape[0], row_block):
        scores = block_scores(query_seq[offset : offset + row_block], key_seq, doc_seq, offset)
        maximum = jnp.max(scores, axis=-1, keepdims=True)
        weights = jnp.exp(scores - maximum)
        denominator = jnp.sum(weights, axis=-1, keepdims=True)
        rounded = (weights / denominator).astype(jnp.bfloat16)
        outputs.append(
            jnp.einsum(
                "hqk,khd->qhd", rounded, value_seq, preferred_element_type=jnp.float32
            ).astype(jnp.bfloat16)
        )
        totals.append((maximum + jnp.log(denominator))[..., 0])
    return (jnp.concatenate(outputs, axis=0), jnp.concatenate(totals, axis=1))


def attend_backward(inputs):
    query_seq, key_seq, value_seq, doc_seq, grad_seq, lse_seq = inputs
    row_block = math.gcd(query_seq.shape[0], ROW_LIMIT)
    factor = 1.0 / math.sqrt(query_seq.shape[-1])
    grad_keys = jnp.zeros(key_seq.shape, jnp.float32)
    grad_values = jnp.zeros(value_seq.shape, jnp.float32)
    grad_rows = []
    for offset in range(0, query_seq.shape[0], row_block):
        query_block = query_seq[offset : offset + row_block]
        grad_block = grad_seq[offset : offset + row_block]
        scores = block_scores(query_block, key_seq, doc_seq, offset)
        weights = jnp.exp(scores - lse_seq[:, offset : offset + row_block, None])
        d_weights = jnp.einsum(
            "qhd,khd->hqk", grad_block, value_seq, preferred_element_type=jnp.float32
        )
        correction = jnp.sum(d_weights * weights, axis=-1, keepdims=True)
        d_scores = (weights * (d_weights - correction)).astype(jnp.bfloat16)
        grad_rows.append(
            jnp.einsum("hqk,khd->qhd", d_scores, key_seq, preferred_element_type=jnp.float32)
            * factor
        )
        grad_keys = (
            grad_keys
            + jnp.einsum("hqk,qhd->khd", d_scores, query_block, preferred_element_type=jnp.float32)
            * factor
        )
        grad_values = grad_values + jnp.einsum(
            "hqk,qhd->khd",
            weights.astype(jnp.bfloat16),
            grad_block,
            preferred_element_type=jnp.float32,
        )
    return (jnp.concatenate(grad_rows, axis=0), grad_keys, grad_values)


def plain_layer(
    tokens,
    doc_ids,
    q_weight,
    k_weight,
    v_weight,
    o_weight,
    q_gain,
    k_gain,
    attn_gain,
    gate_weight,
    up_weight,
    down_weight,
    mlp_gain,
    cotangent,
):
    query_full, key_complete, value_full, output_full, query_gains, key_gains, attn_gains = (
        lax.all_gather(q_weight, "dp", axis=0, tiled=True),
        lax.all_gather(k_weight, "dp", axis=0, tiled=True),
        lax.all_gather(v_weight, "dp", axis=0, tiled=True),
        lax.all_gather(o_weight, "dp", axis=1, tiled=True),
        lax.all_gather(q_gain, "dp", axis=1, tiled=True),
        lax.all_gather(k_gain, "dp", axis=1, tiled=True),
        lax.all_gather(attn_gain, "dp", axis=0, tiled=True),
    )
    gate_full, up_full, down_full, mlp_gains = (
        lax.all_gather(gate_weight, "dp", axis=0, tiled=True),
        lax.all_gather(up_weight, "dp", axis=0, tiled=True),
        lax.all_gather(down_weight, "dp", axis=1, tiled=True),
        lax.all_gather(mlp_gain, "dp", axis=0, tiled=True),
    )
    row_count = tokens.shape[0]
    heads_on_device = q_gain.shape[0]
    local_width = heads_on_device * HEAD_CHANNELS
    sequences = row_count // SEQ_LEN
    seq_shape = (sequences, SEQ_LEN, heads_on_device, HEAD_CHANNELS)
    angles = angles_of(doc_ids, SEQ_LEN, HEAD_CHANNELS)
    doc_seqs = doc_ids.reshape(sequences, SEQ_LEN)
    query_raw = matmul(tokens, query_full)
    key_unnormed = matmul(tokens, key_complete)
    values = matmul(tokens, value_full).astype(jnp.bfloat16)
    query_sq, key_sq = lax.psum(
        (jnp.sum(query_raw * query_raw, axis=1), jnp.sum(key_unnormed * key_unnormed, axis=1)), "mp"
    )
    query_inv = lax.rsqrt(query_sq / D + EPSILON)[:, None]
    key_inverse_norm = lax.rsqrt(key_sq / D + EPSILON)[:, None]
    query_scale = query_gains.reshape(-1)
    key_scale = key_gains.reshape(-1)
    query_rot = rotate(
        (query_raw * query_inv * query_scale).reshape(row_count, heads_on_device, HEAD_CHANNELS),
        angles,
    ).astype(jnp.bfloat16)
    key_rot = rotate(
        (key_unnormed * key_inverse_norm * key_scale).reshape(
            row_count, heads_on_device, HEAD_CHANNELS
        ),
        angles,
    ).astype(jnp.bfloat16)
    query_seqs = query_rot.reshape(seq_shape)
    key_seqs = key_rot.reshape(seq_shape)
    value_seqs = values.reshape(seq_shape)
    attended, lse_all = lax.map(attend_sequence, (query_seqs, key_seqs, value_seqs, doc_seqs))
    attended = attended.reshape(row_count, local_width)
    branch = lax.psum(matmul(attended, output_full), "mp")
    branch_inv = lax.rsqrt(jnp.mean(branch * branch, axis=1, keepdims=True) + EPSILON)
    hidden_state = tokens.astype(jnp.float32) + branch * branch_inv * attn_gains
    hidden_low = hidden_state.astype(jnp.bfloat16)
    gate_act = matmul(hidden_low, gate_full)
    up_part = matmul(hidden_low, up_full)
    product = (jax.nn.silu(gate_act) * up_part).astype(jnp.bfloat16)
    mlp_branch = lax.psum(matmul(product, down_full).astype(jnp.bfloat16), "mp").astype(jnp.float32)
    mlp_inv = lax.rsqrt(jnp.mean(mlp_branch * mlp_branch, axis=1, keepdims=True) + EPSILON)
    block_out = (hidden_state + mlp_branch * mlp_inv * mlp_gains).astype(jnp.bfloat16)
    gate_full, up_full, down_full, mlp_gains = (
        lax.all_gather(gate_weight, "dp", axis=0, tiled=True),
        lax.all_gather(up_weight, "dp", axis=0, tiled=True),
        lax.all_gather(down_weight, "dp", axis=1, tiled=True),
        lax.all_gather(mlp_gain, "dp", axis=0, tiled=True),
    )
    upstream = cotangent.astype(jnp.float32)
    grad_mlp_scale = jnp.sum(upstream * mlp_branch * mlp_inv, axis=0)
    mlp_scaled = mlp_gains * upstream
    mlp_cube = mlp_inv * mlp_inv * mlp_inv
    d_mlp = (
        mlp_inv * mlp_scaled
        - mlp_branch * mlp_cube * jnp.mean(mlp_scaled * mlp_branch, axis=1, keepdims=True)
    ).astype(jnp.bfloat16)
    grad_down = transposed_left(product, d_mlp)
    d_product = transposed_right(d_mlp, down_full)
    sigmoid = jax.nn.sigmoid(gate_act)
    d_gate = (d_product * up_part * sigmoid * (1.0 + gate_act * (1.0 - sigmoid))).astype(
        jnp.bfloat16
    )
    d_up = (d_product * gate_act * sigmoid).astype(jnp.bfloat16)
    grad_gate = transposed_left(hidden_low, d_gate)
    grad_up = transposed_left(hidden_low, d_up)
    mlp_input = transposed_right(d_gate, gate_full) + transposed_right(d_up, up_full)
    d_hidden = upstream + lax.psum(mlp_input.astype(jnp.bfloat16), "mp").astype(jnp.float32)
    mlp_grads = (
        lax.psum_scatter(
            grad_gate.astype(jnp.bfloat16), "dp", scatter_dimension=0, tiled=True
        ).astype(jnp.float32),
        lax.psum_scatter(
            grad_up.astype(jnp.bfloat16), "dp", scatter_dimension=0, tiled=True
        ).astype(jnp.float32),
        lax.psum_scatter(
            grad_down.astype(jnp.bfloat16), "dp", scatter_dimension=1, tiled=True
        ).astype(jnp.float32),
        lax.psum_scatter(
            grad_mlp_scale.astype(jnp.bfloat16), "dp", scatter_dimension=0, tiled=True
        ).astype(jnp.float32),
    )
    query_full, key_complete, value_full, output_full, query_gains, key_gains, attn_gains = (
        lax.all_gather(q_weight, "dp", axis=0, tiled=True),
        lax.all_gather(k_weight, "dp", axis=0, tiled=True),
        lax.all_gather(v_weight, "dp", axis=0, tiled=True),
        lax.all_gather(o_weight, "dp", axis=1, tiled=True),
        lax.all_gather(q_gain, "dp", axis=1, tiled=True),
        lax.all_gather(k_gain, "dp", axis=1, tiled=True),
        lax.all_gather(attn_gain, "dp", axis=0, tiled=True),
    )
    query_scale = query_gains.reshape(-1)
    key_scale = key_gains.reshape(-1)
    grad_attn_scale = jnp.sum(d_hidden * branch * branch_inv, axis=0)
    attn_scaled = attn_gains * d_hidden
    branch_cube = branch_inv * branch_inv * branch_inv
    d_branch = (
        branch_inv * attn_scaled
        - branch * branch_cube * jnp.mean(attn_scaled * branch, axis=1, keepdims=True)
    ).astype(jnp.bfloat16)
    grad_output = transposed_left(attended, d_branch)
    d_attended = transposed_right(d_branch, output_full).astype(jnp.bfloat16)
    grad_qrot, grad_krot, grad_vals = lax.map(
        attend_backward,
        (query_seqs, key_seqs, value_seqs, doc_seqs, d_attended.reshape(seq_shape), lse_all),
    )
    d_values = grad_vals.reshape(row_count, local_width).astype(jnp.bfloat16)
    d_qnorm = rotate_back(
        grad_qrot.reshape(row_count, heads_on_device, HEAD_CHANNELS), angles
    ).reshape(row_count, local_width)
    grad_key_normed = rotate_back(
        grad_krot.reshape(row_count, heads_on_device, HEAD_CHANNELS), angles
    ).reshape(row_count, local_width)
    grad_qscale = jnp.sum(d_qnorm * query_raw * query_inv, axis=0).reshape(
        heads_on_device, HEAD_CHANNELS
    )
    grad_key_rms_factor = jnp.sum(
        grad_key_normed * key_unnormed * key_inverse_norm, axis=0
    ).reshape(heads_on_device, HEAD_CHANNELS)
    query_scaled = query_scale * d_qnorm
    key_scaled = key_scale * grad_key_normed
    query_inner, key_inner = lax.psum(
        (jnp.sum(query_scaled * query_raw, axis=1), jnp.sum(key_scaled * key_unnormed, axis=1)),
        "mp",
    )
    query_cube = query_inv * query_inv * query_inv
    key_cube = key_inverse_norm * key_inverse_norm * key_inverse_norm
    d_query = (
        query_inv * query_scaled - query_raw * query_cube * (query_inner / D)[:, None]
    ).astype(jnp.bfloat16)
    d_key = (
        key_inverse_norm * key_scaled - key_unnormed * key_cube * (key_inner / D)[:, None]
    ).astype(jnp.bfloat16)
    grad_query = transposed_left(tokens, d_query)
    grad_key = transposed_left(tokens, d_key)
    grad_value = transposed_left(tokens, d_values)
    token_back = (
        transposed_right(d_query, query_full)
        + transposed_right(d_key, key_complete)
        + transposed_right(d_values, value_full)
    )
    grad_tokens = (
        d_hidden + lax.psum(token_back.astype(jnp.bfloat16), "mp").astype(jnp.float32)
    ).astype(jnp.bfloat16)
    attn_grads = (
        lax.psum_scatter(
            grad_query.astype(jnp.bfloat16), "dp", scatter_dimension=0, tiled=True
        ).astype(jnp.float32),
        lax.psum_scatter(
            grad_key.astype(jnp.bfloat16), "dp", scatter_dimension=0, tiled=True
        ).astype(jnp.float32),
        lax.psum_scatter(
            grad_value.astype(jnp.bfloat16), "dp", scatter_dimension=0, tiled=True
        ).astype(jnp.float32),
        lax.psum_scatter(
            grad_output.astype(jnp.bfloat16), "dp", scatter_dimension=1, tiled=True
        ).astype(jnp.float32),
        lax.psum_scatter(
            grad_qscale.astype(jnp.bfloat16), "dp", scatter_dimension=1, tiled=True
        ).astype(jnp.float32),
        lax.psum_scatter(
            grad_key_rms_factor.astype(jnp.bfloat16), "dp", scatter_dimension=1, tiled=True
        ).astype(jnp.float32),
        lax.psum_scatter(
            grad_attn_scale.astype(jnp.bfloat16), "dp", scatter_dimension=0, tiled=True
        ).astype(jnp.float32),
    )
    return (
        block_out,
        grad_tokens,
        attn_grads[0],
        attn_grads[1],
        attn_grads[2],
        attn_grads[3],
        attn_grads[4],
        attn_grads[5],
        attn_grads[6],
        mlp_grads[0],
        mlp_grads[1],
        mlp_grads[2],
        mlp_grads[3],
    )


MESH = pl.DeviceIdType.MESH
SUBS = 2
TILE = 256
BLOCK = 256
SMALL = 16


def place_of(index, n):
    odd = lax.rem(index, 2)
    half = lax.div(index, 2)
    return (1 - odd) * half + odd * (n - 1 - half)


def device_at(place, n):
    late = lax.div(place, n // 2)
    return (1 - late) * (2 * place) + late * (2 * (n - 1 - place) + 1)


def holder_of(index, steps, n):
    return device_at(lax.rem(place_of(index, n) + (steps + 2 * n), n), n)


def neighbours(n):
    index = lax.axis_index("dp")
    rank = lax.axis_index("mp")
    core = lax.rem(rank, 2)
    right = {"dp": holder_of(index, 1, n)}
    left = {"dp": holder_of(index, -1, n)}
    twin = {"mp": rank + 1 - 2 * core}
    far = {"mp": lax.rem(rank + 2, 4)}
    return index, core, right, left, twin, far


def greet(targets, meanwhile=None):
    barrier = pltpu.get_barrier_semaphore()
    for target in targets:
        pl.semaphore_signal(barrier, inc=1, device_id=target, device_id_type=MESH)
    if meanwhile is not None:
        meanwhile()
    pl.semaphore_wait(barrier, len(targets))


def exchange(source, target, send, recv, slot, device):
    return pltpu.make_async_remote_copy(
        src_ref=source,
        dst_ref=target,
        send_sem=send.at[slot],
        recv_sem=recv.at[slot],
        device_id=device,
        device_id_type=MESH,
    )


def columns_to_rows(pieces, count):
    lane = lax.broadcasted_iota(jnp.int32, (count, 128), 1)
    spread = jnp.zeros((count, 128), jnp.float32)
    for place, piece in enumerate(pieces):
        spread = jnp.where(lane == place, piece, spread)
    return spread.T[:8]


def rows_to_columns(rows):
    padded = jnp.concatenate([rows] + [jnp.zeros_like(rows)] * 15, axis=0)
    return padded.T


def gather_kernel(
    n,
    query,
    key,
    value,
    output,
    small,
    doc_row,
    frequency,
    down,
    full,
    query_gain,
    key_gain,
    attn_gain,
    mlp_gain,
    cosine,
    sine,
    doc_col,
    down_shard,
    mine,
    down_buf,
    turned_down,
    small_full,
    send,
    recv,
    small_send,
    small_recv,
    load,
    store,
):
    index, core, right, left, twin, far = neighbours(n)
    chunk = query.shape[1]
    local = query.shape[2]
    rows = chunk // SUBS
    count = cosine.shape[0]
    heads = local // HEAD_CHANNELS
    units = down.shape[0]

    loads = [
        pltpu.make_async_copy(
            source, mine.at[:, :, pl.ds(place * local, local)], load.at[place]
        )
        for place, source in enumerate((query, key, value))
    ]
    for copy in loads:
        copy.start()

    def turn_output():
        flipped = output[...].T
        mine[0, :, 3 * local :] = flipped[:chunk]
        mine[1, :, 3 * local :] = flipped[chunk:]

    def hop(way, sub, step, incoming):
        owner = holder_of(index, (step - 1 + incoming) * (2 * way - 1), n)
        span = pl.ds(sub * rows, rows)
        target = full.at[owner, way, span]
        return pltpu.make_async_remote_copy(
            src_ref=mine.at[way, span] if step == 1 and not incoming else target,
            dst_ref=target,
            send_sem=send.at[way, sub, step - 1],
            recv_sem=recv.at[way, sub, step - 1],
            device_id=left if way else right,
            device_id_type=MESH,
        )

    def small_hop(step, incoming):
        target = small_full.at[holder_of(index, 1 - incoming - step, n)]
        source = small if step == 1 and not incoming else target
        return exchange(source, target, small_send, small_recv, step - 1, right)

    greet((right, left), turn_output)
    small_hop(1, 0).start()
    for copy in loads:
        copy.wait()
    for sub in range(SUBS):
        for way in range(2):
            hop(way, sub, 1, 0).start()
    own = pltpu.make_async_copy(mine, full.at[index], store.at[0])
    own.start()
    down_load = pltpu.make_async_copy(down, down_buf, store.at[1])
    down_load.start()
    small_full[index] = small[...]
    docs = doc_row[...].astype(jnp.float32)
    leading = jnp.sum(1.0 - docs, axis=1, keepdims=True)
    doc_col[...] = rows_to_columns(jnp.broadcast_to(docs, (8, count)))

    def table(tile):
        span = pl.ds(pl.multiple_of(tile * 64, 64), 64)
        spot = lax.broadcasted_iota(jnp.int32, (64, HEAD_CHANNELS), 0) + tile * 64
        lane = lax.broadcasted_iota(jnp.int32, (64, HEAD_CHANNELS), 1)
        angles = (spot.astype(jnp.float32) - doc_col[span, 0:1] * leading) * frequency[...]
        cosine[span, :] = jnp.cos(angles)
        wave = jnp.sin(angles)
        sine[span, :] = jnp.where(lane < HEAD_CHANNELS // 2, -wave, wave)

    tiles = count // 64
    for step in range(1, n):
        for sub in range(SUBS):
            for way in range(2):
                hop(way, sub, step, 1).wait_recv()
                if step < n - 1:
                    hop(way, sub, step + 1, 0).start()
        small_hop(step, 1).wait_recv()
        if step < n - 1:
            small_hop(step + 1, 0).start()
        if step <= 4:
            pl.loop((step - 1) * tiles // 4, step * tiles // 4)(table)
        if step == 5:
            down_load.wait()
            for part in range(4):
                span = slice(part * (units // 4), (part + 1) * (units // 4))
                flipped = down_buf[span, :].T
                turned_down[0, :, span] = flipped[:chunk]
                turned_down[1, :, span] = flipped[chunk:]
            down_store = pltpu.make_async_copy(turned_down, down_shard, store.at[2])
            down_store.start()
    lanes = jnp.zeros(small.shape, jnp.float32)
    for owner in range(n):
        part = small_full[owner].astype(jnp.float32)
        lanes = lanes + part
        for row in range(2):
            spot = (2 * owner + row) * 128
            attn_gain[:, spot : spot + 128] = part[8 + row : 9 + row]
            mlp_gain[:, spot : spot + 128] = part[10 + row : 11 + row]
    for head in range(heads):
        spot = head * HEAD_CHANNELS
        query_gain[:, spot : spot + HEAD_CHANNELS] = lanes[head : head + 1]
        key_gain[:, spot : spot + HEAD_CHANNELS] = lanes[4 + head : 5 + head]
    own.wait()
    down_store.wait()
    for step in range(1, n):
        for sub in range(SUBS):
            for way in range(2):
                hop(way, sub, step, 0).wait_send()
        small_hop(step, 0).wait_send()


def kernel_gather(query, key, value, output, small, doc_ids, frequency, down, n):
    rows, local = query.shape
    chunk = rows // 2
    count = doc_ids.shape[0]
    units = down.shape[0]
    low = query.dtype
    full = jnp.float32
    hbm = pl.BlockSpec(memory_space=pl.ANY)
    vmem = pl.BlockSpec(memory_space=pltpu.VMEM)
    dma = pltpu.SemaphoreType.DMA
    shape = jax.ShapeDtypeStruct
    split = [part.reshape(2, chunk, local) for part in (query, key, value)]
    outs = pl.pallas_call(
        functools.partial(gather_kernel, n),
        out_shape=(
            shape((n, 2, chunk, 4 * local), low),
            shape((1, local), full),
            shape((1, local), full),
            shape((1, n * rows), full),
            shape((1, n * rows), full),
            shape((count, HEAD_CHANNELS), full),
            shape((count, HEAD_CHANNELS), full),
            shape((count, 128), full),
            shape((2, chunk, units), low),
        ),
        in_specs=[hbm] * 3 + [vmem] * 4 + [hbm],
        out_specs=(hbm,) + (vmem,) * 7 + (hbm,),
        scratch_shapes=[
            pltpu.VMEM((2, chunk, 4 * local), low),
            pltpu.VMEM((units, rows), low),
            pltpu.VMEM((2, chunk, units), low),
            pltpu.VMEM((n, SMALL, 128), low),
            dma((2, SUBS, n - 1)),
            dma((2, SUBS, n - 1)),
            dma((n - 1,)),
            dma((n - 1,)),
            dma((3,)),
            dma((3,)),
        ],
        compiler_params=pltpu.CompilerParams(
            collective_id=0, has_side_effects=True, vmem_limit_bytes=60 * 2**20
        ),
    )(*split, output, small, doc_ids.reshape(1, count), frequency, down)
    return outs[0].reshape(n * rows, 4 * local), *outs[1:]


def scatter_kernel(
    n,
    grads,
    query_row,
    key_row,
    attn_row,
    mlp_row,
    out_query,
    out_key,
    out_value,
    out_output,
    small_out,
    own,
    inbox,
    tail,
    parts,
    small_inbox,
    small_outbox,
    send,
    recv,
    small_send,
    small_recv,
    own_sem,
):
    index, core, right, left, twin, far = neighbours(n)
    chunk = out_query.shape[1]
    local = out_query.shape[2]
    rows = chunk // SUBS
    heads = local // HEAD_CHANNELS

    def hop(way, sub, step):
        first = grads.at[holder_of(index, 2 * way - 1, n), way, pl.ds(sub * rows, rows)]
        return pltpu.make_async_remote_copy(
            src_ref=first if step == 1 else inbox.at[step - 2, way, sub],
            dst_ref=inbox.at[step - 1, way, sub],
            send_sem=send.at[way, sub, step - 1],
            recv_sem=recv.at[way, sub, step - 1],
            device_id=left if way else right,
            device_id_type=MESH,
        )

    def own_copy(way, sub, step):
        owner = holder_of(index, (1 + step) * (2 * way - 1), n)
        return pltpu.make_async_copy(
            grads.at[owner, way, pl.ds(sub * rows, rows)],
            own.at[way, sub],
            own_sem.at[way, sub],
        )

    def small_hop(step):
        first = parts.at[holder_of(index, -1, n)]
        return exchange(
            first if step == 1 else small_outbox.at[step - 2],
            small_inbox.at[step - 1],
            small_send,
            small_recv,
            step - 1,
            twin if step == n else right,
        )

    greet((right, left, twin))
    for sub in range(SUBS):
        for way in range(2):
            hop(way, sub, 1).start()
            own_copy(way, sub, 1).start()
    for owner in range(n):
        for head in range(heads):
            spot = head * HEAD_CHANNELS
            parts[owner, head : head + 1, :] = query_row[:, spot : spot + HEAD_CHANNELS]
            parts[owner, 4 + head : 5 + head, :] = key_row[:, spot : spot + HEAD_CHANNELS]
        for row in range(2):
            spot = (2 * owner + row) * 128
            parts[owner, 8 + row : 9 + row, :] = attn_row[:, spot : spot + 128]
            parts[owner, 10 + row : 11 + row, :] = mlp_row[:, spot : spot + 128]
        parts[owner, 12:16, :] = jnp.zeros((4, 128), jnp.float32)
    small_hop(1).start()
    for step in range(1, n):
        for sub in range(SUBS):
            for way in range(2):
                own_copy(way, sub, step).wait()
                hop(way, sub, step).wait_recv()

                @pl.loop(0, rows // 16, unroll=2)
                def _(tile, way=way, sub=sub, step=step):
                    near = pl.ds(pl.multiple_of(tile * 16, 16), 16)
                    got = inbox[step - 1, way, sub, near, :]
                    held = own[way, sub, near, :]
                    if step < n - 1:
                        inbox[step - 1, way, sub, near, :] = got + held
                    else:
                        total = got.astype(jnp.float32) + held.astype(jnp.float32)
                        wide = pl.ds(pl.multiple_of(sub * rows + tile * 16, 16), 16)
                        out_query[way, wide, :] = total[:, :local]
                        out_key[way, wide, :] = total[:, local : 2 * local]
                        out_value[way, wide, :] = total[:, 2 * local : 3 * local]
                        deep = pl.ds(
                            pl.multiple_of(way * chunk + sub * rows + tile * 16, 16), 16
                        )
                        tail[deep, :] = total[:, 3 * local :]

                if step < n - 1:
                    hop(way, sub, step + 1).start()
                    own_copy(way, sub, step + 1).start()
        if step < n - 1:
            small_hop(step).wait_recv()
            owner = holder_of(index, -1 - step, n)
            small_outbox[step - 1] = small_inbox[step - 1] + parts[owner]
            small_hop(step + 1).start()
    small_hop(n - 1).wait_recv()
    small_outbox[n - 2] = small_inbox[n - 2] + parts[index]
    small_hop(n).start()
    out_output[...] = tail[...].T
    small_hop(n).wait_recv()
    line = lax.broadcasted_iota(jnp.int32, small_out.shape, 0)
    small_out[...] = small_outbox[n - 2] + jnp.where(line >= 8, small_inbox[n - 1], 0.0)
    for step in range(1, n):
        for sub in range(SUBS):
            for way in range(2):
                hop(way, sub, step).wait_send()
        small_hop(step).wait_send()
    small_hop(n).wait_send()


def kernel_scatter(grads, query_row, key_row, attn_row, mlp_row, n):
    rows, width = grads.shape[0] // n, grads.shape[1]
    chunk, local = rows // 2, width // 4
    deep = chunk // SUBS
    full = jnp.float32
    vmem = pl.BlockSpec(memory_space=pltpu.VMEM)
    dma = pltpu.SemaphoreType.DMA
    shape = jax.ShapeDtypeStruct
    outs = pl.pallas_call(
        functools.partial(scatter_kernel, n),
        out_shape=(shape((2, chunk, local), full),) * 3
        + (shape((local, rows), full), shape((SMALL, 128), full)),
        in_specs=[pl.BlockSpec(memory_space=pl.ANY)] + [vmem] * 4,
        out_specs=(vmem,) * 5,
        scratch_shapes=[
            pltpu.VMEM((2, SUBS, deep, width), grads.dtype),
            pltpu.VMEM((n - 1, 2, SUBS, deep, width), grads.dtype),
            pltpu.VMEM((rows, local), full),
            pltpu.VMEM((n, SMALL, 128), full),
            pltpu.VMEM((n, SMALL, 128), full),
            pltpu.VMEM((n - 1, SMALL, 128), full),
            dma((2, SUBS, n - 1)),
            dma((2, SUBS, n - 1)),
            dma((n,)),
            dma((n,)),
            dma((2, SUBS)),
        ],
        compiler_params=pltpu.CompilerParams(
            collective_id=1, has_side_effects=True, vmem_limit_bytes=60 * 2**20
        ),
    )(grads.reshape(n, 2, chunk, width), query_row, key_row, attn_row, mlp_row)
    return tuple(part.reshape(rows, local) for part in outs[:3]) + outs[3:]


def turned(vectors, cosine, sine):
    return vectors * cosine + pltpu.roll(vectors, HEAD_CHANNELS // 2, 1) * sine


def masked_scores(query, key, doc_col, doc_row, block):
    length = key.shape[0]
    scores = lax.dot_general(
        query, key, (((1,), (1,)), ((), ())), preferred_element_type=jnp.float32
    ) * (1.0 / math.sqrt(HEAD_CHANNELS))
    row = lax.broadcasted_iota(jnp.int32, scores.shape, 0) + block * BLOCK
    col = lax.broadcasted_iota(jnp.int32, scores.shape, 1)
    own = doc_col[block * BLOCK : (block + 1) * BLOCK, 0:1]
    same = own == doc_row[:, :length].astype(jnp.float32)
    return jnp.where((col <= row) & same, scores, MASKED)


def attend_kernel(
    n,
    tokens,
    attn_full,
    gate_shard,
    up_shard,
    cosine,
    sine,
    doc_col,
    doc_row,
    query_gain,
    key_gain,
    attn_gain,
    gate_full,
    up_full,
    query_raw_out,
    key_raw_out,
    query_rot_out,
    key_rot_out,
    value_out,
    attended_out,
    totals,
    inverses,
    branch_out,
    hidden_out,
    hidden_low,
    lhs,
    weights,
    query_raw,
    key_raw,
    query_rot,
    key_rot,
    value,
    attended,
    mixed,
    twin_in,
    pair,
    far_in,
    branch,
    half_buf,
    low_buf,
    stat,
    ring_send,
    ring_recv,
    stat_send,
    stat_recv,
    twin_send,
    twin_recv,
    far_send,
    far_recv,
    join_send,
    join_recv,
    load_sem,
    store_sem,
):
    index, core, right, left, twin, far = neighbours(n)
    count, width = lhs.shape
    half = count // 2
    local = query_raw.shape[1]
    heads = local // HEAD_CHANNELS
    blocks = width // TILE
    shards = (gate_shard, up_shard)
    fulls = (gate_full, up_full)
    right_side = (((1,), (1,)), ((), ()))

    def ring(way, unit, step, incoming):
        owner = holder_of(index, (step - 1 + incoming) * (2 * way - 1), n)
        target = fulls[unit].at[owner, way]
        return pltpu.make_async_remote_copy(
            src_ref=shards[unit].at[way] if step == 1 and not incoming else target,
            dst_ref=target,
            send_sem=ring_send.at[way, unit, step - 1],
            recv_sem=ring_recv.at[way, unit, step - 1],
            device_id=left if way else right,
            device_id_type=MESH,
        )

    events = [(step, unit) for step in range(1, n) for unit in range(2)]

    def serve():
        step, unit = events.pop(0)
        for way in range(2):
            ring(way, unit, step, 1).wait_recv()
            if step < n - 1:
                ring(way, unit, step + 1, 0).start()

    greet((right, left, twin, far))
    for unit in range(2):
        for way in range(2):
            ring(way, unit, 1, 0).start()
    loads = [
        pltpu.make_async_copy(tokens, lhs, load_sem.at[0]),
        pltpu.make_async_copy(attn_full, weights, load_sem.at[1]),
        pltpu.make_async_copy(
            tokens.at[pl.ds(pl.multiple_of(core * half, half), half)], half_buf, load_sem.at[2]
        ),
        pltpu.make_async_copy(gate_shard, gate_full.at[index], load_sem.at[3]),
        pltpu.make_async_copy(up_shard, up_full.at[index], load_sem.at[4]),
    ]
    for copy in loads:
        copy.start()
    loads[0].wait()
    loads[1].wait()

    def project(target, start):
        for tile in range(local // TILE):
            cols = slice(start + tile * TILE, start + (tile + 1) * TILE)
            target[:, tile * TILE : (tile + 1) * TILE] = jnp.dot(
                lhs[...], weights[:, cols], preferred_element_type=jnp.float32
            ).astype(target.dtype)

    project(query_raw, 0)
    project(key_raw, local)
    squares = [
        jnp.sum(raw[...] * raw[...], axis=1, keepdims=True) for raw in (query_raw, key_raw)
    ]
    stat[0] = columns_to_rows(squares, count)
    first = exchange(stat.at[0], stat.at[1], stat_send, stat_recv, 0, twin)
    first.start()
    project(value, 2 * local)
    first.wait()
    stat[2] = stat[0] + stat[1]
    second = exchange(stat.at[2], stat.at[3], stat_send, stat_recv, 1, far)
    second.start()
    serve()
    second.wait()
    inverses[...] = lax.rsqrt(rows_to_columns(stat[2] + stat[3]) / width + EPSILON)

    @pl.loop(0, heads)
    def _(head):
        cols = pl.ds(pl.multiple_of(head * HEAD_CHANNELS, HEAD_CHANNELS), HEAD_CHANNELS)
        for place, (raw, gain, out) in enumerate(
            ((query_raw, query_gain, query_rot), (key_raw, key_gain, key_rot))
        ):
            normed = raw[:, cols] * inverses[:, place : place + 1] * gain[:, cols]
            out[:, cols] = turned(normed, cosine[...], sine[...]).astype(jnp.bfloat16)

    stores = [
        pltpu.make_async_copy(source, target, store_sem.at[place])
        for place, (source, target) in enumerate(
            (
                (query_raw, query_raw_out),
                (key_raw, key_raw_out),
                (query_rot, query_rot_out),
                (key_rot, key_rot_out),
                (value, value_out),
            )
        )
    ]
    for copy in stores:
        copy.start()
    serve()
    totals[...] = jnp.zeros_like(totals)

    @pl.loop(0, heads)
    def _(head):
        cols = pl.ds(pl.multiple_of(head * HEAD_CHANNELS, HEAD_CHANNELS), HEAD_CHANNELS)
        lane = lax.broadcasted_iota(jnp.int32, (BLOCK, 128), 1)
        for block in range(count // BLOCK):
            span = slice(block * BLOCK, (block + 1) * BLOCK)
            length = (block + 1) * BLOCK
            scores = masked_scores(
                query_rot[span, cols], key_rot[:length, cols], doc_col, doc_row, block
            )
            maximum = jnp.max(scores, axis=1, keepdims=True)
            powers = jnp.exp(scores - maximum)
            denominator = jnp.sum(powers, axis=1, keepdims=True)
            rounded = (powers * (1.0 / denominator)).astype(jnp.bfloat16)
            attended[span, cols] = jnp.dot(
                rounded, value[:length, cols], preferred_element_type=jnp.float32
            ).astype(jnp.bfloat16)
            totals[span, :] = jnp.where(
                lane == head, maximum + jnp.log(denominator), totals[span, :]
            )

    stores.append(pltpu.make_async_copy(attended, attended_out, store_sem.at[5]))
    stores[5].start()
    serve()

    def twin_copy(tile):
        span = pl.ds(pl.multiple_of((1 - core) * half, half), half)
        return exchange(
            mixed.at[tile % 4, span], twin_in.at[tile % 4], twin_send, twin_recv, tile, twin
        )

    def far_copy(tile):
        return exchange(pair.at[tile], far_in.at[tile], far_send, far_recv, tile, far)

    def output_tile(tile):
        span = slice(tile * TILE, (tile + 1) * TILE)
        mixed[tile % 4] = lax.dot_general(
            attended[...],
            weights[span, 3 * local :],
            right_side,
            preferred_element_type=jnp.float32,
        ).astype(jnp.bfloat16)
        twin_copy(tile).start()

    def add_twin(tile):
        twin_copy(tile).wait_recv()

        @pl.loop(0, half // 32)
        def _(row):
            span = pl.ds(pl.multiple_of(row * 32, 32), 32)
            mine = pl.ds(pl.multiple_of(core * half + row * 32, 32), 32)
            total = mixed[tile % 4, mine, :].astype(jnp.float32) + twin_in[
                tile % 4, span, :
            ].astype(jnp.float32)
            pair[tile, span, :] = total.astype(jnp.bfloat16)

        far_copy(tile).start()
        twin_copy(tile).wait_send()

    def add_far(tile):
        far_copy(tile).wait_recv()

        @pl.loop(0, half // 32)
        def _(row):
            span = pl.ds(pl.multiple_of(row * 32, 32), 32)
            branch[span, tile * TILE : (tile + 1) * TILE] = pair[tile, span, :].astype(
                jnp.float32
            ) + far_in[tile, span, :].astype(jnp.float32)

    for tile in range(blocks):
        output_tile(tile)
        if tile >= 1:
            add_twin(tile - 1)
    add_twin(blocks - 1)
    serve()
    for tile in range(blocks):
        add_far(tile)
        if tile % 2 == 1:
            serve()
    loads[2].wait()

    def finish(tile):
        span = pl.ds(pl.multiple_of(tile * 16, 16), 16)
        mix = branch[span, :]
        inverse = lax.rsqrt(jnp.sum(mix * mix, axis=1, keepdims=True) / width + EPSILON)
        state = half_buf[span, :].astype(jnp.float32) + mix * inverse * attn_gain[...]
        low_buf[span, :] = state.astype(jnp.bfloat16)
        hidden_out[span, :] = state

    def join(part, kind):
        span = pl.ds(part * (half // 4), half // 4)
        if kind == 2:
            return pltpu.make_async_copy(
                low_buf.at[span], hidden_low.at[core, span], store_sem.at[6 + part]
            )
        target = hidden_low.at[1 - core if kind else core, span]
        return exchange(
            target if kind else low_buf.at[span], target, join_send, join_recv, part, twin
        )

    for part in range(4):
        pl.loop(part * (half // 64), (part + 1) * (half // 64))(finish)
        join(part, 0).start()
        join(part, 2).start()
    stores.append(pltpu.make_async_copy(branch, branch_out, store_sem.at[10]))
    stores[6].start()
    while events:
        serve()
    for part in range(4):
        join(part, 1).wait_recv()
        join(part, 0).wait_send()
        join(part, 2).wait()
    for copy in stores + loads[3:]:
        copy.wait()
    for tile in range(blocks):
        far_copy(tile).wait_send()
    for step in range(1, n):
        for unit in range(2):
            for way in range(2):
                ring(way, unit, step, 0).wait_send()


def kernel_attend(
    tokens,
    attn_full,
    gate_shard,
    up_shard,
    cosine,
    sine,
    doc_col,
    doc_ids,
    query_gain,
    key_gain,
    attn_gain,
    n,
):
    count, width = tokens.shape
    local = query_gain.shape[1]
    units = gate_shard.shape[1]
    half = count // 2
    chunk = width // n // 2
    blocks = width // TILE
    low = jnp.bfloat16
    full = jnp.float32
    hbm = pl.BlockSpec(memory_space=pl.ANY)
    vmem = pl.BlockSpec(memory_space=pltpu.VMEM)
    dma = pltpu.SemaphoreType.DMA
    shape = jax.ShapeDtypeStruct
    outs = pl.pallas_call(
        functools.partial(attend_kernel, n),
        out_shape=(
            shape((n, 2, chunk, units), low),
            shape((n, 2, chunk, units), low),
            shape((count, local), full),
            shape((count, local), full),
            shape((count, local), low),
            shape((count, local), low),
            shape((count, local), low),
            shape((count, local), low),
            shape((count, 128), full),
            shape((count, 128), full),
            shape((half, width), full),
            shape((half, width), full),
            shape((2, half, width), low),
        ),
        in_specs=[hbm] * 4 + [vmem] * 7,
        out_specs=(hbm,) * 8 + (vmem,) * 2 + (hbm, vmem, hbm),
        scratch_shapes=[
            pltpu.VMEM((count, width), low),
            pltpu.VMEM((width, 4 * local), low),
            pltpu.VMEM((count, local), full),
            pltpu.VMEM((count, local), full),
            pltpu.VMEM((count, local), low),
            pltpu.VMEM((count, local), low),
            pltpu.VMEM((count, local), low),
            pltpu.VMEM((count, local), low),
            pltpu.VMEM((4, count, TILE), low),
            pltpu.VMEM((4, half, TILE), low),
            pltpu.VMEM((blocks, half, TILE), low),
            pltpu.VMEM((blocks, half, TILE), low),
            pltpu.VMEM((half, width), full),
            pltpu.VMEM((half, width), low),
            pltpu.VMEM((half, width), low),
            pltpu.VMEM((4, 8, count), full),
            dma((2, 2, n - 1)),
            dma((2, 2, n - 1)),
            dma((2,)),
            dma((2,)),
            dma((blocks,)),
            dma((blocks,)),
            dma((blocks,)),
            dma((blocks,)),
            dma((4,)),
            dma((4,)),
            dma((5,)),
            dma((11,)),
        ],
        compiler_params=pltpu.CompilerParams(
            collective_id=4, has_side_effects=True, vmem_limit_bytes=58 * 2**20
        ),
    )(
        tokens,
        attn_full,
        gate_shard.reshape(2, chunk, units),
        up_shard.reshape(2, chunk, units),
        cosine,
        sine,
        doc_col,
        doc_ids.reshape(1, count),
        query_gain,
        key_gain,
        attn_gain,
    )
    return (
        outs[0].reshape(width, units),
        outs[1].reshape(width, units),
        *outs[2:12],
        outs[12].reshape(count, width),
    )


def feed_kernel(
    n,
    hidden_low,
    gate_full,
    up_full,
    down_shard,
    hidden,
    upstream,
    gains,
    product_out,
    gate_slope,
    silu_out,
    down_full,
    d_mlp,
    block_half,
    gain_grad,
    lhs,
    product,
    held,
    gate_tile,
    up_tile,
    slope_tile,
    silu_tile,
    twin_out,
    twin_in,
    pair,
    far_in,
    branch,
    hidden_buf,
    upstream_buf,
    d_buf,
    block_buf,
    gain_sum,
    ring_send,
    ring_recv,
    twin_send,
    twin_recv,
    far_send,
    far_recv,
    join_send,
    join_recv,
    load_sem,
    tile_sem,
    stage_sem,
    store_sem,
):
    index, core, right, left, twin, far = neighbours(n)
    half = hidden.shape[0]
    chunk = held.shape[2]
    rows = chunk // SUBS
    tiles = product.shape[1] // TILE
    width = branch.shape[1]

    loads = [
        pltpu.make_async_copy(hidden_low, lhs, load_sem.at[0]),
        pltpu.make_async_copy(down_shard, held.at[index], load_sem.at[1]),
        pltpu.make_async_copy(hidden, hidden_buf, load_sem.at[2]),
        pltpu.make_async_copy(
            upstream.at[pl.ds(pl.multiple_of(core * half, half), half)],
            upstream_buf,
            load_sem.at[3],
        ),
    ]

    def weight_copies(tile, slot):
        cols = pl.ds(pl.multiple_of(tile * TILE, TILE), TILE)
        return (
            pltpu.make_async_copy(gate_full.at[:, cols], gate_tile.at[slot], tile_sem.at[slot, 0]),
            pltpu.make_async_copy(up_full.at[:, cols], up_tile.at[slot], tile_sem.at[slot, 1]),
        )

    def stage_copies(tile, slot):
        cols = pl.ds(pl.multiple_of(tile * TILE, TILE), TILE)
        return (
            pltpu.make_async_copy(slope_tile.at[slot], gate_slope.at[:, cols], stage_sem.at[slot, 0]),
            pltpu.make_async_copy(silu_tile.at[slot], silu_out.at[:, cols], stage_sem.at[slot, 1]),
        )

    def ring(way, sub, step, incoming):
        owner = holder_of(index, (step - 1 + incoming) * (2 * way - 1), n)
        span = pl.ds(sub * rows, rows)
        target = held.at[owner, way, span]
        return pltpu.make_async_remote_copy(
            src_ref=down_shard.at[way, span] if step == 1 and not incoming else target,
            dst_ref=target,
            send_sem=ring_send.at[way, sub, step - 1],
            recv_sem=ring_recv.at[way, sub, step - 1],
            device_id=left if way else right,
            device_id_type=MESH,
        )

    def serve(step, sub):
        for way in range(2):
            ring(way, sub, step, 1).wait_recv()
            if step < n - 1:
                ring(way, sub, step + 1, 0).start()

    def columns(sub):
        return pl.ds(0, 2 * chunk) if sub is None else pl.ds(sub * 2 * rows, 2 * rows)

    def twin_copy(step, sub=None):
        return exchange(
            twin_out.at[step, :, columns(sub)],
            twin_in.at[step, :, columns(sub)],
            twin_send,
            twin_recv,
            step + (sub or 0),
            twin,
        )

    def far_copy(step, sub=None):
        return exchange(
            pair.at[step, :, columns(sub)],
            far_in.at[step, :, columns(sub)],
            far_send,
            far_recv,
            step + (sub or 0),
            far,
        )

    for copy in loads:
        copy.start()
    for copy in weight_copies(0, 0):
        copy.start()
    greet((right, left, twin, far))
    for sub in range(SUBS):
        for way in range(2):
            ring(way, sub, 1, 0).start()
    loads[0].wait()

    def feed_tile(tile):
        slot = lax.rem(tile, 2)
        for copy in weight_copies(tile, slot):
            copy.wait()

        @pl.when(tile + 1 < tiles)
        def _():
            for copy in weight_copies(tile + 1, 1 - slot):
                copy.start()

        @pl.when(tile >= 2)
        def _():
            for copy in stage_copies(tile - 2, slot):
                copy.wait()

        cols = pl.ds(pl.multiple_of(tile * TILE, TILE), TILE)

        gate = jnp.dot(lhs[...], gate_tile[slot], preferred_element_type=jnp.float32)
        up = jnp.dot(lhs[...], up_tile[slot], preferred_element_type=jnp.float32)
        sigmoid = jax.nn.sigmoid(gate)
        silu = gate * sigmoid
        product[:, cols] = (silu * up).astype(jnp.bfloat16)
        slope_tile[slot] = (up * sigmoid * (1.0 + gate * (1.0 - sigmoid))).astype(jnp.bfloat16)
        silu_tile[slot] = silu.astype(jnp.bfloat16)

        for copy in stage_copies(tile, slot):
            copy.start()

    events = [(step, sub) for step in range(1, n) for sub in range(SUBS)]
    groups = 4
    for group in range(groups):
        pl.loop(group * tiles // groups, (group + 1) * tiles // groups)(feed_tile)
        serve(*events.pop(0))
    stores = [pltpu.make_async_copy(product, product_out, store_sem.at[0])]
    stores[0].start()
    loads[1].wait()

    def multiply(step, sub=None):
        part = slice(None) if sub is None else slice(sub * rows, (sub + 1) * rows)
        first = held[holder_of(index, -step, n), 0, part]
        second = held[holder_of(index, step, n), 1, part]
        rhs = jnp.concatenate([first, second], axis=0)
        contract = (((1,), (1,)), ((), ()))
        span = pl.ds(pl.multiple_of((1 - core) * half, half), half)
        twin_out[step, :, columns(sub)] = lax.dot_general(
            product[span, :], rhs, contract, preferred_element_type=jnp.float32
        ).astype(jnp.bfloat16)
        twin_copy(step, sub).start()
        span = pl.ds(pl.multiple_of(core * half, half), half)
        pair[step, :, columns(sub)] = lax.dot_general(
            product[span, :], rhs, contract, preferred_element_type=jnp.float32
        ).astype(jnp.bfloat16)

    def add_twin(step, sub=None):
        twin_copy(step, sub).wait_recv()
        cols = columns(sub)

        @pl.loop(0, half // 32, unroll=4)
        def _(tile):
            span = pl.ds(pl.multiple_of(tile * 32, 32), 32)
            total = pair[step, span, cols].astype(jnp.float32) + twin_in[
                step, span, cols
            ].astype(jnp.float32)
            pair[step, span, cols] = total.astype(jnp.bfloat16)

        far_copy(step, sub).start()

    def add_far(step):
        if step < n - 1:
            far_copy(step).wait_recv()
        else:
            for sub in range(SUBS):
                far_copy(step, sub).wait_recv()
        first = pl.multiple_of(holder_of(index, -step, n) * 2 * chunk, chunk)
        second = pl.multiple_of(holder_of(index, step, n) * 2 * chunk + chunk, chunk)

        @pl.loop(0, half // 32, unroll=4)
        def _(tile):
            span = pl.ds(pl.multiple_of(tile * 32, 32), 32)
            total = pair[step, span, :].astype(jnp.float32) + far_in[step, span, :].astype(
                jnp.float32
            )
            if step < n - 1:
                sides = total[:, :chunk], total[:, chunk:]
            else:
                sides = [
                    jnp.concatenate(
                        [
                            total[:, (2 * sub + way) * rows : (2 * sub + way + 1) * rows]
                            for sub in range(SUBS)
                        ],
                        axis=1,
                    )
                    for way in range(2)
                ]
            branch[span, pl.ds(first, chunk)] = sides[0]
            branch[span, pl.ds(second, chunk)] = sides[1]

    def serve_until(step, sub):
        while events and events[0] <= (step, sub):
            serve(*events.pop(0))

    for step in range(n - 1):
        serve_until(step, SUBS - 1)
        multiply(step)
        if step >= 1:
            if step <= 3:
                add_twin(step - 1)
            if step >= 3:
                add_twin(step)
            if step >= 2:
                add_far(step - 2)
        if step < 2 and events:
            serve(*events.pop(0))
    for sub in range(SUBS):
        serve_until(n - 1, sub)
        multiply(n - 1, sub)
        add_twin(n - 1, sub)
        if sub == 0:
            add_far(n - 3)
    stores.append(pltpu.make_async_copy(held, down_full, store_sem.at[1]))
    stores[1].start()
    add_far(n - 2)
    loads[2].wait()
    loads[3].wait()
    gain_sum[...] = jnp.zeros_like(gain_sum)
    add_far(n - 1)

    def finish(tile):
        span = pl.ds(pl.multiple_of(tile * 16, 16), 16)
        mixed = branch[span, :]
        scale = gains[...]
        inverse = lax.rsqrt(jnp.sum(mixed * mixed, axis=1, keepdims=True) / width + EPSILON)
        grad = upstream_buf[span, :].astype(jnp.float32)
        scaled = scale * grad
        mean = jnp.sum(scaled * mixed, axis=1, keepdims=True) / width
        normed = mixed * inverse
        d_buf[span, :] = (
            inverse * scaled - mixed * (inverse * inverse * inverse * mean)
        ).astype(jnp.bfloat16)
        block_buf[span, :] = (hidden_buf[span, :] + normed * scale).astype(jnp.bfloat16)
        terms = grad * normed
        gain_sum[...] += terms[:8] + terms[8:]

    def join(part, own):
        span = pl.ds(part * (half // 4), half // 4)
        if own:
            return pltpu.make_async_copy(d_buf.at[span], d_mlp.at[core, span], store_sem.at[3 + part])
        return pltpu.make_async_remote_copy(
            src_ref=d_buf.at[span],
            dst_ref=d_mlp.at[core, span],
            send_sem=join_send.at[part],
            recv_sem=join_recv.at[part],
            device_id=twin,
            device_id_type=MESH,
        )

    def joined(part):
        span = pl.ds(part * (half // 4), half // 4)
        target = d_mlp.at[1 - core, span]
        return pltpu.make_async_remote_copy(
            src_ref=target,
            dst_ref=target,
            send_sem=join_send.at[part],
            recv_sem=join_recv.at[part],
            device_id=twin,
            device_id_type=MESH,
        )

    for part in range(4):
        pl.loop(part * (half // 64), (part + 1) * (half // 64), unroll=2)(finish)
        join(part, False).start()
        join(part, True).start()
    stores.append(pltpu.make_async_copy(block_buf, block_half, store_sem.at[2]))
    stores[2].start()
    gain_grad[...] = jnp.sum(gain_sum[...], axis=0, keepdims=True)
    for part in range(4):
        joined(part).wait_recv()
        join(part, False).wait_send()
        join(part, True).wait()
    for copy in stores:
        copy.wait()
    for tile in (tiles - 2, tiles - 1):
        for copy in stage_copies(tile, tile % 2):
            copy.wait()
    for step in range(n + 1):
        name = (step, None) if step < n - 1 else (n - 1, step - n + 1)
        twin_copy(*name).wait_send()
        far_copy(*name).wait_send()
    for step in range(1, n):
        for sub in range(SUBS):
            for way in range(2):
                ring(way, sub, step, 0).wait_send()


def kernel_feed(hidden_low, gate_full, up_full, down_shard, hidden, upstream, gains, n):
    count, width = hidden_low.shape
    units = gate_full.shape[1]
    half = count // 2
    chunk = width // n // 2
    rows = chunk // SUBS
    low = jnp.bfloat16
    hbm = pl.BlockSpec(memory_space=pl.ANY)
    vmem = pl.BlockSpec(memory_space=pltpu.VMEM)
    dma = pltpu.SemaphoreType.DMA
    product, slope, silu, down_full, d_mlp, block, gain_grad = pl.pallas_call(
        functools.partial(feed_kernel, n),
        out_shape=(
            jax.ShapeDtypeStruct((count, units), low),
            jax.ShapeDtypeStruct((count, units), low),
            jax.ShapeDtypeStruct((count, units), low),
            jax.ShapeDtypeStruct((n, 2, chunk, units), low),
            jax.ShapeDtypeStruct((2, half, width), low),
            jax.ShapeDtypeStruct((half, width), low),
            jax.ShapeDtypeStruct((1, width), jnp.float32),
        ),
        in_specs=[hbm] * 6 + [vmem],
        out_specs=(hbm,) * 6 + (vmem,),
        scratch_shapes=[
            pltpu.VMEM((count, width), low),
            pltpu.VMEM((count, units), low),
            pltpu.VMEM((n, 2, chunk, units), low),
            pltpu.VMEM((2, width, TILE), low),
            pltpu.VMEM((2, width, TILE), low),
            pltpu.VMEM((2, count, TILE), low),
            pltpu.VMEM((2, count, TILE), low),
            pltpu.VMEM((n, half, 2 * chunk), low),
            pltpu.VMEM((n, half, 2 * chunk), low),
            pltpu.VMEM((n, half, 2 * chunk), low),
            pltpu.VMEM((n, half, 2 * chunk), low),
            pltpu.VMEM((half, width), jnp.float32),
            pltpu.VMEM((half, width), jnp.float32),
            pltpu.VMEM((half, width), low),
            pltpu.VMEM((half, width), low),
            pltpu.VMEM((half, width), low),
            pltpu.VMEM((8, width), jnp.float32),
            dma((2, SUBS, n - 1)),
            dma((2, SUBS, n - 1)),
            dma((n + 1,)),
            dma((n + 1,)),
            dma((n + 1,)),
            dma((n + 1,)),
            dma((4,)),
            dma((4,)),
            dma((4,)),
            dma((2, 2)),
            dma((2, 2)),
            dma((7,)),
        ],
        compiler_params=pltpu.CompilerParams(
            collective_id=2, has_side_effects=True, vmem_limit_bytes=58 * 2**20
        ),
    )(
        hidden_low,
        gate_full,
        up_full,
        down_shard,
        hidden,
        upstream,
        gains,
    )
    return (
        product,
        slope,
        silu,
        down_full.reshape(width, units),
        d_mlp.reshape(count, width),
        block,
        gain_grad,
    )


def back_kernel(
    n,
    d_mlp,
    product,
    down_full,
    gate_slope,
    silu_in,
    gate_full,
    up_full,
    hidden_low,
    block_half,
    out_down,
    d_hidden_out,
    d_gate_out,
    d_up_out,
    head_grads,
    block_out,
    d_out,
    prod,
    d_gate,
    d_up,
    down_tile,
    slope_tile,
    silu_tile,
    gate_tile,
    up_tile,
    hidden_tile,
    first,
    own,
    inbox,
    mixed,
    twin_in,
    pair,
    far_in,
    d_hidden,
    stage,
    ring_send,
    ring_recv,
    twin_send,
    twin_recv,
    far_send,
    far_recv,
    join_send,
    join_recv,
    load_sem,
    down_sem,
    weight_sem,
    hidden_sem,
    stage_sem,
    store_sem,
):
    index, core, right, left, twin, far = neighbours(n)
    side = d_out.shape[2]
    width, units = d_out.shape[3], prod.shape[3]
    pack = 2 * side
    half = d_hidden.shape[0]
    chunk = inbox.shape[3] * SUBS
    rows = chunk // SUBS
    tiles = units // TILE
    blocks = width // TILE
    left_side = (((0,), (0,)), ((), ()))
    right_side = (((1,), (1,)), ((), ()))

    def tile_span(tile):
        return pl.ds(pl.multiple_of(tile * TILE, TILE), TILE)

    def down_copies(group, tile, slot):
        cols = tile_span(tile)
        return (
            pltpu.make_async_copy(down_full.at[:, cols], down_tile.at[slot], down_sem.at[slot, 0]),
            pltpu.make_async_copy(
                gate_slope.at[:, group, :, cols], slope_tile.at[slot], down_sem.at[slot, 1]
            ),
            pltpu.make_async_copy(
                silu_in.at[:, group, :, cols], silu_tile.at[slot], down_sem.at[slot, 2]
            ),
        )

    def weight_copies(tile, slot):
        span = tile_span(tile)
        return (
            pltpu.make_async_copy(gate_full.at[span], gate_tile.at[slot], weight_sem.at[slot, 0]),
            pltpu.make_async_copy(up_full.at[span], up_tile.at[slot], weight_sem.at[slot, 1]),
        )

    def hidden_copy(group, way):
        owner = holder_of(index, 2 * way - 1, n)
        start = pl.multiple_of(owner * 2 * chunk + way * chunk, chunk)
        return pltpu.make_async_copy(
            hidden_low.at[:, group, :, pl.ds(start, chunk)],
            hidden_tile.at[group, :, :, pl.ds(way * chunk, chunk)],
            hidden_sem.at[group, way],
        )

    def stage_copy(which):
        return pltpu.make_async_copy(stage.at[which], head_grads.at[which], stage_sem.at[which])

    def block_copy(kind):
        if kind == 2:
            return pltpu.make_async_copy(block_half, block_out.at[core], store_sem.at[5])
        target = block_out.at[1 - core if kind else core]
        return exchange(target if kind else block_half, target, join_send, join_recv, 0, twin)

    def ring(way, sub, step):
        return pltpu.make_async_remote_copy(
            src_ref=first.at[way, pl.ds(sub * rows, rows)]
            if step == 1
            else inbox.at[step - 2, way, sub],
            dst_ref=inbox.at[step - 1, way, sub],
            send_sem=ring_send.at[way, sub, step - 1],
            recv_sem=ring_recv.at[way, sub, step - 1],
            device_id=left if way else right,
            device_id_type=MESH,
        )

    def grad_block(step):
        cols = []
        for way in range(2):
            owner = holder_of(index, (1 + step) * (2 * way - 1), n)
            start = pl.multiple_of(owner * 2 * chunk + way * chunk, chunk)
            cols.append(d_out[:, :, :, pl.ds(start, chunk)].reshape(2 * pack, chunk))
        block = lax.dot_general(
            jnp.concatenate(cols, axis=1),
            prod[...].reshape(2 * pack, units),
            left_side,
            preferred_element_type=jnp.float32,
        ).astype(jnp.bfloat16)
        target = first if step == 0 else own.at[step % 2]
        target[0] = block[:chunk]
        target[1] = block[chunk:]

    def serve(step, sub):
        for way in range(2):
            ring(way, sub, step).wait_recv()

            @pl.loop(0, rows // 16, unroll=2)
            def _(tile, way=way):
                near = pl.ds(pl.multiple_of(tile * 16, 16), 16)
                mine = pl.ds(pl.multiple_of(sub * rows + tile * 16, 16), 16)
                got = inbox[step - 1, way, sub, near, :]
                held = own[step % 2, way, mine, :]
                if step < n - 1:
                    inbox[step - 1, way, sub, near, :] = got + held
                else:
                    out_down[way, mine, :] = got.astype(jnp.float32) + held.astype(jnp.float32)

            if step < n - 1:
                ring(way, sub, step + 1).start()

    def twin_copy(turn):
        return exchange(
            mixed.at[turn % 4, 1 - core], twin_in.at[turn % 4], twin_send, twin_recv, turn, twin
        )

    def far_copy(turn):
        return exchange(pair.at[turn], far_in.at[turn], far_send, far_recv, turn, far)

    loads = []
    for group in range(2):
        loads += [
            pltpu.make_async_copy(d_mlp.at[:, group], d_out.at[group], load_sem.at[0, group]),
            pltpu.make_async_copy(product.at[:, group], prod.at[group], load_sem.at[1, group]),
        ]
    for copy in loads:
        copy.start()
    for turn in range(2):
        for copy in down_copies(0, turn, turn):
            copy.start()
        for copy in weight_copies(turn, turn):
            copy.start()
    greet((right, left, twin, far))
    for copy in loads:
        copy.wait()
    grad_block(0)
    for sub in range(SUBS):
        for way in range(2):
            ring(way, sub, 1).start()
    block_copy(0).start()
    block_copy(2).start()
    for group in range(2):
        for way in range(2):
            hidden_copy(group, way).start()
    grad_block(1)

    def product_tile(group, tile):
        turn = group * tiles + tile
        slot = lax.rem(turn, 3)
        for copy in down_copies(group, tile, slot):
            copy.wait()

        @pl.when(turn + 2 < 2 * tiles)
        def _():
            later = turn + 2
            for copy in down_copies(
                lax.div(later, tiles), lax.rem(later, tiles), lax.rem(later, 3)
            ):
                copy.start()

        cols = tile_span(tile)
        grad = jnp.dot(
            d_out[group].reshape(pack, width), down_tile[slot], preferred_element_type=jnp.float32
        )
        for target, factor in ((d_gate, slope_tile), (d_up, silu_tile)):
            scaled = grad * factor[slot].reshape(pack, TILE).astype(jnp.float32)
            target[group, :, :, cols] = scaled.astype(jnp.bfloat16).reshape(2, side, TILE)

    def input_tile(turn):
        group, tile = divmod(turn, blocks)
        slot = turn % 3
        for copy in weight_copies(tile, slot):
            copy.wait()
        if turn + 2 < 2 * blocks:
            for copy in weight_copies((tile + 2) % blocks, (turn + 2) % 3):
                copy.start()
        total = lax.dot_general(
            d_gate[group].reshape(pack, units),
            gate_tile[slot],
            right_side,
            preferred_element_type=jnp.float32,
        ) + lax.dot_general(
            d_up[group].reshape(pack, units),
            up_tile[slot],
            right_side,
            preferred_element_type=jnp.float32,
        )
        mixed[turn % 4] = total.astype(jnp.bfloat16).reshape(2, side, TILE)
        twin_copy(turn).start()

    def add_twin(turn):
        twin_copy(turn).wait_recv()

        @pl.loop(0, side // 32)
        def _(row):
            span = pl.ds(pl.multiple_of(row * 32, 32), 32)
            pair[turn, span, :] = mixed[turn % 4, core, span, :] + twin_in[turn % 4, span, :]

        far_copy(turn).start()
        twin_copy(turn).wait_send()

    def add_far(turn):
        group, tile = divmod(turn, blocks)
        far_copy(turn).wait_recv()

        @pl.loop(0, side // 32)
        def _(row):
            span = pl.ds(pl.multiple_of(row * 32, 32), 32)
            wide = pl.ds(pl.multiple_of(group * side + row * 32, 32), 32)
            d_hidden[wide, tile * TILE : (tile + 1) * TILE] = pair[turn, span, :].astype(
                jnp.float32
            ) + far_in[turn, span, :].astype(jnp.float32)

    def weight_block(which, source):
        block = lax.dot_general(
            hidden_tile[...].reshape(2 * pack, TILE),
            source[...].reshape(2 * pack, units),
            left_side,
            preferred_element_type=jnp.float32,
        ).astype(jnp.bfloat16)
        stage[which, 0] = block[:chunk]
        stage[which, 1] = block[chunk:]
        stage_copy(which).start()

    events = [(step, sub) for step in range(1, n) for sub in range(SUBS)]

    def next_event():
        if events:
            step, sub = events.pop(0)
            serve(step, sub)
            if sub == SUBS - 1 and step < n - 1:
                grad_block(step + 1)

    def product_group(group):
        pl.loop(0, tiles // 2)(functools.partial(product_tile, group))
        next_event()
        pl.loop(tiles // 2, tiles)(functools.partial(product_tile, group))
        next_event()

    def grad_store(group):
        return [
            pltpu.make_async_copy(
                source.at[group], target.at[:, group], store_sem.at[6 + 2 * place + group]
            )
            for place, (source, target) in enumerate(((d_gate, d_gate_out), (d_up, d_up_out)))
        ]

    def hidden_store(group):
        span = pl.ds(group * side, side)
        return pltpu.make_async_copy(
            d_hidden.at[span], d_hidden_out.at[span], store_sem.at[group]
        )

    for group in range(2):
        product_group(group)
        for copy in grad_store(group):
            copy.start()
        if group == 1:
            for turn in range(blocks - 3, blocks):
                add_far(turn)
        for turn in range(group * blocks, (group + 1) * blocks):
            input_tile(turn)
            if turn % blocks >= 1:
                add_twin(turn - 1)
            if turn % blocks >= 3:
                add_far(turn - 3)
            if turn % 2 == 1:
                next_event()
        add_twin((group + 1) * blocks - 1)
        if group == 1:
            hidden_store(0).start()
    for group in range(2):
        for way in range(2):
            hidden_copy(group, way).wait()
    weight_block(0, d_gate)
    add_far(2 * blocks - 3)
    next_event()
    weight_block(1, d_up)
    add_far(2 * blocks - 2)
    next_event()
    add_far(2 * blocks - 1)
    hidden_store(1).start()
    while events:
        next_event()
    for group in range(2):
        hidden_store(group).wait()
    for which in range(2):
        stage_copy(which).wait()
        for copy in grad_store(which):
            copy.wait()
    block_copy(0).wait_send()
    block_copy(1).wait_recv()
    block_copy(2).wait()
    for turn in range(2 * blocks):
        far_copy(turn).wait_send()
    for step in range(1, n):
        for sub in range(SUBS):
            for way in range(2):
                ring(way, sub, step).wait_send()


def kernel_back(
    d_mlp,
    product,
    down_full,
    gate_slope,
    silu,
    gate_full,
    up_full,
    hidden_low,
    block_half,
    n,
):
    count, width = d_mlp.shape
    units = product.shape[1]
    half = count // 2
    side = count // 4
    chunk = width // n // 2
    rows = chunk // SUBS
    blocks = width // TILE
    low = jnp.bfloat16
    full = jnp.float32
    hbm = pl.BlockSpec(memory_space=pl.ANY)
    vmem = pl.BlockSpec(memory_space=pltpu.VMEM)
    dma = pltpu.SemaphoreType.DMA
    shape = jax.ShapeDtypeStruct

    def cut(array):
        return array.reshape(2, 2, side, array.shape[1])

    outs = pl.pallas_call(
        functools.partial(back_kernel, n),
        out_shape=(
            shape((2, chunk, units), full),
            shape((half, width), full),
            shape((2, 2, side, units), low),
            shape((2, 2, side, units), low),
            shape((2, 2, chunk, units), low),
            shape((2, half, width), low),
        ),
        in_specs=[hbm] * 9,
        out_specs=(vmem,) + (hbm,) * 5,
        scratch_shapes=[
            pltpu.VMEM((2, 2, side, width), low),
            pltpu.VMEM((2, 2, side, units), low),
            pltpu.VMEM((2, 2, side, units), low),
            pltpu.VMEM((2, 2, side, units), low),
            pltpu.VMEM((3, width, TILE), low),
            pltpu.VMEM((3, 2, side, TILE), low),
            pltpu.VMEM((3, 2, side, TILE), low),
            pltpu.VMEM((3, TILE, units), low),
            pltpu.VMEM((3, TILE, units), low),
            pltpu.VMEM((2, 2, side, TILE), low),
            pltpu.VMEM((2, chunk, units), low),
            pltpu.VMEM((2, 2, chunk, units), low),
            pltpu.VMEM((n - 1, 2, SUBS, rows, units), low),
            pltpu.VMEM((4, 2, side, TILE), low),
            pltpu.VMEM((4, side, TILE), low),
            pltpu.VMEM((2 * blocks, side, TILE), low),
            pltpu.VMEM((2 * blocks, side, TILE), low),
            pltpu.VMEM((half, width), full),
            pltpu.VMEM((2, 2, chunk, units), low),
            dma((2, SUBS, n - 1)),
            dma((2, SUBS, n - 1)),
            dma((2 * blocks,)),
            dma((2 * blocks,)),
            dma((2 * blocks,)),
            dma((2 * blocks,)),
            dma((1,)),
            dma((1,)),
            dma((2, 2)),
            dma((3, 3)),
            dma((3, 2)),
            dma((2, 2)),
            dma((2,)),
            dma((10,)),
        ],
        compiler_params=pltpu.CompilerParams(
            collective_id=3, has_side_effects=True, vmem_limit_bytes=60 * 2**20
        ),
    )(
        cut(d_mlp),
        cut(product),
        down_full,
        cut(gate_slope),
        cut(silu),
        gate_full,
        up_full,
        cut(hidden_low),
        block_half,
    )
    out_down, d_hidden, d_gate, d_up, head_grads, block_out = outs
    return (
        out_down.reshape(2 * chunk, units),
        d_hidden,
        d_gate.reshape(count, units),
        d_up.reshape(count, units),
        head_grads,
        block_out.reshape(count, width),
    )


def detach_kernel(
    n,
    branch,
    upstream,
    attn_gain,
    attn_full,
    attended_in,
    query_rot_in,
    key_rot_in,
    value_in,
    query_raw_in,
    key_raw_in,
    tokens,
    d_hidden,
    head_grads,
    d_gate,
    d_up,
    hidden_low,
    totals,
    inverses,
    cosine,
    sine,
    doc_col,
    doc_row,
    query_gain,
    key_gain,
    out_gate,
    out_up,
    grad_attn,
    grad_tokens,
    query_gain_grad,
    key_gain_grad,
    attn_gain_grad,
    d_branch,
    branch_tile,
    output_tile,
    grad_tile,
    unit_tile,
    weight_tile,
    attended,
    query_rot,
    key_rot,
    value,
    query_raw,
    key_raw,
    d_attended,
    d_query_norm,
    d_key_norm,
    d_key_sum,
    d_value_sum,
    d_projected,
    own,
    inbox,
    total_buf,
    mixed,
    twin_in,
    pair,
    far_in,
    hidden_tile,
    upstream_tile,
    upstream_rows,
    gain_sum,
    stage_output,
    stage,
    stat,
    ring_send,
    ring_recv,
    stat_send,
    stat_recv,
    twin_send,
    twin_recv,
    far_send,
    far_recv,
    join_send,
    join_recv,
    whole_send,
    whole_recv,
    whole_sem,
    row_sem,
    unit_sem,
    grad_sem,
    branch_sem,
    load_sem,
    weight_sem,
    hidden_sem,
    upstream_sem,
    stage_sem,
    store_sem,
    out_sem,
):
    index, core, right, left, twin, far = neighbours(n)
    count, width = tokens.shape
    half = count // 2
    local = query_raw.shape[1]
    heads = local // HEAD_CHANNELS
    blocks = width // TILE
    chunk = inbox.shape[3]
    grads = (d_gate, d_up)
    part_cols = grad_tile.shape[2]
    parts_in = d_gate.shape[1] // part_cols
    outs = (out_gate, out_up)
    left_side = (((0,), (0,)), ((), ()))
    right_side = (((1,), (1,)), ((), ()))
    factor = 1.0 / math.sqrt(HEAD_CHANNELS)

    def ring(way, unit, step):
        first = head_grads.at[unit, way]
        return pltpu.make_async_remote_copy(
            src_ref=first if step == 1 else inbox.at[step - 2, way, unit],
            dst_ref=inbox.at[step - 1, way, unit],
            send_sem=ring_send.at[way, unit, step - 1],
            recv_sem=ring_recv.at[way, unit, step - 1],
            device_id=left if way else right,
            device_id_type=MESH,
        )

    events = [(step, unit) for step in range(1, n) for unit in range(2)]

    def unit_copy(step, way):
        owner = holder_of(index, (1 + step) * (2 * way - 1), n)
        start = pl.multiple_of(owner * 2 * chunk + way * chunk, chunk)
        return pltpu.make_async_copy(
            hidden_low.at[:, pl.ds(start, chunk)],
            unit_tile.at[step % 2, :, pl.ds(way * chunk, chunk)],
            unit_sem.at[step % 2, way],
        )

    def grad_copy(unit, part, slot):
        cols = pl.ds(pl.multiple_of(part * part_cols, part_cols), part_cols)
        return pltpu.make_async_copy(
            grads[unit].at[:, cols], grad_tile.at[slot], grad_sem.at[slot]
        )

    def grad_block(step, unit):
        if unit == 0:
            for way in range(2):
                unit_copy(step, way).wait()
                if step < n - 1:
                    unit_copy(step + 1, way).start()

        base = 2 * (step - 1) + unit
        final = base == 2 * n - 3

        @pl.loop(0, parts_in)
        def _(part):
            slot = lax.rem(base * parts_in + part, 3)
            spare = lax.rem(slot + 2, 3)
            grad_copy(unit, part, slot).wait()

            @pl.when(part + 2 < parts_in)
            def _():
                grad_copy(unit, part + 2, spare).start()

            if not final:

                @pl.when(part + 2 >= parts_in)
                def _():
                    grad_copy(1 - unit, part + 2 - parts_in, spare).start()

            cols = pl.ds(pl.multiple_of(part * part_cols, part_cols), part_cols)
            block = lax.dot_general(
                unit_tile[step % 2],
                grad_tile[slot],
                left_side,
                preferred_element_type=jnp.float32,
            ).astype(jnp.bfloat16)
            own[unit, 0, :, cols] = block[:chunk]
            own[unit, 1, :, cols] = block[chunk:]

    def out_copy(unit):
        return pltpu.make_async_copy(total_buf, outs[unit], out_sem.at[unit])

    def serve():
        step, unit = events.pop(0)
        if step == n - 1 and unit == 1:
            out_copy(0).wait()
        for way in range(2):
            ring(way, unit, step).wait_recv()

            @pl.loop(0, chunk // 16, unroll=2)
            def _(tile, way=way):
                span = pl.ds(pl.multiple_of(tile * 16, 16), 16)
                got = inbox[step - 1, way, unit, span, :]
                held = own[unit, way, span, :]
                if step < n - 1:
                    inbox[step - 1, way, unit, span, :] = got + held
                else:
                    total_buf[way, span, :] = got.astype(jnp.float32) + held.astype(jnp.float32)

            if step < n - 1:
                ring(way, unit, step + 1).start()
        if step < n - 1:
            grad_block(step + 1, unit)
        else:
            out_copy(unit).start()

    greet((right, left, twin, far))
    for unit in range(2):
        for way in range(2):
            ring(way, unit, 1).start()
    for way in range(2):
        unit_copy(1, way).start()
    for part in range(2):
        grad_copy(0, part, part).start()

    def weight_copy(tile, slot):
        return pltpu.make_async_copy(
            attn_full.at[pl.ds(tile * TILE, TILE), pl.ds(0, 3 * local)],
            weight_tile.at[slot],
            weight_sem.at[slot],
        )

    def hidden_copies(tile, slot):
        cols = pl.ds(tile * TILE, TILE)
        mine = pl.ds(pl.multiple_of(core * half, half), half)
        return (
            pltpu.make_async_copy(
                d_hidden.at[:, cols], hidden_tile.at[slot], hidden_sem.at[slot]
            ),
            pltpu.make_async_copy(
                upstream.at[mine, cols], upstream_tile.at[slot], upstream_sem.at[slot]
            ),
        )

    loads = [
        pltpu.make_async_copy(source, target, load_sem.at[place])
        for place, (source, target) in enumerate(
            (
                (attended_in, attended),
                (query_rot_in, query_rot),
                (key_rot_in, key_rot),
                (value_in, value),
                (query_raw_in, query_raw),
                (key_raw_in, key_raw),
            )
        )
    ]

    def branch_copies(tile, source):
        cols = pl.ds(tile * TILE, TILE)
        slot = tile % 2
        copies = [
            pltpu.make_async_copy(source.at[:, cols], branch_tile.at[slot], branch_sem.at[slot, 0])
        ]
        if source is d_branch:
            copies.append(
                pltpu.make_async_copy(
                    attn_full.at[cols, pl.ds(3 * local, local)],
                    output_tile.at[slot],
                    branch_sem.at[slot, 1],
                )
            )
        return copies

    def output_copy(tile):
        return pltpu.make_async_copy(
            stage_output.at[tile % 2],
            grad_attn.at[pl.ds(tile * TILE, TILE), pl.ds(3 * local, local)],
            stage_sem.at[0, tile % 2],
        )

    deep = half // 4

    def row_copies(part):
        span = pl.ds(part * deep, deep)
        mine = pl.ds(pl.multiple_of(core * half + part * deep, deep), deep)
        return [
            pltpu.make_async_copy(d_hidden.at[span], total_buf.at[0], row_sem.at[0]),
            pltpu.make_async_copy(branch.at[span], total_buf.at[1], row_sem.at[1]),
            pltpu.make_async_copy(upstream.at[mine], upstream_rows, row_sem.at[2]),
        ]

    def finish(part, tile):
        near = pl.ds(pl.multiple_of(tile * 16, 16), 16)
        total = total_buf[0, near, :] + upstream_rows[near, :].astype(jnp.float32)
        mix = total_buf[1, near, :]
        inverse = lax.rsqrt(jnp.sum(mix * mix, axis=1, keepdims=True) / width + EPSILON)
        scaled = attn_gain[...] * total
        mean = jnp.sum(scaled * mix, axis=1, keepdims=True) / width
        grad = (inverse * scaled - mix * (inverse * inverse * inverse * mean)).astype(
            jnp.bfloat16
        )
        for block in range(blocks):
            spot = pl.multiple_of((block % 2) * half + part * deep + tile * 16, 16)
            mixed[block // 2, pl.ds(spot, 16), :] = grad[:, block * TILE : (block + 1) * TILE]
        terms = total * mix * inverse
        gain_sum[...] += terms[:8] + terms[8:]

    def whole_copy(block, kind):
        cols = pl.ds(block * TILE, TILE)
        source = mixed.at[block // 2, pl.ds((block % 2) * half, half)]
        keeper = 1 - core if kind == 1 else core
        target = d_branch.at[pl.ds(pl.multiple_of(keeper * half, half), half), cols]
        if kind == 2:
            return pltpu.make_async_copy(source, target, whole_sem.at[block])
        return exchange(
            target if kind else source, target, whole_send, whole_recv, block, twin
        )

    for copy in row_copies(0) + loads:
        copy.start()
    gain_sum[...] = jnp.zeros_like(gain_sum)
    grad_block(1, 0)
    grad_block(1, 1)
    for part in range(4):
        for copy in row_copies(part):
            copy.wait()
        pl.loop(0, deep // 16)(functools.partial(finish, part))
        if part < 3:
            for copy in row_copies(part + 1):
                copy.start()
        if part == 1:
            serve()
    for block in range(blocks):
        whole_copy(block, 0).start()
        whole_copy(block, 2).start()
    attn_gain_grad[...] = jnp.sum(gain_sum[...], axis=0, keepdims=True)
    for block in range(blocks):
        whole_copy(block, 1).wait_recv()
        whole_copy(block, 0).wait_send()
        whole_copy(block, 2).wait()
    for copy in branch_copies(0, d_branch):
        copy.start()
    loads[0].wait()
    for tile in range(blocks):
        for copy in branch_copies(tile, d_branch):
            copy.wait()
        if tile + 1 < blocks:
            for copy in branch_copies(tile + 1, d_branch):
                copy.start()
        product = jnp.dot(
            branch_tile[tile % 2], output_tile[tile % 2], preferred_element_type=jnp.float32
        )
        if tile == 0:
            d_query_norm[...] = product
        else:
            d_query_norm[...] += product
        if tile >= 2:
            output_copy(tile - 2).wait()
        stage_output[tile % 2] = lax.dot_general(
            branch_tile[tile % 2],
            attended[...],
            left_side,
            preferred_element_type=jnp.float32,
        ).astype(jnp.bfloat16)
        output_copy(tile).start()
    d_attended[...] = d_query_norm[...].astype(jnp.bfloat16)
    branch_copies(0, tokens)[0].start()
    weight_copy(0, 0).start()
    for copy in loads[1:]:
        copy.wait()
    serve()

    def unturned(vectors, span):
        return vectors * cosine[span, :] - pltpu.roll(vectors, HEAD_CHANNELS // 2, 1) * sine[span, :]

    def head_backward(head):
        cols = pl.ds(pl.multiple_of(head * HEAD_CHANNELS, HEAD_CHANNELS), HEAD_CHANNELS)
        lane = lax.broadcasted_iota(jnp.int32, (BLOCK, 128), 1)
        for block in reversed(range(count // BLOCK)):
            span = slice(block * BLOCK, (block + 1) * BLOCK)
            length = (block + 1) * BLOCK
            query = query_rot[span, cols]
            key = key_rot[:length, cols]
            grad = d_attended[span, cols]
            scores = masked_scores(query, key, doc_col, doc_row, block)
            total = jnp.sum(jnp.where(lane == head, totals[span, :], 0.0), axis=1, keepdims=True)
            powers = jnp.exp(scores - total)
            d_powers = lax.dot_general(
                grad, value[:length, cols], right_side, preferred_element_type=jnp.float32
            )
            correction = jnp.sum(d_powers * powers, axis=1, keepdims=True)
            d_scores = (powers * (d_powers - correction)).astype(jnp.bfloat16)
            rounded = powers.astype(jnp.bfloat16)
            d_query = jnp.dot(d_scores, key, preferred_element_type=jnp.float32) * factor
            d_query_norm[span, cols] = unturned(d_query, span)
            d_key = lax.dot_general(
                d_scores, query, left_side, preferred_element_type=jnp.float32
            )
            d_value = lax.dot_general(
                rounded, grad, left_side, preferred_element_type=jnp.float32
            )
            if length == count:
                d_key_sum[...] = d_key
                d_value_sum[...] = d_value
            else:
                d_key_sum[:length, :] += d_key
                d_value_sum[:length, :] += d_value
        d_key_norm[:, cols] = unturned(d_key_sum[...] * factor, slice(None))
        start = pl.multiple_of(2 * local + head * HEAD_CHANNELS, HEAD_CHANNELS)
        d_projected[:, pl.ds(start, HEAD_CHANNELS)] = d_value_sum[...].astype(jnp.bfloat16)

    pl.loop(0, heads // 2)(head_backward)
    serve()
    pl.loop(heads // 2, heads)(head_backward)
    serve()
    parts = []
    for place, (norm, raw, gain, gain_grad) in enumerate(
        (
            (d_query_norm, query_raw, query_gain, query_gain_grad),
            (d_key_norm, key_raw, key_gain, key_gain_grad),
        )
    ):
        dots = jnp.zeros((count, HEAD_CHANNELS), jnp.float32)
        for head in range(heads):
            cols = slice(head * HEAD_CHANNELS, (head + 1) * HEAD_CHANNELS)
            both = norm[:, cols] * raw[:, cols]
            gain_grad[:, cols] = jnp.sum(
                both * inverses[:, place : place + 1], axis=0, keepdims=True
            )
            dots = dots + both * gain[:, cols]
        parts.append(jnp.sum(dots, axis=1, keepdims=True))
    stat[0] = columns_to_rows(parts, count)
    first = exchange(stat.at[0], stat.at[1], stat_send, stat_recv, 0, twin)
    first.start()
    first.wait()
    stat[2] = stat[0] + stat[1]
    second = exchange(stat.at[2], stat.at[3], stat_send, stat_recv, 1, far)
    second.start()
    serve()
    second.wait()
    inner = d_key_sum
    inner[...] = rows_to_columns(stat[2] + stat[3]) / width

    @pl.loop(0, heads)
    def _(head):
        cols = pl.ds(pl.multiple_of(head * HEAD_CHANNELS, HEAD_CHANNELS), HEAD_CHANNELS)
        for place, (norm, raw, gain) in enumerate(
            ((d_query_norm, query_raw, query_gain), (d_key_norm, key_raw, key_gain))
        ):
            inverse = inverses[:, place : place + 1]
            cube = inverse * inverse * inverse * inner[:, place : place + 1]
            start = pl.multiple_of(place * local + head * HEAD_CHANNELS, HEAD_CHANNELS)
            d_projected[:, pl.ds(start, HEAD_CHANNELS)] = (
                norm[:, cols] * inverse * gain[:, cols] - raw[:, cols] * cube
            ).astype(jnp.bfloat16)

    def twin_copy(tile):
        span = pl.ds(pl.multiple_of((1 - core) * half, half), half)
        return exchange(
            mixed.at[tile % 4, span], twin_in.at[tile % 4], twin_send, twin_recv, tile, twin
        )

    def far_copy(tile):
        return exchange(pair.at[tile], far_in.at[tile], far_send, far_recv, tile, far)

    def token_tile(tile):
        slot = tile % 2
        weight_copy(tile, slot).wait()
        if tile + 1 < blocks:
            weight_copy(tile + 1, 1 - slot).start()
        mixed[tile % 4] = lax.dot_general(
            d_projected[...], weight_tile[slot], right_side, preferred_element_type=jnp.float32
        ).astype(jnp.bfloat16)
        twin_copy(tile).start()

    def add_twin(tile):
        twin_copy(tile).wait_recv()

        @pl.loop(0, half // 32)
        def _(row):
            span = pl.ds(pl.multiple_of(row * 32, 32), 32)
            mine = pl.ds(pl.multiple_of(core * half + row * 32, 32), 32)
            pair[tile, span, :] = mixed[tile % 4, mine, :] + twin_in[tile % 4, span, :]

        far_copy(tile).start()
        twin_copy(tile).wait_send()

    def join(tile, kind):
        cols = pl.ds(tile * TILE, TILE)
        if kind == 2:
            return pltpu.make_async_copy(
                pair.at[tile], grad_tokens.at[core, :, cols], store_sem.at[tile]
            )
        target = grad_tokens.at[1 - core if kind else core, :, cols]
        return exchange(
            target if kind else pair.at[tile], target, join_send, join_recv, tile, twin
        )

    def add_far(tile):
        slot = tile % 2
        for copy in hidden_copies(tile, slot):
            copy.wait()
        if tile + 1 < blocks:
            for copy in hidden_copies(tile + 1, 1 - slot):
                copy.start()
        far_copy(tile).wait()

        @pl.loop(0, half // 32)
        def _(row):
            span = pl.ds(pl.multiple_of(row * 32, 32), 32)
            total = (
                pair[tile, span, :].astype(jnp.float32)
                + far_in[tile, span, :].astype(jnp.float32)
                + hidden_tile[slot, span, :]
                + upstream_tile[slot, span, :].astype(jnp.float32)
            )
            pair[tile, span, :] = total.astype(jnp.bfloat16)

        join(tile, 0).start()
        join(tile, 2).start()

    def stage_copy(tile):
        return pltpu.make_async_copy(
            stage.at[tile % 2],
            grad_attn.at[pl.ds(tile * TILE, TILE), pl.ds(0, 3 * local)],
            stage_sem.at[1, tile % 2],
        )

    def weight_grad(tile):
        if tile >= 2:
            stage_copy(tile - 2).wait()
        branch_copies(tile, tokens)[0].wait()
        if tile + 1 < blocks:
            branch_copies(tile + 1, tokens)[0].start()
        stage[tile % 2] = lax.dot_general(
            branch_tile[tile % 2],
            d_projected[...],
            left_side,
            preferred_element_type=jnp.float32,
        ).astype(jnp.bfloat16)
        stage_copy(tile).start()

    for copy in hidden_copies(0, 0):
        copy.start()
    for tile in range(blocks):
        token_tile(tile)
        if tile >= 1:
            add_twin(tile - 1)
        if tile == blocks // 2 - 1:
            serve()
    add_twin(blocks - 1)
    serve()
    for tile in range(blocks):
        weight_grad(tile)
        add_far(tile)
        if tile % 2 == 1:
            serve()
    for tile in (blocks - 2, blocks - 1):
        output_copy(tile).wait()
        stage_copy(tile).wait()
    while events:
        serve()
    out_copy(1).wait()
    for tile in range(blocks):
        join(tile, 1).wait_recv()
        join(tile, 0).wait_send()
        join(tile, 2).wait()
    for step in range(1, n):
        for unit in range(2):
            for way in range(2):
                ring(way, unit, step).wait_send()


def kernel_detach(
    branch,
    upstream,
    attn_gain,
    attn_full,
    attended,
    query_rot,
    key_rot,
    value,
    query_raw,
    key_raw,
    tokens,
    d_hidden,
    head_grads,
    d_gate,
    d_up,
    hidden_low,
    totals,
    inverses,
    cosine,
    sine,
    doc_col,
    doc_ids,
    query_gain,
    key_gain,
    n,
):
    count, width = tokens.shape
    local = query_gain.shape[1]
    units = d_gate.shape[1]
    half = count // 2
    chunk = width // n // 2
    blocks = width // TILE
    low = jnp.bfloat16
    full = jnp.float32
    hbm = pl.BlockSpec(memory_space=pl.ANY)
    vmem = pl.BlockSpec(memory_space=pltpu.VMEM)
    dma = pltpu.SemaphoreType.DMA
    shape = jax.ShapeDtypeStruct
    outs = pl.pallas_call(
        functools.partial(detach_kernel, n),
        out_shape=(
            shape((2, chunk, units), full),
            shape((2, chunk, units), full),
            shape((width, 4 * local), low),
            shape((2, half, width), low),
            shape((1, local), full),
            shape((1, local), full),
            shape((1, width), full),
            shape((count, width), low),
        ),
        in_specs=[hbm] * 2 + [vmem] + [hbm] * 13 + [vmem] * 8,
        out_specs=(hbm,) * 4 + (vmem,) * 3 + (hbm,),
        scratch_shapes=[
            pltpu.VMEM((2, count, TILE), low),
            pltpu.VMEM((2, TILE, local), low),
            pltpu.VMEM((3, count, 2 * TILE), low),
            pltpu.VMEM((2, count, TILE), low),
            pltpu.VMEM((2, TILE, 3 * local), low),
            pltpu.VMEM((count, local), low),
            pltpu.VMEM((count, local), low),
            pltpu.VMEM((count, local), low),
            pltpu.VMEM((count, local), low),
            pltpu.VMEM((count, local), full),
            pltpu.VMEM((count, local), full),
            pltpu.VMEM((count, local), low),
            pltpu.VMEM((count, local), full),
            pltpu.VMEM((count, local), full),
            pltpu.VMEM((count, HEAD_CHANNELS), full),
            pltpu.VMEM((count, HEAD_CHANNELS), full),
            pltpu.VMEM((count, 3 * local), low),
            pltpu.VMEM((2, 2, chunk, units), low),
            pltpu.VMEM((n - 1, 2, 2, chunk, units), low),
            pltpu.VMEM((2, chunk, units), full),
            pltpu.VMEM((4, count, TILE), low),
            pltpu.VMEM((4, half, TILE), low),
            pltpu.VMEM((blocks, half, TILE), low),
            pltpu.VMEM((blocks, half, TILE), low),
            pltpu.VMEM((2, half, TILE), full),
            pltpu.VMEM((2, half, TILE), low),
            pltpu.VMEM((half // 4, width), low),
            pltpu.VMEM((8, width), full),
            pltpu.VMEM((2, TILE, local), low),
            pltpu.VMEM((2, TILE, 3 * local), low),
            pltpu.VMEM((4, 8, count), full),
            dma((2, 2, n - 1)),
            dma((2, 2, n - 1)),
            dma((2,)),
            dma((2,)),
            dma((blocks,)),
            dma((blocks,)),
            dma((blocks,)),
            dma((blocks,)),
            dma((blocks,)),
            dma((blocks,)),
            dma((blocks,)),
            dma((blocks,)),
            dma((blocks,)),
            dma((3,)),
            dma((2, 2)),
            dma((3,)),
            dma((2, 2)),
            dma((6,)),
            dma((2,)),
            dma((2,)),
            dma((2,)),
            dma((2, 2)),
            dma((blocks,)),
            dma((2,)),
        ],
        compiler_params=pltpu.CompilerParams(
            collective_id=5, has_side_effects=True, vmem_limit_bytes=60 * 2**20
        ),
    )(
        branch,
        upstream,
        attn_gain,
        attn_full,
        attended,
        query_rot,
        key_rot,
        value,
        query_raw,
        key_raw,
        tokens,
        d_hidden,
        head_grads,
        d_gate,
        d_up,
        hidden_low,
        totals,
        inverses,
        cosine,
        sine,
        doc_col,
        doc_ids.reshape(1, count),
        query_gain,
        key_gain,
    )
    return (
        outs[0].reshape(2 * chunk, units),
        outs[1].reshape(2 * chunk, units),
        outs[2],
        outs[3].reshape(count, width),
        outs[4],
        outs[5],
        outs[6],
    )


def fused_layer(
    n,
    tokens,
    doc_ids,
    q_weight,
    k_weight,
    v_weight,
    o_weight,
    q_gain,
    k_gain,
    attn_gain,
    gate_weight,
    up_weight,
    down_weight,
    mlp_gain,
    cotangent,
):
    index = lax.axis_index("dp")
    heads, channels = q_gain.shape
    small = jnp.concatenate(
        [
            q_gain,
            k_gain,
            jnp.zeros((SMALL - 2 * heads, channels), q_gain.dtype),
        ],
        axis=0,
    )
    small = lax.dynamic_update_slice(
        jnp.zeros((SMALL, HEAD_CHANNELS), q_gain.dtype), small, (0, index * channels)
    )
    small = lax.dynamic_update_slice(
        small, jnp.concatenate([attn_gain, mlp_gain]).reshape(4, 128), (2 * heads, 0)
    )
    frequency = jnp.exp(
        jnp.arange(HEAD_CHANNELS // 2, dtype=jnp.float32)
        * (-2.0 * math.log(ROPE_BASE) / HEAD_CHANNELS)
    )
    frequency = jnp.concatenate([frequency, frequency])[None, :]
    (
        attn_full,
        query_gain,
        key_gain,
        attn_gains,
        mlp_gains,
        cosine,
        sine,
        doc_col,
        down_shard,
    ) = kernel_gather(
        q_weight, k_weight, v_weight, o_weight, small, doc_ids, frequency, down_weight, n
    )
    (
        gate_full,
        up_full,
        query_raw,
        key_raw,
        query_rot,
        key_rot,
        value,
        attended,
        totals,
        inverses,
        branch,
        hidden_state,
        hidden_low,
    ) = kernel_attend(
        tokens,
        attn_full,
        gate_weight,
        up_weight,
        cosine,
        sine,
        doc_col,
        doc_ids,
        query_gain,
        key_gain,
        attn_gains,
        n,
    )
    product, gate_slope, silu, down_full, d_mlp, block_half, mlp_row = kernel_feed(
        hidden_low, gate_full, up_full, down_shard, hidden_state, cotangent, mlp_gains, n
    )
    out_down, d_hidden, d_gate, d_up, head_grads, block_out = kernel_back(
        d_mlp,
        product,
        down_full,
        gate_slope,
        silu,
        gate_full,
        up_full,
        hidden_low,
        block_half,
        n,
    )
    out_gate, out_up, grad_attn, grad_tokens, query_row, key_row, attn_row = kernel_detach(
        branch,
        cotangent,
        attn_gains,
        attn_full,
        attended,
        query_rot,
        key_rot,
        value,
        query_raw,
        key_raw,
        tokens,
        d_hidden,
        head_grads,
        d_gate,
        d_up,
        hidden_low,
        totals,
        inverses,
        cosine,
        sine,
        doc_col,
        doc_ids,
        query_gain,
        key_gain,
        n,
    )
    out_query, out_key, out_value, out_output, summed = kernel_scatter(
        grad_attn, query_row, key_row, attn_row, mlp_row, n
    )
    lanes = lax.dynamic_slice(summed, (0, index * channels), (2 * heads, channels))
    return (
        block_out,
        grad_tokens,
        out_query,
        out_key,
        out_value,
        out_output,
        lanes[:heads],
        lanes[heads:],
        summed[2 * heads : 2 * heads + 2].reshape(-1),
        out_gate,
        out_up,
        out_down.T,
        summed[2 * heads + 2 : 2 * heads + 4].reshape(-1),
    )


def solution(mesh):
    in_specs = (
        P("dp", None),
        P("dp"),
        P("dp", "mp"),
        P("dp", "mp"),
        P("dp", "mp"),
        P("mp", "dp"),
        P("mp", "dp"),
        P("mp", "dp"),
        P("dp"),
        P("dp", "mp"),
        P("dp", "mp"),
        P("mp", "dp"),
        P("dp"),
        P("dp", None),
    )
    out_specs = (
        P("dp", None),
        P("dp", None),
        P("dp", "mp"),
        P("dp", "mp"),
        P("dp", "mp"),
        P("mp", "dp"),
        P("mp", "dp"),
        P("mp", "dp"),
        P("dp"),
        P("dp", "mp"),
        P("dp", "mp"),
        P("mp", "dp"),
        P("dp"),
    )
    n, m = mesh.shape["dp"], mesh.shape["mp"]

    def on_device(*arrays):
        if (n, m, arrays[0].shape[0]) == (RING, 4, SEQ_LEN):
            return fused_layer(n, *arrays)
        return plain_layer(*arrays)

    return jax.shard_map(
        on_device, mesh=mesh, in_specs=in_specs, out_specs=out_specs, check_vma=False
    )
```
